32 devices in a mesh: dp: 4 (over y, core), ctx: 8 (over z, x).
Axes of the slice: x: 2, y: 2, z: 4, core: 2. Of those that a mesh axis runs over, the one named last changes fastest.
Arguments:
- inputs: bfloat16 [8, 1024, 768], P('dp', 'ctx'), may hold values from -6 to 6
- out_grad: bfloat16 [8, 1024, 768], P('dp', 'ctx'), may hold values from -6 to 6
- lengths: int32 [8], P('dp'), may hold values from 256 to 1024, as said below
- token_types: int32 [8, 1024], P('dp', 'ctx'), may hold values from 0 to 1
- query_weight: bfloat16 [768, 768], P(('dp', 'ctx')), may hold values from -0.21875 to 0.21875
- key_weight: bfloat16 [768, 768], P(('dp', 'ctx')), may hold values from -0.21875 to 0.21875
- value_weight: bfloat16 [768, 768], P(('dp', 'ctx')), may hold values from -0.21875 to 0.21875
- value_bias: bfloat16 [768], P(('dp', 'ctx')), may hold values from -1.796875 to 1.796875
- position_weight: bfloat16 [768, 768], P(('dp', 'ctx')), may hold values from -0.21875 to 0.21875
- content_bias: bfloat16 [768], P(('dp', 'ctx')), may hold values from -0.8984375 to 0.8984375
- position_bias: bfloat16 [768], P(('dp', 'ctx')), may hold values from -0.8984375 to 0.8984375
- type_bias: bfloat16 [768], P(('dp', 'ctx')), may hold values from -0.8984375 to 0.8984375
- type_embed: bfloat16 [2, 768], P(None, ('dp', 'ctx')), may hold values from -3 to 3
- output_weight: bfloat16 [768, 768], P(('dp', 'ctx')), may hold values from -0.875 to 0.875
- output_bias: bfloat16 [768], P(('dp', 'ctx')), may hold values from -1.796875 to 1.796875
- first_gain: bfloat16 [768], P(('dp', 'ctx')), may hold values from 0.5 to 1.5
- first_shift: bfloat16 [768], P(('dp', 'ctx')), may hold values from -1.796875 to 1.796875
- inner_weight: bfloat16 [768, 3072], P(('dp', 'ctx')), may hold values from -0.21875 to 0.21875
- inner_bias: bfloat16 [3072], P(('dp', 'ctx')), may hold values from -1.796875 to 1.796875
- outer_weight: bfloat16 [3072, 768], P(('dp', 'ctx')), may hold values from -0.109375 to 0.109375
- outer_bias: bfloat16 [768], P(('dp', 'ctx')), may hold values from -1.796875 to 1.796875
- second_gain: bfloat16 [768], P(('dp', 'ctx')), may hold values from 0.5 to 1.5
- second_shift: bfloat16 [768], P(('dp', 'ctx')), may hold values from -1.796875 to 1.796875
Outputs:
- output: bfloat16 [8, 1024, 768], P('dp', 'ctx')
- input_grad: bfloat16 [8, 1024, 768], P('dp', 'ctx')
- query_weight_grad: float32 [768, 768], P(('dp', 'ctx'))
- key_weight_grad: float32 [768, 768], P(('dp', 'ctx'))
- value_weight_grad: float32 [768, 768], P(('dp', 'ctx'))
- value_bias_grad: float32 [768], P(('dp', 'ctx'))
- position_weight_grad: float32 [768, 768], P(('dp', 'ctx'))
- content_bias_grad: float32 [768], P(('dp', 'ctx'))
- position_bias_grad: float32 [768], P(('dp', 'ctx'))
- type_bias_grad: float32 [768], P(('dp', 'ctx'))
- type_embed_grad: float32 [2, 768], P(None, ('dp', 'ctx'))
- output_weight_grad: float32 [768, 768], P(('dp', 'ctx'))
- output_bias_grad: float32 [768], P(('dp', 'ctx'))
- first_gain_grad: float32 [768], P(('dp', 'ctx'))
- first_shift_grad: float32 [768], P(('dp', 'ctx'))
- inner_weight_grad: float32 [768, 3072], P(('dp', 'ctx'))
- inner_bias_grad: float32 [3072], P(('dp', 'ctx'))
- outer_weight_grad: float32 [3072, 768], P(('dp', 'ctx'))
- outer_bias_grad: float32 [768], P(('dp', 'ctx'))
- second_gain_grad: float32 [768], P(('dp', 'ctx'))
- second_shift_grad: float32 [768], P(('dp', 'ctx'))
- mean_squares: float32 [8, 3], P('dp')
The draws below stay inside these ranges and needn't reach their ends.
Inputs may be any that keep to these rules, and one draw needn't show every extreme that they name: Sequence s holds lengths[s] valid tokens in its first slots; sequence 0 is full.
All inputs are finite; a program needn't handle non-finite values.
Results may differ from the reference program's by a relative error of at most 0.038.
Values may be sent and summed in bfloat16 or wider, within the bound.
No kernel may reach another device: no remote copies, remote signals or barrier semaphores. Data moves between devices by JAX's collectives and lax.ppermute only.
A program may use at most 320 MiB of HBM per device.

```python
import jax
import jax.numpy as jnp
from jax import lax

D = 768
H = 12
DH = 64
FF = 3072
KEY_BLOCK = 512
SEQ_LEN = 1024
SEQS = 8


def draw_lengths(key, part):
    values = jax.random.randint(key, (SEQS,), SEQ_LEN // 4, SEQ_LEN + 1, dtype=jnp.int32)
    return values.at[0].set(SEQ_LEN)


def touch_ends(values, own_key, low, largest):
    longest = values.shape.index(max(values.shape))
    spots = []
    for shift in (0, 1):
        where = [jax.random.randint(jax.random.fold_in(own_key, axis), (), 0, length) for axis, length in enumerate(values.shape)]
        where[longest] = (where[longest] + shift) % values.shape[longest]
        spots.append(tuple(where))
    return values.at[spots[0]].set(low).at[spots[1]].set(largest)


def block_levels(key, extent, shards, low, top_value):
    gain, own = 1.0, jax.random.fold_in(key, 6)
    for axis_at, shards_of in shards:
        steps = jnp.exp(jax.random.uniform(jax.random.fold_in(own, axis_at), (shards_of,), jnp.float32, low / len(shards), top_value / len(shards)))
        gain = gain * jnp.repeat(steps, extent[axis_at] // shards_of).reshape([-1 if axis == axis_at else 1 for axis in range(len(extent))])
    return gain


def normal_values(own_key, dims, deviation, limit, pieces=(), kind=jnp.bfloat16):
    entries = jax.random.normal(own_key, dims, jnp.float32) * deviation
    if len(pieces) > 0:
        entries = block_levels(own_key, dims, pieces, -0.22, 0.18) * entries
    return jnp.clip(entries, min=-limit, max=limit).astype(kind)


def setup_inputs(seed: int = 0) -> dict:
    seeds = jax.random.split(jax.random.key(seed), 24)
    return {
        "inputs": normal_values(seeds[0], (SEQS, SEQ_LEN, D), 1.0, 6.0, ((0, 4), (1, 8))),
        "out_grad": normal_values(seeds[1], (SEQS, SEQ_LEN, D), 1.0, 6.0, ((0, 4), (1, 8))),
        "lengths": draw_lengths(jax.random.fold_in(seeds[23], 71), 0),
        "token_types": touch_ends(jax.random.randint(seeds[3], (SEQS, SEQ_LEN), 0, 2), jax.random.fold_in(seeds[3], 1), 0, 1).astype(jnp.int32),
        "query_weight": normal_values(seeds[4], (D, D), D ** -0.5, 0.21875, ((0, 32),)),
        "key_weight": normal_values(seeds[5], (D, D), D ** -0.5, 0.21875, ((0, 32),)),
        "value_weight": normal_values(seeds[6], (D, D), D ** -0.5, 0.21875, ((0, 32),)),
        "value_bias": normal_values(seeds[7], (D,), 0.3, 1.796875, ((0, 32),)),
        "position_weight": normal_values(seeds[8], (D, D), D ** -0.5, 0.21875, ((0, 32),)),
        "content_bias": normal_values(seeds[9], (D,), 0.15, 0.8984375, ((0, 32),)),
        "position_bias": normal_values(seeds[10], (D,), 0.15, 0.8984375, ((0, 32),)),
        "type_bias": normal_values(seeds[11], (D,), 0.15, 0.8984375, ((0, 32),)),
        "type_embed": normal_values(seeds[12], (2, D), 0.5, 3.0, ((1, 32),)),
        "output_weight": normal_values(seeds[13], (D, D), (D * 64 // SEQ_LEN) ** -0.5, 0.875, ((0, 32),)),
        "output_bias": normal_values(seeds[14], (D,), 0.3, 1.796875, ((0, 32),)),
        "first_gain": jnp.clip(1.0 + 0.1 * jax.random.normal(seeds[15], (D,), jnp.float32), 0.5, 1.5).astype(jnp.bfloat16),
        "first_shift": normal_values(seeds[16], (D,), 0.3, 1.796875, ((0, 32),)),
        "inner_weight": normal_values(seeds[17], (D, FF), D ** -0.5, 0.21875, ((0, 32),)),
        "inner_bias": normal_values(seeds[18], (FF,), 0.3, 1.796875, ((0, 32),)),
        "outer_weight": normal_values(seeds[19], (FF, D), FF ** -0.5, 0.109375, ((0, 32),)),
        "outer_bias": normal_values(seeds[20], (D,), 0.3, 1.796875, ((0, 32),)),
        "second_gain": jnp.clip(1.0 + 0.1 * jax.random.normal(seeds[21], (D,), jnp.float32), 0.5, 1.5).astype(jnp.bfloat16),
        "second_shift": normal_values(seeds[22], (D,), 0.3, 1.796875, ((0, 32),)),
    }


@jax.custom_vjp
def low(v):
    return lax.optimization_barrier(v.astype(jnp.bfloat16)).astype(jnp.float32)

@jax.custom_vjp
def low_back(v):
    return v

def low_keep(v):
    return (low(v), None)

def low_pass(kept, grad):
    return (grad,)

def back_keep(v):
    return (v, None)

def back_low(kept, grad):
    return (low(grad),)
low.defvjp(low_keep, low_pass)
low_back.defvjp(back_keep, back_low)
maximal_precision = lax.Precision.HIGHEST
epsilon = 1e-06
masked_score = -1e+30

def product(left, right):
    return jnp.dot(left, right, precision=maximal_precision, preferred_element_type=jnp.float32)

def layer_norm(hidden, gain_values, shift_values):
    center = hidden - lax.optimization_barrier(jnp.mean(hidden, axis=-1, keepdims=True))
    variance = lax.optimization_barrier(jnp.mean(center * center, axis=-1, keepdims=True))
    return center * lax.rsqrt(variance + epsilon) * gain_values + shift_values

def position_table(anchor, number, columns):
    offsets = (anchor + jnp.arange(number, dtype=jnp.int32)).astype(jnp.float32)
    exponent = 2.0 * jnp.arange(columns // 2, dtype=jnp.float32) / columns
    angles = offsets[:, None] * (10000.0 ** (-exponent))[None, :]
    return jnp.concatenate([jnp.sin(angles), jnp.cos(angles)], axis=1)

def skew_rows(unscaled_scores, keys_count):
    leading = unscaled_scores.shape[:-2]
    rows_count = unscaled_scores.shape[-2]
    span_cols = unscaled_scores.shape[-1]
    flattened = unscaled_scores.reshape(leading + (rows_count * span_cols,))
    flattened = jnp.pad(flattened, [(0, 0)] * len(leading) + [(0, rows_count)])
    return flattened.reshape(leading + (rows_count, span_cols + 1))[..., :keys_count][..., ::-1]

def attention_block(anchor, query_content, query_relative_term, type_terms, seq_kinds, key_rows, value_rows, key_valid, rel_table):
    rows_content = lax.dynamic_slice_in_dim(query_content, anchor, KEY_BLOCK, 0)
    position_row_terms = lax.dynamic_slice_in_dim(query_relative_term, anchor, KEY_BLOCK, 0)
    rows_terms = lax.dynamic_slice_in_dim(type_terms, anchor, KEY_BLOCK, 0)
    rows_kinds = lax.dynamic_slice_in_dim(seq_kinds, anchor, KEY_BLOCK, 0)
    relative_rows = lax.dynamic_slice_in_dim(rel_table, anchor, KEY_BLOCK + SEQ_LEN - 1, 0)
    content = jnp.einsum('qhd,khd->hqk', rows_content, key_rows, precision=maximal_precision)
    unscaled_scores = jnp.einsum('axy,txy->xat', position_row_terms, relative_rows, precision=maximal_precision)
    same_kind = rows_kinds[:, None] == seq_kinds[None, :]
    type_same = jnp.transpose(rows_terms[:, :, 1])[:, :, None]
    type_other = jnp.transpose(rows_terms[:, :, 0])[:, :, None]
    type_part = jnp.where(same_kind[None], type_same, type_other)
    scores = low_back(content + skew_rows(unscaled_scores, SEQ_LEN) + type_part)
    scores = jnp.where(key_valid[None, None, :], scores, masked_score)
    log_total = jax.nn.logsumexp(scores, axis=-1, keepdims=True)
    weights_low = low(jnp.exp(scores - log_total))
    mixed_rows = jnp.einsum('hqk,khd->qhd', weights_low, value_rows, precision=maximal_precision)
    return mixed_rows.reshape(KEY_BLOCK, H * DH)

def sequence_layer(weights, rel_table, sequence_input, seq_kinds, length):
    query_weight, key_weight, value_weight, value_bias, position_weight, content_bias, position_bias, type_bias, type_embed, output_weight, output_bias, first_gain, first_shift, inner_weight, inner_bias, outer_weight, outer_bias, second_gain, second_shift = weights
    heads_shape = (SEQ_LEN, H, DH)
    key_valid = jnp.arange(SEQ_LEN, dtype=jnp.int32) < length
    scaled = low_back(product(sequence_input, query_weight) * DH ** (-0.5))
    query_content = low(scaled + content_bias).reshape(heads_shape)
    query_relative_term = low(scaled + position_bias).reshape(heads_shape)
    with_type = (scaled + type_bias).reshape(heads_shape)
    type_terms = jnp.einsum('qhd,shd->qhs', with_type, type_embed.reshape(2, H, DH), precision=maximal_precision)
    key_rows = low(low_back(product(sequence_input, key_weight))).reshape(heads_shape)
    value_rows = low(low_back(product(sequence_input, value_weight) + value_bias)).reshape(heads_shape)

    def one_block(anchor):
        return attention_block(anchor, query_content, query_relative_term, type_terms, seq_kinds, key_rows, value_rows, key_valid, rel_table)
    anchors = jnp.arange(SEQ_LEN // KEY_BLOCK, dtype=jnp.int32) * KEY_BLOCK
    attended = lax.map(jax.checkpoint(one_block), anchors).reshape(SEQ_LEN, H * DH)
    attn_out = low_back(product(low(low_back(attended)), output_weight) + output_bias)
    first_sum = sequence_input + attn_out
    normed = layer_norm(first_sum, first_gain, first_shift)
    inner = low_back(product(low(normed), inner_weight) + inner_bias)
    activated = low(jax.nn.gelu(inner, approximate=True))
    outer = low_back(product(activated, outer_weight) + outer_bias)
    result = layer_norm(normed + outer, second_gain, second_shift)
    row_valid = key_valid.astype(jnp.float32)[:, None]
    seq_sums = jnp.stack([jnp.sum(first_sum * first_sum * row_valid), jnp.sum(attn_out * attn_out * row_valid), jnp.sum(outer * outer * row_valid)])
    return (result, seq_sums)

def reference(inputs, out_grad, lengths, token_types, query_weight, key_weight, value_weight, value_bias, position_weight, content_bias, position_bias, type_bias, type_embed, output_weight, output_bias, first_gain, first_shift, inner_weight, inner_bias, outer_weight, outer_bias, second_gain, second_shift):
    params = tuple((weight_item.astype(jnp.float32) for weight_item in (query_weight, key_weight, value_weight, value_bias, position_weight, content_bias, position_bias, type_bias, type_embed, output_weight, output_bias, first_gain, first_shift, inner_weight, inner_bias, outer_weight, outer_bias, second_gain, second_shift)))
    table_low = low(position_table(1 - SEQ_LEN, 2 * SEQ_LEN - 1, D))
    valid = (jnp.arange(SEQ_LEN, dtype=jnp.int32)[None, :] < lengths[:, None]).astype(jnp.float32)

    def forward(seq_inputs, weights):
        rel_table = low(product(table_low, weights[4])).reshape(2 * SEQ_LEN - 1, H, DH)

        def seq_step(state_none, packed):
            sequence_input, seq_kinds, length = packed
            result, seq_sums = sequence_layer(weights, rel_table, sequence_input, seq_kinds, length)
            return (state_none, (result, seq_sums))
        unused, (results, all_sums) = lax.scan(jax.checkpoint(seq_step), None, (seq_inputs, token_types, lengths))
        return (results, all_sums)
    results, pullback, all_sums = jax.vjp(forward, inputs.astype(jnp.float32), params, has_aux=True)
    input_grad, weight_grads = pullback(out_grad.astype(jnp.float32) * valid[:, :, None])
    mean_squares = all_sums / (lengths.astype(jnp.float32)[:, None] * D)
    return (results.astype(jnp.bfloat16), input_grad.astype(jnp.bfloat16), weight_grads[0], weight_grads[1], weight_grads[2], weight_grads[3], weight_grads[4], weight_grads[5], weight_grads[6], weight_grads[7], weight_grads[8], weight_grads[9], weight_grads[10], weight_grads[11], weight_grads[12], weight_grads[13], weight_grads[14], weight_grads[15], weight_grads[16], weight_grads[17], weight_grads[18], mean_squares)
```

```python
import functools

import jax
import jax.numpy as jnp
from jax import lax
from jax.experimental import pallas as pl
from jax.experimental.pallas import tpu as pltpu
from jax.sharding import PartitionSpec as P

DP = "dp"
CTX = "ctx"
ALL = (DP, CTX)
H = 12
DH = 64
KEY_BLOCK = 512
MICRO = 2
SEQ_MB = 1


epsilon = 1e-06
masked_score = -1e30
maximal_precision = lax.Precision.HIGHEST


def layer_norm(hidden, gain_values, shift_values):
    center = hidden - jnp.mean(hidden, axis=-1, keepdims=True)
    variance = jnp.mean(center * center, axis=-1, keepdims=True)
    return center * lax.rsqrt(variance + epsilon) * gain_values + shift_values


def gelu_tanh(inner):
    return jax.nn.gelu(inner, approximate=True)


def position_table(anchor, number, columns):
    offsets = (anchor + jnp.arange(number, dtype=jnp.int32)).astype(jnp.float32)
    exponent = 2.0 * jnp.arange(columns // 2, dtype=jnp.float32) / columns
    angles = offsets[:, None] * (10000.0 ** (-exponent))[None, :]
    return jnp.concatenate([jnp.sin(angles), jnp.cos(angles)], axis=1)


def skew_rows(unscaled_scores, keys_count):
    leading = unscaled_scores.shape[:-2]
    rows_count = unscaled_scores.shape[-2]
    span_cols = unscaled_scores.shape[-1]
    flattened = unscaled_scores.reshape(leading + (rows_count * span_cols,))
    flattened = jnp.pad(flattened, [(0, 0)] * len(leading) + [(0, rows_count)])
    return flattened.reshape(leading + (rows_count, span_cols + 1))[..., :keys_count][..., ::-1]


def unskew_rows(grads_block, span_cols):
    leading = grads_block.shape[:-2]
    rows_count = grads_block.shape[-2]
    keys_count = grads_block.shape[-1]
    padded = jnp.pad(
        grads_block[..., ::-1], [(0, 0)] * (len(leading) + 1) + [(0, span_cols + 1 - keys_count)]
    )
    flattened = padded.reshape(leading + (rows_count * (span_cols + 1),))
    return flattened[..., : rows_count * span_cols].reshape(leading + (rows_count, span_cols))


def block_scores(
    query_content,
    query_relative_term,
    type_terms,
    query_kinds,
    key_rows,
    key_kinds,
    key_valid,
    relative_rows,
):
    content = jnp.einsum(
        "bqhd,bkhd->bhqk", query_content, key_rows, preferred_element_type=jnp.float32
    )
    unscaled_scores = jnp.einsum(
        "uply,xly->ulpx", query_relative_term, relative_rows, preferred_element_type=jnp.float32
    )
    same_kind = query_kinds[:, :, None] == key_kinds[:, None, :]
    type_same = jnp.transpose(type_terms[..., 1], (0, 2, 1))[..., None]
    type_other = jnp.transpose(type_terms[..., 0], (0, 2, 1))[..., None]
    summed = (
        content
        + skew_rows(unscaled_scores, key_rows.shape[1])
        + jnp.where(same_kind[:, None], type_same, type_other)
    )
    return (jnp.where(key_valid[:, None, None, :], summed, masked_score), same_kind)


def block_grads(
    query_content,
    query_relative_term,
    type_terms,
    query_kinds,
    log_total,
    row_delta,
    grad_rows,
    key_rows,
    value_rows,
    key_kinds,
    key_valid,
    relative_rows,
):
    scores, same_kind = block_scores(
        query_content,
        query_relative_term,
        type_terms,
        query_kinds,
        key_rows,
        key_kinds,
        key_valid,
        relative_rows,
    )
    probability = jnp.exp(scores - log_total[..., None])
    value_grad = jnp.einsum(
        "bhqk,bqhd->bkhd",
        probability.astype(jnp.bfloat16),
        grad_rows,
        preferred_element_type=jnp.float32,
    )
    prob_grad = jnp.einsum(
        "bqhd,bkhd->bhqk", grad_rows, value_rows, preferred_element_type=jnp.float32
    )
    score_grad = (probability * (prob_grad - row_delta[..., None])).astype(jnp.bfloat16)
    content_grad = jnp.einsum(
        "bhqk,bkhd->bqhd", score_grad, key_rows, preferred_element_type=jnp.float32
    )
    key_grad = jnp.einsum(
        "bhqk,bqhd->bkhd", score_grad, query_content, preferred_element_type=jnp.float32
    )
    unscaled_gradient = unskew_rows(score_grad, relative_rows.shape[0])
    position_grad = jnp.einsum(
        "aioy,yin->aoin", unscaled_gradient, relative_rows, preferred_element_type=jnp.float32
    )
    rel_grad = jnp.einsum(
        "gcrj,grcl->jcl", unscaled_gradient, query_relative_term, preferred_element_type=jnp.float32
    )
    wide_grad = score_grad.astype(jnp.float32)
    same_sum = jnp.sum(jnp.where(same_kind[:, None], wide_grad, 0.0), axis=-1)
    other_sum = jnp.sum(jnp.where(same_kind[:, None], 0.0, wide_grad), axis=-1)
    type_grad = jnp.transpose(jnp.stack([other_sum, same_sum], axis=-1), (0, 2, 1, 3))
    return (content_grad, position_grad, type_grad, key_grad, value_grad, rel_grad)


def per_device(
    inputs,
    out_grad,
    lengths,
    token_types,
    query_weight,
    key_weight,
    value_weight,
    value_bias,
    position_weight,
    content_bias,
    position_bias,
    type_bias,
    type_embed,
    output_weight,
    output_bias,
    first_gain,
    first_shift,
    inner_weight,
    inner_bias,
    outer_weight,
    outer_bias,
    second_gain,
    second_shift,
):
    stretch = inputs.shape[1]
    width = inputs.shape[2]
    seq_len = stretch * lax.axis_size(CTX)
    stretch_start = lax.axis_index(CTX) * stretch
    window = seq_len + stretch - 1
    scale_query = DH ** (-0.5)
    own_positions = stretch_start + jnp.arange(stretch, dtype=jnp.int32)
    table_forward = position_table(stretch_start - seq_len + 1, window, width).astype(jnp.bfloat16)
    outputs_list = []
    input_grads = []
    stat_rows = []
    grads_total = None
    rel_total = jnp.zeros((window, width), jnp.float32)
    for micro_index in range(MICRO):
        first_seq = micro_index * SEQ_MB
        sequence_input = inputs[first_seq : first_seq + SEQ_MB]
        seq_grad = out_grad[first_seq : first_seq + SEQ_MB]
        seq_kinds = token_types[first_seq : first_seq + SEQ_MB].astype(jnp.bfloat16)
        length_col = lengths[first_seq : first_seq + SEQ_MB][:, None]
        seq_count = sequence_input.shape[0]
        heads_shape = (seq_count, stretch, H, DH)
        full_shape = (seq_count, seq_len, H, DH)
        row_valid = (own_positions[None, :] < length_col).astype(jnp.float32)[..., None]
        gathered = (
            lax.all_gather(query_weight, ALL, axis=0, tiled=True),
            lax.all_gather(key_weight, ALL, axis=0, tiled=True),
            lax.all_gather(value_weight, ALL, axis=0, tiled=True),
            lax.all_gather(value_bias, ALL, axis=0, tiled=True),
            lax.all_gather(position_weight, ALL, axis=0, tiled=True),
            lax.all_gather(content_bias, ALL, axis=0, tiled=True),
            lax.all_gather(position_bias, ALL, axis=0, tiled=True),
            lax.all_gather(type_bias, ALL, axis=0, tiled=True),
            lax.all_gather(type_embed, ALL, axis=1, tiled=True),
            lax.all_gather(output_weight, ALL, axis=0, tiled=True),
            lax.all_gather(output_bias, ALL, axis=0, tiled=True),
            lax.all_gather(first_gain, ALL, axis=0, tiled=True),
            lax.all_gather(first_shift, ALL, axis=0, tiled=True),
            lax.all_gather(inner_weight, ALL, axis=0, tiled=True),
            lax.all_gather(inner_bias, ALL, axis=0, tiled=True),
            lax.all_gather(outer_weight, ALL, axis=0, tiled=True),
            lax.all_gather(outer_bias, ALL, axis=0, tiled=True),
            lax.all_gather(second_gain, ALL, axis=0, tiled=True),
            lax.all_gather(second_shift, ALL, axis=0, tiled=True),
        )
        (
            query_matrix,
            key_matrix,
            value_matrix,
            value_add,
            position_mat,
            content_add,
            position_add,
            type_add,
            type_table,
            output_matrix,
            output_add,
            gain_one,
            shift_one,
            inner_matrix,
            inner_add,
            outer_matrix,
            outer_add,
            gain_two,
            shift_two,
        ) = gathered
        scaled = (
            jnp.dot(sequence_input, query_matrix, preferred_element_type=jnp.float32) * scale_query
        )
        query_content = (
            (scaled + content_add.astype(jnp.float32)).astype(jnp.bfloat16).reshape(heads_shape)
        )
        query_relative_term = (
            (scaled + position_add.astype(jnp.float32)).astype(jnp.bfloat16).reshape(heads_shape)
        )
        with_type = (scaled + type_add.astype(jnp.float32)).reshape(heads_shape)
        type_heads = type_table.astype(jnp.float32).reshape(2, H, DH)
        type_terms = jnp.einsum(
            "bqhd,shd->bqhs", with_type, type_heads, precision=maximal_precision
        )
        key_rows = jnp.dot(sequence_input, key_matrix, preferred_element_type=jnp.float32).astype(
            jnp.bfloat16
        )
        value_rows = (
            jnp.dot(sequence_input, value_matrix, preferred_element_type=jnp.float32)
            + value_add.astype(jnp.float32)
        ).astype(jnp.bfloat16)
        rel_forward = (
            jnp.dot(table_forward, position_mat, preferred_element_type=jnp.float32)
            .astype(jnp.bfloat16)
            .reshape(window, H, DH)
        )
        start_state = (
            jnp.full((seq_count, H, stretch), masked_score, jnp.float32),
            jnp.zeros((seq_count, H, stretch), jnp.float32),
            jnp.zeros(heads_shape, jnp.float32),
        )
        piece_keys = lax.all_gather(key_rows, CTX, axis=1, tiled=True)
        piece_values = lax.all_gather(value_rows, CTX, axis=1, tiled=True)
        piece_kinds = lax.all_gather(seq_kinds, CTX, axis=1, tiled=True)
        number = piece_keys.shape[1]
        block_rows = KEY_BLOCK

        def one_block(running, offset):
            run_max, run_total, run_acc = running
            part_keys = lax.dynamic_slice_in_dim(piece_keys, offset, block_rows, 1).reshape(
                seq_count, block_rows, H, DH
            )
            part_values = lax.dynamic_slice_in_dim(piece_values, offset, block_rows, 1).reshape(
                seq_count, block_rows, H, DH
            )
            part_kinds = lax.dynamic_slice_in_dim(piece_kinds, offset, block_rows, 1)
            relative_rows = lax.dynamic_slice_in_dim(
                rel_forward, seq_len - offset - block_rows, stretch + block_rows - 1, 0
            )
            key_valid = (offset + jnp.arange(block_rows, dtype=jnp.int32))[None, :] < length_col
            scores, same_kind = block_scores(
                query_content,
                query_relative_term,
                type_terms,
                seq_kinds,
                part_keys,
                part_kinds,
                key_valid,
                relative_rows,
            )
            new_max = jnp.maximum(run_max, jnp.max(scores, axis=-1))
            factor = jnp.exp(run_max - new_max)
            weights_block = jnp.exp(scores - new_max[..., None])
            run_total = run_total * factor + jnp.sum(weights_block, axis=-1)
            mixed_rows = jnp.einsum(
                "bhqk,bkhd->bqhd",
                weights_block.astype(jnp.bfloat16),
                part_values,
                preferred_element_type=jnp.float32,
            )
            run_acc = run_acc * jnp.transpose(factor, (0, 2, 1))[..., None] + mixed_rows
            return ((new_max, run_total, run_acc), None)

        offsets = jnp.arange(number // block_rows, dtype=jnp.int32) * block_rows
        result_state, unused = lax.scan(one_block, start_state, offsets)
        run_max, run_total, run_acc = result_state
        log_total = run_max + jnp.log(run_total)
        attended = run_acc / jnp.transpose(run_total, (0, 2, 1))[..., None]
        attended_reduced = attended.astype(jnp.bfloat16).reshape(seq_count, stretch, width)
        attn_out = jnp.dot(
            attended_reduced, output_matrix, preferred_element_type=jnp.float32
        ) + output_add.astype(jnp.float32)
        first_sum = sequence_input.astype(jnp.float32) + attn_out
        normed = layer_norm(first_sum, gain_one.astype(jnp.float32), shift_one.astype(jnp.float32))
        normed_reduced = normed.astype(jnp.bfloat16)
        inner = jnp.dot(
            normed_reduced, inner_matrix, preferred_element_type=jnp.float32
        ) + inner_add.astype(jnp.float32)
        activated_reduced = gelu_tanh(inner).astype(jnp.bfloat16)
        outer = jnp.dot(
            activated_reduced, outer_matrix, preferred_element_type=jnp.float32
        ) + outer_add.astype(jnp.float32)
        second_sum = normed + outer
        result = layer_norm(second_sum, gain_two.astype(jnp.float32), shift_two.astype(jnp.float32))
        outputs_list.append(result.astype(jnp.bfloat16))
        stat_rows.append(
            jnp.stack(
                [
                    jnp.sum(first_sum * first_sum * row_valid, axis=(1, 2)),
                    jnp.sum(attn_out * attn_out * row_valid, axis=(1, 2)),
                    jnp.sum(outer * outer * row_valid, axis=(1, 2)),
                ],
                axis=1,
            )
        )
        back_set = (
            lax.all_gather(query_weight, ALL, axis=0, tiled=True),
            lax.all_gather(key_weight, ALL, axis=0, tiled=True),
            lax.all_gather(value_weight, ALL, axis=0, tiled=True),
            lax.all_gather(value_bias, ALL, axis=0, tiled=True),
            lax.all_gather(position_weight, ALL, axis=0, tiled=True),
            lax.all_gather(content_bias, ALL, axis=0, tiled=True),
            lax.all_gather(position_bias, ALL, axis=0, tiled=True),
            lax.all_gather(type_bias, ALL, axis=0, tiled=True),
            lax.all_gather(type_embed, ALL, axis=1, tiled=True),
            lax.all_gather(output_weight, ALL, axis=0, tiled=True),
            lax.all_gather(output_bias, ALL, axis=0, tiled=True),
            lax.all_gather(first_gain, ALL, axis=0, tiled=True),
            lax.all_gather(first_shift, ALL, axis=0, tiled=True),
            lax.all_gather(inner_weight, ALL, axis=0, tiled=True),
            lax.all_gather(inner_bias, ALL, axis=0, tiled=True),
            lax.all_gather(outer_weight, ALL, axis=0, tiled=True),
            lax.all_gather(outer_bias, ALL, axis=0, tiled=True),
            lax.all_gather(second_gain, ALL, axis=0, tiled=True),
            lax.all_gather(second_shift, ALL, axis=0, tiled=True),
        )
        (
            query_matrix,
            key_matrix,
            value_matrix,
            value_add,
            position_mat,
            content_add,
            position_add,
            type_add,
            type_table,
            output_matrix,
            output_add,
            gain_one,
            shift_one,
            inner_matrix,
            inner_add,
            outer_matrix,
            outer_add,
            gain_two,
            shift_two,
        ) = back_set
        type_heads = type_table.astype(jnp.float32).reshape(2, H, DH)
        cotangent = seq_grad.astype(jnp.float32) * row_valid
        unused_two, second_back = jax.vjp(
            layer_norm, second_sum, gain_two.astype(jnp.float32), shift_two.astype(jnp.float32)
        )
        second_grad, gain_two_grad, shift_two_grad = second_back(cotangent)
        outer_reduced = second_grad.astype(jnp.bfloat16)
        outer_add_grad = jnp.sum(outer_reduced.astype(jnp.float32), axis=(0, 1))
        outer_mat_grad = jnp.einsum(
            "hpi,hpt->it", activated_reduced, outer_reduced, preferred_element_type=jnp.float32
        )
        activated_grad = jnp.einsum(
            "unk,rk->unr", outer_reduced, outer_matrix, preferred_element_type=jnp.float32
        )
        unused_three, gelu_back = jax.vjp(gelu_tanh, inner)
        inner_reduced = gelu_back(activated_grad)[0].astype(jnp.bfloat16)
        inner_add_grad = jnp.sum(inner_reduced.astype(jnp.float32), axis=(0, 1))
        inner_mat_grad = jnp.einsum(
            "psu,psy->uy", normed_reduced, inner_reduced, preferred_element_type=jnp.float32
        )
        normed_grad = second_grad + jnp.einsum(
            "tma,ra->tmr", inner_reduced, inner_matrix, preferred_element_type=jnp.float32
        )
        unused_four, first_back = jax.vjp(
            layer_norm, first_sum, gain_one.astype(jnp.float32), shift_one.astype(jnp.float32)
        )
        first_grad, gain_one_grad, shift_one_grad = first_back(normed_grad)
        attention_reduced = first_grad.astype(jnp.bfloat16)
        output_add_grad = jnp.sum(attention_reduced.astype(jnp.float32), axis=(0, 1))
        output_mat_grad = jnp.einsum(
            "yim,yig->mg", attended_reduced, attention_reduced, preferred_element_type=jnp.float32
        )
        grad_rows = (
            jnp.einsum(
                "jcy,py->jcp", attention_reduced, output_matrix, preferred_element_type=jnp.float32
            )
            .astype(jnp.bfloat16)
            .reshape(heads_shape)
        )
        row_delta = jnp.einsum(
            "bqhd,bqhd->bhq", grad_rows.astype(jnp.float32), attended, precision=maximal_precision
        )
        all_keys, all_values, all_kinds = (
            lax.all_gather(key_rows, CTX, axis=1, tiled=True),
            lax.all_gather(value_rows, CTX, axis=1, tiled=True),
            lax.all_gather(seq_kinds, CTX, axis=1, tiled=True),
        )

        def key_step(running, key_start):
            content_acc, position_acc, type_acc, key_acc, value_acc, rel_acc = running
            part_keys = lax.dynamic_slice_in_dim(all_keys, key_start, KEY_BLOCK, 1).reshape(
                seq_count, KEY_BLOCK, H, DH
            )
            part_values = lax.dynamic_slice_in_dim(all_values, key_start, KEY_BLOCK, 1).reshape(
                seq_count, KEY_BLOCK, H, DH
            )
            part_kinds = lax.dynamic_slice_in_dim(all_kinds, key_start, KEY_BLOCK, 1)
            rel_start = seq_len - key_start - KEY_BLOCK
            relative_rows = lax.dynamic_slice_in_dim(
                rel_forward, rel_start, stretch + KEY_BLOCK - 1, 0
            )
            key_valid = (key_start + jnp.arange(KEY_BLOCK, dtype=jnp.int32))[None, :] < length_col
            pieces = block_grads(
                query_content,
                query_relative_term,
                type_terms,
                seq_kinds,
                log_total,
                row_delta,
                grad_rows,
                part_keys,
                part_values,
                part_kinds,
                key_valid,
                relative_rows,
            )
            content_part, position_part, type_part, key_part, value_part, rel_part = pieces
            key_acc = lax.dynamic_update_slice_in_dim(key_acc, key_part, key_start, 1)
            value_acc = lax.dynamic_update_slice_in_dim(value_acc, value_part, key_start, 1)
            rel_old = lax.dynamic_slice_in_dim(rel_acc, rel_start, stretch + KEY_BLOCK - 1, 0)
            rel_acc = lax.dynamic_update_slice_in_dim(rel_acc, rel_old + rel_part, rel_start, 0)
            return (
                (
                    content_acc + content_part,
                    position_acc + position_part,
                    type_acc + type_part,
                    key_acc,
                    value_acc,
                    rel_acc,
                ),
                None,
            )

        start_grads = (
            jnp.zeros(heads_shape, jnp.float32),
            jnp.zeros(heads_shape, jnp.float32),
            jnp.zeros((seq_count, stretch, H, 2), jnp.float32),
            jnp.zeros(full_shape, jnp.float32),
            jnp.zeros(full_shape, jnp.float32),
            jnp.zeros((window, H, DH), jnp.float32),
        )
        final_grads, unused_five = lax.scan(
            key_step, start_grads, jnp.arange(seq_len // KEY_BLOCK, dtype=jnp.int32) * KEY_BLOCK
        )
        content_grad, position_grad, type_grad, key_all, value_all, rel_grad = final_grads
        key_grad, value_grad = (
            lax.psum_scatter(
                key_all.astype(jnp.bfloat16), CTX, scatter_dimension=1, tiled=True
            ).astype(jnp.float32),
            lax.psum_scatter(
                value_all.astype(jnp.bfloat16), CTX, scatter_dimension=1, tiled=True
            ).astype(jnp.float32),
        )
        type_part_grad = jnp.einsum(
            "bqhs,shd->bqhd", type_grad, type_heads, precision=maximal_precision
        )
        query_grad = content_grad + position_grad + type_part_grad
        content_add_grad = jnp.sum(content_grad, axis=(0, 1)).reshape(width)
        position_add_grad = jnp.sum(position_grad, axis=(0, 1)).reshape(width)
        type_add_grad = jnp.sum(type_part_grad, axis=(0, 1)).reshape(width)
        rel_total = rel_total + rel_grad.reshape(window, width)
        query_reduced = query_grad.astype(jnp.bfloat16).reshape(seq_count, stretch, width)
        key_reduced = key_grad.astype(jnp.bfloat16).reshape(seq_count, stretch, width)
        value_reduced = value_grad.astype(jnp.bfloat16).reshape(seq_count, stretch, width)
        type_table_grad = jnp.einsum(
            "bqhs,bqhd->shd", type_grad, with_type, precision=maximal_precision
        ).reshape(2, width)
        query_mat_grad = (
            jnp.einsum(
                "orh,org->hg", sequence_input, query_reduced, preferred_element_type=jnp.float32
            )
            * scale_query
        )
        key_mat_grad = jnp.einsum(
            "orh,org->hg", sequence_input, key_reduced, preferred_element_type=jnp.float32
        )
        value_mat_grad = jnp.einsum(
            "orh,org->hg", sequence_input, value_reduced, preferred_element_type=jnp.float32
        )
        value_add_grad = jnp.sum(value_reduced.astype(jnp.float32), axis=(0, 1))
        input_grad = (
            first_grad
            + jnp.einsum(
                "sux,fx->suf", query_reduced, query_matrix, preferred_element_type=jnp.float32
            )
            * scale_query
            + jnp.einsum("sux,fx->suf", key_reduced, key_matrix, preferred_element_type=jnp.float32)
            + jnp.einsum(
                "sux,fx->suf", value_reduced, value_matrix, preferred_element_type=jnp.float32
            )
        )
        input_grads.append(input_grad.astype(jnp.bfloat16))
        micro_grads = (
            query_mat_grad,
            key_mat_grad,
            value_mat_grad,
            value_add_grad,
            content_add_grad,
            position_add_grad,
            type_add_grad,
            type_table_grad,
            output_mat_grad,
            output_add_grad,
            gain_one_grad,
            shift_one_grad,
            inner_mat_grad,
            inner_add_grad,
            outer_mat_grad,
            outer_add_grad,
            gain_two_grad,
            shift_two_grad,
        )
        if grads_total is None:
            grads_total = micro_grads
        else:
            grads_total = jax.tree.map(jnp.add, grads_total, micro_grads)
    rel_high = rel_total.astype(jnp.bfloat16)
    rel_rest = (rel_total - rel_high.astype(jnp.float32)).astype(jnp.bfloat16)
    contract_rows = (((0,), (0,)), ((), ()))
    position_mat_grad = lax.dot_general(
        table_forward, rel_high, contract_rows, preferred_element_type=jnp.float32
    ) + lax.dot_general(table_forward, rel_rest, contract_rows, preferred_element_type=jnp.float32)
    (
        query_total,
        key_total,
        value_total,
        value_add_total,
        content_total,
        position_total,
        type_total,
        table_total,
        output_total,
        output_add_total,
        gain_one_total,
        shift_one_total,
        inner_total,
        inner_add_total,
        outer_total,
        outer_add_total,
        gain_two_total,
        shift_two_total,
    ) = grads_total
    reduced = (
        lax.psum_scatter(query_total, ALL, scatter_dimension=0, tiled=True),
        lax.psum_scatter(key_total, ALL, scatter_dimension=0, tiled=True),
        lax.psum_scatter(value_total, ALL, scatter_dimension=0, tiled=True),
        lax.psum_scatter(value_add_total, ALL, scatter_dimension=0, tiled=True),
        lax.psum_scatter(position_mat_grad, ALL, scatter_dimension=0, tiled=True),
        lax.psum_scatter(content_total, ALL, scatter_dimension=0, tiled=True),
        lax.psum_scatter(position_total, ALL, scatter_dimension=0, tiled=True),
        lax.psum_scatter(type_total, ALL, scatter_dimension=0, tiled=True),
        lax.psum_scatter(table_total, ALL, scatter_dimension=1, tiled=True),
        lax.psum_scatter(output_total, ALL, scatter_dimension=0, tiled=True),
        lax.psum_scatter(output_add_total, ALL, scatter_dimension=0, tiled=True),
        lax.psum_scatter(gain_one_total, ALL, scatter_dimension=0, tiled=True),
        lax.psum_scatter(shift_one_total, ALL, scatter_dimension=0, tiled=True),
        lax.psum_scatter(inner_total, ALL, scatter_dimension=0, tiled=True),
        lax.psum_scatter(inner_add_total, ALL, scatter_dimension=0, tiled=True),
        lax.psum_scatter(outer_total, ALL, scatter_dimension=0, tiled=True),
        lax.psum_scatter(outer_add_total, ALL, scatter_dimension=0, tiled=True),
        lax.psum_scatter(gain_two_total, ALL, scatter_dimension=0, tiled=True),
        lax.psum_scatter(shift_two_total, ALL, scatter_dimension=0, tiled=True),
    )
    sums_all = lax.psum(jnp.concatenate(stat_rows, axis=0), CTX)
    mean_squares = sums_all / (lengths.astype(jnp.float32)[:, None] * width)
    return (
        (jnp.concatenate(outputs_list, axis=0), jnp.concatenate(input_grads, axis=0))
        + tuple(reduced)
        + (mean_squares,)
    )


LANES = 128
BF = jnp.bfloat16
F32 = jnp.float32
ROWS_CC = (((1,), (1,)), ((), ()))
COLS_CC = (((0,), (0,)), ((), ()))
ROWCOL = (((1,), (0,)), ((), ()))


def mm(a, b, dims):
    return lax.dot_general(a, b, dims, preferred_element_type=F32)


def split3(v):
    hi = v.astype(BF).astype(F32)
    mid = (v - hi).astype(BF).astype(F32)
    lo = (v - hi - mid).astype(BF).astype(F32)
    return hi, mid, lo


def attention_forward_kernel(tile, x_ref, w_ref, vec_ref, kext_ref, trig_ref,
                             att_ref, qt_ref, kb_ref, v1_ref, qp_ref, save_ref, scl_ref, kt_ref):
    step = pl.program_id(1)
    rows = x_ref.shape[0]
    width = x_ref.shape[1]
    half = width // 2
    lane = lax.broadcasted_iota(jnp.int32, (tile, LANES), 1)
    low = lane < DH

    @pl.when((pl.program_id(0) == 0) & (step == 0))
    def _():
        kt_ref[:, :width] = trig_ref[...].astype(BF)

    @pl.when(step == 0)
    def _():
        vec = vec_ref[0]
        w = w_ref[0]
        w_lane = lax.broadcasted_iota(jnp.int32, (width, LANES), 1)
        w_pos = jnp.where(w_lane < DH, pltpu.roll(w[:, LANES:].astype(F32), DH, 1), 0.0).astype(BF)

        def body(i, carry):
            at = pl.ds(pl.multiple_of(i * tile, tile), tile)
            proj = mm(x_ref[at, :], w, ROWCOL)
            kext = kext_ref[at, :].astype(F32)
            kind = kext[:, DH + 3:DH + 4]
            scaled = jnp.where(low, proj[:, :LANES] * DH ** -0.5, 0.0)
            scl_ref[0, at, :] = scaled
            kb = jnp.where(low, pltpu.roll(proj[:, :LANES], DH, 1), kext).astype(BF)
            kb_ref[0, at, :] = kb
            kt_ref[at, width:] = kb
            one_v = (lane >= DH) & (lane < DH + 3)
            v1_ref[0, at, :] = jnp.where(low, proj[:, LANES:] + vec[3:4, :], jnp.where(one_v, 1.0, 0.0)).astype(BF)
            with_type = scaled + vec[2:3, :]
            term0 = jnp.sum(with_type * vec[4:5, :], axis=1, keepdims=True)
            term1 = jnp.sum(with_type * vec[5:6, :], axis=1, keepdims=True)
            base = jnp.where(kind > 0.5, term0, term1)
            slope = jnp.where(kind > 0.5, term1 - term0, term0 - term1)
            b_hi, b_mid, b_lo = split3(base)
            s_hi, s_mid, s_lo = split3(slope)
            ext = jnp.where(lane == DH, b_hi, 0.0)
            ext = jnp.where(lane == DH + 1, b_mid, ext)
            ext = jnp.where(lane == DH + 2, b_lo, ext)
            ext = jnp.where(lane == DH + 3, s_hi, ext)
            ext = jnp.where(lane == DH + 4, s_mid, ext)
            ext = jnp.where(lane == DH + 5, 1.0, ext)
            qt_ref[0, at, width:] = jnp.where(low, scaled + vec[0:1, :], ext).astype(BF)
            qp = jnp.where(low, scaled + vec[1:2, :], 0.0).astype(BF)
            qp_ref[0, at, :] = qp
            grow = mm(qp, w_pos, ROWS_CC)
            q_sin = grow[:, :half]
            q_cos = grow[:, half:]
            c = trig_ref[at, :half]
            s = trig_ref[at, half:]
            qt_ref[0, at, :half] = (q_sin * s + q_cos * c).astype(BF)
            qt_ref[0, at, half:width] = (q_cos * s - q_sin * c).astype(BF)
            return carry

        lax.fori_loop(0, rows // tile, body, 0)

    at = pl.ds(pl.multiple_of(step * tile, tile), tile)
    scores = mm(qt_ref[0, at, :], kt_ref[...], ROWS_CC)
    top = jnp.max(scores, axis=1, keepdims=True)
    prob = jnp.exp(scores - top)
    mixed = mm(prob.astype(BF), v1_ref[0], ROWCOL)
    total = mixed[:, DH:DH + 1]
    att = mixed / total
    save_ref[0] = jnp.where(low, att, top + jnp.log(total))
    att_ref[...] = jnp.transpose(att)[:DH, :].astype(BF)


def attention_backward_kernel(tile, do_ref, w_ref, vec_ref, kext_ref, trig_ref,
                              qt_ref, kb_ref, v1_ref, qp_ref, save_ref, scl_ref,
                              d_ref, dwp_ref, small_ref,
                              kt_ref, q_ref, dk_acc, dv_acc):
    step = pl.program_id(1)
    width = trig_ref.shape[1]
    half = width // 2
    lane = lax.broadcasted_iota(jnp.int32, (tile, LANES), 1)
    low = lane < DH

    @pl.when((pl.program_id(0) == 0) & (step == 0))
    def _():
        kt_ref[:, :width] = trig_ref[...].astype(BF)

    @pl.when(step == 0)
    def _():
        kt_ref[:, width:] = kb_ref[0]
        dk_acc[...] = jnp.zeros_like(dk_acc)
        dv_acc[...] = jnp.zeros_like(dv_acc)
        dwp_ref[...] = jnp.zeros_like(dwp_ref)
        small_ref[...] = jnp.zeros_like(small_ref)

    at = pl.ds(pl.multiple_of(step * tile, tile), tile)
    w = w_ref[0]
    w_lane = lax.broadcasted_iota(jnp.int32, (width, LANES), 1)
    w_pos = jnp.where(w_lane < DH, pltpu.roll(w[:, LANES:].astype(F32), DH, 1), 0.0).astype(BF)
    save = save_ref[0]
    lse = save[:, DH:DH + 1]
    do_t = do_ref[...].astype(F32)
    d_out = jnp.transpose(jnp.concatenate([do_t, jnp.zeros_like(do_t)], axis=0))
    delta = jnp.sum(d_out * save, axis=1, keepdims=True)
    l_hi, l_mid, l_lo = split3(-lse)
    d_hi, d_mid, d_lo = split3(-delta)
    q_block = qt_ref[0, :, width:].astype(F32)
    q_ref[:, :width] = qt_ref[0, :, :width]
    q_block = jnp.where(lane == DH + 6, l_hi, q_block)
    q_block = jnp.where(lane == DH + 7, l_mid, q_block)
    q_block = jnp.where(lane == DH + 8, l_lo, q_block)
    q_block = q_block.astype(BF)
    q_ref[:, width:] = q_block
    ext = jnp.where(lane == DH, d_hi, d_out)
    ext = jnp.where(lane == DH + 1, d_mid, ext)
    ext = jnp.where(lane == DH + 2, d_lo, ext)
    d_ext = ext.astype(BF)
    prob = jnp.exp(mm(q_ref[...], kt_ref[...], ROWS_CC))
    dv_acc[...] += mm(d_ext, prob.astype(BF), COLS_CC)
    d_score = (prob * mm(d_ext, v1_ref[0], ROWS_CC)).astype(BF)
    dk_acc[...] += mm(q_block, d_score, COLS_CC)
    dq = mm(d_score, kt_ref[...], ROWCOL)
    c = trig_ref[at, :half]
    s = trig_ref[at, half:]
    du_c = dq[:, :half]
    du_s = dq[:, half:width]
    back = jnp.concatenate([s * du_c - c * du_s, c * du_c + s * du_s], axis=1).astype(BF)
    d_block = dq[:, width:]
    d_pos = mm(back, w_pos, ROWCOL)
    dwp_ref[0] += mm(qp_ref[0], back, COLS_CC)[:DH, :]
    vec = vec_ref[0]
    kind = kext_ref[...][:, DH + 3:DH + 4].astype(F32)
    every = d_block[:, DH:DH + 1]
    ones = d_block[:, DH + 3:DH + 4]
    g_same = jnp.where(kind > 0.5, ones, every - ones)
    g_other = jnp.where(kind > 0.5, every - ones, ones)
    type_part = g_other * vec[4:5, :] + g_same * vec[5:6, :]
    d_content = jnp.where(low, d_block, 0.0)
    with_type = jnp.where(low, scl_ref[0] + vec[2:3, :], 0.0)
    d_scaled = d_content + d_pos + type_part
    d_ref[0, :DH, at] = (jnp.transpose(d_scaled)[:DH, :] * DH ** -0.5).astype(BF)
    sums = [jnp.sum(v, axis=0, keepdims=True) for v in
            (d_content, d_pos, type_part, g_other * with_type, g_same * with_type)]
    small_ref[0] += jnp.concatenate(sums + [jnp.zeros((3, LANES), F32)], axis=0)

    @pl.when(step == pl.num_programs(1) - 1)
    def _():
        d_ref[0, DH:2 * DH] = dk_acc[:DH, :].astype(BF)
        d_ref[0, 2 * DH:] = dv_acc[:DH, :].astype(BF)


def attention_forward(x, w, vec, kext, trig, tile=512):
    rows, width = x.shape
    heads = w.shape[0]
    full = width + LANES
    per_head = lambda shape: pl.BlockSpec((1,) + shape, lambda h, t: (h, 0, 0))
    fixed = lambda shape: pl.BlockSpec(shape, lambda h, t: (0, 0))
    flops = heads * rows * 2 * (width * 256 + rows * full + rows * LANES)
    return pl.pallas_call(
        functools.partial(attention_forward_kernel, tile),
        grid=(heads, rows // tile),
        in_specs=[fixed((rows, width)), per_head((width, 256)), per_head((8, LANES)),
                  fixed((rows, LANES)), fixed((rows, width))],
        out_specs=[pl.BlockSpec((DH, tile), lambda h, t: (h, t)),
                   per_head((rows, full)), per_head((rows, LANES)), per_head((rows, LANES)),
                   per_head((rows, LANES)),
                   pl.BlockSpec((1, tile, LANES), lambda h, t: (h, t, 0)),
                   per_head((rows, LANES))],
        out_shape=[jax.ShapeDtypeStruct((heads * DH, rows), BF),
                   jax.ShapeDtypeStruct((heads, rows, full), BF),
                   jax.ShapeDtypeStruct((heads, rows, LANES), BF),
                   jax.ShapeDtypeStruct((heads, rows, LANES), BF),
                   jax.ShapeDtypeStruct((heads, rows, LANES), BF),
                   jax.ShapeDtypeStruct((heads, rows, LANES), F32),
                   jax.ShapeDtypeStruct((heads, rows, LANES), F32)],
        scratch_shapes=[pltpu.VMEM((rows, full), BF)],
        compiler_params=pltpu.CompilerParams(dimension_semantics=("arbitrary", "arbitrary"),
                                             vmem_limit_bytes=56 * 2 ** 20),
        cost_estimate=pl.CostEstimate(flops=flops, bytes_accessed=rows * width * 16, transcendentals=heads * rows * rows),
        name="attention_forward",
    )(x, w, vec, kext, trig)


def attention_backward(do_t, w, vec, kext, trig, qt, kb, v1, qp, save, scl, tile=512):
    heads, rows, full = qt.shape
    width = full - LANES
    per_head = lambda shape: pl.BlockSpec((1,) + shape, lambda h, t: (h, 0, 0))
    per_tile = lambda cols: pl.BlockSpec((1, tile, cols), lambda h, t: (h, t, 0))
    flops = heads * rows * 2 * (2 * rows * full + 3 * rows * LANES)
    return pl.pallas_call(
        functools.partial(attention_backward_kernel, tile),
        grid=(heads, rows // tile),
        in_specs=[pl.BlockSpec((DH, tile), lambda h, t: (h, t)), per_head((width, 256)), per_head((8, LANES)),
                  pl.BlockSpec((tile, LANES), lambda h, t: (t, 0)), pl.BlockSpec((rows, width), lambda h, t: (0, 0)),
                  per_tile(full), per_head((rows, LANES)), per_head((rows, LANES)), per_tile(LANES),
                  per_tile(LANES), per_tile(LANES)],
        out_specs=[per_head((3 * DH, rows)), per_head((DH, width)), per_head((8, LANES))],
        out_shape=[jax.ShapeDtypeStruct((heads, 3 * DH, rows), BF),
                   jax.ShapeDtypeStruct((heads, DH, width), F32),
                   jax.ShapeDtypeStruct((heads, 8, LANES), F32)],
        scratch_shapes=[pltpu.VMEM((rows, full), BF), pltpu.VMEM((tile, full), BF),
                        pltpu.VMEM((LANES, rows), F32), pltpu.VMEM((LANES, rows), F32)],
        compiler_params=pltpu.CompilerParams(dimension_semantics=("arbitrary", "arbitrary"),
                                             vmem_limit_bytes=56 * 2 ** 20),
        cost_estimate=pl.CostEstimate(flops=flops, bytes_accessed=rows * width * 20, transcendentals=heads * rows * rows),
        name="attention_backward",
    )(do_t, w, vec, kext, trig, qt, kb, v1, qp, save, scl)


def key_extension(kinds, valid):
    rows = kinds.shape[0]
    lane = jnp.arange(LANES)[None, :]
    k = kinds[:, None]
    out = jnp.where((lane >= DH) & (lane < DH + 3) | (lane >= DH + 6) & (lane < DH + 9), 1.0, 0.0)
    out = jnp.where((lane == DH + 3) | (lane == DH + 4), k, out)
    out = jnp.where(lane == DH + 5, jnp.where(valid[:, None] > 0, 0.0, -1e30), out)
    return jnp.broadcast_to(out, (rows, LANES)).astype(BF)


def takes_head_layout(mesh):
    return dict(mesh.shape) == {DP: 4, CTX: 8}


def swap(x, axis, bit):
    count = lax.axis_size(axis)
    return lax.ppermute(x, axis, [(i, i ^ bit) for i in range(count)])


def in_order(bit, own, received, axis):
    first = jnp.where(bit == 0, own, received)
    second = jnp.where(bit == 0, received, own)
    return jnp.stack([first, second], axis=axis)


def flip_if(bit, x, axis):
    return jnp.where(bit == 0, x, jnp.flip(x, axis))


def pick(x, index, axis):
    return lax.dynamic_index_in_dim(x, index, axis, keepdims=False)


def gather_rows(shard, order):
    d, c = lax.axis_index(DP), lax.axis_index(CTX)
    z, x, y, k = c // 2, c % 2, d // 2, d % 2
    pieces = [shard] + [swap(shard, CTX, 2 * m) for m in (1, 2, 3)]
    block = jnp.stack(pieces).reshape((2, 2) + shard.shape)
    block = flip_if(z // 2, flip_if(z % 2, block, 1), 0).reshape((4,) + shard.shape)
    block = block[None, :, None]
    for name in order:
        if name == "x":
            other = swap(block, CTX, 1)
            block = in_order(x, block[:, :, 0], other[:, :, 0], 2)
        else:
            other = swap(block, DP, 2)
            block = in_order(y, block[0], other[0], 0)
    other = swap(block, DP, 1)
    block = in_order(k, block, other, 1)
    return block.reshape((-1,) + shard.shape[1:])


def add_low(a, b):
    return (a.astype(F32) + b.astype(F32)).astype(BF)


def scatter_rows(full, order):
    d, c = lax.axis_index(DP), lax.axis_index(CTX)
    z, x, y, k = c // 2, c % 2, d // 2, d % 2
    block = full.reshape((2, 2, 4, 2, -1) + full.shape[1:])
    block = add_low(pick(block, k, 1), swap(pick(block, 1 - k, 1), DP, 1))
    for name in order:
        if name == "x":
            block = add_low(pick(block, x, -3), swap(pick(block, 1 - x, -3), CTX, 1))
        else:
            block = add_low(pick(block, y, 0), swap(pick(block, 1 - y, 0), DP, 2))
    total = pick(block, z, 0).astype(F32)
    for m in (1, 2, 3):
        total = total + swap(pick(block, z ^ m, 0), CTX, 2 * m).astype(F32)
    return total


def head_layout(
    inputs,
    out_grad,
    lengths,
    token_types,
    query_weight,
    key_weight,
    value_weight,
    value_bias,
    position_weight,
    content_bias,
    position_bias,
    type_bias,
    type_embed,
    output_weight,
    output_bias,
    first_gain,
    first_shift,
    inner_weight,
    inner_bias,
    outer_weight,
    outer_bias,
    second_gain,
    second_shift,
):
    d, c = lax.axis_index(DP), lax.axis_index(CTX)
    members = lax.axis_size(CTX)
    devices = lax.axis_size(DP) * members
    seqs, stretch, width = inputs.shape
    seq_len = stretch * members
    groups = members // seqs
    heads = H // groups
    span = heads * DH
    half = width // 2
    shard = width // devices
    inner_shard = inner_bias.shape[0]
    s, g = c // groups, c % groups
    bit_z, bit_b, bit_x = c // 4, (c // 2) % 2, c % 2

    own = pick(inputs, s, 0)
    kinds = token_types.astype(BF)
    row = jnp.zeros((seqs, 8, half), BF).at[:, 0, :stretch].set(kinds)
    left = jnp.concatenate([inputs[:, :, :half], row], axis=1)
    right = inputs[:, :, half:]
    left = jnp.stack([pick(left, s, 0), swap(pick(left, 1 - s, 0), CTX, 4)])
    right = jnp.stack([pick(right, s, 0), swap(pick(right, 1 - s, 0), CTX, 4)])
    left = jnp.stack([left, swap(left, CTX, 1)], axis=1)
    left = jnp.stack([left, swap(left, CTX, 2)], axis=1)
    right = jnp.stack([right, swap(right, CTX, 2)], axis=1)
    right = jnp.stack([right, swap(right, CTX, 1)], axis=2)
    left = left.reshape(members, stretch + 8, half)
    right = right.reshape(members, stretch, half)
    x_seq = jnp.concatenate([left[:, :stretch], right], axis=2).reshape(seq_len, width)
    kind_seq = left[:, stretch, :stretch].reshape(seq_len).astype(F32)

    small = jnp.concatenate(
        [
            value_bias,
            content_bias,
            position_bias,
            type_bias,
            type_embed[0],
            type_embed[1],
            output_bias,
            first_gain,
            first_shift,
            outer_bias,
            second_gain,
            second_shift,
            inner_bias,
        ]
    )
    columns = 4 * DH
    small_rows = jnp.zeros((8 * columns,), BF).at[: small.shape[0]].set(small).reshape(8, columns)
    stacked = jnp.stack([query_weight, key_weight, value_weight, position_weight])
    stacked = stacked.reshape(4, shard, groups, heads, DH).transpose(2, 3, 1, 0, 4)
    stacked = stacked.reshape(groups, heads * shard, columns)
    stacked = jnp.concatenate(
        [stacked, jnp.broadcast_to(small_rows[None], (groups, 8, columns))], axis=1
    )
    pieces = [pick(stacked, g, 0)]
    for r in range(1, groups):
        pieces.append(swap(pick(stacked, g ^ r, 0), CTX, r))
    block = jnp.stack(pieces).reshape((2, 2) + pieces[0].shape)
    block = flip_if(bit_b, flip_if(bit_x, block, 1), 0).reshape((groups,) + pieces[0].shape)
    block = in_order(bit_z, block, swap(block, CTX, 4), 0)[None]
    block = in_order(d // 2, block, swap(block, DP, 2), 0)
    block = in_order(d % 2, block, swap(block, DP, 1), 1)
    block = block.reshape((devices,) + pieces[0].shape)
    w_heads = block[:, : heads * shard].reshape(devices, heads, shard, columns)
    w_heads = w_heads.transpose(1, 0, 2, 3).reshape(heads, width, columns)
    small_all = block[:, heads * shard : heads * shard + 2].reshape(devices, 2 * columns)
    vectors = small_all[:, : 12 * shard].reshape(devices, 12, shard)
    vectors = vectors.transpose(1, 0, 2).reshape(12, width).astype(F32)
    inner_add = small_all[:, 12 * shard : 12 * shard + inner_shard].reshape(-1).astype(F32)
    output_add, gain_one, shift_one, outer_add, gain_two, shift_two = (
        vectors[6],
        vectors[7],
        vectors[8],
        vectors[9],
        vectors[10],
        vectors[11],
    )
    mine = pick(vectors.reshape(12, groups, heads, DH), g, 1)
    order = [1, 2, 3, 0, 4, 5]
    vec = jnp.zeros((heads, 8, LANES), F32)
    vec = vec.at[:, :6, :DH].set(jnp.stack([mine[i] for i in order], axis=1))

    inner_matrix = gather_rows(inner_weight, "xy")
    outer_and_output = gather_rows(
        jnp.concatenate([outer_weight, output_weight], axis=0), "yx"
    ).reshape(devices, inner_shard + shard, width)
    outer_matrix = outer_and_output[:, :inner_shard].reshape(-1, width)
    output_matrix = outer_and_output[:, inner_shard:].reshape(width, width)

    exponent = 2.0 * jnp.arange(half, dtype=F32) / width
    rates = (10000.0 ** (-exponent))[None, :]
    owners = c ^ jnp.arange(members, dtype=jnp.int32)
    starts = (owners * stretch).astype(F32)[:, None] * rates
    steps = jnp.arange(stretch, dtype=F32)[:, None] * rates
    cos_a, sin_a = jnp.cos(starts)[:, None], jnp.sin(starts)[:, None]
    cos_b, sin_b = jnp.cos(steps)[None], jnp.sin(steps)[None]
    trig = jnp.concatenate(
        [cos_a * cos_b - sin_a * sin_b, sin_a * cos_b + cos_a * sin_b], axis=2
    ).reshape(seq_len, width)
    slots = owners[:, None] * stretch + jnp.arange(stretch, dtype=jnp.int32)[None, :]
    key_valid = (slots.reshape(-1) < pick(lengths, s, 0)).astype(F32)
    kext = key_extension(kind_seq, key_valid)

    att, qt, kb, v1, qp, save, scl = attention_forward(x_seq, w_heads, vec, kext, trig)

    pieces = [att[:, :stretch]]
    for r in range(1, members):
        pieces.append(swap(att[:, r * stretch : (r + 1) * stretch], CTX, r))
    mixed = jnp.stack(pieces).reshape(2, 2, 2, span, stretch)
    mixed = flip_if(bit_z, flip_if(bit_b, flip_if(bit_x, mixed, 2), 1), 0)
    mixed = mixed.reshape(seqs, width, stretch)

    own_slots = c * stretch + jnp.arange(stretch, dtype=jnp.int32)
    row_valid = (own_slots[None, :] < lengths[:, None]).astype(F32)[..., None]
    attn_out = (
        jnp.einsum("bft,fw->btw", mixed, output_matrix, preferred_element_type=F32) + output_add
    )
    first_sum = inputs.astype(F32) + attn_out
    normed = layer_norm(first_sum, gain_one, shift_one)
    normed_low = normed.astype(BF)
    inner = jnp.einsum("btw,wf->btf", normed_low, inner_matrix, preferred_element_type=F32)
    inner = inner + inner_add
    activated_low = gelu_tanh(inner).astype(BF)
    outer = jnp.einsum("btf,fw->btw", activated_low, outer_matrix, preferred_element_type=F32)
    outer = outer + outer_add
    second_sum = normed + outer
    result = layer_norm(second_sum, gain_two, shift_two).astype(BF)
    sums = jnp.stack(
        [
            jnp.sum(first_sum * first_sum * row_valid, axis=(1, 2)),
            jnp.sum(attn_out * attn_out * row_valid, axis=(1, 2)),
            jnp.sum(outer * outer * row_valid, axis=(1, 2)),
        ],
        axis=1,
    )

    cotangent = out_grad.astype(F32) * row_valid
    unused_two, second_back = jax.vjp(layer_norm, second_sum, gain_two, shift_two)
    second_grad, gain_two_grad, shift_two_grad = second_back(cotangent)
    outer_low = second_grad.astype(BF)
    outer_add_grad = jnp.sum(outer_low.astype(F32), axis=(0, 1))
    outer_grad = jnp.einsum("btf,btw->fw", activated_low, outer_low, preferred_element_type=F32)
    activated_grad = jnp.einsum("btw,fw->btf", outer_low, outer_matrix, preferred_element_type=F32)
    unused_three, gelu_back = jax.vjp(gelu_tanh, inner)
    inner_low = gelu_back(activated_grad)[0].astype(BF)
    inner_add_grad = jnp.sum(inner_low.astype(F32), axis=(0, 1))
    inner_grad = jnp.einsum("btw,btf->wf", normed_low, inner_low, preferred_element_type=F32)
    normed_grad = second_grad + jnp.einsum(
        "btf,wf->btw", inner_low, inner_matrix, preferred_element_type=F32
    )
    unused_four, first_back = jax.vjp(layer_norm, first_sum, gain_one, shift_one)
    first_grad, gain_one_grad, shift_one_grad = first_back(normed_grad)
    attn_low = first_grad.astype(BF)
    output_add_grad = jnp.sum(attn_low.astype(F32), axis=(0, 1))
    output_grad = jnp.einsum("bft,btw->fw", mixed, attn_low, preferred_element_type=F32)
    mixed_grad = jnp.einsum("fw,btw->bft", output_matrix, attn_low, preferred_element_type=F32)

    mixed_grad = mixed_grad.astype(BF).reshape(2, 2, 2, span, stretch)
    mixed_grad = flip_if(bit_z, flip_if(bit_b, flip_if(bit_x, mixed_grad, 2), 1), 0)
    mixed_grad = mixed_grad.reshape(members, span, stretch)
    flat = jnp.zeros((stretch,), F32).at[: 3 * seqs].set(sums.reshape(-1))
    flat_high = lax.reduce_precision(flat, 8, 7)
    riders = jnp.zeros((8, stretch), BF)
    riders = riders.at[0].set(flat_high.astype(BF)).at[1].set((flat - flat_high).astype(BF))
    pieces = [jnp.concatenate([mixed_grad[0], riders], axis=0)]
    for r in range(1, members):
        pieces.append(swap(jnp.concatenate([mixed_grad[r], riders], axis=0), CTX, r))
    d_out = jnp.concatenate([piece[:span] for piece in pieces], axis=1)
    sums_all = sum(piece[span : span + 2].astype(F32) for piece in pieces)
    sums_all = (sums_all[0] + sums_all[1])[: 3 * seqs].reshape(seqs, 3)
    mean_squares = sums_all / (lengths.astype(F32)[:, None] * width)

    d_all, dwp, head_sums = attention_backward(
        d_out, w_heads, vec, kext, trig, qt, kb, v1, qp, save, scl
    )

    inner_own = scatter_rows(inner_grad.astype(BF), "yx")
    outer_and_output = jnp.concatenate(
        [
            outer_grad.astype(BF).reshape(devices, inner_shard, width),
            output_grad.astype(BF).reshape(devices, shard, width),
        ],
        axis=1,
    ).reshape(-1, width)
    outer_and_output = scatter_rows(outer_and_output, "xy")
    outer_own, output_own = outer_and_output[:inner_shard], outer_and_output[inner_shard:]

    partial = jnp.einsum(
        "hdt,hwd->tw", d_all, w_heads[:, :, : 3 * DH], preferred_element_type=F32
    ).astype(BF)
    partial = partial.reshape(2, 2, 2, stretch, width)
    left, right = partial[..., :half], partial[..., half:]
    left = add_low(left[:, :, 0], swap(left[:, :, 1], CTX, 1))
    right = add_low(right[:, 0], swap(right[:, 1], CTX, 2))
    left = add_low(left[:, 0], swap(left[:, 1], CTX, 2))
    right = add_low(right[:, 0], swap(right[:, 1], CTX, 1))
    both = jnp.concatenate([left, right], axis=2)
    input_terms = in_order(s, both[0], swap(both[1], CTX, 4), 0)
    input_grad = (first_grad + input_terms.astype(F32)).astype(BF)

    w_grad = jnp.einsum("tw,hdt->whd", x_seq, d_all, preferred_element_type=F32)
    w_grad = jnp.concatenate([w_grad, dwp.transpose(2, 0, 1)], axis=2).astype(BF)
    block = w_grad.reshape(2, 2, 2, groups, shard, heads * columns)
    block = add_low(pick(block, d % 2, 1), swap(pick(block, 1 - d % 2, 1), DP, 1))
    block = add_low(pick(block, d // 2, 0), swap(pick(block, 1 - d // 2, 0), DP, 2))
    block = add_low(pick(block, s, 0), swap(pick(block, 1 - s, 0), CTX, 4))
    pieces = [pick(block, g, 0)]
    for r in range(1, groups):
        pieces.append(swap(pick(block, g ^ r, 0), CTX, r))
    block = jnp.stack(pieces).reshape(2, 2, shard, heads * columns)
    block = flip_if(bit_b, flip_if(bit_x, block, 1), 0)
    block = block.reshape(groups, shard, heads, 4, DH).transpose(3, 1, 0, 2, 4)
    block = block.reshape(4, shard, width).astype(F32)

    value_sums = jnp.sum(d_all[:, 2 * DH :].astype(F32), axis=2)
    wide = jnp.concatenate(
        [value_sums[None], head_sums[:, :5, :DH].transpose(1, 0, 2)], axis=0
    ).reshape(6, span)
    wide = lax.dynamic_update_slice(jnp.zeros((6, width), F32), wide, (0, g * span))
    rest = jnp.stack(
        [
            output_add_grad,
            gain_one_grad,
            shift_one_grad,
            outer_add_grad,
            gain_two_grad,
            shift_two_grad,
        ]
    )
    table = jnp.concatenate([wide, rest]).reshape(12, devices, shard).transpose(1, 0, 2)
    table = jnp.concatenate(
        [
            table.reshape(devices, 12 * shard),
            inner_add_grad.reshape(devices, inner_shard),
        ],
        axis=1,
    )
    table = table.reshape(2, 2, 2, groups, -1)
    table = pick(table, d % 2, 1) + swap(pick(table, 1 - d % 2, 1), DP, 1)
    table = pick(table, d // 2, 0) + swap(pick(table, 1 - d // 2, 0), DP, 2)
    table = pick(table, s, 0) + swap(pick(table, 1 - s, 0), CTX, 4)
    total = pick(table, g, 0)
    for r in range(1, groups):
        total = total + swap(pick(table, g ^ r, 0), CTX, r)
    v = [total[i * shard : (i + 1) * shard] for i in range(12)]
    return (
        result,
        input_grad,
        block[0],
        block[1],
        block[2],
        v[0],
        block[3],
        v[1],
        v[2],
        v[3],
        jnp.stack([v[4], v[5]]),
        output_own,
        v[6],
        v[7],
        v[8],
        inner_own,
        total[12 * shard :],
        outer_own,
        v[9],
        v[10],
        v[11],
        mean_squares,
    )


def solution(mesh):
    in_specs = (
        P(DP, CTX, None),
        P(DP, CTX, None),
        P(DP),
        P(DP, CTX),
        P(ALL, None),
        P(ALL, None),
        P(ALL, None),
        P(ALL),
        P(ALL, None),
        P(ALL),
        P(ALL),
        P(ALL),
        P(None, ALL),
        P(ALL, None),
        P(ALL),
        P(ALL),
        P(ALL),
        P(ALL, None),
        P(ALL),
        P(ALL, None),
        P(ALL),
        P(ALL),
        P(ALL),
    )
    out_specs = (
        P(DP, CTX, None),
        P(DP, CTX, None),
        P(ALL, None),
        P(ALL, None),
        P(ALL, None),
        P(ALL),
        P(ALL, None),
        P(ALL),
        P(ALL),
        P(ALL),
        P(None, ALL),
        P(ALL, None),
        P(ALL),
        P(ALL),
        P(ALL),
        P(ALL, None),
        P(ALL),
        P(ALL, None),
        P(ALL),
        P(ALL),
        P(ALL),
        P(DP, None),
    )
    body = head_layout if takes_head_layout(mesh) else per_device
    return jax.shard_map(
        body, mesh=mesh, in_specs=in_specs, out_specs=out_specs, check_vma=False
    )
```

```python
import functools

import jax
import jax.numpy as jnp
from jax import lax
from jax.experimental import pallas as pl
from jax.experimental.pallas import tpu as pltpu
from jax.sharding import PartitionSpec as P

DP = "dp"
CTX = "ctx"
ALL = (DP, CTX)
H = 12
DH = 64
KEY_BLOCK = 512
MICRO = 2
SEQ_MB = 1


epsilon = 1e-06
masked_score = -1e30
maximal_precision = lax.Precision.HIGHEST


def layer_norm(hidden, gain_values, shift_values):
    center = hidden - jnp.mean(hidden, axis=-1, keepdims=True)
    variance = jnp.mean(center * center, axis=-1, keepdims=True)
    return center * lax.rsqrt(variance + epsilon) * gain_values + shift_values


def gelu_tanh(inner):
    return jax.nn.gelu(inner, approximate=True)


def position_table(anchor, number, columns):
    offsets = (anchor + jnp.arange(number, dtype=jnp.int32)).astype(jnp.float32)
    exponent = 2.0 * jnp.arange(columns // 2, dtype=jnp.float32) / columns
    angles = offsets[:, None] * (10000.0 ** (-exponent))[None, :]
    return jnp.concatenate([jnp.sin(angles), jnp.cos(angles)], axis=1)


def skew_rows(unscaled_scores, keys_count):
    leading = unscaled_scores.shape[:-2]
    rows_count = unscaled_scores.shape[-2]
    span_cols = unscaled_scores.shape[-1]
    flattened = unscaled_scores.reshape(leading + (rows_count * span_cols,))
    flattened = jnp.pad(flattened, [(0, 0)] * len(leading) + [(0, rows_count)])
    return flattened.reshape(leading + (rows_count, span_cols + 1))[..., :keys_count][..., ::-1]


def unskew_rows(grads_block, span_cols):
    leading = grads_block.shape[:-2]
    rows_count = grads_block.shape[-2]
    keys_count = grads_block.shape[-1]
    padded = jnp.pad(
        grads_block[..., ::-1], [(0, 0)] * (len(leading) + 1) + [(0, span_cols + 1 - keys_count)]
    )
    flattened = padded.reshape(leading + (rows_count * (span_cols + 1),))
    return flattened[..., : rows_count * span_cols].reshape(leading + (rows_count, span_cols))


def block_scores(
    query_content,
    query_relative_term,
    type_terms,
    query_kinds,
    key_rows,
    key_kinds,
    key_valid,
    relative_rows,
):
    content = jnp.einsum(
        "bqhd,bkhd->bhqk", query_content, key_rows, preferred_element_type=jnp.float32
    )
    unscaled_scores = jnp.einsum(
        "uply,xly->ulpx", query_relative_term, relative_rows, preferred_element_type=jnp.float32
    )
    same_kind = query_kinds[:, :, None] == key_kinds[:, None, :]
    type_same = jnp.transpose(type_terms[..., 1], (0, 2, 1))[..., None]
    type_other = jnp.transpose(type_terms[..., 0], (0, 2, 1))[..., None]
    summed = (
        content
        + skew_rows(unscaled_scores, key_rows.shape[1])
        + jnp.where(same_kind[:, None], type_same, type_other)
    )
    return (jnp.where(key_valid[:, None, None, :], summed, masked_score), same_kind)


def block_grads(
    query_content,
    query_relative_term,
    type_terms,
    query_kinds,
    log_total,
    row_delta,
    grad_rows,
    key_rows,
    value_rows,
    key_kinds,
    key_valid,
    relative_rows,
):
    scores, same_kind = block_scores(
        query_content,
        query_relative_term,
        type_terms,
        query_kinds,
        key_rows,
        key_kinds,
        key_valid,
        relative_rows,
    )
    probability = jnp.exp(scores - log_total[..., None])
    value_grad = jnp.einsum(
        "bhqk,bqhd->bkhd",
        probability.astype(jnp.bfloat16),
        grad_rows,
        preferred_element_type=jnp.float32,
    )
    prob_grad = jnp.einsum(
        "bqhd,bkhd->bhqk", grad_rows, value_rows, preferred_element_type=jnp.float32
    )
    score_grad = (probability * (prob_grad - row_delta[..., None])).astype(jnp.bfloat16)
    content_grad = jnp.einsum(
        "bhqk,bkhd->bqhd", score_grad, key_rows, preferred_element_type=jnp.float32
    )
    key_grad = jnp.einsum(
        "bhqk,bqhd->bkhd", score_grad, query_content, preferred_element_type=jnp.float32
    )
    unscaled_gradient = unskew_rows(score_grad, relative_rows.shape[0])
    position_grad = jnp.einsum(
        "aioy,yin->aoin", unscaled_gradient, relative_rows, preferred_element_type=jnp.float32
    )
    rel_grad = jnp.einsum(
        "gcrj,grcl->jcl", unscaled_gradient, query_relative_term, preferred_element_type=jnp.float32
    )
    wide_grad = score_grad.astype(jnp.float32)
    same_sum = jnp.sum(jnp.where(same_kind[:, None], wide_grad, 0.0), axis=-1)
    other_sum = jnp.sum(jnp.where(same_kind[:, None], 0.0, wide_grad), axis=-1)
    type_grad = jnp.transpose(jnp.stack([other_sum, same_sum], axis=-1), (0, 2, 1, 3))
    return (content_grad, position_grad, type_grad, key_grad, value_grad, rel_grad)


def per_device(
    inputs,
    out_grad,
    lengths,
    token_types,
    query_weight,
    key_weight,
    value_weight,
    value_bias,
    position_weight,
    content_bias,
    position_bias,
    type_bias,
    type_embed,
    output_weight,
    output_bias,
    first_gain,
    first_shift,
    inner_weight,
    inner_bias,
    outer_weight,
    outer_bias,
    second_gain,
    second_shift,
):
    stretch = inputs.shape[1]
    width = inputs.shape[2]
    seq_len = stretch * lax.axis_size(CTX)
    stretch_start = lax.axis_index(CTX) * stretch
    window = seq_len + stretch - 1
    scale_query = DH ** (-0.5)
    own_positions = stretch_start + jnp.arange(stretch, dtype=jnp.int32)
    table_forward = position_table(stretch_start - seq_len + 1, window, width).astype(jnp.bfloat16)
    outputs_list = []
    input_grads = []
    stat_rows = []
    grads_total = None
    rel_total = jnp.zeros((window, width), jnp.float32)
    for micro_index in range(MICRO):
        first_seq = micro_index * SEQ_MB
        sequence_input = inputs[first_seq : first_seq + SEQ_MB]
        seq_grad = out_grad[first_seq : first_seq + SEQ_MB]
        seq_kinds = token_types[first_seq : first_seq + SEQ_MB].astype(jnp.bfloat16)
        length_col = lengths[first_seq : first_seq + SEQ_MB][:, None]
        seq_count = sequence_input.shape[0]
        heads_shape = (seq_count, stretch, H, DH)
        full_shape = (seq_count, seq_len, H, DH)
        row_valid = (own_positions[None, :] < length_col).astype(jnp.float32)[..., None]
        gathered = (
            lax.all_gather(query_weight, ALL, axis=0, tiled=True),
            lax.all_gather(key_weight, ALL, axis=0, tiled=True),
            lax.all_gather(value_weight, ALL, axis=0, tiled=True),
            lax.all_gather(value_bias, ALL, axis=0, tiled=True),
            lax.all_gather(position_weight, ALL, axis=0, tiled=True),
            lax.all_gather(content_bias, ALL, axis=0, tiled=True),
            lax.all_gather(position_bias, ALL, axis=0, tiled=True),
            lax.all_gather(type_bias, ALL, axis=0, tiled=True),
            lax.all_gather(type_embed, ALL, axis=1, tiled=True),
            lax.all_gather(output_weight, ALL, axis=0, tiled=True),
            lax.all_gather(output_bias, ALL, axis=0, tiled=True),
            lax.all_gather(first_gain, ALL, axis=0, tiled=True),
            lax.all_gather(first_shift, ALL, axis=0, tiled=True),
            lax.all_gather(inner_weight, ALL, axis=0, tiled=True),
            lax.all_gather(inner_bias, ALL, axis=0, tiled=True),
            lax.all_gather(outer_weight, ALL, axis=0, tiled=True),
            lax.all_gather(outer_bias, ALL, axis=0, tiled=True),
            lax.all_gather(second_gain, ALL, axis=0, tiled=True),
            lax.all_gather(second_shift, ALL, axis=0, tiled=True),
        )
        (
            query_matrix,
            key_matrix,
            value_matrix,
            value_add,
            position_mat,
            content_add,
            position_add,
            type_add,
            type_table,
            output_matrix,
            output_add,
            gain_one,
            shift_one,
            inner_matrix,
            inner_add,
            outer_matrix,
            outer_add,
            gain_two,
            shift_two,
        ) = gathered
        scaled = (
            jnp.dot(sequence_input, query_matrix, preferred_element_type=jnp.float32) * scale_query
        )
        query_content = (
            (scaled + content_add.astype(jnp.float32)).astype(jnp.bfloat16).reshape(heads_shape)
        )
        query_relative_term = (
            (scaled + position_add.astype(jnp.float32)).astype(jnp.bfloat16).reshape(heads_shape)
        )
        with_type = (scaled + type_add.astype(jnp.float32)).reshape(heads_shape)
        type_heads = type_table.astype(jnp.float32).reshape(2, H, DH)
        type_terms = jnp.einsum(
            "bqhd,shd->bqhs", with_type, type_heads, precision=maximal_precision
        )
        key_rows = jnp.dot(sequence_input, key_matrix, preferred_element_type=jnp.float32).astype(
            jnp.bfloat16
        )
        value_rows = (
            jnp.dot(sequence_input, value_matrix, preferred_element_type=jnp.float32)
            + value_add.astype(jnp.float32)
        ).astype(jnp.bfloat16)
        rel_forward = (
            jnp.dot(table_forward, position_mat, preferred_element_type=jnp.float32)
            .astype(jnp.bfloat16)
            .reshape(window, H, DH)
        )
        start_state = (
            jnp.full((seq_count, H, stretch), masked_score, jnp.float32),
            jnp.zeros((seq_count, H, stretch), jnp.float32),
            jnp.zeros(heads_shape, jnp.float32),
        )
        piece_keys = lax.all_gather(key_rows, CTX, axis=1, tiled=True)
        piece_values = lax.all_gather(value_rows, CTX, axis=1, tiled=True)
        piece_kinds = lax.all_gather(seq_kinds, CTX, axis=1, tiled=True)
        number = piece_keys.shape[1]
        block_rows = KEY_BLOCK

        def one_block(running, offset):
            run_max, run_total, run_acc = running
            part_keys = lax.dynamic_slice_in_dim(piece_keys, offset, block_rows, 1).reshape(
                seq_count, block_rows, H, DH
            )
            part_values = lax.dynamic_slice_in_dim(piece_values, offset, block_rows, 1).reshape(
                seq_count, block_rows, H, DH
            )
            part_kinds = lax.dynamic_slice_in_dim(piece_kinds, offset, block_rows, 1)
            relative_rows = lax.dynamic_slice_in_dim(
                rel_forward, seq_len - offset - block_rows, stretch + block_rows - 1, 0
            )
            key_valid = (offset + jnp.arange(block_rows, dtype=jnp.int32))[None, :] < length_col
            scores, same_kind = block_scores(
                query_content,
                query_relative_term,
                type_terms,
                seq_kinds,
                part_keys,
                part_kinds,
                key_valid,
                relative_rows,
            )
            new_max = jnp.maximum(run_max, jnp.max(scores, axis=-1))
            factor = jnp.exp(run_max - new_max)
            weights_block = jnp.exp(scores - new_max[..., None])
            run_total = run_total * factor + jnp.sum(weights_block, axis=-1)
            mixed_rows = jnp.einsum(
                "bhqk,bkhd->bqhd",
                weights_block.astype(jnp.bfloat16),
                part_values,
                preferred_element_type=jnp.float32,
            )
            run_acc = run_acc * jnp.transpose(factor, (0, 2, 1))[..., None] + mixed_rows
            return ((new_max, run_total, run_acc), None)

        offsets = jnp.arange(number // block_rows, dtype=jnp.int32) * block_rows
        result_state, unused = lax.scan(one_block, start_state, offsets)
        run_max, run_total, run_acc = result_state
        log_total = run_max + jnp.log(run_total)
        attended = run_acc / jnp.transpose(run_total, (0, 2, 1))[..., None]
        attended_reduced = attended.astype(jnp.bfloat16).reshape(seq_count, stretch, width)
        attn_out = jnp.dot(
            attended_reduced, output_matrix, preferred_element_type=jnp.float32
        ) + output_add.astype(jnp.float32)
        first_sum = sequence_input.astype(jnp.float32) + attn_out
        normed = layer_norm(first_sum, gain_one.astype(jnp.float32), shift_one.astype(jnp.float32))
        normed_reduced = normed.astype(jnp.bfloat16)
        inner = jnp.dot(
            normed_reduced, inner_matrix, preferred_element_type=jnp.float32
        ) + inner_add.astype(jnp.float32)
        activated_reduced = gelu_tanh(inner).astype(jnp.bfloat16)
        outer = jnp.dot(
            activated_reduced, outer_matrix, preferred_element_type=jnp.float32
        ) + outer_add.astype(jnp.float32)
        second_sum = normed + outer
        result = layer_norm(second_sum, gain_two.astype(jnp.float32), shift_two.astype(jnp.float32))
        outputs_list.append(result.astype(jnp.bfloat16))
        stat_rows.append(
            jnp.stack(
                [
                    jnp.sum(first_sum * first_sum * row_valid, axis=(1, 2)),
                    jnp.sum(attn_out * attn_out * row_valid, axis=(1, 2)),
                    jnp.sum(outer * outer * row_valid, axis=(1, 2)),
                ],
                axis=1,
            )
        )
        back_set = (
            lax.all_gather(query_weight, ALL, axis=0, tiled=True),
            lax.all_gather(key_weight, ALL, axis=0, tiled=True),
            lax.all_gather(value_weight, ALL, axis=0, tiled=True),
            lax.all_gather(value_bias, ALL, axis=0, tiled=True),
            lax.all_gather(position_weight, ALL, axis=0, tiled=True),
            lax.all_gather(content_bias, ALL, axis=0, tiled=True),
            lax.all_gather(position_bias, ALL, axis=0, tiled=True),
            lax.all_gather(type_bias, ALL, axis=0, tiled=True),
            lax.all_gather(type_embed, ALL, axis=1, tiled=True),
            lax.all_gather(output_weight, ALL, axis=0, tiled=True),
            lax.all_gather(output_bias, ALL, axis=0, tiled=True),
            lax.all_gather(first_gain, ALL, axis=0, tiled=True),
            lax.all_gather(first_shift, ALL, axis=0, tiled=True),
            lax.all_gather(inner_weight, ALL, axis=0, tiled=True),
            lax.all_gather(inner_bias, ALL, axis=0, tiled=True),
            lax.all_gather(outer_weight, ALL, axis=0, tiled=True),
            lax.all_gather(outer_bias, ALL, axis=0, tiled=True),
            lax.all_gather(second_gain, ALL, axis=0, tiled=True),
            lax.all_gather(second_shift, ALL, axis=0, tiled=True),
        )
        (
            query_matrix,
            key_matrix,
            value_matrix,
            value_add,
            position_mat,
            content_add,
            position_add,
            type_add,
            type_table,
            output_matrix,
            output_add,
            gain_one,
            shift_one,
            inner_matrix,
            inner_add,
            outer_matrix,
            outer_add,
            gain_two,
            shift_two,
        ) = back_set
        type_heads = type_table.astype(jnp.float32).reshape(2, H, DH)
        cotangent = seq_grad.astype(jnp.float32) * row_valid
        unused_two, second_back = jax.vjp(
            layer_norm, second_sum, gain_two.astype(jnp.float32), shift_two.astype(jnp.float32)
        )
        second_grad, gain_two_grad, shift_two_grad = second_back(cotangent)
        outer_reduced = second_grad.astype(jnp.bfloat16)
        outer_add_grad = jnp.sum(outer_reduced.astype(jnp.float32), axis=(0, 1))
        outer_mat_grad = jnp.einsum(
            "hpi,hpt->it", activated_reduced, outer_reduced, preferred_element_type=jnp.float32
        )
        activated_grad = jnp.einsum(
            "unk,rk->unr", outer_reduced, outer_matrix, preferred_element_type=jnp.float32
        )
        unused_three, gelu_back = jax.vjp(gelu_tanh, inner)
        inner_reduced = gelu_back(activated_grad)[0].astype(jnp.bfloat16)
        inner_add_grad = jnp.sum(inner_reduced.astype(jnp.float32), axis=(0, 1))
        inner_mat_grad = jnp.einsum(
            "psu,psy->uy", normed_reduced, inner_reduced, preferred_element_type=jnp.float32
        )
        normed_grad = second_grad + jnp.einsum(
            "tma,ra->tmr", inner_reduced, inner_matrix, preferred_element_type=jnp.float32
        )
        unused_four, first_back = jax.vjp(
            layer_norm, first_sum, gain_one.astype(jnp.float32), shift_one.astype(jnp.float32)
        )
        first_grad, gain_one_grad, shift_one_grad = first_back(normed_grad)
        attention_reduced = first_grad.astype(jnp.bfloat16)
        output_add_grad = jnp.sum(attention_reduced.astype(jnp.float32), axis=(0, 1))
        output_mat_grad = jnp.einsum(
            "yim,yig->mg", attended_reduced, attention_reduced, preferred_element_type=jnp.float32
        )
        grad_rows = (
            jnp.einsum(
                "jcy,py->jcp", attention_reduced, output_matrix, preferred_element_type=jnp.float32
            )
            .astype(jnp.bfloat16)
            .reshape(heads_shape)
        )
        row_delta = jnp.einsum(
            "bqhd,bqhd->bhq", grad_rows.astype(jnp.float32), attended, precision=maximal_precision
        )
        all_keys, all_values, all_kinds = (
            lax.all_gather(key_rows, CTX, axis=1, tiled=True),
            lax.all_gather(value_rows, CTX, axis=1, tiled=True),
            lax.all_gather(seq_kinds, CTX, axis=1, tiled=True),
        )

        def key_step(running, key_start):
            content_acc, position_acc, type_acc, key_acc, value_acc, rel_acc = running
            part_keys = lax.dynamic_slice_in_dim(all_keys, key_start, KEY_BLOCK, 1).reshape(
                seq_count, KEY_BLOCK, H, DH
            )
            part_values = lax.dynamic_slice_in_dim(all_values, key_start, KEY_BLOCK, 1).reshape(
                seq_count, KEY_BLOCK, H, DH
            )
            part_kinds = lax.dynamic_slice_in_dim(all_kinds, key_start, KEY_BLOCK, 1)
            rel_start = seq_len - key_start - KEY_BLOCK
            relative_rows = lax.dynamic_slice_in_dim(
                rel_forward, rel_start, stretch + KEY_BLOCK - 1, 0
            )
            key_valid = (key_start + jnp.arange(KEY_BLOCK, dtype=jnp.int32))[None, :] < length_col
            pieces = block_grads(
                query_content,
                query_relative_term,
                type_terms,
                seq_kinds,
                log_total,
                row_delta,
                grad_rows,
                part_keys,
                part_values,
                part_kinds,
                key_valid,
                relative_rows,
            )
            content_part, position_part, type_part, key_part, value_part, rel_part = pieces
            key_acc = lax.dynamic_update_slice_in_dim(key_acc, key_part, key_start, 1)
            value_acc = lax.dynamic_update_slice_in_dim(value_acc, value_part, key_start, 1)
            rel_old = lax.dynamic_slice_in_dim(rel_acc, rel_start, stretch + KEY_BLOCK - 1, 0)
            rel_acc = lax.dynamic_update_slice_in_dim(rel_acc, rel_old + rel_part, rel_start, 0)
            return (
                (
                    content_acc + content_part,
                    position_acc + position_part,
                    type_acc + type_part,
                    key_acc,
                    value_acc,
                    rel_acc,
                ),
                None,
            )

        start_grads = (
            jnp.zeros(heads_shape, jnp.float32),
            jnp.zeros(heads_shape, jnp.float32),
            jnp.zeros((seq_count, stretch, H, 2), jnp.float32),
            jnp.zeros(full_shape, jnp.float32),
            jnp.zeros(full_shape, jnp.float32),
            jnp.zeros((window, H, DH), jnp.float32),
        )
        final_grads, unused_five = lax.scan(
            key_step, start_grads, jnp.arange(seq_len // KEY_BLOCK, dtype=jnp.int32) * KEY_BLOCK
        )
        content_grad, position_grad, type_grad, key_all, value_all, rel_grad = final_grads
        key_grad, value_grad = (
            lax.psum_scatter(
                key_all.astype(jnp.bfloat16), CTX, scatter_dimension=1, tiled=True
            ).astype(jnp.float32),
            lax.psum_scatter(
                value_all.astype(jnp.bfloat16), CTX, scatter_dimension=1, tiled=True
            ).astype(jnp.float32),
        )
        type_part_grad = jnp.einsum(
            "bqhs,shd->bqhd", type_grad, type_heads, precision=maximal_precision
        )
        query_grad = content_grad + position_grad + type_part_grad
        content_add_grad = jnp.sum(content_grad, axis=(0, 1)).reshape(width)
        position_add_grad = jnp.sum(position_grad, axis=(0, 1)).reshape(width)
        type_add_grad = jnp.sum(type_part_grad, axis=(0, 1)).reshape(width)
        rel_total = rel_total + rel_grad.reshape(window, width)
        query_reduced = query_grad.astype(jnp.bfloat16).reshape(seq_count, stretch, width)
        key_reduced = key_grad.astype(jnp.bfloat16).reshape(seq_count, stretch, width)
        value_reduced = value_grad.astype(jnp.bfloat16).reshape(seq_count, stretch, width)
        type_table_grad = jnp.einsum(
            "bqhs,bqhd->shd", type_grad, with_type, precision=maximal_precision
        ).reshape(2, width)
        query_mat_grad = (
            jnp.einsum(
                "orh,org->hg", sequence_input, query_reduced, preferred_element_type=jnp.float32
            )
            * scale_query
        )
        key_mat_grad = jnp.einsum(
            "orh,org->hg", sequence_input, key_reduced, preferred_element_type=jnp.float32
        )
        value_mat_grad = jnp.einsum(
            "orh,org->hg", sequence_input, value_reduced, preferred_element_type=jnp.float32
        )
        value_add_grad = jnp.sum(value_reduced.astype(jnp.float32), axis=(0, 1))
        input_grad = (
            first_grad
            + jnp.einsum(
                "sux,fx->suf", query_reduced, query_matrix, preferred_element_type=jnp.float32
            )
            * scale_query
            + jnp.einsum("sux,fx->suf", key_reduced, key_matrix, preferred_element_type=jnp.float32)
            + jnp.einsum(
                "sux,fx->suf", value_reduced, value_matrix, preferred_element_type=jnp.float32
            )
        )
        input_grads.append(input_grad.astype(jnp.bfloat16))
        micro_grads = (
            query_mat_grad,
            key_mat_grad,
            value_mat_grad,
            value_add_grad,
            content_add_grad,
            position_add_grad,
            type_add_grad,
            type_table_grad,
            output_mat_grad,
            output_add_grad,
            gain_one_grad,
            shift_one_grad,
            inner_mat_grad,
            inner_add_grad,
            outer_mat_grad,
            outer_add_grad,
            gain_two_grad,
            shift_two_grad,
        )
        if grads_total is None:
            grads_total = micro_grads
        else:
            grads_total = jax.tree.map(jnp.add, grads_total, micro_grads)
    rel_high = rel_total.astype(jnp.bfloat16)
    rel_rest = (rel_total - rel_high.astype(jnp.float32)).astype(jnp.bfloat16)
    contract_rows = (((0,), (0,)), ((), ()))
    position_mat_grad = lax.dot_general(
        table_forward, rel_high, contract_rows, preferred_element_type=jnp.float32
    ) + lax.dot_general(table_forward, rel_rest, contract_rows, preferred_element_type=jnp.float32)
    (
        query_total,
        key_total,
        value_total,
        value_add_total,
        content_total,
        position_total,
        type_total,
        table_total,
        output_total,
        output_add_total,
        gain_one_total,
        shift_one_total,
        inner_total,
        inner_add_total,
        outer_total,
        outer_add_total,
        gain_two_total,
        shift_two_total,
    ) = grads_total
    reduced = (
        lax.psum_scatter(query_total, ALL, scatter_dimension=0, tiled=True),
        lax.psum_scatter(key_total, ALL, scatter_dimension=0, tiled=True),
        lax.psum_scatter(value_total, ALL, scatter_dimension=0, tiled=True),
        lax.psum_scatter(value_add_total, ALL, scatter_dimension=0, tiled=True),
        lax.psum_scatter(position_mat_grad, ALL, scatter_dimension=0, tiled=True),
        lax.psum_scatter(content_total, ALL, scatter_dimension=0, tiled=True),
        lax.psum_scatter(position_total, ALL, scatter_dimension=0, tiled=True),
        lax.psum_scatter(type_total, ALL, scatter_dimension=0, tiled=True),
        lax.psum_scatter(table_total, ALL, scatter_dimension=1, tiled=True),
        lax.psum_scatter(output_total, ALL, scatter_dimension=0, tiled=True),
        lax.psum_scatter(output_add_total, ALL, scatter_dimension=0, tiled=True),
        lax.psum_scatter(gain_one_total, ALL, scatter_dimension=0, tiled=True),
        lax.psum_scatter(shift_one_total, ALL, scatter_dimension=0, tiled=True),
        lax.psum_scatter(inner_total, ALL, scatter_dimension=0, tiled=True),
        lax.psum_scatter(inner_add_total, ALL, scatter_dimension=0, tiled=True),
        lax.psum_scatter(outer_total, ALL, scatter_dimension=0, tiled=True),
        lax.psum_scatter(outer_add_total, ALL, scatter_dimension=0, tiled=True),
        lax.psum_scatter(gain_two_total, ALL, scatter_dimension=0, tiled=True),
        lax.psum_scatter(shift_two_total, ALL, scatter_dimension=0, tiled=True),
    )
    sums_all = lax.psum(jnp.concatenate(stat_rows, axis=0), CTX)
    mean_squares = sums_all / (lengths.astype(jnp.float32)[:, None] * width)
    return (
        (jnp.concatenate(outputs_list, axis=0), jnp.concatenate(input_grads, axis=0))
        + tuple(reduced)
        + (mean_squares,)
    )


LANES = 128
BF = jnp.bfloat16
F32 = jnp.float32
ROWS_CC = (((1,), (1,)), ((), ()))
COLS_CC = (((0,), (0,)), ((), ()))
ROWCOL = (((1,), (0,)), ((), ()))


def mm(a, b, dims):
    return lax.dot_general(a, b, dims, preferred_element_type=F32)


def split3(v):
    hi = v.astype(BF).astype(F32)
    mid = (v - hi).astype(BF).astype(F32)
    lo = (v - hi - mid).astype(BF).astype(F32)
    return hi, mid, lo


def attention_forward_kernel(tile, x_ref, w_ref, vec_ref, kext_ref, trig_ref,
                             att_ref, qt_ref, kb_ref, v1_ref, qp_ref, save_ref, scl_ref, wh_ref, kt_ref):
    step = pl.program_id(1)
    rows = x_ref.shape[0]
    width = x_ref.shape[1]
    half = width // 2
    lane = lax.broadcasted_iota(jnp.int32, (tile, LANES), 1)
    low = lane < DH

    @pl.when((pl.program_id(0) == 0) & (step == 0))
    def _():
        kt_ref[:, :width] = trig_ref[...].astype(BF)

    @pl.when(step == 0)
    def _():
        vec = vec_ref[0]
        w = w_ref[...].astype(F32).reshape(width, 2 * LANES).astype(BF)
        wh_ref[0] = w
        w_lane = lax.broadcasted_iota(jnp.int32, (width, LANES), 1)
        w_pos = jnp.where(w_lane < DH, pltpu.roll(w[:, LANES:].astype(F32), DH, 1), 0.0).astype(BF)

        def body(i, carry):
            at = pl.ds(pl.multiple_of(i * tile, tile), tile)
            proj = mm(x_ref[at, :], w, ROWCOL)
            kext = kext_ref[at, :].astype(F32)
            kind = kext[:, DH + 3:DH + 4]
            scaled = jnp.where(low, proj[:, :LANES] * DH ** -0.5, 0.0)
            scl_ref[0, at, :] = scaled
            kb = jnp.where(low, pltpu.roll(proj[:, :LANES], DH, 1), kext).astype(BF)
            kb_ref[0, at, :] = kb
            kt_ref[at, width:] = kb
            one_v = (lane >= DH) & (lane < DH + 3)
            v1_ref[0, at, :] = jnp.where(low, proj[:, LANES:] + vec[3:4, :], jnp.where(one_v, 1.0, 0.0)).astype(BF)
            with_type = scaled + vec[2:3, :]
            term0 = jnp.sum(with_type * vec[4:5, :], axis=1, keepdims=True)
            term1 = jnp.sum(with_type * vec[5:6, :], axis=1, keepdims=True)
            base = jnp.where(kind > 0.5, term0, term1)
            slope = jnp.where(kind > 0.5, term1 - term0, term0 - term1)
            b_hi, b_mid, b_lo = split3(base)
            s_hi, s_mid, s_lo = split3(slope)
            ext = jnp.where(lane == DH, b_hi, 0.0)
            ext = jnp.where(lane == DH + 1, b_mid, ext)
            ext = jnp.where(lane == DH + 2, b_lo, ext)
            ext = jnp.where(lane == DH + 3, s_hi, ext)
            ext = jnp.where(lane == DH + 4, s_mid, ext)
            ext = jnp.where(lane == DH + 5, 1.0, ext)
            qt_ref[0, at, width:] = jnp.where(low, scaled + vec[0:1, :], ext).astype(BF)
            qp = jnp.where(low, scaled + vec[1:2, :], 0.0).astype(BF)
            qp_ref[0, at, :] = qp
            grow = mm(qp, w_pos, ROWS_CC)
            q_sin = grow[:, :half]
            q_cos = grow[:, half:]
            c = trig_ref[at, :half]
            s = trig_ref[at, half:]
            qt_ref[0, at, :half] = (q_sin * s + q_cos * c).astype(BF)
            qt_ref[0, at, half:width] = (q_cos * s - q_sin * c).astype(BF)
            return carry

        lax.fori_loop(0, rows // tile, body, 0)

    at = pl.ds(pl.multiple_of(step * tile, tile), tile)
    scores = mm(qt_ref[0, at, :], kt_ref[...], ROWS_CC)
    top = jnp.max(scores, axis=1, keepdims=True)
    prob = jnp.exp(scores - top)
    mixed = mm(prob.astype(BF), v1_ref[0], ROWCOL)
    total = mixed[:, DH:DH + 1]
    att = mixed / total
    save_ref[0] = jnp.where(low, att, top + jnp.log(total))
    att_t = jnp.transpose(att)[:DH, :].astype(BF)
    for i in range(tile // LANES):
        att_ref[i] = att_t[:, i * LANES:(i + 1) * LANES]


def attention_backward_kernel(tile, do_ref, x_ref, w_ref, vec_ref, kext_ref, trig_ref,
                              qt_ref, kb_ref, v1_ref, qp_ref, save_ref, scl_ref,
                              dx_ref, dw_ref, small_ref,
                              kt_ref, q_ref, dk_acc, dv_acc, d_ref, dwp_ref, dx_acc):
    step = pl.program_id(1)
    width = trig_ref.shape[1]
    half = width // 2
    lane = lax.broadcasted_iota(jnp.int32, (tile, LANES), 1)
    low = lane < DH

    @pl.when((pl.program_id(0) == 0) & (step == 0))
    def _():
        kt_ref[:, :width] = trig_ref[...].astype(BF)

    @pl.when(step == 0)
    def _():
        kt_ref[:, width:] = kb_ref[0]
        dk_acc[...] = jnp.zeros_like(dk_acc)
        dv_acc[...] = jnp.zeros_like(dv_acc)
        dwp_ref[...] = jnp.zeros_like(dwp_ref)
        small_ref[...] = jnp.zeros_like(small_ref)

    at = pl.ds(pl.multiple_of(step * tile, tile), tile)
    w = w_ref[0]
    w_lane = lax.broadcasted_iota(jnp.int32, (width, LANES), 1)
    w_pos = jnp.where(w_lane < DH, pltpu.roll(w[:, LANES:].astype(F32), DH, 1), 0.0).astype(BF)
    save = save_ref[0]
    lse = save[:, DH:DH + 1]
    do_t = jnp.concatenate([do_ref[i] for i in range(tile // LANES)], axis=1).astype(F32)
    d_out = jnp.transpose(jnp.concatenate([do_t, jnp.zeros_like(do_t)], axis=0))
    delta = jnp.sum(d_out * save, axis=1, keepdims=True)
    l_hi, l_mid, l_lo = split3(-lse)
    d_hi, d_mid, d_lo = split3(-delta)
    q_block = qt_ref[0, :, width:].astype(F32)
    q_ref[:, :width] = qt_ref[0, :, :width]
    q_block = jnp.where(lane == DH + 6, l_hi, q_block)
    q_block = jnp.where(lane == DH + 7, l_mid, q_block)
    q_block = jnp.where(lane == DH + 8, l_lo, q_block)
    q_block = q_block.astype(BF)
    q_ref[:, width:] = q_block
    ext = jnp.where(lane == DH, d_hi, d_out)
    ext = jnp.where(lane == DH + 1, d_mid, ext)
    ext = jnp.where(lane == DH + 2, d_lo, ext)
    d_ext = ext.astype(BF)
    prob = jnp.exp(mm(q_ref[...], kt_ref[...], ROWS_CC))
    dv_acc[...] += mm(d_ext, prob.astype(BF), COLS_CC)
    d_score = (prob * mm(d_ext, v1_ref[0], ROWS_CC)).astype(BF)
    dk_acc[...] += mm(q_block, d_score, COLS_CC)
    dq = mm(d_score, kt_ref[...], ROWCOL)
    c = trig_ref[at, :half]
    s = trig_ref[at, half:]
    du_c = dq[:, :half]
    du_s = dq[:, half:width]
    back = jnp.concatenate([s * du_c - c * du_s, c * du_c + s * du_s], axis=1).astype(BF)
    d_block = dq[:, width:]
    d_pos = mm(back, w_pos, ROWCOL)
    dwp_ref[...] += mm(qp_ref[0], back, COLS_CC)[:DH, :]
    vec = vec_ref[0]
    kind = kext_ref[...][:, DH + 3:DH + 4].astype(F32)
    every = d_block[:, DH:DH + 1]
    ones = d_block[:, DH + 3:DH + 4]
    g_same = jnp.where(kind > 0.5, ones, every - ones)
    g_other = jnp.where(kind > 0.5, every - ones, ones)
    type_part = g_other * vec[4:5, :] + g_same * vec[5:6, :]
    d_content = jnp.where(low, d_block, 0.0)
    with_type = jnp.where(low, scl_ref[0] + vec[2:3, :], 0.0)
    d_scaled = d_content + d_pos + type_part
    d_ref[:DH, at] = (jnp.transpose(d_scaled)[:DH, :] * DH ** -0.5).astype(BF)
    sums = [jnp.sum(v, axis=0, keepdims=True) for v in
            (d_content, d_pos, type_part, g_other * with_type, g_same * with_type)]
    small_ref[0] += jnp.concatenate(sums + [jnp.zeros((3, LANES), F32)], axis=0)

    @pl.when(step == pl.num_programs(1) - 1)
    def _():
        d_ref[DH:2 * DH] = dk_acc[:DH, :].astype(BF)
        dv_low = dv_acc[:DH, :].astype(BF)
        d_ref[2 * DH:] = dv_low
        dv_sum = jnp.sum(dv_low.astype(F32), axis=1, keepdims=True)
        dv_sum = jnp.transpose(jnp.broadcast_to(jnp.concatenate([dv_sum, dv_sum], axis=0), (LANES, LANES)))
        small_ref[0, 5:6, :] = dv_sum[:1, :]
        d_wt = mm(d_ref[...], x_ref[...], ROWCOL)
        d_w = jnp.transpose(jnp.concatenate([d_wt, dwp_ref[...]], axis=0))
        shard = dw_ref.shape[1]
        for i in range(dw_ref.shape[0]):
            dw_ref[i] = d_w[i * shard:(i + 1) * shard, :].astype(BF)
        d_x = lax.dot_general(d_ref[...], w_ref[0][:, :3 * DH], (((0,), (1,)), ((), ())), preferred_element_type=F32)

        @pl.when(pl.program_id(0) == 0)
        def _():
            dx_acc[...] = d_x

        @pl.when(pl.program_id(0) > 0)
        def _():
            dx_acc[...] += d_x

        @pl.when(pl.program_id(0) == pl.num_programs(0) - 1)
        def _():
            dx_ref[...] = dx_acc[...].astype(BF)


def attention_forward(x, w_block, first, count, heads, vec, kext, trig, previous=(), tile=512):
    rows, width = x.shape
    owners = w_block.shape[0]
    shard = width // owners
    full = width + LANES
    per_head = lambda shape: pl.BlockSpec((1,) + shape, lambda h, t: (first + h, 0, 0))
    fixed = lambda shape: pl.BlockSpec(shape, lambda h, t: (0, 0))
    flops = count * rows * 2 * (width * 256 + rows * full + rows * LANES)
    S = jax.ShapeDtypeStruct
    kernel = functools.partial(attention_forward_kernel, tile)
    skip = len(previous)
    return pl.pallas_call(
        lambda *refs: kernel(*refs[:5], *refs[5 + skip:]),
        grid=(count, rows // tile),
        in_specs=[fixed((rows, width)), pl.BlockSpec((owners, shard, 2 * LANES), lambda h, t: (0, first + h, 0)),
                  per_head((8, LANES)), fixed((rows, LANES)), fixed((rows, width))]
        + [pl.BlockSpec(memory_space=pl.ANY)] * skip,
        out_specs=[pl.BlockSpec((tile // LANES, DH, LANES), lambda h, t: (t, first + h, 0)),
                   per_head((rows, full)), per_head((rows, LANES)), per_head((rows, LANES)),
                   per_head((rows, LANES)),
                   pl.BlockSpec((1, tile, LANES), lambda h, t: (first + h, t, 0)),
                   per_head((rows, LANES)), per_head((width, 2 * LANES))],
        out_shape=[S((rows // LANES, heads * DH, LANES), BF), S((heads, rows, full), BF),
                   S((heads, rows, LANES), BF), S((heads, rows, LANES), BF), S((heads, rows, LANES), BF),
                   S((heads, rows, LANES), F32), S((heads, rows, LANES), F32), S((heads, width, 2 * LANES), BF)],
        input_output_aliases={5 + i: i for i in range(skip)},
        scratch_shapes=[pltpu.VMEM((rows, full), BF)],
        compiler_params=pltpu.CompilerParams(dimension_semantics=("arbitrary", "arbitrary"),
                                             vmem_limit_bytes=56 * 2 ** 20),
        cost_estimate=pl.CostEstimate(flops=flops, bytes_accessed=rows * width * 16, transcendentals=count * rows * rows),
        name="attention_forward",
    )(x, w_block, vec, kext, trig, *previous)


def attention_backward(d_out, x, w, vec, kext, trig, qt, kb, v1, qp, save, scl, owners, block_rows, tile=512):
    heads, rows, full = qt.shape
    width = full - LANES
    shard = width // owners
    per_head = lambda shape: pl.BlockSpec((1,) + shape, lambda h, t: (h, 0, 0))
    per_tile = lambda cols: pl.BlockSpec((1, tile, cols), lambda h, t: (h, t, 0))
    fixed = lambda shape: pl.BlockSpec(shape, lambda h, t: (0, 0))
    flops = heads * rows * 2 * (2 * rows * full + 3 * rows * LANES)
    return pl.pallas_call(
        functools.partial(attention_backward_kernel, tile),
        grid=(heads, rows // tile),
        in_specs=[pl.BlockSpec((tile // LANES, DH, LANES), lambda h, t: (t, h, 0)), fixed((rows, width)),
                  per_head((width, 256)), per_head((8, LANES)),
                  pl.BlockSpec((tile, LANES), lambda h, t: (t, 0)), fixed((rows, width)),
                  per_tile(full), per_head((rows, LANES)), per_head((rows, LANES)), per_tile(LANES),
                  per_tile(LANES), per_tile(LANES)],
        out_specs=[fixed((rows, width)), pl.BlockSpec((owners, shard, 2 * LANES), lambda h, t: (0, h, 0)),
                   per_head((8, LANES))],
        out_shape=[jax.ShapeDtypeStruct((rows, width), BF),
                   jax.ShapeDtypeStruct((owners, block_rows, 2 * LANES), BF),
                   jax.ShapeDtypeStruct((heads, 8, LANES), F32)],
        scratch_shapes=[pltpu.VMEM((rows, full), BF), pltpu.VMEM((tile, full), BF),
                        pltpu.VMEM((LANES, rows), F32), pltpu.VMEM((LANES, rows), F32),
                        pltpu.VMEM((3 * DH, rows), BF), pltpu.VMEM((DH, width), F32),
                        pltpu.VMEM((rows, width), F32)],
        compiler_params=pltpu.CompilerParams(dimension_semantics=("arbitrary", "arbitrary"),
                                             vmem_limit_bytes=56 * 2 ** 20),
        cost_estimate=pl.CostEstimate(flops=flops, bytes_accessed=rows * width * 20, transcendentals=heads * rows * rows),
        name="attention_backward",
    )(d_out, x, w, vec, kext, trig, qt, kb, v1, qp, save, scl)


def key_extension(kinds, valid):
    rows = kinds.shape[0]
    lane = jnp.arange(LANES)[None, :]
    k = kinds[:, None]
    out = jnp.where((lane >= DH) & (lane < DH + 3) | (lane >= DH + 6) & (lane < DH + 9), 1.0, 0.0)
    out = jnp.where((lane == DH + 3) | (lane == DH + 4), k, out)
    out = jnp.where(lane == DH + 5, jnp.where(valid[:, None] > 0, 0.0, -1e30), out)
    return jnp.broadcast_to(out, (rows, LANES)).astype(BF)


def pack_kernel(heads, groups, *refs):
    mats, smalls, wide_ref, out_ref = refs[:4], refs[4:16], refs[16], refs[17]
    rows = mats[0].shape[0]
    for g in range(groups):
        for h in range(heads):
            at = pl.ds((g * heads + h) * DH, DH)
            out_ref[g, h * rows:(h + 1) * rows, :] = jnp.concatenate([m[:, at] for m in mats], axis=1)
    pad = jnp.zeros((1, LANES - rows), F32)
    lines = [jnp.concatenate([v[...].astype(F32), pad], axis=1) for v in smalls]
    none = jnp.zeros((1, LANES), F32)
    inner = jnp.concatenate([wide_ref[...].astype(F32), jnp.zeros((1, LANES - wide_ref.shape[1]), F32)], axis=1)
    left = jnp.concatenate(lines[:8], axis=0)
    right = jnp.concatenate(lines[8:] + [inner, none, none, none], axis=0)
    both = jnp.concatenate([left, right], axis=1).astype(BF)
    for g in range(groups):
        out_ref[g, heads * rows:, :] = both


def pack(mats, smalls, wide, heads, groups):
    rows = mats[0].shape[0]
    return pl.pallas_call(
        functools.partial(pack_kernel, heads, groups),
        out_shape=jax.ShapeDtypeStruct((groups, heads * rows + 8, 2 * LANES), BF),
        name="pack_columns",
    )(*mats, *smalls, wide)


def unpack_kernel(heads, groups, shard, g_ref, block_ref, vecs_ref, wide_ref, vec_ref):
    owners = block_ref.shape[0]
    wide = wide_ref.shape[1] // owners
    for o in range(owners):
        t = block_ref[o].astype(F32)
        vecs_ref[:8, o * shard:(o + 1) * shard] = t[:, :shard]
        vecs_ref[8:, o * shard:(o + 1) * shard] = t[:, LANES:LANES + shard]
        wide_ref[:, o * wide:(o + 1) * wide] = t[4:5, LANES:LANES + wide]
    zeros = jnp.zeros((8, LANES - DH), F32)
    for g in range(groups):
        @pl.when(g_ref[0] == g)
        def _():
            for h in range(heads):
                part = vecs_ref[:8, (g * heads + h) * DH:(g * heads + h + 1) * DH]
                vec_ref[h] = jnp.concatenate([part, zeros], axis=1)


def unpack(block, g, heads, groups, shard, wide):
    owners, rows, _ = block.shape
    return pl.pallas_call(
        functools.partial(unpack_kernel, heads, groups, shard),
        grid=(1,),
        in_specs=[pl.BlockSpec(memory_space=pltpu.SMEM),
                  pl.BlockSpec((owners, 8, 2 * LANES), lambda i: (0, rows // 8 - 1, 0))],
        out_specs=[pl.BlockSpec((16, owners * shard), lambda i: (0, 0)), pl.BlockSpec((1, owners * wide), lambda i: (0, 0)),
                   pl.BlockSpec((heads, 8, LANES), lambda i: (0, 0, 0))],
        out_shape=[jax.ShapeDtypeStruct((16, owners * shard), F32), jax.ShapeDtypeStruct((1, owners * wide), F32),
                   jax.ShapeDtypeStruct((heads, 8, LANES), F32)],
        name="unpack_small",
    )(g.reshape(1), block)


def small_kernel(heads, groups, shard, g_ref, heads_ref, rest_ref, wide_ref, unused_ref, out_ref, table_ref):
    owners = out_ref.shape[0]
    wide = wide_ref.shape[1] // owners
    table_ref[:6] = jnp.zeros((6, table_ref.shape[1]), F32)
    for g in range(groups):
        @pl.when(g_ref[0] == g)
        def _():
            for h in range(heads):
                table_ref[:6, (g * heads + h) * DH:(g * heads + h + 1) * DH] = heads_ref[h, :6, :DH]
    table_ref[6:12] = rest_ref[...]
    pad = jnp.zeros((8, LANES - shard), F32)
    for o in range(owners):
        left = table_ref[:8, o * shard:(o + 1) * shard]
        right = jnp.concatenate([table_ref[8:12, o * shard:(o + 1) * shard], jnp.zeros((4, LANES - shard), F32)], axis=1)
        inner = jnp.concatenate([wide_ref[:, o * wide:(o + 1) * wide], jnp.zeros((1, LANES - wide), F32)], axis=1)
        right = jnp.concatenate([right, inner, jnp.zeros((3, LANES), F32)], axis=0)
        out_ref[o] = jnp.concatenate([left, pad, right], axis=1).astype(BF)


def small_rows(block, g, head_sums, rest, wide_sums, groups, shard):
    owners, rows, _ = block.shape
    heads = head_sums.shape[0]
    whole = lambda a: pl.BlockSpec(a.shape, lambda i: (0,) * a.ndim)
    return pl.pallas_call(
        functools.partial(small_kernel, heads, groups, shard),
        grid=(1,),
        in_specs=[pl.BlockSpec(memory_space=pltpu.SMEM), whole(head_sums), whole(rest), whole(wide_sums),
                  pl.BlockSpec(memory_space=pl.ANY)],
        out_specs=pl.BlockSpec((owners, 8, 2 * LANES), lambda i: (0, rows // 8 - 1, 0)),
        out_shape=jax.ShapeDtypeStruct(block.shape, BF),
        input_output_aliases={4: 0},
        scratch_shapes=[pltpu.VMEM((16, owners * shard), F32)],
        name="small_gradients",
    )(g.reshape(1), head_sums, rest, wide_sums, block)


def finish_kernel(heads, block_ref, *refs):
    outs, small_ref = refs[:-1], refs[-1]
    groups = block_ref.shape[0]
    shard = outs[0].shape[0]
    small_ref[...] = sum(block_ref[g, heads * shard:, :].astype(F32) for g in range(groups))
    for g in range(groups):
        for h in range(heads):
            part = block_ref[g, h * shard:(h + 1) * shard, :].astype(F32)
            at = (g * heads + h) * DH
            for m in range(4):
                outs[m][:, at:at + DH] = part[:, m * DH:(m + 1) * DH]


def finish(block, heads, shard, width):
    return pl.pallas_call(
        functools.partial(finish_kernel, heads),
        out_shape=[jax.ShapeDtypeStruct((shard, width), F32)] * 4 + [jax.ShapeDtypeStruct((8, 2 * LANES), F32)],
        name="finish_columns",
    )(block)


def token_kernel(core_ref, valid_ref, mixed_ref, x_ref, og_ref, vec_ref, wide_ref,
                 inner_own, inner_other, outer_own, outer_other,
                 result_ref, first_ref, grad_ref, gi_keep, gi_send, go_keep, go_send, rest_ref, gw_ref,
                 wi, wo, act, slope, normed_t, acc, gi_ref, go_ref, sems):
    core = core_ref[0]
    seqs, width, stretch = mixed_ref.shape
    tokens = seqs * stretch
    count = wi.shape[1] // width
    members, rows = wo.shape[1], wo.shape[2]
    block = width // count
    shard = block // members
    wide = rows - shard
    copies = []
    for y in range(2):
        for i, (src_i, src_o, k) in enumerate(((inner_own, outer_own, core), (inner_other, outer_other, 1 - core))):
            at = 2 * y + k
            copies.append(pltpu.make_async_copy(
                src_o.at[y], wo.at[at], sems.at[2 * y + i]))
            copies.append(pltpu.make_async_copy(
                src_i.at[y], wi.at[pl.ds(pl.multiple_of(at * block, block), block), :], sems.at[4 + 2 * y + i]))
    for copy in copies:
        copy.start()
    for copy in copies[0::2]:
        copy.wait()
    w_out = wo[:, :, wide:, :].astype(F32).reshape(width, width).astype(BF)
    vec = vec_ref[...]
    line = lambda i: vec[i:i + 1, :]
    mean = lambda v: jnp.mean(v, axis=1, keepdims=True)
    attn = jnp.concatenate([mm(mixed_ref[b], w_out, COLS_CC) for b in range(seqs)], axis=0) + line(6)
    first = x_ref[...].astype(F32) + attn
    center = first - mean(first)
    r_one = lax.rsqrt(mean(center * center) + epsilon)
    hat_one = center * r_one
    normed = hat_one * line(7) + line(8)
    low = normed.astype(BF)
    normed_t[...] = jnp.transpose(normed).astype(BF)
    acc[...] = jnp.zeros_like(acc)
    for copy in copies[1::2]:
        copy.wait()

    def forward(j, carry):
        at = pl.ds(pl.multiple_of(j * width, width), width)
        u = mm(low, wi[:, at], ROWCOL) + wide_ref[:, at]
        c = 0.7978845608028654
        sq = u * u
        t = jnp.tanh(c * u * (1.0 + 0.044715 * sq))
        half = 0.5 * (1.0 + t)
        a = (u * half).astype(BF)
        act[:, at] = a
        slope[:, at] = half + 0.5 * u * (1.0 - t * t) * (c * (1.0 + 3 * 0.044715 * sq))
        acc[...] += mm(a, wo[j, :, :wide, :].reshape(width, width), ROWCOL)
        return carry

    lax.fori_loop(0, count, forward, 0)
    outer = acc[...] + line(9)
    second = normed + outer
    center = second - mean(second)
    r_two = lax.rsqrt(mean(center * center) + epsilon)
    hat_two = center * r_two
    result_ref[...] = (hat_two * line(10) + line(11)).astype(BF)
    valid = valid_ref[...]
    cot = og_ref[...].astype(F32) * valid
    d_hat = cot * line(10)
    d_second = r_two * (d_hat - mean(d_hat) - hat_two * mean(d_hat * hat_two))
    d_low = d_second.astype(BF)
    total = lambda v: jnp.sum(v, axis=0, keepdims=True)
    outer_sum = total(d_low.astype(F32))
    two = [total(cot * hat_two), total(cot)]
    acc[...] = d_second

    def backward(j, carry):
        at = pl.ds(pl.multiple_of(j * width, width), width)
        d_act = mm(d_low, wo[j, :, :wide, :].reshape(width, width), ROWS_CC)
        d_in = d_act * slope[:, at]
        d_in_low = d_in.astype(BF)
        gw_ref[:, at] = total(d_in_low.astype(F32))
        acc[...] += mm(d_in_low, wi[:, at], ROWS_CC)
        go = mm(act[:, at], d_low, COLS_CC)
        go_ref[(j % 2) ^ core, j // 2, :, :wide, :] = go.astype(BF).reshape(members, wide, width)
        for b in range(count):
            gi = mm(normed_t[b * block:(b + 1) * block, :], d_in_low, ROWCOL)
            gi_ref[(b % 2) ^ core, b // 2, :, at] = gi.astype(BF)
        return carry

    lax.fori_loop(0, count, backward, 0)
    backs = [pltpu.make_async_copy(gi_ref.at[0], gi_keep, sems.at[8]), pltpu.make_async_copy(gi_ref.at[1], gi_send, sems.at[9]),
             pltpu.make_async_copy(go_ref.at[0], go_keep, sems.at[10]), pltpu.make_async_copy(go_ref.at[1], go_send, sems.at[11])]
    backs[1].start()
    backs[0].start()
    d_normed = acc[...]
    one = [total(d_normed * hat_one), total(d_normed)]
    d_hat = d_normed * line(7)
    d_first = r_one * (d_hat - mean(d_hat) - hat_one * mean(d_hat * hat_one))
    first_ref[...] = d_first
    a_low = d_first.astype(BF)
    rest_ref[...] = jnp.concatenate([total(a_low.astype(F32))] + one + [outer_sum] + two, axis=0)
    grad = mm(w_out, a_low, ROWS_CC).astype(BF)
    span = grad_ref.shape[1] - 8
    groups = width // span
    lane = lax.broadcasted_iota(jnp.int32, (1, stretch), 1)
    sums = jnp.zeros((1, stretch), F32)
    everything = lambda v: jnp.sum(jnp.sum(v, axis=0, keepdims=True), axis=1, keepdims=True)
    for b in range(seqs):
        at = slice(b * stretch, (b + 1) * stretch)
        for i, v in enumerate((first, attn, outer)):
            sums = jnp.where(lane == 3 * b + i, everything(v[at] * v[at] * valid[at]), sums)
    high = sums.astype(BF).astype(F32)
    riders = jnp.concatenate([high, sums - high, jnp.zeros((6, stretch), F32)], axis=0).astype(BF)
    for b in range(seqs):
        for g in range(groups):
            grad_ref[b * groups + g, :span, :] = grad[g * span:(g + 1) * span, b * stretch:(b + 1) * stretch]
            grad_ref[b * groups + g, span:, :] = riders
    out = mm(mixed_ref[0], a_low[:stretch], ROWCOL)
    for b in range(1, seqs):
        out += mm(mixed_ref[b], a_low[b * stretch:(b + 1) * stretch], ROWCOL)
    for b in range(count):
        for i in range(members):
            at = b * block + i * shard
            go_ref[(b % 2) ^ core, b // 2, i, wide:, :] = out[at:at + shard, :].astype(BF)
    backs[3].start()
    backs[2].start()
    for back in backs:
        back.wait()


def token_block(core, valid, mixed, x, out_grad, vectors, inner_add, inner_own, inner_other, outer_own, outer_other, span):
    seqs, width, stretch = mixed.shape
    tokens = seqs * stretch
    ff = inner_add.shape[1]
    count = ff // width
    members, rows = outer_own.shape[1], outer_own.shape[2]
    groups = width // span
    vmem = pl.BlockSpec(memory_space=pltpu.VMEM)
    hbm = pl.BlockSpec(memory_space=pl.ANY)
    S = jax.ShapeDtypeStruct
    return pl.pallas_call(
        token_kernel,
        in_specs=[pl.BlockSpec(memory_space=pltpu.SMEM)] + [vmem] * 6 + [hbm] * 4,
        out_specs=[vmem] * 3 + [hbm] * 4 + [vmem] * 2,
        out_shape=[S((tokens, width), BF), S((tokens, width), F32), S((seqs * groups, span + 8, stretch), BF),
                   S((2, width // count, ff), BF), S((2, width // count, ff), BF),
                   S((2, members, rows, width), BF), S((2, members, rows, width), BF),
                   S((6, width), F32), S((1, ff), F32)],
        scratch_shapes=[pltpu.VMEM((width, ff), BF), pltpu.VMEM((count, members, rows, width), BF),
                        pltpu.VMEM((tokens, ff), BF), pltpu.VMEM((tokens, ff), F32),
                        pltpu.VMEM((width, tokens), BF), pltpu.VMEM((tokens, width), F32),
                        pltpu.VMEM((2, 2, width // count, ff), BF), pltpu.VMEM((2, 2, members, rows, width), BF),
                        pltpu.SemaphoreType.DMA((12,))],
        compiler_params=pltpu.CompilerParams(vmem_limit_bytes=60 * 2 ** 20),
        cost_estimate=pl.CostEstimate(flops=tokens * 2 * width * (6 * ff + 4 * width), bytes_accessed=30 * 2 ** 20, transcendentals=tokens * ff),
        name="token_block",
    )(core.reshape(1), valid, mixed, x, out_grad, vectors, inner_add, inner_own, inner_other, outer_own, outer_other)


def takes_head_layout(mesh):
    return dict(mesh.shape) == {DP: 4, CTX: 8}


def swap(x, axis, bit):
    count = lax.axis_size(axis)
    return lax.ppermute(x, axis, [(i, i ^ bit) for i in range(count)])


def in_order(bit, own, received, axis):
    first = jnp.where(bit == 0, own, received)
    second = jnp.where(bit == 0, received, own)
    return jnp.stack([first, second], axis=axis)


def flip_if(bit, x, axis):
    return jnp.where(bit == 0, x, jnp.flip(x, axis))


def pick(x, index, axis):
    return lax.dynamic_index_in_dim(x, index, axis, keepdims=False)


def after(x, *others):
    return lax.optimization_barrier((x,) + others)[0]


def add_low(a, b):
    return (a.astype(F32) + b.astype(F32)).astype(BF)


def in_z_order(pieces):
    z = lax.axis_index(CTX) // 2
    block = jnp.stack(pieces).reshape((2, 2) + pieces[0].shape)
    return flip_if(z // 2, flip_if(z % 2, block, 1), 0).reshape((4,) + pieces[0].shape)


def grow_y(block):
    return in_order(lax.axis_index(DP) // 2, block, swap(block, DP, 2), 0)


def grow_core(block):
    return in_order(lax.axis_index(DP) % 2, block, swap(block, DP, 1), 1)


def halve(block, axis, mesh_axis, step, bit):
    return add_low(pick(block, bit, axis), swap(pick(block, 1 - bit, axis), mesh_axis, step))


def end_scatter(block):
    z = lax.axis_index(CTX) // 2
    total = pick(block, z, 0).astype(F32)
    for m in (1, 2, 3):
        total = total + swap(pick(block, z ^ m, 0), CTX, 2 * m).astype(F32)
    return total


def head_layout(
    inputs,
    out_grad,
    lengths,
    token_types,
    query_weight,
    key_weight,
    value_weight,
    value_bias,
    position_weight,
    content_bias,
    position_bias,
    type_bias,
    type_embed,
    output_weight,
    output_bias,
    first_gain,
    first_shift,
    inner_weight,
    inner_bias,
    outer_weight,
    outer_bias,
    second_gain,
    second_shift,
):
    d, c = lax.axis_index(DP), lax.axis_index(CTX)
    members = lax.axis_size(CTX)
    devices = lax.axis_size(DP) * members
    seqs, stretch, width = inputs.shape
    seq_len = stretch * members
    groups = members // seqs
    heads = H // groups
    span = heads * DH
    half = width // 2
    shard = width // devices
    inner_shard = inner_bias.shape[0]
    s, g = c // groups, c % groups
    bit_b, bit_x = (c // 2) % 2, c % 2
    core, bit_y = d % 2, d // 2

    smalls = (
        content_bias,
        position_bias,
        type_bias,
        value_bias,
        type_embed[0],
        type_embed[1],
        output_bias,
        first_gain,
        first_shift,
        outer_bias,
        second_gain,
        second_shift,
    )
    stacked = pack(
        (query_weight, key_weight, value_weight, position_weight),
        tuple(v.reshape(1, shard) for v in smalls),
        inner_bias.reshape(1, inner_shard),
        heads,
        groups,
    )

    row = jnp.zeros((seqs, 8, half), BF).at[:, 0, :stretch].set(token_types.astype(BF))
    left = jnp.concatenate([inputs[:, :, :half], row], axis=1)
    right = inputs[:, :, half:]
    left = in_order(s, pick(left, s, 0), swap(pick(left, 1 - s, 0), CTX, 4), 0)
    right = in_order(s, pick(right, s, 0), swap(pick(right, 1 - s, 0), CTX, 4), 0)
    left = in_order(bit_x, left, swap(left, CTX, 1), 1)
    right = in_order(bit_b, right, swap(right, CTX, 2), 1)
    left = in_order(bit_b, left, swap(left, CTX, 2), 1)
    right = in_order(bit_x, right, swap(right, CTX, 1), 2)
    left = left.reshape(members, stretch + 8, half)
    right = right.reshape(members, stretch, half)
    x_seq = jnp.concatenate([left[:, :stretch], right], axis=2).reshape(seq_len, width)
    kind_seq = left[:, stretch, :stretch].reshape(seq_len).astype(F32)

    pieces = [pick(stacked, g, 0)]
    for r in range(1, groups):
        pieces.append(swap(pick(stacked, g ^ r, 0), CTX, r))
    block = jnp.stack(pieces).reshape((2, 2) + pieces[0].shape)
    block = flip_if(bit_b, flip_if(bit_x, block, 1), 0).reshape((groups,) + pieces[0].shape)
    block = in_order(s, block, swap(block, CTX, 4), 0)[None]
    block = grow_core(grow_y(block))
    block = block.reshape((devices,) + pieces[0].shape)
    exponent = 2.0 * jnp.arange(half, dtype=F32) / width
    rates = (10000.0 ** (-exponent))[None, :]
    starts = (jnp.arange(members, dtype=jnp.int32) * stretch).astype(F32)[:, None] * rates
    steps = jnp.arange(stretch, dtype=F32)[:, None] * rates
    starts, steps = lax.optimization_barrier((starts, steps))
    cos_a, sin_a = jnp.cos(starts)[:, None], jnp.sin(starts)[:, None]
    cos_b, sin_b = jnp.cos(steps)[None], jnp.sin(steps)[None]
    trig = jnp.concatenate(
        [cos_a * cos_b - sin_a * sin_b, sin_a * cos_b + cos_a * sin_b], axis=2
    ).reshape(seq_len, width)
    key_valid = (jnp.arange(seq_len, dtype=jnp.int32) < pick(lengths, s, 0)).astype(F32)
    kext = key_extension(kind_seq, key_valid)

    outer_shard = jnp.concatenate([outer_weight, output_weight], axis=0)
    inner_z = [swap(inner_weight, CTX, 2 * m) for m in (1, 2, 3)]
    outer_z = [swap(outer_shard, CTX, 2 * m) for m in (1, 2, 3)]
    x_seq, block, inner_z, outer_z = lax.optimization_barrier((x_seq, block, inner_z, outer_z))
    vectors, inner_add, vec = unpack(block, g, heads, groups, shard, inner_shard)
    inner_block = in_z_order([inner_weight] + inner_z)
    outer_block = in_z_order([outer_shard] + outer_z)
    inner_x = swap(inner_block, CTX, 1)
    outer_y = swap(outer_block, DP, 2)
    saved = attention_forward(
        x_seq, block, 0, 1, heads, after(vec, inner_block, outer_block), kext, trig
    )
    inner_x, outer_y, probe = lax.optimization_barrier((inner_x, outer_y, saved[0]))
    inner_block = in_order(bit_x, inner_block, inner_x, 1)
    outer_block = in_order(bit_y, outer_block, outer_y, 0)
    inner_y = swap(inner_block, DP, 2)
    outer_x = swap(outer_block, CTX, 1)
    saved = (probe,) + tuple(saved[1:])
    saved = attention_forward(
        x_seq, block, 1, heads - 1, heads, after(vec, inner_block, outer_block), kext, trig, saved
    )
    att, qt, kb, v1, qp, save, scl, w_heads = saved
    inner_y, outer_x, att = lax.optimization_barrier((inner_y, outer_x, att))
    mixed = lax.all_to_all(att, CTX, 0, 0, tiled=True).reshape(seqs, width, stretch)
    inner_own = in_order(bit_y, inner_block, inner_y, 0).reshape(2, -1, inner_weight.shape[1])
    outer_own = in_order(bit_x, outer_block, outer_x, 2)
    outer_own = outer_own.reshape(2, members, inner_shard + shard, width)
    inner_other = swap(inner_own, DP, 1)
    outer_other = swap(outer_own, DP, 1)

    own_slots = c * stretch + jnp.arange(stretch, dtype=jnp.int32)
    row_valid = (own_slots[None, :] < lengths[:, None]).astype(F32)
    result, first_grad, mixed_grad, inner_keep, inner_send, outer_keep, outer_send, rest, wide = (
        token_block(
            core,
            row_valid.reshape(-1, 1),
            mixed,
            inputs.reshape(-1, width),
            out_grad.reshape(-1, width),
            vectors,
            inner_add,
            inner_own,
            inner_other,
            outer_own,
            outer_other,
            span,
        )
    )
    result = result.reshape(inputs.shape)
    first_grad = first_grad.reshape(inputs.shape)

    d_out = lax.all_to_all(mixed_grad, CTX, 0, 0, tiled=True)
    sums_all = jnp.sum(d_out[:, span : span + 2].astype(F32), axis=(0, 1))
    sums_all = sums_all[: 3 * seqs].reshape(seqs, 3)
    mean_squares = sums_all / (lengths.astype(F32)[:, None] * width)
    inner_block = add_low(inner_keep, swap(inner_send, DP, 1)).reshape(2, 4, 2, shard, -1)
    outer_block = add_low(outer_keep, swap(outer_send, DP, 1))
    outer_block = outer_block.reshape(2, 4, 2, inner_shard + shard, width)
    inner_keep, inner_send = pick(inner_block, bit_y, 0), pick(inner_block, 1 - bit_y, 0)
    outer_keep, outer_send = pick(outer_block, bit_x, 2), pick(outer_block, 1 - bit_x, 2)
    inner_y = swap(inner_send, DP, 2)
    outer_x = swap(outer_send, CTX, 1)

    d_x, w_grad, head_sums = attention_backward(
        after(d_out, inner_send, outer_send),
        x_seq,
        w_heads,
        vec,
        kext,
        trig,
        qt,
        kb,
        v1,
        qp,
        save,
        scl,
        devices,
        heads * shard + 8,
    )
    d_x, inner_y, outer_x = lax.optimization_barrier((d_x, inner_y, outer_x))
    inner_block = halve(add_low(inner_keep, inner_y), 1, CTX, 1, bit_x)
    outer_block = halve(add_low(outer_keep, outer_x), 0, DP, 2, bit_y)

    block = small_rows(w_grad, g, head_sums, rest, wide, groups, shard)
    block = block.reshape((2, 2, 2, groups) + block.shape[1:])
    block = halve(block, 1, DP, 1, core)
    block = halve(block, 0, DP, 2, bit_y)
    block = halve(block, 0, CTX, 4, s)
    pieces = [pick(block, g, 0)]
    for r in range(1, groups):
        pieces.append(swap(pick(block, g ^ r, 0), CTX, r))
    block = jnp.stack(pieces).reshape((2, 2) + pieces[0].shape)
    block = flip_if(bit_b, flip_if(bit_x, block, 1), 0).reshape((groups,) + pieces[0].shape)
    query_own, key_own, value_own, position_own, small = finish(block, heads, shard, width)
    v = [small[i, :shard] for i in range(8)] + [small[i, LANES : LANES + shard] for i in range(4)]

    d_x = d_x.reshape(2, 2, 2, stretch, width)
    left, right = d_x[..., :half], d_x[..., half:]
    left = halve(left, 2, CTX, 1, bit_x)
    right = halve(right, 1, CTX, 2, bit_b)
    left = halve(left, 1, CTX, 2, bit_b)
    right = halve(right, 1, CTX, 1, bit_x)
    both = jnp.concatenate([left, right], axis=2)
    input_terms = in_order(s, pick(both, s, 0), swap(pick(both, 1 - s, 0), CTX, 4), 0)
    input_grad = (first_grad + input_terms.astype(F32)).astype(BF)

    inner_own = end_scatter(inner_block)
    outer_block = end_scatter(outer_block)
    outer_own, output_own = outer_block[:inner_shard], outer_block[inner_shard:]
    return (
        result,
        input_grad,
        query_own,
        key_own,
        value_own,
        v[5],
        position_own,
        v[0],
        v[1],
        v[2],
        jnp.stack([v[3], v[4]]),
        output_own,
        v[6],
        v[7],
        v[8],
        inner_own,
        small[4, LANES : LANES + inner_shard],
        outer_own,
        v[9],
        v[10],
        v[11],
        mean_squares,
    )


def solution(mesh):
    in_specs = (
        P(DP, CTX, None),
        P(DP, CTX, None),
        P(DP),
        P(DP, CTX),
        P(ALL, None),
        P(ALL, None),
        P(ALL, None),
        P(ALL),
        P(ALL, None),
        P(ALL),
        P(ALL),
        P(ALL),
        P(None, ALL),
        P(ALL, None),
        P(ALL),
        P(ALL),
        P(ALL),
        P(ALL, None),
        P(ALL),
        P(ALL, None),
        P(ALL),
        P(ALL),
        P(ALL),
    )
    out_specs = (
        P(DP, CTX, None),
        P(DP, CTX, None),
        P(ALL, None),
        P(ALL, None),
        P(ALL, None),
        P(ALL),
        P(ALL, None),
        P(ALL),
        P(ALL),
        P(ALL),
        P(None, ALL),
        P(ALL, None),
        P(ALL),
        P(ALL),
        P(ALL),
        P(ALL, None),
        P(ALL),
        P(ALL, None),
        P(ALL),
        P(ALL),
        P(ALL),
        P(DP, None),
    )
    body = head_layout if takes_head_layout(mesh) else per_device
    return jax.shard_map(
        body, mesh=mesh, in_specs=in_specs, out_specs=out_specs, check_vma=False
    )
```

```python
import functools

import jax
import jax.numpy as jnp
from jax import lax
from jax.experimental import pallas as pl
from jax.experimental.pallas import tpu as pltpu
from jax.sharding import PartitionSpec as P

DP = "dp"
CTX = "ctx"
ALL = (DP, CTX)
H = 12
DH = 64
KEY_BLOCK = 512
MICRO = 2
SEQ_MB = 1


epsilon = 1e-06
masked_score = -1e30
maximal_precision = lax.Precision.HIGHEST


def layer_norm(hidden, gain_values, shift_values):
    center = hidden - jnp.mean(hidden, axis=-1, keepdims=True)
    variance = jnp.mean(center * center, axis=-1, keepdims=True)
    return center * lax.rsqrt(variance + epsilon) * gain_values + shift_values


def gelu_tanh(inner):
    return jax.nn.gelu(inner, approximate=True)


def position_table(anchor, number, columns):
    offsets = (anchor + jnp.arange(number, dtype=jnp.int32)).astype(jnp.float32)
    exponent = 2.0 * jnp.arange(columns // 2, dtype=jnp.float32) / columns
    angles = offsets[:, None] * (10000.0 ** (-exponent))[None, :]
    return jnp.concatenate([jnp.sin(angles), jnp.cos(angles)], axis=1)


def skew_rows(unscaled_scores, keys_count):
    leading = unscaled_scores.shape[:-2]
    rows_count = unscaled_scores.shape[-2]
    span_cols = unscaled_scores.shape[-1]
    flattened = unscaled_scores.reshape(leading + (rows_count * span_cols,))
    flattened = jnp.pad(flattened, [(0, 0)] * len(leading) + [(0, rows_count)])
    return flattened.reshape(leading + (rows_count, span_cols + 1))[..., :keys_count][..., ::-1]


def unskew_rows(grads_block, span_cols):
    leading = grads_block.shape[:-2]
    rows_count = grads_block.shape[-2]
    keys_count = grads_block.shape[-1]
    padded = jnp.pad(
        grads_block[..., ::-1], [(0, 0)] * (len(leading) + 1) + [(0, span_cols + 1 - keys_count)]
    )
    flattened = padded.reshape(leading + (rows_count * (span_cols + 1),))
    return flattened[..., : rows_count * span_cols].reshape(leading + (rows_count, span_cols))


def block_scores(
    query_content,
    query_relative_term,
    type_terms,
    query_kinds,
    key_rows,
    key_kinds,
    key_valid,
    relative_rows,
):
    content = jnp.einsum(
        "bqhd,bkhd->bhqk", query_content, key_rows, preferred_element_type=jnp.float32
    )
    unscaled_scores = jnp.einsum(
        "uply,xly->ulpx", query_relative_term, relative_rows, preferred_element_type=jnp.float32
    )
    same_kind = query_kinds[:, :, None] == key_kinds[:, None, :]
    type_same = jnp.transpose(type_terms[..., 1], (0, 2, 1))[..., None]
    type_other = jnp.transpose(type_terms[..., 0], (0, 2, 1))[..., None]
    summed = (
        content
        + skew_rows(unscaled_scores, key_rows.shape[1])
        + jnp.where(same_kind[:, None], type_same, type_other)
    )
    return (jnp.where(key_valid[:, None, None, :], summed, masked_score), same_kind)


def block_grads(
    query_content,
    query_relative_term,
    type_terms,
    query_kinds,
    log_total,
    row_delta,
    grad_rows,
    key_rows,
    value_rows,
    key_kinds,
    key_valid,
    relative_rows,
):
    scores, same_kind = block_scores(
        query_content,
        query_relative_term,
        type_terms,
        query_kinds,
        key_rows,
        key_kinds,
        key_valid,
        relative_rows,
    )
    probability = jnp.exp(scores - log_total[..., None])
    value_grad = jnp.einsum(
        "bhqk,bqhd->bkhd",
        probability.astype(jnp.bfloat16),
        grad_rows,
        preferred_element_type=jnp.float32,
    )
    prob_grad = jnp.einsum(
        "bqhd,bkhd->bhqk", grad_rows, value_rows, preferred_element_type=jnp.float32
    )
    score_grad = (probability * (prob_grad - row_delta[..., None])).astype(jnp.bfloat16)
    content_grad = jnp.einsum(
        "bhqk,bkhd->bqhd", score_grad, key_rows, preferred_element_type=jnp.float32
    )
    key_grad = jnp.einsum(
        "bhqk,bqhd->bkhd", score_grad, query_content, preferred_element_type=jnp.float32
    )
    unscaled_gradient = unskew_rows(score_grad, relative_rows.shape[0])
    position_grad = jnp.einsum(
        "aioy,yin->aoin", unscaled_gradient, relative_rows, preferred_element_type=jnp.float32
    )
    rel_grad = jnp.einsum(
        "gcrj,grcl->jcl", unscaled_gradient, query_relative_term, preferred_element_type=jnp.float32
    )
    wide_grad = score_grad.astype(jnp.float32)
    same_sum = jnp.sum(jnp.where(same_kind[:, None], wide_grad, 0.0), axis=-1)
    other_sum = jnp.sum(jnp.where(same_kind[:, None], 0.0, wide_grad), axis=-1)
    type_grad = jnp.transpose(jnp.stack([other_sum, same_sum], axis=-1), (0, 2, 1, 3))
    return (content_grad, position_grad, type_grad, key_grad, value_grad, rel_grad)


def per_device(
    inputs,
    out_grad,
    lengths,
    token_types,
    query_weight,
    key_weight,
    value_weight,
    value_bias,
    position_weight,
    content_bias,
    position_bias,
    type_bias,
    type_embed,
    output_weight,
    output_bias,
    first_gain,
    first_shift,
    inner_weight,
    inner_bias,
    outer_weight,
    outer_bias,
    second_gain,
    second_shift,
):
    stretch = inputs.shape[1]
    width = inputs.shape[2]
    seq_len = stretch * lax.axis_size(CTX)
    stretch_start = lax.axis_index(CTX) * stretch
    window = seq_len + stretch - 1
    scale_query = DH ** (-0.5)
    own_positions = stretch_start + jnp.arange(stretch, dtype=jnp.int32)
    table_forward = position_table(stretch_start - seq_len + 1, window, width).astype(jnp.bfloat16)
    outputs_list = []
    input_grads = []
    stat_rows = []
    grads_total = None
    rel_total = jnp.zeros((window, width), jnp.float32)
    for micro_index in range(MICRO):
        first_seq = micro_index * SEQ_MB
        sequence_input = inputs[first_seq : first_seq + SEQ_MB]
        seq_grad = out_grad[first_seq : first_seq + SEQ_MB]
        seq_kinds = token_types[first_seq : first_seq + SEQ_MB].astype(jnp.bfloat16)
        length_col = lengths[first_seq : first_seq + SEQ_MB][:, None]
        seq_count = sequence_input.shape[0]
        heads_shape = (seq_count, stretch, H, DH)
        full_shape = (seq_count, seq_len, H, DH)
        row_valid = (own_positions[None, :] < length_col).astype(jnp.float32)[..., None]
        gathered = (
            lax.all_gather(query_weight, ALL, axis=0, tiled=True),
            lax.all_gather(key_weight, ALL, axis=0, tiled=True),
            lax.all_gather(value_weight, ALL, axis=0, tiled=True),
            lax.all_gather(value_bias, ALL, axis=0, tiled=True),
            lax.all_gather(position_weight, ALL, axis=0, tiled=True),
            lax.all_gather(content_bias, ALL, axis=0, tiled=True),
            lax.all_gather(position_bias, ALL, axis=0, tiled=True),
            lax.all_gather(type_bias, ALL, axis=0, tiled=True),
            lax.all_gather(type_embed, ALL, axis=1, tiled=True),
            lax.all_gather(output_weight, ALL, axis=0, tiled=True),
            lax.all_gather(output_bias, ALL, axis=0, tiled=True),
            lax.all_gather(first_gain, ALL, axis=0, tiled=True),
            lax.all_gather(first_shift, ALL, axis=0, tiled=True),
            lax.all_gather(inner_weight, ALL, axis=0, tiled=True),
            lax.all_gather(inner_bias, ALL, axis=0, tiled=True),
            lax.all_gather(outer_weight, ALL, axis=0, tiled=True),
            lax.all_gather(outer_bias, ALL, axis=0, tiled=True),
            lax.all_gather(second_gain, ALL, axis=0, tiled=True),
            lax.all_gather(second_shift, ALL, axis=0, tiled=True),
        )
        (
            query_matrix,
            key_matrix,
            value_matrix,
            value_add,
            position_mat,
            content_add,
            position_add,
            type_add,
            type_table,
            output_matrix,
            output_add,
            gain_one,
            shift_one,
            inner_matrix,
            inner_add,
            outer_matrix,
            outer_add,
            gain_two,
            shift_two,
        ) = gathered
        scaled = (
            jnp.dot(sequence_input, query_matrix, preferred_element_type=jnp.float32) * scale_query
        )
        query_content = (
            (scaled + content_add.astype(jnp.float32)).astype(jnp.bfloat16).reshape(heads_shape)
        )
        query_relative_term = (
            (scaled + position_add.astype(jnp.float32)).astype(jnp.bfloat16).reshape(heads_shape)
        )
        with_type = (scaled + type_add.astype(jnp.float32)).reshape(heads_shape)
        type_heads = type_table.astype(jnp.float32).reshape(2, H, DH)
        type_terms = jnp.einsum(
            "bqhd,shd->bqhs", with_type, type_heads, precision=maximal_precision
        )
        key_rows = jnp.dot(sequence_input, key_matrix, preferred_element_type=jnp.float32).astype(
            jnp.bfloat16
        )
        value_rows = (
            jnp.dot(sequence_input, value_matrix, preferred_element_type=jnp.float32)
            + value_add.astype(jnp.float32)
        ).astype(jnp.bfloat16)
        rel_forward = (
            jnp.dot(table_forward, position_mat, preferred_element_type=jnp.float32)
            .astype(jnp.bfloat16)
            .reshape(window, H, DH)
        )
        start_state = (
            jnp.full((seq_count, H, stretch), masked_score, jnp.float32),
            jnp.zeros((seq_count, H, stretch), jnp.float32),
            jnp.zeros(heads_shape, jnp.float32),
        )
        piece_keys = lax.all_gather(key_rows, CTX, axis=1, tiled=True)
        piece_values = lax.all_gather(value_rows, CTX, axis=1, tiled=True)
        piece_kinds = lax.all_gather(seq_kinds, CTX, axis=1, tiled=True)
        number = piece_keys.shape[1]
        block_rows = KEY_BLOCK

        def one_block(running, offset):
            run_max, run_total, run_acc = running
            part_keys = lax.dynamic_slice_in_dim(piece_keys, offset, block_rows, 1).reshape(
                seq_count, block_rows, H, DH
            )
            part_values = lax.dynamic_slice_in_dim(piece_values, offset, block_rows, 1).reshape(
                seq_count, block_rows, H, DH
            )
            part_kinds = lax.dynamic_slice_in_dim(piece_kinds, offset, block_rows, 1)
            relative_rows = lax.dynamic_slice_in_dim(
                rel_forward, seq_len - offset - block_rows, stretch + block_rows - 1, 0
            )
            key_valid = (offset + jnp.arange(block_rows, dtype=jnp.int32))[None, :] < length_col
            scores, same_kind = block_scores(
                query_content,
                query_relative_term,
                type_terms,
                seq_kinds,
                part_keys,
                part_kinds,
                key_valid,
                relative_rows,
            )
            new_max = jnp.maximum(run_max, jnp.max(scores, axis=-1))
            factor = jnp.exp(run_max - new_max)
            weights_block = jnp.exp(scores - new_max[..., None])
            run_total = run_total * factor + jnp.sum(weights_block, axis=-1)
            mixed_rows = jnp.einsum(
                "bhqk,bkhd->bqhd",
                weights_block.astype(jnp.bfloat16),
                part_values,
                preferred_element_type=jnp.float32,
            )
            run_acc = run_acc * jnp.transpose(factor, (0, 2, 1))[..., None] + mixed_rows
            return ((new_max, run_total, run_acc), None)

        offsets = jnp.arange(number // block_rows, dtype=jnp.int32) * block_rows
        result_state, unused = lax.scan(one_block, start_state, offsets)
        run_max, run_total, run_acc = result_state
        log_total = run_max + jnp.log(run_total)
        attended = run_acc / jnp.transpose(run_total, (0, 2, 1))[..., None]
        attended_reduced = attended.astype(jnp.bfloat16).reshape(seq_count, stretch, width)
        attn_out = jnp.dot(
            attended_reduced, output_matrix, preferred_element_type=jnp.float32
        ) + output_add.astype(jnp.float32)
        first_sum = sequence_input.astype(jnp.float32) + attn_out
        normed = layer_norm(first_sum, gain_one.astype(jnp.float32), shift_one.astype(jnp.float32))
        normed_reduced = normed.astype(jnp.bfloat16)
        inner = jnp.dot(
            normed_reduced, inner_matrix, preferred_element_type=jnp.float32
        ) + inner_add.astype(jnp.float32)
        activated_reduced = gelu_tanh(inner).astype(jnp.bfloat16)
        outer = jnp.dot(
            activated_reduced, outer_matrix, preferred_element_type=jnp.float32
        ) + outer_add.astype(jnp.float32)
        second_sum = normed + outer
        result = layer_norm(second_sum, gain_two.astype(jnp.float32), shift_two.astype(jnp.float32))
        outputs_list.append(result.astype(jnp.bfloat16))
        stat_rows.append(
            jnp.stack(
                [
                    jnp.sum(first_sum * first_sum * row_valid, axis=(1, 2)),
                    jnp.sum(attn_out * attn_out * row_valid, axis=(1, 2)),
                    jnp.sum(outer * outer * row_valid, axis=(1, 2)),
                ],
                axis=1,
            )
        )
        back_set = (
            lax.all_gather(query_weight, ALL, axis=0, tiled=True),
            lax.all_gather(key_weight, ALL, axis=0, tiled=True),
            lax.all_gather(value_weight, ALL, axis=0, tiled=True),
            lax.all_gather(value_bias, ALL, axis=0, tiled=True),
            lax.all_gather(position_weight, ALL, axis=0, tiled=True),
            lax.all_gather(content_bias, ALL, axis=0, tiled=True),
            lax.all_gather(position_bias, ALL, axis=0, tiled=True),
            lax.all_gather(type_bias, ALL, axis=0, tiled=True),
            lax.all_gather(type_embed, ALL, axis=1, tiled=True),
            lax.all_gather(output_weight, ALL, axis=0, tiled=True),
            lax.all_gather(output_bias, ALL, axis=0, tiled=True),
            lax.all_gather(first_gain, ALL, axis=0, tiled=True),
            lax.all_gather(first_shift, ALL, axis=0, tiled=True),
            lax.all_gather(inner_weight, ALL, axis=0, tiled=True),
            lax.all_gather(inner_bias, ALL, axis=0, tiled=True),
            lax.all_gather(outer_weight, ALL, axis=0, tiled=True),
            lax.all_gather(outer_bias, ALL, axis=0, tiled=True),
            lax.all_gather(second_gain, ALL, axis=0, tiled=True),
            lax.all_gather(second_shift, ALL, axis=0, tiled=True),
        )
        (
            query_matrix,
            key_matrix,
            value_matrix,
            value_add,
            position_mat,
            content_add,
            position_add,
            type_add,
            type_table,
            output_matrix,
            output_add,
            gain_one,
            shift_one,
            inner_matrix,
            inner_add,
            outer_matrix,
            outer_add,
            gain_two,
            shift_two,
        ) = back_set
        type_heads = type_table.astype(jnp.float32).reshape(2, H, DH)
        cotangent = seq_grad.astype(jnp.float32) * row_valid
        unused_two, second_back = jax.vjp(
            layer_norm, second_sum, gain_two.astype(jnp.float32), shift_two.astype(jnp.float32)
        )
        second_grad, gain_two_grad, shift_two_grad = second_back(cotangent)
        outer_reduced = second_grad.astype(jnp.bfloat16)
        outer_add_grad = jnp.sum(outer_reduced.astype(jnp.float32), axis=(0, 1))
        outer_mat_grad = jnp.einsum(
            "hpi,hpt->it", activated_reduced, outer_reduced, preferred_element_type=jnp.float32
        )
        activated_grad = jnp.einsum(
            "unk,rk->unr", outer_reduced, outer_matrix, preferred_element_type=jnp.float32
        )
        unused_three, gelu_back = jax.vjp(gelu_tanh, inner)
        inner_reduced = gelu_back(activated_grad)[0].astype(jnp.bfloat16)
        inner_add_grad = jnp.sum(inner_reduced.astype(jnp.float32), axis=(0, 1))
        inner_mat_grad = jnp.einsum(
            "psu,psy->uy", normed_reduced, inner_reduced, preferred_element_type=jnp.float32
        )
        normed_grad = second_grad + jnp.einsum(
            "tma,ra->tmr", inner_reduced, inner_matrix, preferred_element_type=jnp.float32
        )
        unused_four, first_back = jax.vjp(
            layer_norm, first_sum, gain_one.astype(jnp.float32), shift_one.astype(jnp.float32)
        )
        first_grad, gain_one_grad, shift_one_grad = first_back(normed_grad)
        attention_reduced = first_grad.astype(jnp.bfloat16)
        output_add_grad = jnp.sum(attention_reduced.astype(jnp.float32), axis=(0, 1))
        output_mat_grad = jnp.einsum(
            "yim,yig->mg", attended_reduced, attention_reduced, preferred_element_type=jnp.float32
        )
        grad_rows = (
            jnp.einsum(
                "jcy,py->jcp", attention_reduced, output_matrix, preferred_element_type=jnp.float32
            )
            .astype(jnp.bfloat16)
            .reshape(heads_shape)
        )
        row_delta = jnp.einsum(
            "bqhd,bqhd->bhq", grad_rows.astype(jnp.float32), attended, precision=maximal_precision
        )
        all_keys, all_values, all_kinds = (
            lax.all_gather(key_rows, CTX, axis=1, tiled=True),
            lax.all_gather(value_rows, CTX, axis=1, tiled=True),
            lax.all_gather(seq_kinds, CTX, axis=1, tiled=True),
        )

        def key_step(running, key_start):
            content_acc, position_acc, type_acc, key_acc, value_acc, rel_acc = running
            part_keys = lax.dynamic_slice_in_dim(all_keys, key_start, KEY_BLOCK, 1).reshape(
                seq_count, KEY_BLOCK, H, DH
            )
            part_values = lax.dynamic_slice_in_dim(all_values, key_start, KEY_BLOCK, 1).reshape(
                seq_count, KEY_BLOCK, H, DH
            )
            part_kinds = lax.dynamic_slice_in_dim(all_kinds, key_start, KEY_BLOCK, 1)
            rel_start = seq_len - key_start - KEY_BLOCK
            relative_rows = lax.dynamic_slice_in_dim(
                rel_forward, rel_start, stretch + KEY_BLOCK - 1, 0
            )
            key_valid = (key_start + jnp.arange(KEY_BLOCK, dtype=jnp.int32))[None, :] < length_col
            pieces = block_grads(
                query_content,
                query_relative_term,
                type_terms,
                seq_kinds,
                log_total,
                row_delta,
                grad_rows,
                part_keys,
                part_values,
                part_kinds,
                key_valid,
                relative_rows,
            )
            content_part, position_part, type_part, key_part, value_part, rel_part = pieces
            key_acc = lax.dynamic_update_slice_in_dim(key_acc, key_part, key_start, 1)
            value_acc = lax.dynamic_update_slice_in_dim(value_acc, value_part, key_start, 1)
            rel_old = lax.dynamic_slice_in_dim(rel_acc, rel_start, stretch + KEY_BLOCK - 1, 0)
            rel_acc = lax.dynamic_update_slice_in_dim(rel_acc, rel_old + rel_part, rel_start, 0)
            return (
                (
                    content_acc + content_part,
                    position_acc + position_part,
                    type_acc + type_part,
                    key_acc,
                    value_acc,
                    rel_acc,
                ),
                None,
            )

        start_grads = (
            jnp.zeros(heads_shape, jnp.float32),
            jnp.zeros(heads_shape, jnp.float32),
            jnp.zeros((seq_count, stretch, H, 2), jnp.float32),
            jnp.zeros(full_shape, jnp.float32),
            jnp.zeros(full_shape, jnp.float32),
            jnp.zeros((window, H, DH), jnp.float32),
        )
        final_grads, unused_five = lax.scan(
            key_step, start_grads, jnp.arange(seq_len // KEY_BLOCK, dtype=jnp.int32) * KEY_BLOCK
        )
        content_grad, position_grad, type_grad, key_all, value_all, rel_grad = final_grads
        key_grad, value_grad = (
            lax.psum_scatter(
                key_all.astype(jnp.bfloat16), CTX, scatter_dimension=1, tiled=True
            ).astype(jnp.float32),
            lax.psum_scatter(
                value_all.astype(jnp.bfloat16), CTX, scatter_dimension=1, tiled=True
            ).astype(jnp.float32),
        )
        type_part_grad = jnp.einsum(
            "bqhs,shd->bqhd", type_grad, type_heads, precision=maximal_precision
        )
        query_grad = content_grad + position_grad + type_part_grad
        content_add_grad = jnp.sum(content_grad, axis=(0, 1)).reshape(width)
        position_add_grad = jnp.sum(position_grad, axis=(0, 1)).reshape(width)
        type_add_grad = jnp.sum(type_part_grad, axis=(0, 1)).reshape(width)
        rel_total = rel_total + rel_grad.reshape(window, width)
        query_reduced = query_grad.astype(jnp.bfloat16).reshape(seq_count, stretch, width)
        key_reduced = key_grad.astype(jnp.bfloat16).reshape(seq_count, stretch, width)
        value_reduced = value_grad.astype(jnp.bfloat16).reshape(seq_count, stretch, width)
        type_table_grad = jnp.einsum(
            "bqhs,bqhd->shd", type_grad, with_type, precision=maximal_precision
        ).reshape(2, width)
        query_mat_grad = (
            jnp.einsum(
                "orh,org->hg", sequence_input, query_reduced, preferred_element_type=jnp.float32
            )
            * scale_query
        )
        key_mat_grad = jnp.einsum(
            "orh,org->hg", sequence_input, key_reduced, preferred_element_type=jnp.float32
        )
        value_mat_grad = jnp.einsum(
            "orh,org->hg", sequence_input, value_reduced, preferred_element_type=jnp.float32
        )
        value_add_grad = jnp.sum(value_reduced.astype(jnp.float32), axis=(0, 1))
        input_grad = (
            first_grad
            + jnp.einsum(
                "sux,fx->suf", query_reduced, query_matrix, preferred_element_type=jnp.float32
            )
            * scale_query
            + jnp.einsum("sux,fx->suf", key_reduced, key_matrix, preferred_element_type=jnp.float32)
            + jnp.einsum(
                "sux,fx->suf", value_reduced, value_matrix, preferred_element_type=jnp.float32
            )
        )
        input_grads.append(input_grad.astype(jnp.bfloat16))
        micro_grads = (
            query_mat_grad,
            key_mat_grad,
            value_mat_grad,
            value_add_grad,
            content_add_grad,
            position_add_grad,
            type_add_grad,
            type_table_grad,
            output_mat_grad,
            output_add_grad,
            gain_one_grad,
            shift_one_grad,
            inner_mat_grad,
            inner_add_grad,
            outer_mat_grad,
            outer_add_grad,
            gain_two_grad,
            shift_two_grad,
        )
        if grads_total is None:
            grads_total = micro_grads
        else:
            grads_total = jax.tree.map(jnp.add, grads_total, micro_grads)
    rel_high = rel_total.astype(jnp.bfloat16)
    rel_rest = (rel_total - rel_high.astype(jnp.float32)).astype(jnp.bfloat16)
    contract_rows = (((0,), (0,)), ((), ()))
    position_mat_grad = lax.dot_general(
        table_forward, rel_high, contract_rows, preferred_element_type=jnp.float32
    ) + lax.dot_general(table_forward, rel_rest, contract_rows, preferred_element_type=jnp.float32)
    (
        query_total,
        key_total,
        value_total,
        value_add_total,
        content_total,
        position_total,
        type_total,
        table_total,
        output_total,
        output_add_total,
        gain_one_total,
        shift_one_total,
        inner_total,
        inner_add_total,
        outer_total,
        outer_add_total,
        gain_two_total,
        shift_two_total,
    ) = grads_total
    reduced = (
        lax.psum_scatter(query_total, ALL, scatter_dimension=0, tiled=True),
        lax.psum_scatter(key_total, ALL, scatter_dimension=0, tiled=True),
        lax.psum_scatter(value_total, ALL, scatter_dimension=0, tiled=True),
        lax.psum_scatter(value_add_total, ALL, scatter_dimension=0, tiled=True),
        lax.psum_scatter(position_mat_grad, ALL, scatter_dimension=0, tiled=True),
        lax.psum_scatter(content_total, ALL, scatter_dimension=0, tiled=True),
        lax.psum_scatter(position_total, ALL, scatter_dimension=0, tiled=True),
        lax.psum_scatter(type_total, ALL, scatter_dimension=0, tiled=True),
        lax.psum_scatter(table_total, ALL, scatter_dimension=1, tiled=True),
        lax.psum_scatter(output_total, ALL, scatter_dimension=0, tiled=True),
        lax.psum_scatter(output_add_total, ALL, scatter_dimension=0, tiled=True),
        lax.psum_scatter(gain_one_total, ALL, scatter_dimension=0, tiled=True),
        lax.psum_scatter(shift_one_total, ALL, scatter_dimension=0, tiled=True),
        lax.psum_scatter(inner_total, ALL, scatter_dimension=0, tiled=True),
        lax.psum_scatter(inner_add_total, ALL, scatter_dimension=0, tiled=True),
        lax.psum_scatter(outer_total, ALL, scatter_dimension=0, tiled=True),
        lax.psum_scatter(outer_add_total, ALL, scatter_dimension=0, tiled=True),
        lax.psum_scatter(gain_two_total, ALL, scatter_dimension=0, tiled=True),
        lax.psum_scatter(shift_two_total, ALL, scatter_dimension=0, tiled=True),
    )
    sums_all = lax.psum(jnp.concatenate(stat_rows, axis=0), CTX)
    mean_squares = sums_all / (lengths.astype(jnp.float32)[:, None] * width)
    return (
        (jnp.concatenate(outputs_list, axis=0), jnp.concatenate(input_grads, axis=0))
        + tuple(reduced)
        + (mean_squares,)
    )


LANES = 128
BF = jnp.bfloat16
F32 = jnp.float32
ROWS_CC = (((1,), (1,)), ((), ()))
COLS_CC = (((0,), (0,)), ((), ()))
ROWCOL = (((1,), (0,)), ((), ()))


def mm(a, b, dims):
    return lax.dot_general(a, b, dims, preferred_element_type=F32)


def split3(v):
    hi = v.astype(BF).astype(F32)
    mid = (v - hi).astype(BF).astype(F32)
    lo = (v - hi - mid).astype(BF).astype(F32)
    return hi, mid, lo


def attention_forward_kernel(tile, x_ref, w_ref, vec_ref, kext_ref, trig_ref,
                             att_ref, qb_ref, kb_ref, v1_ref, qp_ref, save_ref, scl_ref, wh_ref, prob_ref,
                             kt_ref, qt_ref):
    step = pl.program_id(1)
    rows = x_ref.shape[0]
    width = x_ref.shape[1]
    half = width // 2
    lane = lax.broadcasted_iota(jnp.int32, (tile, LANES), 1)
    low = lane < DH

    @pl.when((pl.program_id(0) == 0) & (step == 0))
    def _():
        kt_ref[:, :width] = trig_ref[...]

    @pl.when(step == 0)
    def _():
        vec = vec_ref[0]
        w = w_ref[...].astype(F32).reshape(width, 2 * LANES).astype(BF)
        wh_ref[0] = w
        w_lane = lax.broadcasted_iota(jnp.int32, (width, LANES), 1)
        w_pos = jnp.where(w_lane < DH, pltpu.roll(w[:, LANES:].astype(F32), DH, 1), 0.0).astype(BF)

        def body(i, carry):
            at = slice(i * 256, (i + 1) * 256)
            lane = lax.broadcasted_iota(jnp.int32, (256, LANES), 1)
            low = lane < DH
            proj = mm(x_ref[at, :], w, ROWCOL)
            kext = kext_ref[at, :].astype(F32)
            kind = kext[:, DH + 3:DH + 4]
            scaled = jnp.where(low, proj[:, :LANES] * DH ** -0.5, 0.0)
            scl_ref[0, at, :] = scaled
            kb = jnp.where(low, pltpu.roll(proj[:, :LANES], DH, 1), kext).astype(BF)
            kb_ref[0, at, :] = kb
            kt_ref[at, width:] = kb
            one_v = (lane >= DH) & (lane < DH + 3)
            v1_ref[0, at, :] = jnp.where(low, proj[:, LANES:] + vec[3:4, :], jnp.where(one_v, 1.0, 0.0)).astype(BF)
            with_type = scaled + vec[2:3, :]
            term0 = jnp.sum(with_type * vec[4:5, :], axis=1, keepdims=True)
            term1 = jnp.sum(with_type * vec[5:6, :], axis=1, keepdims=True)
            base = jnp.where(kind > 0.5, term0, term1)
            slope = jnp.where(kind > 0.5, term1 - term0, term0 - term1)
            b_hi, b_mid, b_lo = split3(base)
            s_hi, s_mid, s_lo = split3(slope)
            ext = jnp.where(lane == DH, b_hi, 0.0)
            ext = jnp.where(lane == DH + 1, b_mid, ext)
            ext = jnp.where(lane == DH + 2, b_lo, ext)
            ext = jnp.where(lane == DH + 3, s_hi, ext)
            ext = jnp.where(lane == DH + 4, s_mid, ext)
            ext = jnp.where(lane == DH + 5, 1.0, ext)
            q_block = jnp.where(low, scaled + vec[0:1, :], ext).astype(BF)
            qb_ref[0, at, :] = q_block
            qt_ref[at, width:] = q_block
            qp = jnp.where(low, scaled + vec[1:2, :], 0.0).astype(BF)
            qp_ref[0, at, :] = qp
            grow = mm(qp, w_pos, ROWS_CC)
            q_sin = grow[:, :half]
            q_cos = grow[:, half:]
            c = trig_ref[at, :half].astype(F32)
            s = trig_ref[at, half:].astype(F32)
            qt_ref[at, :half] = (q_sin * s + q_cos * c).astype(BF)
            qt_ref[at, half:width] = (q_cos * s - q_sin * c).astype(BF)
            return carry

        for i in range(rows // 256):
            body(i, 0)

    att_parts = att_ref.shape[0]
    sub = 256
    count = tile // sub
    small_lane = lax.broadcasted_iota(jnp.int32, (sub, LANES), 1) < DH

    def scores_of(i):
        at = pl.ds(pl.multiple_of(step * tile + i * sub, sub), sub)
        return mm(qt_ref[at, :], kt_ref[...], ROWS_CC)

    later = scores_of(0)
    for i in range(count):
        scores = later
        if i + 1 < count:
            later = scores_of(i + 1)
        top = jnp.max(scores, axis=1, keepdims=True)
        prob = jnp.exp(scores - top).astype(BF)
        prob_ref[0, i * sub:(i + 1) * sub, :] = prob
        mixed = mm(prob, v1_ref[0], ROWCOL)
        total = mixed[:, DH:DH + 1]
        att = mixed / total
        save_ref[0, i * sub:(i + 1) * sub, :] = jnp.where(small_lane, att, 1.0 / total)
        att_t = jnp.transpose(att)[:DH, :].astype(BF)
        for n in range(sub // LANES):
            b = i * (sub // LANES) + n
            att_ref[b % att_parts, b // att_parts] = att_t[:, n * LANES:(n + 1) * LANES]


def attention_backward_kernel(tile, core_ref, do_ref, x_ref, w_ref, vec_ref, kext_ref, trig_ref,
                              qb_ref, kb_ref, v1_ref, qp_ref, save_ref, scl_ref, prob_ref,
                              dx_ref, dw_ref, small_ref,
                              kt_ref, dk_acc, dv_acc, d_ref, dwp_ref, dx_acc):
    step = pl.program_id(1)
    width = trig_ref.shape[1]
    half = width // 2
    lane = lax.broadcasted_iota(jnp.int32, (tile, LANES), 1)
    low = lane < DH

    @pl.when((pl.program_id(0) == 0) & (step == 0))
    def _():
        kt_ref[:, :width] = trig_ref[...]

    @pl.when(step == 0)
    def _():
        kt_ref[:, width:] = kb_ref[0]
        dk_acc[...] = jnp.zeros_like(dk_acc)
        dv_acc[...] = jnp.zeros_like(dv_acc)
        dwp_ref[...] = jnp.zeros_like(dwp_ref)
        small_ref[...] = jnp.zeros_like(small_ref)

    at = pl.ds(pl.multiple_of(step * tile, tile), tile)
    w = w_ref[0]
    w_lane = lax.broadcasted_iota(jnp.int32, (width, LANES), 1)
    w_pos = jnp.where(w_lane < DH, pltpu.roll(w[:, LANES:].astype(F32), DH, 1), 0.0).astype(BF)
    save = save_ref[0]
    inverse = save[:, DH:DH + 1]
    parts = do_ref.shape[0]
    do_t = jnp.concatenate([do_ref[i % parts, i // parts] for i in range(tile // LANES)], axis=1).astype(F32)
    d_out = jnp.transpose(jnp.concatenate([do_t, jnp.zeros_like(do_t)], axis=0))
    d_out = d_out * inverse
    delta = jnp.sum(d_out * save, axis=1, keepdims=True)
    d_hi, d_mid, d_lo = split3(-delta)
    q_block = qb_ref[0]
    ext = jnp.where(lane == DH, d_hi, d_out)
    ext = jnp.where(lane == DH + 1, d_mid, ext)
    ext = jnp.where(lane == DH + 2, d_lo, ext)
    d_ext = ext.astype(BF)
    prob = prob_ref[0]
    dv_acc[...] += mm(d_ext, prob, COLS_CC)
    d_score = (prob.astype(F32) * mm(d_ext, v1_ref[0], ROWS_CC)).astype(BF)
    dk_acc[...] += mm(q_block, d_score, COLS_CC)
    dq = mm(d_score, kt_ref[...], ROWCOL)
    c = trig_ref[at, :half].astype(F32)
    s = trig_ref[at, half:].astype(F32)
    du_c = dq[:, :half]
    du_s = dq[:, half:width]
    back = jnp.concatenate([s * du_c - c * du_s, c * du_c + s * du_s], axis=1).astype(BF)
    d_block = dq[:, width:]
    d_pos = mm(back, w_pos, ROWCOL)
    dwp_ref[...] += mm(qp_ref[0], back, COLS_CC)[:DH, :]
    vec = vec_ref[0]
    kind = kext_ref[...][:, DH + 3:DH + 4].astype(F32)
    every = d_block[:, DH:DH + 1]
    ones = d_block[:, DH + 3:DH + 4]
    g_same = jnp.where(kind > 0.5, ones, every - ones)
    g_other = jnp.where(kind > 0.5, every - ones, ones)
    type_part = g_other * vec[4:5, :] + g_same * vec[5:6, :]
    d_content = jnp.where(low, d_block, 0.0)
    with_type = jnp.where(low, scl_ref[0] + vec[2:3, :], 0.0)
    d_scaled = d_content + d_pos + type_part
    d_ref[:DH, at] = (jnp.transpose(d_scaled)[:DH, :] * DH ** -0.5).astype(BF)
    sums = [jnp.sum(v, axis=0, keepdims=True) for v in
            (d_content, d_pos, type_part, g_other * with_type, g_same * with_type)]
    small_ref[0] += jnp.concatenate(sums + [jnp.zeros((3, LANES), F32)], axis=0)

    @pl.when(step == pl.num_programs(1) - 1)
    def _():
        d_ref[DH:2 * DH] = dk_acc[:DH, :].astype(BF)
        dv_low = dv_acc[:DH, :].astype(BF)
        d_ref[2 * DH:] = dv_low
        dv_sum = jnp.sum(dv_low.astype(F32), axis=1, keepdims=True)
        dv_sum = jnp.transpose(jnp.broadcast_to(jnp.concatenate([dv_sum, dv_sum], axis=0), (LANES, LANES)))
        small_ref[0, 5:6, :] = dv_sum[:1, :]
        d_wt = mm(d_ref[...], x_ref[...], ROWCOL)
        d_w = jnp.transpose(jnp.concatenate([d_wt, dwp_ref[...]], axis=0))
        shard = dw_ref.shape[3]
        members = dw_ref.shape[2]
        for i in range(4 * members):
            dw_ref[(i // members % 2) ^ core_ref[0], i // (2 * members), i % members] = d_w[i * shard:(i + 1) * shard, :].astype(BF)
        d_x = lax.dot_general(d_ref[...], w_ref[0][:, :3 * DH], (((0,), (1,)), ((), ())), preferred_element_type=F32)

        @pl.when(pl.program_id(0) == 0)
        def _():
            dx_acc[...] = d_x

        @pl.when(pl.program_id(0) > 0)
        def _():
            dx_acc[...] += d_x

        @pl.when(pl.program_id(0) == pl.num_programs(0) - 1)
        def _():
            dx_ref[...] = dx_acc[...].astype(BF)


def attention_forward(x, w_block, first, count, heads, vec, kext, trig, previous=(), tile=1024):
    rows, width = x.shape
    owners = w_block.shape[0]
    shard = width // owners
    full = width + LANES
    per_head = lambda shape: pl.BlockSpec((1,) + shape, lambda h, t: (first + h, 0, 0))
    fixed = lambda shape: pl.BlockSpec(shape, lambda h, t: (0, 0))
    flops = count * rows * 2 * (width * 256 + rows * full + rows * LANES)
    S = jax.ShapeDtypeStruct
    kernel = functools.partial(attention_forward_kernel, tile)
    skip = len(previous)
    return pl.pallas_call(
        lambda *refs: kernel(*refs[:5], *refs[5 + skip:]),
        grid=(count, rows // tile),
        in_specs=[fixed((rows, width)), pl.BlockSpec((owners, shard, 2 * LANES), lambda h, t: (0, first + h, 0)),
                  per_head((8, LANES)), fixed((rows, LANES)), fixed((rows, width))]
        + [pl.BlockSpec(memory_space=pl.ANY)] * skip,
        out_specs=[pl.BlockSpec((2, tile // (2 * LANES), DH, LANES), lambda h, t: (0, t, first + h, 0)),
                   per_head((rows, LANES)), per_head((rows, LANES)), per_head((rows, LANES)),
                   per_head((rows, LANES)),
                   pl.BlockSpec((1, tile, LANES), lambda h, t: (first + h, t, 0)),
                   per_head((rows, LANES)), per_head((width, 2 * LANES)),
                   pl.BlockSpec((1, tile, rows), lambda h, t: (first + h, t, 0))],
        out_shape=[S((2, rows // (2 * LANES), heads * DH, LANES), BF), S((heads, rows, LANES), BF),
                   S((heads, rows, LANES), BF), S((heads, rows, LANES), BF), S((heads, rows, LANES), BF),
                   S((heads, rows, LANES), F32), S((heads, rows, LANES), F32), S((heads, width, 2 * LANES), BF),
                   S((heads, rows, rows), BF)],
        input_output_aliases={5 + i: i for i in range(skip)},
        scratch_shapes=[pltpu.VMEM((rows, full), BF), pltpu.VMEM((rows, full), BF)],
        compiler_params=pltpu.CompilerParams(dimension_semantics=("arbitrary", "arbitrary"),
                                             vmem_limit_bytes=56 * 2 ** 20),
        cost_estimate=pl.CostEstimate(flops=flops, bytes_accessed=rows * width * 16, transcendentals=count * rows * rows),
        name="attention_forward",
    )(x, w_block, vec, kext, trig, *previous)


def attention_backward(core, d_out, x, w, vec, kext, trig, qb, kb, v1, qp, save, scl, prob, owners, block_rows, tile=1024):
    heads, rows, _ = qb.shape
    width = x.shape[1]
    full = width + LANES
    shard = width // owners
    per_head = lambda shape: pl.BlockSpec((1,) + shape, lambda h, t: (h, 0, 0))
    per_tile = lambda cols: pl.BlockSpec((1, tile, cols), lambda h, t: (h, t, 0))
    fixed = lambda shape: pl.BlockSpec(shape, lambda h, t: (0, 0))
    flops = heads * rows * 2 * (2 * rows * full + 3 * rows * LANES)
    return pl.pallas_call(
        functools.partial(attention_backward_kernel, tile),
        grid=(heads, rows // tile),
        in_specs=[pl.BlockSpec(memory_space=pltpu.SMEM), pl.BlockSpec((2, tile // (2 * LANES), DH, LANES), lambda h, t: (0, t, h, 0)), fixed((rows, width)),
                  per_head((width, 256)), per_head((8, LANES)),
                  pl.BlockSpec((tile, LANES), lambda h, t: (t, 0)), fixed((rows, width)),
                  per_tile(LANES), per_head((rows, LANES)), per_head((rows, LANES)), per_tile(LANES),
                  per_tile(LANES), per_tile(LANES), per_tile(rows)],
        out_specs=[fixed((rows, width)), pl.BlockSpec((2, 2, owners // 4, shard, 2 * LANES), lambda h, t: (0, 0, 0, h, 0)),
                   per_head((8, LANES))],
        out_shape=[jax.ShapeDtypeStruct((rows, width), BF),
                   jax.ShapeDtypeStruct((2, 2, owners // 4, block_rows, 2 * LANES), BF),
                   jax.ShapeDtypeStruct((heads, 8, LANES), F32)],
        scratch_shapes=[pltpu.VMEM((rows, full), BF),
                        pltpu.VMEM((LANES, rows), F32), pltpu.VMEM((LANES, rows), F32),
                        pltpu.VMEM((3 * DH, rows), BF), pltpu.VMEM((DH, width), F32),
                        pltpu.VMEM((rows, width), F32)],
        compiler_params=pltpu.CompilerParams(dimension_semantics=("arbitrary", "arbitrary"),
                                             vmem_limit_bytes=56 * 2 ** 20),
        cost_estimate=pl.CostEstimate(flops=flops, bytes_accessed=rows * width * 20, transcendentals=heads * rows * rows),
        name="attention_backward",
    )(core.reshape(1), d_out, x, w, vec, kext, trig, qb, kb, v1, qp, save, scl, prob)


def key_extension(kinds, valid):
    rows = kinds.shape[0]
    lane = jnp.arange(LANES)[None, :]
    k = kinds[:, None]
    out = jnp.where((lane >= DH) & (lane < DH + 3) | (lane >= DH + 6) & (lane < DH + 9), 1.0, 0.0)
    out = jnp.where((lane == DH + 3) | (lane == DH + 4), k, out)
    out = jnp.where(lane == DH + 5, jnp.where(valid[:, None] > 0, 0.0, -1e30), out)
    return jnp.broadcast_to(out, (rows, LANES)).astype(BF)


def pack_kernel(heads, groups, *refs):
    mats, smalls, (wide_ref, kinds_ref, inner_ref, outer_ref, output_ref, out_ref, packed_ref, third_ref) = refs[:4], refs[4:16], refs[16:]
    rows, width = mats[0].shape
    for g in range(groups):
        for h in range(heads):
            at = pl.ds((g * heads + h) * DH, DH)
            value = jnp.concatenate([m[:, at] for m in mats], axis=1)
            for c in range(g, out_ref.shape[0], groups):
                out_ref[c, h * rows:(h + 1) * rows, :] = value
    pad = jnp.zeros((1, LANES - rows), F32)
    lines = [jnp.concatenate([v[...].astype(F32), pad], axis=1) for v in smalls]
    none = jnp.zeros((1, LANES), F32)
    inner = jnp.concatenate([wide_ref[...].astype(F32), jnp.zeros((1, LANES - wide_ref.shape[1]), F32)], axis=1)
    left = jnp.concatenate(lines[:8], axis=0)
    kinds = kinds_ref[...].astype(F32)
    right = jnp.concatenate(lines[8:] + [inner, kinds, none], axis=0)
    both = jnp.concatenate([left, right], axis=1).astype(BF)
    for c in range(out_ref.shape[0]):
        out_ref[c, heads * rows:, :] = both
    count = inner_ref.shape[1] // width
    for i in range(count):
        packed_ref[i * rows:(i + 1) * rows, :] = inner_ref[:, i * width:(i + 1) * width]
    wide = outer_ref.shape[0] // 2
    third_ref[...] = outer_ref[:wide, :]
    packed_ref[count * rows:count * rows + wide, :] = outer_ref[wide:, :]
    packed_ref[count * rows + wide:, :] = output_ref[...]


def pack(mats, smalls, wide, kinds, inner, outer, output, heads, groups, members):
    rows, width = mats[0].shape
    third = outer.shape[0] // 2
    total = inner.shape[1] // width * rows + third + output.shape[0]
    return pl.pallas_call(
        functools.partial(pack_kernel, heads, groups),
        out_shape=[jax.ShapeDtypeStruct((members, heads * rows + 8, 2 * LANES), BF),
                   jax.ShapeDtypeStruct((total, width), BF), jax.ShapeDtypeStruct((third, width), BF)],
        name="pack_columns",
    )(*mats, *smalls, wide, kinds, inner, outer, output)


def unpack_kernel(heads, groups, shard, g_ref, block_ref, vecs_ref, wide_ref, vec_ref):
    owners = block_ref.shape[0]
    wide = wide_ref.shape[1] // owners
    for o in range(owners):
        t = block_ref[o].astype(F32)
        vecs_ref[:8, o * shard:(o + 1) * shard] = t[:, :shard]
        vecs_ref[8:, o * shard:(o + 1) * shard] = t[:, LANES:LANES + shard]
        wide_ref[:, o * wide:(o + 1) * wide] = t[4:5, LANES:LANES + wide]
    zeros = jnp.zeros((8, LANES - DH), F32)
    for g in range(groups):
        @pl.when(g_ref[0] == g)
        def _():
            for h in range(heads):
                part = vecs_ref[:8, (g * heads + h) * DH:(g * heads + h + 1) * DH]
                vec_ref[h] = jnp.concatenate([part, zeros], axis=1)


def unpack(block, g, heads, groups, shard, wide):
    owners, rows, _ = block.shape
    return pl.pallas_call(
        functools.partial(unpack_kernel, heads, groups, shard),
        grid=(1,),
        in_specs=[pl.BlockSpec(memory_space=pltpu.SMEM),
                  pl.BlockSpec((owners, 8, 2 * LANES), lambda i: (0, rows // 8 - 1, 0))],
        out_specs=[pl.BlockSpec((16, owners * shard), lambda i: (0, 0)), pl.BlockSpec((1, owners * wide), lambda i: (0, 0)),
                   pl.BlockSpec((heads, 8, LANES), lambda i: (0, 0, 0))],
        out_shape=[jax.ShapeDtypeStruct((16, owners * shard), F32), jax.ShapeDtypeStruct((1, owners * wide), F32),
                   jax.ShapeDtypeStruct((heads, 8, LANES), F32)],
        name="unpack_small",
    )(g.reshape(1), block)


def small_kernel(heads, groups, shard, g_ref, heads_ref, rest_ref, wide_ref, unused_ref, out_ref, table_ref):
    members = out_ref.shape[2]
    owners = 4 * members
    wide = wide_ref.shape[1] // owners
    table_ref[:6] = jnp.zeros((6, table_ref.shape[1]), F32)
    for g in range(groups):
        @pl.when(g_ref[0] == g)
        def _():
            for h in range(heads):
                table_ref[:6, (g * heads + h) * DH:(g * heads + h + 1) * DH] = heads_ref[h, :6, :DH]
    table_ref[6:12] = rest_ref[...]
    pad = jnp.zeros((8, LANES - shard), F32)
    for o in range(owners):
        left = table_ref[:8, o * shard:(o + 1) * shard]
        right = jnp.concatenate([table_ref[8:12, o * shard:(o + 1) * shard], jnp.zeros((4, LANES - shard), F32)], axis=1)
        inner = jnp.concatenate([wide_ref[:, o * wide:(o + 1) * wide], jnp.zeros((1, LANES - wide), F32)], axis=1)
        right = jnp.concatenate([right, inner, jnp.zeros((3, LANES), F32)], axis=0)
        out_ref[(o // members % 2) ^ g_ref[1], o // (2 * members), o % members] = jnp.concatenate([left, pad, right], axis=1).astype(BF)


def small_rows(block, g, head_sums, rest, wide_sums, groups, shard):
    members, rows = block.shape[2:4]
    owners = 4 * members
    heads = head_sums.shape[0]
    whole = lambda a: pl.BlockSpec(a.shape, lambda i: (0,) * a.ndim)
    return pl.pallas_call(
        functools.partial(small_kernel, heads, groups, shard),
        grid=(1,),
        in_specs=[pl.BlockSpec(memory_space=pltpu.SMEM), whole(head_sums), whole(rest), whole(wide_sums),
                  pl.BlockSpec(memory_space=pl.ANY)],
        out_specs=pl.BlockSpec((2, 2, members, 8, 2 * LANES), lambda i: (0, 0, 0, rows // 8 - 1, 0)),
        out_shape=jax.ShapeDtypeStruct(block.shape, BF),
        input_output_aliases={4: 0},
        scratch_shapes=[pltpu.VMEM((16, owners * shard), F32)],
        name="small_gradients",
    )(g, head_sums, rest, wide_sums, block)


def finish_kernel(heads, block_ref, *refs):
    outs, small_ref = refs[:-1], refs[-1]
    groups = block_ref.shape[0] // 2
    shard = outs[0].shape[0]
    small_ref[...] = sum(block_ref[g, heads * shard:, :].astype(F32) for g in range(2 * groups))
    for g in range(groups):
        for h in range(heads):
            part = block_ref[g, h * shard:(h + 1) * shard, :].astype(F32)
            part = part + block_ref[groups + g, h * shard:(h + 1) * shard, :].astype(F32)
            at = (g * heads + h) * DH
            for m in range(4):
                outs[m][:, at:at + DH] = part[:, m * DH:(m + 1) * DH]


def finish(block, heads, shard, width):
    return pl.pallas_call(
        functools.partial(finish_kernel, heads),
        out_shape=[jax.ShapeDtypeStruct((shard, width), F32)] * 4 + [jax.ShapeDtypeStruct((8, 2 * LANES), F32)],
        name="finish_columns",
    )(block)


def token_kernel(core_ref, valid_ref, mixed_ref, x_ref, og_ref, vec_ref, wide_ref,
                 inner_one, inner_two, inner_three, inner_four, outer_one, outer_two, outer_three, outer_four, third_one, third_two,
                 result_ref, first_ref, grad_ref, gi_keep, gi_send, go_keep, go_send, rest_ref, gw_ref,
                 packed, wi, act, slope, normed_t, acc, gi_ref, go_ref, sems):
    core, bit_y, bit_x = core_ref[0], core_ref[1], core_ref[2]
    seqs, width, stretch = mixed_ref.shape
    tokens = seqs * stretch
    count = wi.shape[1] // width
    members = 2 * packed.shape[1]
    block = width // count
    shard = block // members
    wide = packed.shape[3] - (count + 1) * shard
    base = count * shard
    copies = []
    sources = ((outer_one, core, bit_x), (outer_two, 1 - core, bit_x), (outer_three, core, 1 - bit_x), (outer_four, 1 - core, 1 - bit_x))
    for i, (src, k, x) in enumerate(sources):
        for y in range(2):
            copies.append(pltpu.make_async_copy(src.at[y], packed.at[2 * y + k, :, x, base + wide // 2:, :], sems.at[4 + 2 * i + y]))
    for i, (src, k) in enumerate(((third_one, core), (third_two, 1 - core))):
        for y in range(2):
            copies.append(pltpu.make_async_copy(src.at[:, y], packed.at[2 * y + k, :, :, base:base + wide // 2, :], sems.at[26 + 2 * i + y]))
    sources = ((inner_one, core, bit_y), (inner_two, 1 - core, bit_y), (inner_three, core, 1 - bit_y), (inner_four, 1 - core, 1 - bit_y))
    for i, (src, k, y) in enumerate(sources):
        for x in range(2):
            copies.append(pltpu.make_async_copy(src.at[x], packed.at[2 * y + k, :, x, :base, :], sems.at[12 + 2 * i + x]))
    for copy in copies:
        copy.start()
    for copy in copies[:8]:
        copy.wait()
    w_out = packed[:, :, :, base + wide:, :].astype(F32).reshape(width, width).astype(BF)
    def w_outer(j):
        return packed[j, :, :, base:base + wide, :].reshape(width, width)

    vec = vec_ref[...]
    line = lambda i: vec[i:i + 1, :]
    mean = lambda v: jnp.mean(v, axis=1, keepdims=True)
    attn = jnp.concatenate([mm(mixed_ref[b], w_out, COLS_CC) for b in range(seqs)], axis=0) + line(6)
    first = x_ref[...].astype(F32) + attn
    center = first - mean(first)
    r_one = lax.rsqrt(mean(center * center) + epsilon)
    hat_one = center * r_one
    normed = hat_one * line(7) + line(8)
    low = normed.astype(BF)
    normed_t[...] = jnp.transpose(normed).astype(BF)
    acc[...] = jnp.zeros_like(acc)

    for copy in copies[8:]:
        copy.wait()
    for i in range(count):
        wi[:, i * width:(i + 1) * width] = packed[:, :, :, i * shard:(i + 1) * shard, :].astype(F32).reshape(width, width).astype(BF)

    def forward(j, carry):
        at = pl.ds(pl.multiple_of(j * width, width), width)
        u = mm(low, wi[:, at], ROWCOL) + wide_ref[:, at]
        c = 0.7978845608028654
        sq = u * u
        t = jnp.tanh(c * u * (1.0 + 0.044715 * sq))
        half = 0.5 * (1.0 + t)
        a = (u * half).astype(BF)
        act[:, at] = a
        slope[:, at] = half + 0.5 * u * (1.0 - t * t) * (c * (1.0 + 3 * 0.044715 * sq))
        acc[...] += mm(a, w_outer(j), ROWCOL)
        return carry

    lax.fori_loop(0, count, forward, 0)
    outer = acc[...] + line(9)
    second = normed + outer
    center = second - mean(second)
    r_two = lax.rsqrt(mean(center * center) + epsilon)
    hat_two = center * r_two
    result_ref[...] = (hat_two * line(10) + line(11)).astype(BF)
    valid = valid_ref[...]
    cot = og_ref[...].astype(F32) * valid
    d_hat = cot * line(10)
    d_second = r_two * (d_hat - mean(d_hat) - hat_two * mean(d_hat * hat_two))
    d_low = d_second.astype(BF)
    total = lambda v: jnp.sum(v, axis=0, keepdims=True)
    outer_sum = total(d_low.astype(F32))
    two = [total(cot * hat_two), total(cot)]
    acc[...] = d_second

    def upper(which, y, j):
        target = (go_keep, go_send)[which]
        return pltpu.make_async_copy(go_ref.at[which, y, :, :wide, :], target.at[y, :, :wide, :], sems.at[20 + j])

    def lower(which, y):
        target = (go_keep, go_send)[which]
        return pltpu.make_async_copy(go_ref.at[which, y, :, wide:, :], target.at[y, :, wide:, :], sems.at[2 * which + y])

    def backward(j, carry):
        at = pl.ds(pl.multiple_of(j * width, width), width)
        d_act = mm(d_low, w_outer(j), ROWS_CC)
        d_in = d_act * slope[:, at]
        d_in_low = d_in.astype(BF)
        gw_ref[:, at] = total(d_in_low.astype(F32))
        acc[...] += mm(d_in_low, wi[:, at], ROWS_CC)
        go = mm(act[:, at], d_low, COLS_CC)
        which = (j % 2) ^ core
        go_ref[which, j // 2, :, :wide, :] = go.astype(BF).reshape(members, wide, width)

        @pl.when(which == 0)
        def _():
            upper(0, j // 2, j).start()

        @pl.when(which == 1)
        def _():
            upper(1, j // 2, j).start()

        for b in range(count):
            gi = mm(normed_t[b * block:(b + 1) * block, :], d_in_low, ROWCOL)
            gi = gi.reshape(members, shard, width).astype(BF)
            for n in range(count):
                @pl.when(j == n)
                def _():
                    gi_ref[(b % 2) ^ core, b // 2, :, n * shard:(n + 1) * shard, :] = gi
        return carry

    lax.fori_loop(0, count, backward, 0)
    backs = [pltpu.make_async_copy(gi_ref.at[0], gi_keep, sems.at[24]), pltpu.make_async_copy(gi_ref.at[1], gi_send, sems.at[25]),
             ]
    backs[1].start()
    backs[0].start()
    d_normed = acc[...]
    one = [total(d_normed * hat_one), total(d_normed)]
    d_hat = d_normed * line(7)
    d_first = r_one * (d_hat - mean(d_hat) - hat_one * mean(d_hat * hat_one))
    first_ref[...] = d_first
    a_low = d_first.astype(BF)
    rest_ref[...] = jnp.concatenate([total(a_low.astype(F32))] + one + [outer_sum] + two, axis=0)
    grad = mm(w_out, a_low, ROWS_CC).astype(BF)
    span = grad_ref.shape[1] - 8
    groups = width // span
    lane = lax.broadcasted_iota(jnp.int32, (1, stretch), 1)
    sums = jnp.zeros((1, stretch), F32)
    everything = lambda v: jnp.sum(jnp.sum(v, axis=0, keepdims=True), axis=1, keepdims=True)
    for b in range(seqs):
        at = slice(b * stretch, (b + 1) * stretch)
        for i, v in enumerate((first, attn, outer)):
            sums = jnp.where(lane == 3 * b + i, everything(v[at] * v[at] * valid[at]), sums)
    high = sums.astype(BF).astype(F32)
    riders = jnp.concatenate([high, sums - high, jnp.zeros((6, stretch), F32)], axis=0).astype(BF)
    for b in range(seqs):
        for g in range(groups):
            grad_ref[b * groups + g, :span, :] = grad[g * span:(g + 1) * span, b * stretch:(b + 1) * stretch]
            grad_ref[b * groups + g, span:, :] = riders
    out = mm(mixed_ref[0], a_low[:stretch], ROWCOL)
    for b in range(1, seqs):
        out += mm(mixed_ref[b], a_low[b * stretch:(b + 1) * stretch], ROWCOL)
    for b in range(count):
        for i in range(members):
            at = b * block + i * shard
            go_ref[(b % 2) ^ core, b // 2, i, wide:, :] = out[at:at + shard, :].astype(BF)
    lowers = [lower(which, y) for which in range(2) for y in range(2)]
    for back in lowers:
        back.start()
    for j in range(count):
        upper(0, 0, j).wait()
    for back in backs + lowers:
        back.wait()


def token_block(core, valid, mixed, x, out_grad, vectors, inner_add, inner_parts, outer_parts, third_parts, span):
    seqs, width, stretch = mixed.shape
    tokens = seqs * stretch
    ff = inner_add.shape[1]
    count = ff // width
    members = inner_parts[0].shape[0] * inner_parts[0].shape[1]
    owners = members * count
    rows = ff // owners + width // owners
    base = ff // width * (width // owners)
    groups = width // span
    vmem = pl.BlockSpec(memory_space=pltpu.VMEM)
    hbm = pl.BlockSpec(memory_space=pl.ANY)
    S = jax.ShapeDtypeStruct
    return pl.pallas_call(
        token_kernel,
        in_specs=[pl.BlockSpec(memory_space=pltpu.SMEM)] + [vmem] * 6 + [hbm] * 10,
        out_specs=[vmem] * 3 + [hbm] * 4 + [vmem] * 2,
        out_shape=[S((tokens, width), BF), S((tokens, width), F32), S((seqs * groups, span + 8, stretch), BF),
                   S((2, members, base, width), BF), S((2, members, base, width), BF),
                   S((2, members, rows, width), BF), S((2, members, rows, width), BF),
                   S((6, width), F32), S((1, ff), F32)],
        scratch_shapes=[pltpu.VMEM((count, members // 2, 2, (count + 1) * (width // owners) + ff // owners, width), BF), pltpu.VMEM((width, ff), BF),
                        pltpu.VMEM((tokens, ff), BF), pltpu.VMEM((tokens, ff), F32),
                        pltpu.VMEM((width, tokens), BF), pltpu.VMEM((tokens, width), F32),
                        pltpu.VMEM((2, 2, members, base, width), BF), pltpu.VMEM((2, 2, members, rows, width), BF),
                        pltpu.SemaphoreType.DMA((30,))],
        compiler_params=pltpu.CompilerParams(vmem_limit_bytes=60 * 2 ** 20),
        cost_estimate=pl.CostEstimate(flops=tokens * 2 * width * (6 * ff + 4 * width), bytes_accessed=30 * 2 ** 20, transcendentals=tokens * ff),
        name="token_block",
    )(core, valid, mixed, x, out_grad, vectors, inner_add, *inner_parts, *outer_parts, *third_parts)


def takes_head_layout(mesh):
    return dict(mesh.shape) == {DP: 4, CTX: 8}


def swap(x, axis, bit):
    count = lax.axis_size(axis)
    return lax.ppermute(x, axis, [(i, i ^ bit) for i in range(count)])


def in_order(bit, own, received, axis):
    first = jnp.where(bit == 0, own, received)
    second = jnp.where(bit == 0, received, own)
    return jnp.stack([first, second], axis=axis)


def pick(x, index, axis):
    return lax.dynamic_index_in_dim(x, index, axis, keepdims=False)


def after(x, *others):
    return lax.optimization_barrier((x,) + others)[0]


def exchange(x, along_z):
    count = lax.axis_size(CTX)
    if along_z:
        sets = [[m for m in range(count) if m % 2 == i] for i in range(2)]
    else:
        sets = [list(range(count // 2)), list(range(count // 2, count))]
    return lax.all_to_all(x, CTX, 0, 0, axis_index_groups=sets, tiled=True)


def in_z_order(pieces):
    z = lax.axis_index(CTX) // 2
    block = jnp.stack(pieces).reshape((2, 2) + pieces[0].shape)
    for axis, bit in ((1, z % 2), (0, z // 2)):
        block = jnp.where(bit == 0, block, jnp.flip(block, axis))
    return block.reshape((4,) + pieces[0].shape)


def total_low(terms):
    return sum(t.astype(F32) for t in terms).astype(BF)


def picks(terms, bit, axis):
    return [pick(t, bit, axis) for t in terms]


def head_layout(
    inputs,
    out_grad,
    lengths,
    token_types,
    query_weight,
    key_weight,
    value_weight,
    value_bias,
    position_weight,
    content_bias,
    position_bias,
    type_bias,
    type_embed,
    output_weight,
    output_bias,
    first_gain,
    first_shift,
    inner_weight,
    inner_bias,
    outer_weight,
    outer_bias,
    second_gain,
    second_shift,
):
    d, c = lax.axis_index(DP), lax.axis_index(CTX)
    members = lax.axis_size(CTX)
    devices = lax.axis_size(DP) * members
    seqs, stretch, width = inputs.shape
    seq_len = stretch * members
    groups = members // seqs
    heads = H // groups
    span = heads * DH
    half = width // 2
    shard = width // devices
    inner_shard = inner_bias.shape[0]
    s, g = c // groups, c % groups
    bit_x = c % 2
    core, bit_y = d % 2, d // 2

    x_send = pick(inputs, 1 - s, 0)
    own = pick(inputs, s, 0)

    smalls = (
        content_bias,
        position_bias,
        type_bias,
        value_bias,
        type_embed[0],
        type_embed[1],
        output_bias,
        first_gain,
        first_shift,
        outer_bias,
        second_gain,
        second_shift,
    )
    stacked, packed, third = pack(
        (after(query_weight, x_send), key_weight, value_weight, position_weight),
        tuple(v.reshape(1, shard) for v in smalls),
        inner_bias.reshape(1, inner_shard),
        token_types,
        inner_weight,
        outer_weight,
        output_weight,
        heads,
        groups,
        members,
    )
    cut = (inner_weight.shape[1] // width) * shard
    block = lax.all_to_all(stacked, CTX, 0, 0, tiled=True)
    x_pair = in_order(s, own, swap(x_send, CTX, 4), 0)
    packed, third = after((packed, third), x_pair)
    third_y = swap(third, DP, 2)
    packed_z = [swap(packed, CTX, 2 * m) for m in (1, 2, 3)]
    lines = block[:, heads * shard + 5 : heads * shard + 5 + seqs, LANES:]
    kind_seq = pick(lines, s, 1).reshape(2, groups, stretch).transpose(1, 0, 2)
    kind_seq = kind_seq.reshape(seq_len).astype(F32)
    x_pair = jnp.broadcast_to(after(x_pair, block)[None], (groups, 2, stretch, width))
    x_all = exchange(x_pair, False)
    block = block[None]
    block = in_order(bit_y, block, swap(block, DP, 2), 0)
    third = in_order(bit_y, third, after(third_y, block), 0)
    third_x = swap(third, CTX, 1)
    packed_z = after(packed_z, x_pair, block, third)
    packed_z = in_z_order([packed] + packed_z)
    inner_block, outer_block = packed_z[:, :cut], packed_z[:, cut:]
    inner_x, outer_y = swap(inner_block, CTX, 1), swap(outer_block, DP, 2)
    block = in_order(core, block, after(swap(block, DP, 1), inner_block, outer_block), 1)
    block = block.reshape((devices,) + stacked.shape[1:])
    x_seq = after(x_all, block).reshape(seq_len, width)

    exponent = 2.0 * jnp.arange(half, dtype=F32) / width
    rates = (10000.0 ** (-exponent))[None, :]
    owners = jnp.arange(members, dtype=jnp.int32).reshape(2, groups).T.reshape(-1)
    starts = (owners * stretch).astype(F32)[:, None] * rates
    steps = jnp.arange(stretch, dtype=F32)[:, None] * rates
    starts, steps = lax.optimization_barrier((starts, steps))
    cos_a, sin_a = jnp.cos(starts)[:, None], jnp.sin(starts)[:, None]
    cos_b, sin_b = jnp.cos(steps)[None], jnp.sin(steps)[None]
    trig = jnp.concatenate(
        [cos_a * cos_b - sin_a * sin_b, sin_a * cos_b + cos_a * sin_b], axis=2
    ).reshape(seq_len, width).astype(BF)
    slots = owners[:, None] * stretch + jnp.arange(stretch, dtype=jnp.int32)[None, :]
    key_valid = (slots.reshape(-1) < pick(lengths, s, 0)).astype(F32)
    kext = key_extension(kind_seq, key_valid)

    vectors, inner_add, vec = unpack(block, g, heads, groups, shard, inner_shard)

    inner_x, outer_y, third_x = after((inner_x, outer_y, third_x), x_seq)
    third = in_order(bit_x, third, third_x, 1)
    inner_block = in_order(bit_x, inner_block, inner_x, 0)
    outer_block = in_order(bit_y, outer_block, outer_y, 0)
    inner_y, outer_x = swap(inner_block, DP, 2), swap(outer_block, CTX, 1)
    third_z = [swap(third, CTX, 2 * m) for m in (1, 2, 3)]
    saved = attention_forward(
        x_seq, block, 0, heads, heads, after(vec, inner_block, outer_block, third), kext, trig
    )
    att, q_block, kb, v1, qp, save, scl, w_heads, prob = saved
    third_z = after(third_z, att)
    att = after(att, third_z).reshape(members, span, stretch)
    mixed = lax.all_to_all(att, CTX, 0, 0, tiled=True).reshape(seqs, width, stretch)
    inner_block, outer_block = after((inner_block, outer_block), att)
    inner_far, outer_far = swap(inner_block, DP, 1), swap(outer_block, DP, 1)
    third = in_z_order([third] + third_z)
    inner_y, outer_x = after((inner_y, outer_x), mixed)
    third_parts = (third, swap(third, DP, 1))
    inner_parts = (inner_block, inner_far, inner_y, swap(inner_y, DP, 1))
    outer_parts = (outer_block, outer_far, outer_x, swap(outer_x, DP, 1))

    own_slots = c * stretch + jnp.arange(stretch, dtype=jnp.int32)
    row_valid = (own_slots[None, :] < lengths[:, None]).astype(F32)
    result, first_grad, mixed_grad, inner_keep, inner_send, outer_keep, outer_send, rest, wide = (
        token_block(
            jnp.stack([core, bit_y, bit_x]),
            row_valid.reshape(-1, 1),
            mixed,
            inputs.reshape(-1, width),
            out_grad.reshape(-1, width),
            vectors,
            inner_add,
            inner_parts,
            outer_parts,
            third_parts,
            span,
        )
    )
    result = result.reshape(inputs.shape)
    first_grad = first_grad.reshape(inputs.shape)

    d_out = lax.all_to_all(mixed_grad, CTX, 0, 0, tiled=True)
    z = c // 2
    first_half = inner_shard // 2
    inner_terms = [inner_keep, swap(inner_send, DP, 1)]
    inner_terms = [t.reshape(2, 4, 2, cut, width) for t in inner_terms]
    outer_terms = [outer_keep, swap(outer_send, DP, 1)]
    outer_terms = [t.reshape(2, 4, 2, inner_shard + shard, width) for t in outer_terms]
    inner_send = total_low(picks(inner_terms, 1 - bit_y, 0))
    outer_terms[1] = after(outer_terms[1], inner_send)
    third_terms = [t[..., :first_half, :] for t in outer_terms]
    outer_terms = [t[..., first_half:, :] for t in outer_terms]
    third_send = [total_low(picks(third_terms, z ^ m, 1)) for m in (1, 2, 3)]
    outer_send = total_low(picks(outer_terms, 1 - bit_x, 2))
    inner_y = swap(inner_send, DP, 2)
    outer_x = swap(outer_send, CTX, 1)
    third_z = [swap(third_send[m - 1], CTX, 2 * m) for m in (1, 2, 3)]
    d_out = after(d_out, inner_send, outer_send, *third_send)
    d_blocks = d_out.reshape(2, groups, span + 8, stretch)

    d_x, w_grad, head_sums = attention_backward(
        core,
        d_blocks,
        x_seq,
        w_heads,
        vec,
        kext,
        trig,
        q_block,
        kb,
        v1,
        qp,
        save,
        scl,
        prob,
        devices,
        heads * shard + 8,
    )
    d_x, w_grad, head_sums, inner_y, outer_x, third_z = lax.optimization_barrier(
        (d_x, w_grad, head_sums, inner_y, outer_x, third_z)
    )
    d_x = exchange(d_x.reshape(groups, 2, stretch, width), False)
    outer_terms = picks(outer_terms, bit_x, 2) + [outer_x]
    outer_send = [total_low(picks(outer_terms, z ^ m, 1)) for m in (1, 2, 3)]
    outer_z = [swap(outer_send[m - 1], CTX, 2 * m) for m in (1, 2, 3)]
    inner_terms = picks(inner_terms, bit_y, 0) + [inner_y]
    inner_send = total_low(picks(inner_terms, 1 - bit_x, 1))
    inner_x = swap(inner_send, CTX, 1)

    w_grad = after(w_grad, inner_send, *outer_send)
    block = small_rows(w_grad, jnp.stack([g, core]), head_sums, rest, wide, groups, shard)
    block = [block[0], swap(block[1], DP, 1)]
    third_terms = picks(third_terms, z, 1) + third_z
    third_send = total_low(picks(third_terms, 1 - bit_y, 0))
    block[1] = after(block[1], third_send)
    third_y = swap(third_send, DP, 2)
    block_send = total_low(picks(block, 1 - bit_y, 0))
    block_y = swap(block_send, DP, 2)

    d_x, outer_z, inner_x, third_y, block_y = lax.optimization_barrier(
        (d_x, outer_z, inner_x, third_y, block_y)
    )
    d_x = jnp.sum(d_x.astype(F32), axis=0).astype(BF)
    d_x_send = pick(d_x, 1 - s, 0)
    d_x_z = swap(d_x_send, CTX, 4)
    inner_sum = total_low(picks(inner_terms, bit_x, 1) + [after(inner_x, d_x_send)])
    inner_z = [swap(pick(inner_sum, z ^ m, 0), CTX, 2 * m) for m in (1, 2, 3)]
    block = total_low(picks(block, bit_y, 0) + [after(block_y, inner_sum)])
    outer_z = after(outer_z, block)
    block = lax.all_to_all(block, CTX, 0, 0, tiled=True)
    outer_terms = picks(outer_terms, z, 1) + outer_z
    outer_y = swap(total_low(picks(outer_terms, 1 - bit_y, 0)), DP, 2)
    third_terms = picks(third_terms, bit_y, 0) + [third_y]
    third_x = swap(total_low(picks(third_terms, 1 - bit_x, 0)), CTX, 1)
    inner_own = sum(t.astype(F32) for t in [pick(inner_sum, z, 0)] + inner_z)
    inner_own = jnp.concatenate(
        [inner_own[i : i + shard] for i in range(0, cut, shard)], axis=1
    )
    third_own = sum(t.astype(F32) for t in picks(third_terms, bit_x, 0) + [third_x])
    outer_sum = sum(t.astype(F32) for t in picks(outer_terms, bit_y, 0) + [outer_y])
    outer_own = jnp.concatenate([third_own, outer_sum[:first_half]], axis=0)
    output_own = outer_sum[first_half:]
    query_own, key_own, value_own, position_own, small = finish(block, heads, shard, width)
    v = [small[i, :shard] for i in range(8)] + [small[i, LANES : LANES + shard] for i in range(4)]
    input_terms = in_order(s, pick(d_x, s, 0), d_x_z, 0)
    input_grad = (first_grad + input_terms.astype(F32)).astype(BF)
    sums_all = jnp.sum(d_out[:, span : span + 2].astype(F32), axis=(0, 1))
    sums_all = sums_all[: 3 * seqs].reshape(seqs, 3)
    mean_squares = sums_all / (lengths.astype(F32)[:, None] * width)
    return (
        result,
        input_grad,
        query_own,
        key_own,
        value_own,
        v[5],
        position_own,
        v[0],
        v[1],
        v[2],
        jnp.stack([v[3], v[4]]),
        output_own,
        v[6],
        v[7],
        v[8],
        inner_own,
        small[4, LANES : LANES + inner_shard],
        outer_own,
        v[9],
        v[10],
        v[11],
        mean_squares,
    )


def solution(mesh):
    in_specs = (
        P(DP, CTX, None),
        P(DP, CTX, None),
        P(DP),
        P(DP, CTX),
        P(ALL, None),
        P(ALL, None),
        P(ALL, None),
        P(ALL),
        P(ALL, None),
        P(ALL),
        P(ALL),
        P(ALL),
        P(None, ALL),
        P(ALL, None),
        P(ALL),
        P(ALL),
        P(ALL),
        P(ALL, None),
        P(ALL),
        P(ALL, None),
        P(ALL),
        P(ALL),
        P(ALL),
    )
    out_specs = (
        P(DP, CTX, None),
        P(DP, CTX, None),
        P(ALL, None),
        P(ALL, None),
        P(ALL, None),
        P(ALL),
        P(ALL, None),
        P(ALL),
        P(ALL),
        P(ALL),
        P(None, ALL),
        P(ALL, None),
        P(ALL),
        P(ALL),
        P(ALL),
        P(ALL, None),
        P(ALL),
        P(ALL, None),
        P(ALL),
        P(ALL),
        P(ALL),
        P(DP, None),
    )
    body = head_layout if takes_head_layout(mesh) else per_device
    return jax.shard_map(
        body, mesh=mesh, in_specs=in_specs, out_specs=out_specs, check_vma=False
    )
```

```python
import functools

import jax
import jax.numpy as jnp
from jax import lax
from jax.experimental import pallas as pl
from jax.experimental.pallas import tpu as pltpu
from jax.sharding import PartitionSpec as P

DP = "dp"
CTX = "ctx"
ALL = (DP, CTX)
H = 12
DH = 64
KEY_BLOCK = 512
MICRO = 2
SEQ_MB = 1


epsilon = 1e-06
masked_score = -1e30
maximal_precision = lax.Precision.HIGHEST


def layer_norm(hidden, gain_values, shift_values):
    center = hidden - jnp.mean(hidden, axis=-1, keepdims=True)
    variance = jnp.mean(center * center, axis=-1, keepdims=True)
    return center * lax.rsqrt(variance + epsilon) * gain_values + shift_values


def gelu_tanh(inner):
    return jax.nn.gelu(inner, approximate=True)


def position_table(anchor, number, columns):
    offsets = (anchor + jnp.arange(number, dtype=jnp.int32)).astype(jnp.float32)
    exponent = 2.0 * jnp.arange(columns // 2, dtype=jnp.float32) / columns
    angles = offsets[:, None] * (10000.0 ** (-exponent))[None, :]
    return jnp.concatenate([jnp.sin(angles), jnp.cos(angles)], axis=1)


def skew_rows(unscaled_scores, keys_count):
    leading = unscaled_scores.shape[:-2]
    rows_count = unscaled_scores.shape[-2]
    span_cols = unscaled_scores.shape[-1]
    flattened = unscaled_scores.reshape(leading + (rows_count * span_cols,))
    flattened = jnp.pad(flattened, [(0, 0)] * len(leading) + [(0, rows_count)])
    return flattened.reshape(leading + (rows_count, span_cols + 1))[..., :keys_count][..., ::-1]


def unskew_rows(grads_block, span_cols):
    leading = grads_block.shape[:-2]
    rows_count = grads_block.shape[-2]
    keys_count = grads_block.shape[-1]
    padded = jnp.pad(
        grads_block[..., ::-1], [(0, 0)] * (len(leading) + 1) + [(0, span_cols + 1 - keys_count)]
    )
    flattened = padded.reshape(leading + (rows_count * (span_cols + 1),))
    return flattened[..., : rows_count * span_cols].reshape(leading + (rows_count, span_cols))


def block_scores(
    query_content,
    query_relative_term,
    type_terms,
    query_kinds,
    key_rows,
    key_kinds,
    key_valid,
    relative_rows,
):
    content = jnp.einsum(
        "bqhd,bkhd->bhqk", query_content, key_rows, preferred_element_type=jnp.float32
    )
    unscaled_scores = jnp.einsum(
        "uply,xly->ulpx", query_relative_term, relative_rows, preferred_element_type=jnp.float32
    )
    same_kind = query_kinds[:, :, None] == key_kinds[:, None, :]
    type_same = jnp.transpose(type_terms[..., 1], (0, 2, 1))[..., None]
    type_other = jnp.transpose(type_terms[..., 0], (0, 2, 1))[..., None]
    summed = (
        content
        + skew_rows(unscaled_scores, key_rows.shape[1])
        + jnp.where(same_kind[:, None], type_same, type_other)
    )
    return (jnp.where(key_valid[:, None, None, :], summed, masked_score), same_kind)


def block_grads(
    query_content,
    query_relative_term,
    type_terms,
    query_kinds,
    log_total,
    row_delta,
    grad_rows,
    key_rows,
    value_rows,
    key_kinds,
    key_valid,
    relative_rows,
):
    scores, same_kind = block_scores(
        query_content,
        query_relative_term,
        type_terms,
        query_kinds,
        key_rows,
        key_kinds,
        key_valid,
        relative_rows,
    )
    probability = jnp.exp(scores - log_total[..., None])
    value_grad = jnp.einsum(
        "bhqk,bqhd->bkhd",
        probability.astype(jnp.bfloat16),
        grad_rows,
        preferred_element_type=jnp.float32,
    )
    prob_grad = jnp.einsum(
        "bqhd,bkhd->bhqk", grad_rows, value_rows, preferred_element_type=jnp.float32
    )
    score_grad = (probability * (prob_grad - row_delta[..., None])).astype(jnp.bfloat16)
    content_grad = jnp.einsum(
        "bhqk,bkhd->bqhd", score_grad, key_rows, preferred_element_type=jnp.float32
    )
    key_grad = jnp.einsum(
        "bhqk,bqhd->bkhd", score_grad, query_content, preferred_element_type=jnp.float32
    )
    unscaled_gradient = unskew_rows(score_grad, relative_rows.shape[0])
    position_grad = jnp.einsum(
        "aioy,yin->aoin", unscaled_gradient, relative_rows, preferred_element_type=jnp.float32
    )
    rel_grad = jnp.einsum(
        "gcrj,grcl->jcl", unscaled_gradient, query_relative_term, preferred_element_type=jnp.float32
    )
    wide_grad = score_grad.astype(jnp.float32)
    same_sum = jnp.sum(jnp.where(same_kind[:, None], wide_grad, 0.0), axis=-1)
    other_sum = jnp.sum(jnp.where(same_kind[:, None], 0.0, wide_grad), axis=-1)
    type_grad = jnp.transpose(jnp.stack([other_sum, same_sum], axis=-1), (0, 2, 1, 3))
    return (content_grad, position_grad, type_grad, key_grad, value_grad, rel_grad)


def per_device(
    inputs,
    out_grad,
    lengths,
    token_types,
    query_weight,
    key_weight,
    value_weight,
    value_bias,
    position_weight,
    content_bias,
    position_bias,
    type_bias,
    type_embed,
    output_weight,
    output_bias,
    first_gain,
    first_shift,
    inner_weight,
    inner_bias,
    outer_weight,
    outer_bias,
    second_gain,
    second_shift,
):
    stretch = inputs.shape[1]
    width = inputs.shape[2]
    seq_len = stretch * lax.axis_size(CTX)
    stretch_start = lax.axis_index(CTX) * stretch
    window = seq_len + stretch - 1
    scale_query = DH ** (-0.5)
    own_positions = stretch_start + jnp.arange(stretch, dtype=jnp.int32)
    table_forward = position_table(stretch_start - seq_len + 1, window, width).astype(jnp.bfloat16)
    outputs_list = []
    input_grads = []
    stat_rows = []
    grads_total = None
    rel_total = jnp.zeros((window, width), jnp.float32)
    for micro_index in range(MICRO):
        first_seq = micro_index * SEQ_MB
        sequence_input = inputs[first_seq : first_seq + SEQ_MB]
        seq_grad = out_grad[first_seq : first_seq + SEQ_MB]
        seq_kinds = token_types[first_seq : first_seq + SEQ_MB].astype(jnp.bfloat16)
        length_col = lengths[first_seq : first_seq + SEQ_MB][:, None]
        seq_count = sequence_input.shape[0]
        heads_shape = (seq_count, stretch, H, DH)
        full_shape = (seq_count, seq_len, H, DH)
        row_valid = (own_positions[None, :] < length_col).astype(jnp.float32)[..., None]
        gathered = (
            lax.all_gather(query_weight, ALL, axis=0, tiled=True),
            lax.all_gather(key_weight, ALL, axis=0, tiled=True),
            lax.all_gather(value_weight, ALL, axis=0, tiled=True),
            lax.all_gather(value_bias, ALL, axis=0, tiled=True),
            lax.all_gather(position_weight, ALL, axis=0, tiled=True),
            lax.all_gather(content_bias, ALL, axis=0, tiled=True),
            lax.all_gather(position_bias, ALL, axis=0, tiled=True),
            lax.all_gather(type_bias, ALL, axis=0, tiled=True),
            lax.all_gather(type_embed, ALL, axis=1, tiled=True),
            lax.all_gather(output_weight, ALL, axis=0, tiled=True),
            lax.all_gather(output_bias, ALL, axis=0, tiled=True),
            lax.all_gather(first_gain, ALL, axis=0, tiled=True),
            lax.all_gather(first_shift, ALL, axis=0, tiled=True),
            lax.all_gather(inner_weight, ALL, axis=0, tiled=True),
            lax.all_gather(inner_bias, ALL, axis=0, tiled=True),
            lax.all_gather(outer_weight, ALL, axis=0, tiled=True),
            lax.all_gather(outer_bias, ALL, axis=0, tiled=True),
            lax.all_gather(second_gain, ALL, axis=0, tiled=True),
            lax.all_gather(second_shift, ALL, axis=0, tiled=True),
        )
        (
            query_matrix,
            key_matrix,
            value_matrix,
            value_add,
            position_mat,
            content_add,
            position_add,
            type_add,
            type_table,
            output_matrix,
            output_add,
            gain_one,
            shift_one,
            inner_matrix,
            inner_add,
            outer_matrix,
            outer_add,
            gain_two,
            shift_two,
        ) = gathered
        scaled = (
            jnp.dot(sequence_input, query_matrix, preferred_element_type=jnp.float32) * scale_query
        )
        query_content = (
            (scaled + content_add.astype(jnp.float32)).astype(jnp.bfloat16).reshape(heads_shape)
        )
        query_relative_term = (
            (scaled + position_add.astype(jnp.float32)).astype(jnp.bfloat16).reshape(heads_shape)
        )
        with_type = (scaled + type_add.astype(jnp.float32)).reshape(heads_shape)
        type_heads = type_table.astype(jnp.float32).reshape(2, H, DH)
        type_terms = jnp.einsum(
            "bqhd,shd->bqhs", with_type, type_heads, precision=maximal_precision
        )
        key_rows = jnp.dot(sequence_input, key_matrix, preferred_element_type=jnp.float32).astype(
            jnp.bfloat16
        )
        value_rows = (
            jnp.dot(sequence_input, value_matrix, preferred_element_type=jnp.float32)
            + value_add.astype(jnp.float32)
        ).astype(jnp.bfloat16)
        rel_forward = (
            jnp.dot(table_forward, position_mat, preferred_element_type=jnp.float32)
            .astype(jnp.bfloat16)
            .reshape(window, H, DH)
        )
        start_state = (
            jnp.full((seq_count, H, stretch), masked_score, jnp.float32),
            jnp.zeros((seq_count, H, stretch), jnp.float32),
            jnp.zeros(heads_shape, jnp.float32),
        )
        piece_keys = lax.all_gather(key_rows, CTX, axis=1, tiled=True)
        piece_values = lax.all_gather(value_rows, CTX, axis=1, tiled=True)
        piece_kinds = lax.all_gather(seq_kinds, CTX, axis=1, tiled=True)
        number = piece_keys.shape[1]
        block_rows = KEY_BLOCK

        def one_block(running, offset):
            run_max, run_total, run_acc = running
            part_keys = lax.dynamic_slice_in_dim(piece_keys, offset, block_rows, 1).reshape(
                seq_count, block_rows, H, DH
            )
            part_values = lax.dynamic_slice_in_dim(piece_values, offset, block_rows, 1).reshape(
                seq_count, block_rows, H, DH
            )
            part_kinds = lax.dynamic_slice_in_dim(piece_kinds, offset, block_rows, 1)
            relative_rows = lax.dynamic_slice_in_dim(
                rel_forward, seq_len - offset - block_rows, stretch + block_rows - 1, 0
            )
            key_valid = (offset + jnp.arange(block_rows, dtype=jnp.int32))[None, :] < length_col
            scores, same_kind = block_scores(
                query_content,
                query_relative_term,
                type_terms,
                seq_kinds,
                part_keys,
                part_kinds,
                key_valid,
                relative_rows,
            )
            new_max = jnp.maximum(run_max, jnp.max(scores, axis=-1))
            factor = jnp.exp(run_max - new_max)
            weights_block = jnp.exp(scores - new_max[..., None])
            run_total = run_total * factor + jnp.sum(weights_block, axis=-1)
            mixed_rows = jnp.einsum(
                "bhqk,bkhd->bqhd",
                weights_block.astype(jnp.bfloat16),
                part_values,
                preferred_element_type=jnp.float32,
            )
            run_acc = run_acc * jnp.transpose(factor, (0, 2, 1))[..., None] + mixed_rows
            return ((new_max, run_total, run_acc), None)

        offsets = jnp.arange(number // block_rows, dtype=jnp.int32) * block_rows
        result_state, unused = lax.scan(one_block, start_state, offsets)
        run_max, run_total, run_acc = result_state
        log_total = run_max + jnp.log(run_total)
        attended = run_acc / jnp.transpose(run_total, (0, 2, 1))[..., None]
        attended_reduced = attended.astype(jnp.bfloat16).reshape(seq_count, stretch, width)
        attn_out = jnp.dot(
            attended_reduced, output_matrix, preferred_element_type=jnp.float32
        ) + output_add.astype(jnp.float32)
        first_sum = sequence_input.astype(jnp.float32) + attn_out
        normed = layer_norm(first_sum, gain_one.astype(jnp.float32), shift_one.astype(jnp.float32))
        normed_reduced = normed.astype(jnp.bfloat16)
        inner = jnp.dot(
            normed_reduced, inner_matrix, preferred_element_type=jnp.float32
        ) + inner_add.astype(jnp.float32)
        activated_reduced = gelu_tanh(inner).astype(jnp.bfloat16)
        outer = jnp.dot(
            activated_reduced, outer_matrix, preferred_element_type=jnp.float32
        ) + outer_add.astype(jnp.float32)
        second_sum = normed + outer
        result = layer_norm(second_sum, gain_two.astype(jnp.float32), shift_two.astype(jnp.float32))
        outputs_list.append(result.astype(jnp.bfloat16))
        stat_rows.append(
            jnp.stack(
                [
                    jnp.sum(first_sum * first_sum * row_valid, axis=(1, 2)),
                    jnp.sum(attn_out * attn_out * row_valid, axis=(1, 2)),
                    jnp.sum(outer * outer * row_valid, axis=(1, 2)),
                ],
                axis=1,
            )
        )
        back_set = (
            lax.all_gather(query_weight, ALL, axis=0, tiled=True),
            lax.all_gather(key_weight, ALL, axis=0, tiled=True),
            lax.all_gather(value_weight, ALL, axis=0, tiled=True),
            lax.all_gather(value_bias, ALL, axis=0, tiled=True),
            lax.all_gather(position_weight, ALL, axis=0, tiled=True),
            lax.all_gather(content_bias, ALL, axis=0, tiled=True),
            lax.all_gather(position_bias, ALL, axis=0, tiled=True),
            lax.all_gather(type_bias, ALL, axis=0, tiled=True),
            lax.all_gather(type_embed, ALL, axis=1, tiled=True),
            lax.all_gather(output_weight, ALL, axis=0, tiled=True),
            lax.all_gather(output_bias, ALL, axis=0, tiled=True),
            lax.all_gather(first_gain, ALL, axis=0, tiled=True),
            lax.all_gather(first_shift, ALL, axis=0, tiled=True),
            lax.all_gather(inner_weight, ALL, axis=0, tiled=True),
            lax.all_gather(inner_bias, ALL, axis=0, tiled=True),
            lax.all_gather(outer_weight, ALL, axis=0, tiled=True),
            lax.all_gather(outer_bias, ALL, axis=0, tiled=True),
            lax.all_gather(second_gain, ALL, axis=0, tiled=True),
            lax.all_gather(second_shift, ALL, axis=0, tiled=True),
        )
        (
            query_matrix,
            key_matrix,
            value_matrix,
            value_add,
            position_mat,
            content_add,
            position_add,
            type_add,
            type_table,
            output_matrix,
            output_add,
            gain_one,
            shift_one,
            inner_matrix,
            inner_add,
            outer_matrix,
            outer_add,
            gain_two,
            shift_two,
        ) = back_set
        type_heads = type_table.astype(jnp.float32).reshape(2, H, DH)
        cotangent = seq_grad.astype(jnp.float32) * row_valid
        unused_two, second_back = jax.vjp(
            layer_norm, second_sum, gain_two.astype(jnp.float32), shift_two.astype(jnp.float32)
        )
        second_grad, gain_two_grad, shift_two_grad = second_back(cotangent)
        outer_reduced = second_grad.astype(jnp.bfloat16)
        outer_add_grad = jnp.sum(outer_reduced.astype(jnp.float32), axis=(0, 1))
        outer_mat_grad = jnp.einsum(
            "hpi,hpt->it", activated_reduced, outer_reduced, preferred_element_type=jnp.float32
        )
        activated_grad = jnp.einsum(
            "unk,rk->unr", outer_reduced, outer_matrix, preferred_element_type=jnp.float32
        )
        unused_three, gelu_back = jax.vjp(gelu_tanh, inner)
        inner_reduced = gelu_back(activated_grad)[0].astype(jnp.bfloat16)
        inner_add_grad = jnp.sum(inner_reduced.astype(jnp.float32), axis=(0, 1))
        inner_mat_grad = jnp.einsum(
            "psu,psy->uy", normed_reduced, inner_reduced, preferred_element_type=jnp.float32
        )
        normed_grad = second_grad + jnp.einsum(
            "tma,ra->tmr", inner_reduced, inner_matrix, preferred_element_type=jnp.float32
        )
        unused_four, first_back = jax.vjp(
            layer_norm, first_sum, gain_one.astype(jnp.float32), shift_one.astype(jnp.float32)
        )
        first_grad, gain_one_grad, shift_one_grad = first_back(normed_grad)
        attention_reduced = first_grad.astype(jnp.bfloat16)
        output_add_grad = jnp.sum(attention_reduced.astype(jnp.float32), axis=(0, 1))
        output_mat_grad = jnp.einsum(
            "yim,yig->mg", attended_reduced, attention_reduced, preferred_element_type=jnp.float32
        )
        grad_rows = (
            jnp.einsum(
                "jcy,py->jcp", attention_reduced, output_matrix, preferred_element_type=jnp.float32
            )
            .astype(jnp.bfloat16)
            .reshape(heads_shape)
        )
        row_delta = jnp.einsum(
            "bqhd,bqhd->bhq", grad_rows.astype(jnp.float32), attended, precision=maximal_precision
        )
        all_keys, all_values, all_kinds = (
            lax.all_gather(key_rows, CTX, axis=1, tiled=True),
            lax.all_gather(value_rows, CTX, axis=1, tiled=True),
            lax.all_gather(seq_kinds, CTX, axis=1, tiled=True),
        )

        def key_step(running, key_start):
            content_acc, position_acc, type_acc, key_acc, value_acc, rel_acc = running
            part_keys = lax.dynamic_slice_in_dim(all_keys, key_start, KEY_BLOCK, 1).reshape(
                seq_count, KEY_BLOCK, H, DH
            )
            part_values = lax.dynamic_slice_in_dim(all_values, key_start, KEY_BLOCK, 1).reshape(
                seq_count, KEY_BLOCK, H, DH
            )
            part_kinds = lax.dynamic_slice_in_dim(all_kinds, key_start, KEY_BLOCK, 1)
            rel_start = seq_len - key_start - KEY_BLOCK
            relative_rows = lax.dynamic_slice_in_dim(
                rel_forward, rel_start, stretch + KEY_BLOCK - 1, 0
            )
            key_valid = (key_start + jnp.arange(KEY_BLOCK, dtype=jnp.int32))[None, :] < length_col
            pieces = block_grads(
                query_content,
                query_relative_term,
                type_terms,
                seq_kinds,
                log_total,
                row_delta,
                grad_rows,
                part_keys,
                part_values,
                part_kinds,
                key_valid,
                relative_rows,
            )
            content_part, position_part, type_part, key_part, value_part, rel_part = pieces
            key_acc = lax.dynamic_update_slice_in_dim(key_acc, key_part, key_start, 1)
            value_acc = lax.dynamic_update_slice_in_dim(value_acc, value_part, key_start, 1)
            rel_old = lax.dynamic_slice_in_dim(rel_acc, rel_start, stretch + KEY_BLOCK - 1, 0)
            rel_acc = lax.dynamic_update_slice_in_dim(rel_acc, rel_old + rel_part, rel_start, 0)
            return (
                (
                    content_acc + content_part,
                    position_acc + position_part,
                    type_acc + type_part,
                    key_acc,
                    value_acc,
                    rel_acc,
                ),
                None,
            )

        start_grads = (
            jnp.zeros(heads_shape, jnp.float32),
            jnp.zeros(heads_shape, jnp.float32),
            jnp.zeros((seq_count, stretch, H, 2), jnp.float32),
            jnp.zeros(full_shape, jnp.float32),
            jnp.zeros(full_shape, jnp.float32),
            jnp.zeros((window, H, DH), jnp.float32),
        )
        final_grads, unused_five = lax.scan(
            key_step, start_grads, jnp.arange(seq_len // KEY_BLOCK, dtype=jnp.int32) * KEY_BLOCK
        )
        content_grad, position_grad, type_grad, key_all, value_all, rel_grad = final_grads
        key_grad, value_grad = (
            lax.psum_scatter(
                key_all.astype(jnp.bfloat16), CTX, scatter_dimension=1, tiled=True
            ).astype(jnp.float32),
            lax.psum_scatter(
                value_all.astype(jnp.bfloat16), CTX, scatter_dimension=1, tiled=True
            ).astype(jnp.float32),
        )
        type_part_grad = jnp.einsum(
            "bqhs,shd->bqhd", type_grad, type_heads, precision=maximal_precision
        )
        query_grad = content_grad + position_grad + type_part_grad
        content_add_grad = jnp.sum(content_grad, axis=(0, 1)).reshape(width)
        position_add_grad = jnp.sum(position_grad, axis=(0, 1)).reshape(width)
        type_add_grad = jnp.sum(type_part_grad, axis=(0, 1)).reshape(width)
        rel_total = rel_total + rel_grad.reshape(window, width)
        query_reduced = query_grad.astype(jnp.bfloat16).reshape(seq_count, stretch, width)
        key_reduced = key_grad.astype(jnp.bfloat16).reshape(seq_count, stretch, width)
        value_reduced = value_grad.astype(jnp.bfloat16).reshape(seq_count, stretch, width)
        type_table_grad = jnp.einsum(
            "bqhs,bqhd->shd", type_grad, with_type, precision=maximal_precision
        ).reshape(2, width)
        query_mat_grad = (
            jnp.einsum(
                "orh,org->hg", sequence_input, query_reduced, preferred_element_type=jnp.float32
            )
            * scale_query
        )
        key_mat_grad = jnp.einsum(
            "orh,org->hg", sequence_input, key_reduced, preferred_element_type=jnp.float32
        )
        value_mat_grad = jnp.einsum(
            "orh,org->hg", sequence_input, value_reduced, preferred_element_type=jnp.float32
        )
        value_add_grad = jnp.sum(value_reduced.astype(jnp.float32), axis=(0, 1))
        input_grad = (
            first_grad
            + jnp.einsum(
                "sux,fx->suf", query_reduced, query_matrix, preferred_element_type=jnp.float32
            )
            * scale_query
            + jnp.einsum("sux,fx->suf", key_reduced, key_matrix, preferred_element_type=jnp.float32)
            + jnp.einsum(
                "sux,fx->suf", value_reduced, value_matrix, preferred_element_type=jnp.float32
            )
        )
        input_grads.append(input_grad.astype(jnp.bfloat16))
        micro_grads = (
            query_mat_grad,
            key_mat_grad,
            value_mat_grad,
            value_add_grad,
            content_add_grad,
            position_add_grad,
            type_add_grad,
            type_table_grad,
            output_mat_grad,
            output_add_grad,
            gain_one_grad,
            shift_one_grad,
            inner_mat_grad,
            inner_add_grad,
            outer_mat_grad,
            outer_add_grad,
            gain_two_grad,
            shift_two_grad,
        )
        if grads_total is None:
            grads_total = micro_grads
        else:
            grads_total = jax.tree.map(jnp.add, grads_total, micro_grads)
    rel_high = rel_total.astype(jnp.bfloat16)
    rel_rest = (rel_total - rel_high.astype(jnp.float32)).astype(jnp.bfloat16)
    contract_rows = (((0,), (0,)), ((), ()))
    position_mat_grad = lax.dot_general(
        table_forward, rel_high, contract_rows, preferred_element_type=jnp.float32
    ) + lax.dot_general(table_forward, rel_rest, contract_rows, preferred_element_type=jnp.float32)
    (
        query_total,
        key_total,
        value_total,
        value_add_total,
        content_total,
        position_total,
        type_total,
        table_total,
        output_total,
        output_add_total,
        gain_one_total,
        shift_one_total,
        inner_total,
        inner_add_total,
        outer_total,
        outer_add_total,
        gain_two_total,
        shift_two_total,
    ) = grads_total
    reduced = (
        lax.psum_scatter(query_total, ALL, scatter_dimension=0, tiled=True),
        lax.psum_scatter(key_total, ALL, scatter_dimension=0, tiled=True),
        lax.psum_scatter(value_total, ALL, scatter_dimension=0, tiled=True),
        lax.psum_scatter(value_add_total, ALL, scatter_dimension=0, tiled=True),
        lax.psum_scatter(position_mat_grad, ALL, scatter_dimension=0, tiled=True),
        lax.psum_scatter(content_total, ALL, scatter_dimension=0, tiled=True),
        lax.psum_scatter(position_total, ALL, scatter_dimension=0, tiled=True),
        lax.psum_scatter(type_total, ALL, scatter_dimension=0, tiled=True),
        lax.psum_scatter(table_total, ALL, scatter_dimension=1, tiled=True),
        lax.psum_scatter(output_total, ALL, scatter_dimension=0, tiled=True),
        lax.psum_scatter(output_add_total, ALL, scatter_dimension=0, tiled=True),
        lax.psum_scatter(gain_one_total, ALL, scatter_dimension=0, tiled=True),
        lax.psum_scatter(shift_one_total, ALL, scatter_dimension=0, tiled=True),
        lax.psum_scatter(inner_total, ALL, scatter_dimension=0, tiled=True),
        lax.psum_scatter(inner_add_total, ALL, scatter_dimension=0, tiled=True),
        lax.psum_scatter(outer_total, ALL, scatter_dimension=0, tiled=True),
        lax.psum_scatter(outer_add_total, ALL, scatter_dimension=0, tiled=True),
        lax.psum_scatter(gain_two_total, ALL, scatter_dimension=0, tiled=True),
        lax.psum_scatter(shift_two_total, ALL, scatter_dimension=0, tiled=True),
    )
    sums_all = lax.psum(jnp.concatenate(stat_rows, axis=0), CTX)
    mean_squares = sums_all / (lengths.astype(jnp.float32)[:, None] * width)
    return (
        (jnp.concatenate(outputs_list, axis=0), jnp.concatenate(input_grads, axis=0))
        + tuple(reduced)
        + (mean_squares,)
    )


LANES = 128
BF = jnp.bfloat16
F32 = jnp.float32
ROWS_CC = (((1,), (1,)), ((), ()))
COLS_CC = (((0,), (0,)), ((), ()))
ROWCOL = (((1,), (0,)), ((), ()))


def mm(a, b, dims):
    return lax.dot_general(a, b, dims, preferred_element_type=F32)


def split3(v):
    hi = v.astype(BF).astype(F32)
    mid = (v - hi).astype(BF).astype(F32)
    lo = (v - hi - mid).astype(BF).astype(F32)
    return hi, mid, lo


def attention_forward_kernel(tile, x_ref, w_ref, vec_ref, kext_ref, trig_ref,
                             att_ref, qb_ref, kb_ref, v1_ref, qp_ref, save_ref, scl_ref, wh_ref, prob_ref,
                             kt_ref, qt_ref):
    step = pl.program_id(1)
    rows = x_ref.shape[0]
    width = x_ref.shape[1]
    half = width // 2
    lane = lax.broadcasted_iota(jnp.int32, (tile, LANES), 1)
    low = lane < DH

    @pl.when((pl.program_id(0) == 0) & (step == 0))
    def _():
        kt_ref[:, :width] = trig_ref[...]

    @pl.when(step == 0)
    def _():
        vec = vec_ref[0]
        w = w_ref[...].astype(F32).reshape(width, 2 * LANES).astype(BF)
        wh_ref[0] = w
        w_lane = lax.broadcasted_iota(jnp.int32, (width, LANES), 1)
        w_pos = jnp.where(w_lane < DH, pltpu.roll(w[:, LANES:].astype(F32), DH, 1), 0.0).astype(BF)

        def body(i, carry):
            at = slice(i * 256, (i + 1) * 256)
            lane = lax.broadcasted_iota(jnp.int32, (256, LANES), 1)
            low = lane < DH
            proj = mm(x_ref[at, :], w, ROWCOL)
            kext = kext_ref[at, :].astype(F32)
            kind = kext[:, DH + 3:DH + 4]
            scaled = jnp.where(low, proj[:, :LANES] * DH ** -0.5, 0.0)
            scl_ref[0, at, :] = scaled
            kb = jnp.where(low, pltpu.roll(proj[:, :LANES], DH, 1), kext).astype(BF)
            kb_ref[0, at, :] = kb
            kt_ref[at, width:] = kb
            one_v = (lane >= DH) & (lane < DH + 3)
            v1_ref[0, at, :] = jnp.where(low, proj[:, LANES:] + vec[3:4, :], jnp.where(one_v, 1.0, 0.0)).astype(BF)
            with_type = scaled + vec[2:3, :]
            term0 = jnp.sum(with_type * vec[4:5, :], axis=1, keepdims=True)
            term1 = jnp.sum(with_type * vec[5:6, :], axis=1, keepdims=True)
            base = jnp.where(kind > 0.5, term0, term1)
            slope = jnp.where(kind > 0.5, term1 - term0, term0 - term1)
            b_hi, b_mid, b_lo = split3(base)
            s_hi, s_mid, s_lo = split3(slope)
            ext = jnp.where(lane == DH, b_hi, 0.0)
            ext = jnp.where(lane == DH + 1, b_mid, ext)
            ext = jnp.where(lane == DH + 2, b_lo, ext)
            ext = jnp.where(lane == DH + 3, s_hi, ext)
            ext = jnp.where(lane == DH + 4, s_mid, ext)
            ext = jnp.where(lane == DH + 5, 1.0, ext)
            q_block = jnp.where(low, scaled + vec[0:1, :], ext).astype(BF)
            qb_ref[0, at, :] = q_block
            qt_ref[at, width:] = q_block
            qp = jnp.where(low, scaled + vec[1:2, :], 0.0).astype(BF)
            qp_ref[0, at, :] = qp
            grow = mm(qp, w_pos, ROWS_CC)
            q_sin = grow[:, :half]
            q_cos = grow[:, half:]
            c = trig_ref[at, :half].astype(F32)
            s = trig_ref[at, half:].astype(F32)
            qt_ref[at, :half] = (q_sin * s + q_cos * c).astype(BF)
            qt_ref[at, half:width] = (q_cos * s - q_sin * c).astype(BF)
            return carry

        for i in range(rows // 256):
            body(i, 0)

    att_parts = att_ref.shape[0]
    sub = 256
    count = tile // sub
    small_lane = lax.broadcasted_iota(jnp.int32, (sub, LANES), 1) < DH

    def scores_of(i):
        at = pl.ds(pl.multiple_of(step * tile + i * sub, sub), sub)
        return mm(qt_ref[at, :], kt_ref[...], ROWS_CC)

    later = scores_of(0)
    for i in range(count):
        scores = later
        if i + 1 < count:
            later = scores_of(i + 1)
        top = jnp.max(scores, axis=1, keepdims=True)
        prob = jnp.exp(scores - top).astype(BF)
        prob_ref[0, i * sub:(i + 1) * sub, :] = prob
        mixed = mm(prob, v1_ref[0], ROWCOL)
        total = mixed[:, DH:DH + 1]
        att = mixed / total
        save_ref[0, i * sub:(i + 1) * sub, :] = jnp.where(small_lane, att, 1.0 / total)
        att_t = jnp.transpose(att)[:DH, :].astype(BF)
        for n in range(sub // LANES):
            b = i * (sub // LANES) + n
            att_ref[b % att_parts, b // att_parts] = att_t[:, n * LANES:(n + 1) * LANES]


def attention_backward_kernel(tile, core_ref, do_ref, x_ref, w_ref, vec_ref, kext_ref, trig_ref,
                              qb_ref, kb_ref, v1_ref, qp_ref, save_ref, scl_ref, prob_ref,
                              dx_ref, dw_ref, small_ref,
                              kt_ref, dk_acc, dv_acc, d_ref, dwp_ref, dx_acc):
    step = pl.program_id(1)
    width = trig_ref.shape[1]
    half = width // 2
    lane = lax.broadcasted_iota(jnp.int32, (tile, LANES), 1)
    low = lane < DH

    @pl.when((pl.program_id(0) == 0) & (step == 0))
    def _():
        kt_ref[:, :width] = trig_ref[...]

    @pl.when(step == 0)
    def _():
        kt_ref[:, width:] = kb_ref[0]
        dk_acc[...] = jnp.zeros_like(dk_acc)
        dv_acc[...] = jnp.zeros_like(dv_acc)
        dwp_ref[...] = jnp.zeros_like(dwp_ref)
        small_ref[...] = jnp.zeros_like(small_ref)

    at = pl.ds(pl.multiple_of(step * tile, tile), tile)
    w = w_ref[0]
    w_lane = lax.broadcasted_iota(jnp.int32, (width, LANES), 1)
    w_pos = jnp.where(w_lane < DH, pltpu.roll(w[:, LANES:].astype(F32), DH, 1), 0.0).astype(BF)
    save = save_ref[0]
    inverse = save[:, DH:DH + 1]
    parts = do_ref.shape[0]
    do_t = jnp.concatenate([do_ref[i % parts, i // parts] for i in range(tile // LANES)], axis=1).astype(F32)
    d_out = jnp.transpose(jnp.concatenate([do_t, jnp.zeros_like(do_t)], axis=0))
    d_out = d_out * inverse
    delta = jnp.sum(d_out * save, axis=1, keepdims=True)
    d_hi, d_mid, d_lo = split3(-delta)
    q_block = qb_ref[0]
    ext = jnp.where(lane == DH, d_hi, d_out)
    ext = jnp.where(lane == DH + 1, d_mid, ext)
    ext = jnp.where(lane == DH + 2, d_lo, ext)
    d_ext = ext.astype(BF)
    prob = prob_ref[0]
    dv_acc[...] += mm(d_ext, prob, COLS_CC)
    d_score = (prob.astype(F32) * mm(d_ext, v1_ref[0], ROWS_CC)).astype(BF)
    dk_acc[...] += mm(q_block, d_score, COLS_CC)
    dq = mm(d_score, kt_ref[...], ROWCOL)
    c = trig_ref[at, :half].astype(F32)
    s = trig_ref[at, half:].astype(F32)
    du_c = dq[:, :half]
    du_s = dq[:, half:width]
    back = jnp.concatenate([s * du_c - c * du_s, c * du_c + s * du_s], axis=1).astype(BF)
    d_block = dq[:, width:]
    d_pos = mm(back, w_pos, ROWCOL)
    dwp_ref[...] += mm(qp_ref[0], back, COLS_CC)[:DH, :]
    vec = vec_ref[0]
    kind = kext_ref[...][:, DH + 3:DH + 4].astype(F32)
    every = d_block[:, DH:DH + 1]
    ones = d_block[:, DH + 3:DH + 4]
    g_same = jnp.where(kind > 0.5, ones, every - ones)
    g_other = jnp.where(kind > 0.5, every - ones, ones)
    type_part = g_other * vec[4:5, :] + g_same * vec[5:6, :]
    d_content = jnp.where(low, d_block, 0.0)
    with_type = jnp.where(low, scl_ref[0] + vec[2:3, :], 0.0)
    d_scaled = d_content + d_pos + type_part
    d_ref[:DH, at] = (jnp.transpose(d_scaled)[:DH, :] * DH ** -0.5).astype(BF)
    sums = [jnp.sum(v, axis=0, keepdims=True) for v in
            (d_content, d_pos, type_part, g_other * with_type, g_same * with_type)]
    small_ref[0] += jnp.concatenate(sums + [jnp.zeros((3, LANES), F32)], axis=0)

    @pl.when(step == pl.num_programs(1) - 1)
    def _():
        d_ref[DH:2 * DH] = dk_acc[:DH, :].astype(BF)
        dv_low = dv_acc[:DH, :].astype(BF)
        d_ref[2 * DH:] = dv_low
        dv_sum = jnp.sum(dv_low.astype(F32), axis=1, keepdims=True)
        dv_sum = jnp.transpose(jnp.broadcast_to(jnp.concatenate([dv_sum, dv_sum], axis=0), (LANES, LANES)))
        small_ref[0, 5:6, :] = dv_sum[:1, :]
        d_wt = mm(d_ref[...], x_ref[...], ROWCOL)
        d_w = jnp.transpose(jnp.concatenate([d_wt, dwp_ref[...]], axis=0))
        shard = dw_ref.shape[3]
        members = dw_ref.shape[2]
        for i in range(4 * members):
            dw_ref[(i // members % 2) ^ core_ref[0], i // (2 * members), i % members] = d_w[i * shard:(i + 1) * shard, :].astype(BF)
        d_x = lax.dot_general(d_ref[...], w_ref[0][:, :3 * DH], (((0,), (1,)), ((), ())), preferred_element_type=F32)

        @pl.when(pl.program_id(0) == 0)
        def _():
            dx_acc[...] = d_x

        @pl.when(pl.program_id(0) > 0)
        def _():
            dx_acc[...] += d_x

        @pl.when(pl.program_id(0) == pl.num_programs(0) - 1)
        def _():
            dx_ref[...] = dx_acc[...].astype(BF)


def attention_forward(x, w_block, first, count, heads, vec, kext, trig, previous=(), tile=1024):
    rows, width = x.shape
    owners = w_block.shape[0]
    shard = width // owners
    full = width + LANES
    per_head = lambda shape: pl.BlockSpec((1,) + shape, lambda h, t: (first + h, 0, 0))
    fixed = lambda shape: pl.BlockSpec(shape, lambda h, t: (0, 0))
    flops = count * rows * 2 * (width * 256 + rows * full + rows * LANES)
    S = jax.ShapeDtypeStruct
    kernel = functools.partial(attention_forward_kernel, tile)
    skip = len(previous)
    return pl.pallas_call(
        lambda *refs: kernel(*refs[:5], *refs[5 + skip:]),
        grid=(count, rows // tile),
        in_specs=[fixed((rows, width)), pl.BlockSpec((owners, shard, 2 * LANES), lambda h, t: (0, first + h, 0)),
                  per_head((8, LANES)), fixed((rows, LANES)), fixed((rows, width))]
        + [pl.BlockSpec(memory_space=pl.ANY)] * skip,
        out_specs=[pl.BlockSpec((2, tile // (2 * LANES), DH, LANES), lambda h, t: (0, t, first + h, 0)),
                   per_head((rows, LANES)), per_head((rows, LANES)), per_head((rows, LANES)),
                   per_head((rows, LANES)),
                   pl.BlockSpec((1, tile, LANES), lambda h, t: (first + h, t, 0)),
                   per_head((rows, LANES)), per_head((width, 2 * LANES)),
                   pl.BlockSpec((1, tile, rows), lambda h, t: (first + h, t, 0))],
        out_shape=[S((2, rows // (2 * LANES), heads * DH, LANES), BF), S((heads, rows, LANES), BF),
                   S((heads, rows, LANES), BF), S((heads, rows, LANES), BF), S((heads, rows, LANES), BF),
                   S((heads, rows, LANES), F32), S((heads, rows, LANES), F32), S((heads, width, 2 * LANES), BF),
                   S((heads, rows, rows), BF)],
        input_output_aliases={5 + i: i for i in range(skip)},
        scratch_shapes=[pltpu.VMEM((rows, full), BF), pltpu.VMEM((rows, full), BF)],
        compiler_params=pltpu.CompilerParams(dimension_semantics=("arbitrary", "arbitrary"),
                                             vmem_limit_bytes=63 * 2 ** 20),
        cost_estimate=pl.CostEstimate(flops=flops, bytes_accessed=rows * width * 16, transcendentals=count * rows * rows),
        name="attention_forward",
    )(x, w_block, vec, kext, trig, *previous)


def attention_backward(core, d_out, x, w, vec, kext, trig, qb, kb, v1, qp, save, scl, prob, owners, block_rows, tile=1024):
    heads, rows, _ = qb.shape
    width = x.shape[1]
    full = width + LANES
    shard = width // owners
    per_head = lambda shape: pl.BlockSpec((1,) + shape, lambda h, t: (h, 0, 0))
    per_tile = lambda cols: pl.BlockSpec((1, tile, cols), lambda h, t: (h, t, 0))
    fixed = lambda shape: pl.BlockSpec(shape, lambda h, t: (0, 0))
    flops = heads * rows * 2 * (2 * rows * full + 3 * rows * LANES)
    return pl.pallas_call(
        functools.partial(attention_backward_kernel, tile),
        grid=(heads, rows // tile),
        in_specs=[pl.BlockSpec(memory_space=pltpu.SMEM), pl.BlockSpec((2, tile // (2 * LANES), DH, LANES), lambda h, t: (0, t, h, 0)), fixed((rows, width)),
                  per_head((width, 256)), per_head((8, LANES)),
                  pl.BlockSpec((tile, LANES), lambda h, t: (t, 0)), fixed((rows, width)),
                  per_tile(LANES), per_head((rows, LANES)), per_head((rows, LANES)), per_tile(LANES),
                  per_tile(LANES), per_tile(LANES), per_tile(rows)],
        out_specs=[fixed((rows, width)), pl.BlockSpec((2, 2, owners // 4, shard, 2 * LANES), lambda h, t: (0, 0, 0, h, 0)),
                   per_head((8, LANES))],
        out_shape=[jax.ShapeDtypeStruct((rows, width), BF),
                   jax.ShapeDtypeStruct((2, 2, owners // 4, block_rows, 2 * LANES), BF),
                   jax.ShapeDtypeStruct((heads, 8, LANES), F32)],
        scratch_shapes=[pltpu.VMEM((rows, full), BF),
                        pltpu.VMEM((LANES, rows), F32), pltpu.VMEM((LANES, rows), F32),
                        pltpu.VMEM((3 * DH, rows), BF), pltpu.VMEM((DH, width), F32),
                        pltpu.VMEM((rows, width), F32)],
        compiler_params=pltpu.CompilerParams(dimension_semantics=("arbitrary", "arbitrary"),
                                             vmem_limit_bytes=63 * 2 ** 20),
        cost_estimate=pl.CostEstimate(flops=flops, bytes_accessed=rows * width * 20, transcendentals=heads * rows * rows),
        name="attention_backward",
    )(core.reshape(1), d_out, x, w, vec, kext, trig, qb, kb, v1, qp, save, scl, prob)


def key_extension(kinds, valid):
    rows = kinds.shape[0]
    lane = jnp.arange(LANES)[None, :]
    k = kinds[:, None]
    out = jnp.where((lane >= DH) & (lane < DH + 3) | (lane >= DH + 6) & (lane < DH + 9), 1.0, 0.0)
    out = jnp.where((lane == DH + 3) | (lane == DH + 4), k, out)
    out = jnp.where(lane == DH + 5, jnp.where(valid[:, None] > 0, 0.0, -1e30), out)
    return jnp.broadcast_to(out, (rows, LANES)).astype(BF)


def pack_kernel(heads, groups, *refs):
    mats, smalls, (wide_ref, kinds_ref, inner_ref, outer_ref, output_ref, out_ref, packed_ref, third_ref) = refs[:4], refs[4:16], refs[16:]
    rows, width = mats[0].shape
    for g in range(groups):
        for h in range(heads):
            at = pl.ds((g * heads + h) * DH, DH)
            value = jnp.concatenate([m[:, at] for m in mats], axis=1)
            for c in range(g, out_ref.shape[0], groups):
                out_ref[c, h * rows:(h + 1) * rows, :] = value
    pad = jnp.zeros((1, LANES - rows), F32)
    lines = [jnp.concatenate([v[...].astype(F32), pad], axis=1) for v in smalls]
    none = jnp.zeros((1, LANES), F32)
    inner = jnp.concatenate([wide_ref[...].astype(F32), jnp.zeros((1, LANES - wide_ref.shape[1]), F32)], axis=1)
    left = jnp.concatenate(lines[:8], axis=0)
    kinds = kinds_ref[...].astype(F32)
    right = jnp.concatenate(lines[8:] + [inner, kinds, none], axis=0)
    both = jnp.concatenate([left, right], axis=1).astype(BF)
    for c in range(out_ref.shape[0]):
        out_ref[c, heads * rows:, :] = both
    count = inner_ref.shape[1] // width
    for i in range(count):
        packed_ref[i * rows:(i + 1) * rows, :] = inner_ref[:, i * width:(i + 1) * width]
    packed_ref[count * rows:, :] = outer_ref[...]
    third_ref[...] = output_ref[...]


def pack(mats, smalls, wide, kinds, inner, outer, output, heads, groups, members):
    rows, width = mats[0].shape
    third = output.shape[0]
    total = inner.shape[1] // width * rows + outer.shape[0]
    return pl.pallas_call(
        functools.partial(pack_kernel, heads, groups),
        out_shape=[jax.ShapeDtypeStruct((members, heads * rows + 8, 2 * LANES), BF),
                   jax.ShapeDtypeStruct((total, width), BF), jax.ShapeDtypeStruct((third, width), BF)],
        name="pack_columns",
    )(*mats, *smalls, wide, kinds, inner, outer, output)


def unpack_kernel(heads, groups, shard, g_ref, block_ref, vecs_ref, wide_ref, vec_ref):
    owners = block_ref.shape[0]
    wide = wide_ref.shape[1] // owners
    for o in range(owners):
        t = block_ref[o].astype(F32)
        vecs_ref[:8, o * shard:(o + 1) * shard] = t[:, :shard]
        vecs_ref[8:, o * shard:(o + 1) * shard] = t[:, LANES:LANES + shard]
        wide_ref[:, o * wide:(o + 1) * wide] = t[4:5, LANES:LANES + wide]
    zeros = jnp.zeros((8, LANES - DH), F32)
    for g in range(groups):
        @pl.when(g_ref[0] == g)
        def _():
            for h in range(heads):
                part = vecs_ref[:8, (g * heads + h) * DH:(g * heads + h + 1) * DH]
                vec_ref[h] = jnp.concatenate([part, zeros], axis=1)


def unpack(block, g, heads, groups, shard, wide):
    owners, rows, _ = block.shape
    return pl.pallas_call(
        functools.partial(unpack_kernel, heads, groups, shard),
        grid=(1,),
        in_specs=[pl.BlockSpec(memory_space=pltpu.SMEM),
                  pl.BlockSpec((owners, 8, 2 * LANES), lambda i: (0, rows // 8 - 1, 0))],
        out_specs=[pl.BlockSpec((16, owners * shard), lambda i: (0, 0)), pl.BlockSpec((1, owners * wide), lambda i: (0, 0)),
                   pl.BlockSpec((heads, 8, LANES), lambda i: (0, 0, 0))],
        out_shape=[jax.ShapeDtypeStruct((16, owners * shard), F32), jax.ShapeDtypeStruct((1, owners * wide), F32),
                   jax.ShapeDtypeStruct((heads, 8, LANES), F32)],
        name="unpack_small",
    )(g.reshape(1), block)


def small_kernel(heads, groups, shard, g_ref, heads_ref, rest_ref, wide_ref, unused_ref, out_ref, table_ref):
    members = out_ref.shape[2]
    owners = 4 * members
    wide = wide_ref.shape[1] // owners
    table_ref[:6] = jnp.zeros((6, table_ref.shape[1]), F32)
    for g in range(groups):
        @pl.when(g_ref[0] == g)
        def _():
            for h in range(heads):
                table_ref[:6, (g * heads + h) * DH:(g * heads + h + 1) * DH] = heads_ref[h, :6, :DH]
    table_ref[6:12] = rest_ref[...]
    pad = jnp.zeros((8, LANES - shard), F32)
    for o in range(owners):
        left = table_ref[:8, o * shard:(o + 1) * shard]
        right = jnp.concatenate([table_ref[8:12, o * shard:(o + 1) * shard], jnp.zeros((4, LANES - shard), F32)], axis=1)
        inner = jnp.concatenate([wide_ref[:, o * wide:(o + 1) * wide], jnp.zeros((1, LANES - wide), F32)], axis=1)
        right = jnp.concatenate([right, inner, jnp.zeros((3, LANES), F32)], axis=0)
        out_ref[(o // members % 2) ^ g_ref[1], o // (2 * members), o % members] = jnp.concatenate([left, pad, right], axis=1).astype(BF)


def small_rows(block, g, head_sums, rest, wide_sums, groups, shard):
    members, rows = block.shape[2:4]
    owners = 4 * members
    heads = head_sums.shape[0]
    whole = lambda a: pl.BlockSpec(a.shape, lambda i: (0,) * a.ndim)
    return pl.pallas_call(
        functools.partial(small_kernel, heads, groups, shard),
        grid=(1,),
        in_specs=[pl.BlockSpec(memory_space=pltpu.SMEM), whole(head_sums), whole(rest), whole(wide_sums),
                  pl.BlockSpec(memory_space=pl.ANY)],
        out_specs=pl.BlockSpec((2, 2, members, 8, 2 * LANES), lambda i: (0, 0, 0, rows // 8 - 1, 0)),
        out_shape=jax.ShapeDtypeStruct(block.shape, BF),
        input_output_aliases={4: 0},
        scratch_shapes=[pltpu.VMEM((16, owners * shard), F32)],
        cost_estimate=pl.CostEstimate(flops=2 * 10 ** 10, bytes_accessed=2 ** 20, transcendentals=0),
        name="small_gradients",
    )(g, head_sums, rest, wide_sums, block)


def finish_kernel(heads, block_ref, *refs):
    outs, vectors, pair_ref, wide_ref = refs[:4], refs[4:14], refs[14], refs[15]
    groups = block_ref.shape[0] // 2
    shard = outs[0].shape[0]
    total = sum(block_ref[g, heads * shard:, :].astype(F32) for g in range(2 * groups))
    for n, i in enumerate((0, 1, 2, 5, 6, 7)):
        vectors[n][...] = total[i, :shard]
    for i in range(4):
        vectors[6 + i][...] = total[i, LANES:LANES + shard]
    pair_ref[...] = total[3:5, :shard]
    wide_ref[...] = total[4, LANES:LANES + wide_ref.shape[0]]
    for g in range(groups):
        for h in range(heads):
            part = block_ref[g, h * shard:(h + 1) * shard, :].astype(F32)
            part = part + block_ref[groups + g, h * shard:(h + 1) * shard, :].astype(F32)
            at = (g * heads + h) * DH
            for m in range(4):
                outs[m][:, at:at + DH] = part[:, m * DH:(m + 1) * DH]


def finish(block, heads, shard, width, wide):
    S = jax.ShapeDtypeStruct
    return pl.pallas_call(
        functools.partial(finish_kernel, heads),
        out_shape=[S((shard, width), F32)] * 4 + [S((shard,), F32)] * 10 + [S((2, shard), F32), S((wide,), F32)],
        name="finish_columns",
    )(block)


def row_sum_kernel(bit_ref, keep_ref, first_ref, *refs):
    bit = bit_ref[0]
    total = keep_ref[0, bit].astype(F32) + first_ref[bit].astype(F32)
    for ref in refs[:-1]:
        total = total + ref[...].astype(F32)
    refs[-1][...] = total.astype(BF)


def row_sum(bit, keep, first, *more):
    vmem = pl.BlockSpec(memory_space=pltpu.VMEM)
    return pl.pallas_call(
        row_sum_kernel,
        in_specs=[pl.BlockSpec(memory_space=pltpu.SMEM)] + [vmem] * (2 + len(more)),
        out_specs=vmem,
        out_shape=jax.ShapeDtypeStruct(first.shape[1:], BF),
        cost_estimate=pl.CostEstimate(flops=2 * 10 ** 10, bytes_accessed=2 ** 20, transcendentals=0),
        name="row_sum",
    )(bit.reshape(1), keep, first, *more)


def token_kernel(core_ref, valid_ref, mixed_ref, x_ref, og_ref, vec_ref, wide_ref,
                 inner_one, inner_two, inner_three, inner_four, outer_one, outer_two, outer_three, outer_four, third_one, third_two,
                 result_ref, first_ref, grad_ref, gi_keep, gi_send, go_keep, go_send, gt_keep, gt_send, rest_ref, gw_ref,
                 packed, wi, act, slope, normed_t, acc, gi_ref, go_ref, sems, back_sems):
    core, bit_y, bit_x = core_ref[0], core_ref[1], core_ref[2]
    seqs, width, stretch = mixed_ref.shape
    tokens = seqs * stretch
    count = wi.shape[1] // width
    members = 2 * packed.shape[1]
    block = width // count
    shard = block // members
    wide = packed.shape[3] - (count + 1) * shard
    base = count * shard
    copies = []
    for i, (src, k) in enumerate(((third_one, core), (third_two, 1 - core))):
        for y in range(2):
            copies.append(pltpu.make_async_copy(src.at[:, y], packed.at[2 * y + k, :, :, base + wide:, :], sems.at[26 + 2 * i + y]))
    sources = ((outer_one, core, bit_x), (outer_two, 1 - core, bit_x), (outer_three, core, 1 - bit_x), (outer_four, 1 - core, 1 - bit_x))
    for i, (src, k, x) in enumerate(sources):
        for y in range(2):
            copies.append(pltpu.make_async_copy(src.at[y], packed.at[2 * y + k, :, x, base:base + wide, :], sems.at[4 + 2 * i + y]))
    sources = ((inner_one, core, bit_y), (inner_two, 1 - core, bit_y), (inner_three, core, 1 - bit_y), (inner_four, 1 - core, 1 - bit_y))
    for i, (src, k, y) in enumerate(sources):
        for x in range(2):
            copies.append(pltpu.make_async_copy(src.at[x], packed.at[2 * y + k, :, x, :base, :], sems.at[12 + 2 * i + x]))
    for copy in copies:
        copy.start()
    for copy in copies[:4]:
        copy.wait()
    w_out = packed[:, :, :, base + wide:, :].astype(F32).reshape(width, width).astype(BF)
    def w_outer(j):
        return packed[j, :, :, base:base + wide, :].reshape(width, width)

    vec = vec_ref[...]
    line = lambda i: vec[i:i + 1, :]
    mean = lambda v: jnp.mean(v, axis=1, keepdims=True)
    attn = jnp.concatenate([mm(mixed_ref[b], w_out, COLS_CC) for b in range(seqs)], axis=0) + line(6)
    first = x_ref[...].astype(F32) + attn
    center = first - mean(first)
    r_one = lax.rsqrt(mean(center * center) + epsilon)
    hat_one = center * r_one
    normed = hat_one * line(7) + line(8)
    low = normed.astype(BF)
    normed_t[...] = jnp.transpose(normed).astype(BF)
    acc[...] = jnp.zeros_like(acc)

    for copy in copies[4:]:
        copy.wait()
    for i in range(count):
        wi[:, i * width:(i + 1) * width] = packed[:, :, :, i * shard:(i + 1) * shard, :].astype(F32).reshape(width, width).astype(BF)

    def forward(j, carry):
        at = pl.ds(pl.multiple_of(j * width, width), width)
        u = mm(low, wi[:, at], ROWCOL) + wide_ref[:, at]
        c = 0.7978845608028654
        sq = u * u
        t = jnp.tanh(c * u * (1.0 + 0.044715 * sq))
        half = 0.5 * (1.0 + t)
        a = (u * half).astype(BF)
        act[:, at] = a
        slope[:, at] = half + 0.5 * u * (1.0 - t * t) * (c * (1.0 + 3 * 0.044715 * sq))
        acc[...] += mm(a, w_outer(j), ROWCOL)
        return carry

    lax.fori_loop(0, count, forward, 0)
    outer = acc[...] + line(9)
    second = normed + outer
    center = second - mean(second)
    r_two = lax.rsqrt(mean(center * center) + epsilon)
    hat_two = center * r_two
    result_ref[...] = (hat_two * line(10) + line(11)).astype(BF)
    valid = valid_ref[...]
    cot = og_ref[...].astype(F32) * valid
    d_hat = cot * line(10)
    d_second = r_two * (d_hat - mean(d_hat) - hat_two * mean(d_hat * hat_two))
    d_low = d_second.astype(BF)
    total = lambda v: jnp.sum(v, axis=0, keepdims=True)
    outer_sum = total(d_low.astype(F32))
    two = [total(cot * hat_two), total(cot)]
    acc[...] = d_second

    part = wide // 2

    def inner_back(j):
        return [
            pltpu.make_async_copy(gi_ref.at[which, y, j], (gi_keep, gi_send)[which].at[y, j], back_sems.at[j, 2 * which + y])
            for which in range(2) for y in range(2)]

    def upper(which, y, j):
        low_part = pltpu.make_async_copy(go_ref.at[which, y, :, :part, :], (gt_keep, gt_send)[which].at[y], sems.at[20 + j])
        high_part = pltpu.make_async_copy(
            go_ref.at[which, y, :, part:wide, :], (go_keep, go_send)[which].at[y, :, :part, :], sems.at[30 + j])
        return low_part, high_part

    def lower(which, y):
        target = (go_keep, go_send)[which]
        return pltpu.make_async_copy(go_ref.at[which, y, :, wide:, :], target.at[y, :, part:, :], sems.at[2 * which + y])

    def backward(j, carry):
        at = pl.ds(pl.multiple_of(j * width, width), width)
        d_act = mm(d_low, w_outer(j), ROWS_CC)
        d_in = d_act * slope[:, at]
        d_in_low = d_in.astype(BF)
        gw_ref[:, at] = total(d_in_low.astype(F32))
        acc[...] += mm(d_in_low, wi[:, at], ROWS_CC)
        go = mm(act[:, at], d_low, COLS_CC)
        which = (j % 2) ^ core
        go_ref[which, j // 2, :, :wide, :] = go.astype(BF).reshape(members, wide, width)

        @pl.when(which == 0)
        def _():
            for copy in upper(0, j // 2, j):
                copy.start()

        @pl.when(which == 1)
        def _():
            for copy in upper(1, j // 2, j):
                copy.start()

        for b in range(count):
            gi = mm(normed_t[b * block:(b + 1) * block, :], d_in_low, ROWCOL)
            gi_ref[(b % 2) ^ core, b // 2, j] = gi.reshape(members, shard, width).astype(BF)
        for copy in inner_back(j):
            copy.start()
        return carry

    lax.fori_loop(0, count, backward, 0)
    d_normed = acc[...]
    one = [total(d_normed * hat_one), total(d_normed)]
    d_hat = d_normed * line(7)
    d_first = r_one * (d_hat - mean(d_hat) - hat_one * mean(d_hat * hat_one))
    first_ref[...] = d_first
    a_low = d_first.astype(BF)
    rest_ref[...] = jnp.concatenate([total(a_low.astype(F32))] + one + [outer_sum] + two, axis=0)
    grad = mm(w_out, a_low, ROWS_CC).astype(BF)
    span = grad_ref.shape[1] - 8
    groups = width // span
    lane = lax.broadcasted_iota(jnp.int32, (1, stretch), 1)
    sums = jnp.zeros((1, stretch), F32)
    everything = lambda v: jnp.sum(jnp.sum(v, axis=0, keepdims=True), axis=1, keepdims=True)
    for b in range(seqs):
        at = slice(b * stretch, (b + 1) * stretch)
        for i, v in enumerate((first, attn, outer)):
            sums = jnp.where(lane == 3 * b + i, everything(v[at] * v[at] * valid[at]), sums)
    high = sums.astype(BF).astype(F32)
    riders = jnp.concatenate([high, sums - high, jnp.zeros((6, stretch), F32)], axis=0).astype(BF)
    for b in range(seqs):
        for g in range(groups):
            grad_ref[b * groups + g, :span, :] = grad[g * span:(g + 1) * span, b * stretch:(b + 1) * stretch]
            grad_ref[b * groups + g, span:, :] = riders
    out = mm(mixed_ref[0], a_low[:stretch], ROWCOL)
    for b in range(1, seqs):
        out += mm(mixed_ref[b], a_low[b * stretch:(b + 1) * stretch], ROWCOL)
    for b in range(count):
        for i in range(members):
            at = b * block + i * shard
            go_ref[(b % 2) ^ core, b // 2, i, wide:, :] = out[at:at + shard, :].astype(BF)
    lowers = [lower(which, y) for which in range(2) for y in range(2)]
    for back in lowers:
        back.start()
    for j in range(count):
        for copy in upper(0, 0, j):
            copy.wait()
    for j in range(count):
        for copy in inner_back(j):
            copy.wait()
    for back in lowers:
        back.wait()


def token_block(core, valid, mixed, x, out_grad, vectors, inner_add, inner_parts, outer_parts, third_parts, span):
    seqs, width, stretch = mixed.shape
    tokens = seqs * stretch
    ff = inner_add.shape[1]
    count = ff // width
    members = inner_parts[0].shape[0] * inner_parts[0].shape[1]
    owners = members * count
    rows = ff // owners + width // owners
    half_rows = ff // owners // 2
    base = ff // width * (width // owners)
    groups = width // span
    vmem = pl.BlockSpec(memory_space=pltpu.VMEM)
    hbm = pl.BlockSpec(memory_space=pl.ANY)
    S = jax.ShapeDtypeStruct
    return pl.pallas_call(
        token_kernel,
        in_specs=[pl.BlockSpec(memory_space=pltpu.SMEM)] + [vmem] * 6 + [hbm] * 10,
        out_specs=[vmem] * 3 + [hbm] * 6 + [vmem] * 2,
        out_shape=[S((tokens, width), BF), S((tokens, width), F32), S((seqs * groups, span + 8, stretch), BF),
                   S((2, count, members, width // owners, width), BF), S((2, count, members, width // owners, width), BF),
                   S((2, members, rows - half_rows, width), BF), S((2, members, rows - half_rows, width), BF),
                   S((2, members, half_rows, width), BF), S((2, members, half_rows, width), BF),
                   S((6, width), F32), S((1, ff), F32)],
        scratch_shapes=[pltpu.VMEM((count, members // 2, 2, (count + 1) * (width // owners) + ff // owners, width), BF), pltpu.VMEM((width, ff), BF),
                        pltpu.VMEM((tokens, ff), BF), pltpu.VMEM((tokens, ff), F32),
                        pltpu.VMEM((width, tokens), BF), pltpu.VMEM((tokens, width), F32),
                        pltpu.VMEM((2, 2, count, members, width // owners, width), BF), pltpu.VMEM((2, 2, members, rows, width), BF),
                        pltpu.SemaphoreType.DMA((34,)), pltpu.SemaphoreType.DMA((count, 4))],
        compiler_params=pltpu.CompilerParams(vmem_limit_bytes=63 * 2 ** 20),
        cost_estimate=pl.CostEstimate(flops=tokens * 2 * width * (6 * ff + 4 * width), bytes_accessed=30 * 2 ** 20, transcendentals=tokens * ff),
        name="token_block",
    )(core, valid, mixed, x, out_grad, vectors, inner_add, *inner_parts, *outer_parts, *third_parts)


def takes_head_layout(mesh):
    return dict(mesh.shape) == {DP: 4, CTX: 8}


def swap(x, axis, bit):
    count = lax.axis_size(axis)
    return lax.ppermute(x, axis, [(i, i ^ bit) for i in range(count)])


def in_order(bit, own, received, axis):
    first = jnp.where(bit == 0, own, received)
    second = jnp.where(bit == 0, received, own)
    return jnp.stack([first, second], axis=axis)


def pick(x, index, axis):
    return lax.dynamic_index_in_dim(x, index, axis, keepdims=False)


def after(x, *others):
    return lax.optimization_barrier((x,) + others)[0]


def exchange(x, along_z):
    count = lax.axis_size(CTX)
    if along_z:
        sets = [[m for m in range(count) if m % 2 == i] for i in range(2)]
    else:
        sets = [list(range(count // 2)), list(range(count // 2, count))]
    return lax.all_to_all(x, CTX, 0, 0, axis_index_groups=sets, tiled=True)


def in_z_order(pieces):
    z = lax.axis_index(CTX) // 2
    block = jnp.stack(pieces).reshape((2, 2) + pieces[0].shape)
    for axis, bit in ((1, z % 2), (0, z // 2)):
        block = jnp.where(bit == 0, block, jnp.flip(block, axis))
    return block.reshape((4,) + pieces[0].shape)


def total_low(terms):
    return sum(t.astype(F32) for t in terms).astype(BF)


def picks(terms, bit, axis):
    return [pick(t, bit, axis) for t in terms]


def head_layout(
    inputs,
    out_grad,
    lengths,
    token_types,
    query_weight,
    key_weight,
    value_weight,
    value_bias,
    position_weight,
    content_bias,
    position_bias,
    type_bias,
    type_embed,
    output_weight,
    output_bias,
    first_gain,
    first_shift,
    inner_weight,
    inner_bias,
    outer_weight,
    outer_bias,
    second_gain,
    second_shift,
):
    d, c = lax.axis_index(DP), lax.axis_index(CTX)
    members = lax.axis_size(CTX)
    devices = lax.axis_size(DP) * members
    seqs, stretch, width = inputs.shape
    seq_len = stretch * members
    groups = members // seqs
    heads = H // groups
    span = heads * DH
    half = width // 2
    shard = width // devices
    inner_shard = inner_bias.shape[0]
    s, g = c // groups, c % groups
    bit_x = c % 2
    core, bit_y = d % 2, d // 2

    x_send = pick(inputs, 1 - s, 0)
    own = pick(inputs, s, 0)

    smalls = (
        content_bias,
        position_bias,
        type_bias,
        value_bias,
        type_embed[0],
        type_embed[1],
        output_bias,
        first_gain,
        first_shift,
        outer_bias,
        second_gain,
        second_shift,
    )
    stacked, packed, third = pack(
        (after(query_weight, x_send), key_weight, value_weight, position_weight),
        tuple(v.reshape(1, shard) for v in smalls),
        inner_bias.reshape(1, inner_shard),
        token_types,
        inner_weight,
        outer_weight,
        output_weight,
        heads,
        groups,
        members,
    )
    cut = (inner_weight.shape[1] // width) * shard
    block = lax.all_to_all(stacked, CTX, 0, 0, tiled=True)
    x_pair = in_order(s, own, swap(x_send, CTX, 4), 0)
    packed, third = after((packed, third), x_pair)
    third_y = swap(third, DP, 2)
    packed_z = [swap(packed, CTX, 2 * m) for m in (1, 2, 3)]
    lines = block[:, heads * shard + 5 : heads * shard + 5 + seqs, LANES:]
    kind_seq = pick(lines, s, 1).reshape(2, groups, stretch).transpose(1, 0, 2)
    kind_seq = kind_seq.reshape(seq_len).astype(F32)
    x_pair = jnp.broadcast_to(after(x_pair, block)[None], (groups, 2, stretch, width))
    x_all = exchange(x_pair, False)
    block = block[None]
    block = in_order(bit_y, block, swap(block, DP, 2), 0)
    third = in_order(bit_y, third, after(third_y, block), 0)
    third_x = swap(third, CTX, 1)
    packed_z = after(packed_z, x_pair, block, third)
    packed_z = in_z_order([packed] + packed_z)
    inner_block, outer_block = packed_z[:, :cut], packed_z[:, cut:]
    inner_x, outer_y = swap(inner_block, CTX, 1), swap(outer_block, DP, 2)
    block = in_order(core, block, after(swap(block, DP, 1), inner_block, outer_block), 1)
    block = block.reshape((devices,) + stacked.shape[1:])
    x_seq = after(x_all, block).reshape(seq_len, width)

    exponent = 2.0 * jnp.arange(half, dtype=F32) / width
    rates = (10000.0 ** (-exponent))[None, :]
    owners = jnp.arange(members, dtype=jnp.int32).reshape(2, groups).T.reshape(-1)
    starts = (owners * stretch).astype(F32)[:, None] * rates
    steps = jnp.arange(stretch, dtype=F32)[:, None] * rates
    starts, steps = lax.optimization_barrier((starts, steps))
    cos_a, sin_a = jnp.cos(starts)[:, None], jnp.sin(starts)[:, None]
    cos_b, sin_b = jnp.cos(steps)[None], jnp.sin(steps)[None]
    trig = jnp.concatenate(
        [cos_a * cos_b - sin_a * sin_b, sin_a * cos_b + cos_a * sin_b], axis=2
    ).reshape(seq_len, width).astype(BF)
    slots = owners[:, None] * stretch + jnp.arange(stretch, dtype=jnp.int32)[None, :]
    key_valid = (slots.reshape(-1) < pick(lengths, s, 0)).astype(F32)
    kext = key_extension(kind_seq, key_valid)

    vectors, inner_add, vec = unpack(block, g, heads, groups, shard, inner_shard)

    saved = attention_forward(x_seq, block, 0, 1, heads, vec, kext, trig)
    inner_x, outer_y, third_x = after((inner_x, outer_y, third_x), saved[0])
    third = in_order(bit_x, third, third_x, 1)
    inner_block = in_order(bit_x, inner_block, inner_x, 0)
    outer_block = in_order(bit_y, outer_block, outer_y, 0)
    inner_y, outer_x = swap(inner_block, DP, 2), swap(outer_block, CTX, 1)
    third_z = [swap(third, CTX, 2 * m) for m in (1, 2, 3)]
    saved = attention_forward(
        x_seq,
        block,
        1,
        heads - 1,
        heads,
        after(vec, inner_block, outer_block, third),
        kext,
        trig,
        saved,
    )
    att, q_block, kb, v1, qp, save, scl, w_heads, prob = saved
    third_z = after(third_z, att)
    att = after(att, third_z).reshape(members, span, stretch)
    mixed = lax.all_to_all(att, CTX, 0, 0, tiled=True).reshape(seqs, width, stretch)
    inner_block, outer_block = after((inner_block, outer_block), att)
    inner_far, outer_far = swap(inner_block, DP, 1), swap(outer_block, DP, 1)
    third = in_z_order([third] + third_z)
    third_parts = (third, swap(third, DP, 1))
    mixed = after(mixed, third_parts[1], inner_far, outer_far)
    inner_y, outer_x = after((inner_y, outer_x), mixed)
    inner_parts = (inner_block, inner_far, inner_y, swap(inner_y, DP, 1))
    outer_parts = (outer_block, outer_far, outer_x, swap(outer_x, DP, 1))

    own_slots = c * stretch + jnp.arange(stretch, dtype=jnp.int32)
    row_valid = (own_slots[None, :] < lengths[:, None]).astype(F32)
    result, first_grad, mixed_grad, inner_keep, inner_send, outer_keep, outer_send, third_keep, third_send, rest, wide = (
        token_block(
            jnp.stack([core, bit_y, bit_x]),
            row_valid.reshape(-1, 1),
            mixed,
            inputs.reshape(-1, width),
            out_grad.reshape(-1, width),
            vectors,
            inner_add,
            inner_parts,
            outer_parts,
            third_parts,
            span,
        )
    )
    result = result.reshape(inputs.shape)
    first_grad = first_grad.reshape(inputs.shape)

    d_out = lax.all_to_all(mixed_grad, CTX, 0, 0, tiled=True)
    z = c // 2
    first_half = inner_shard // 2
    third_terms = [third_keep, swap(third_send, DP, 1)]
    inner_send, outer_send = after((inner_send, outer_send), third_terms[1])
    inner_terms = [inner_keep, swap(inner_send, DP, 1)]
    inner_terms = [t.reshape(2, -1, 4, 2, shard, width) for t in inner_terms]
    third_terms = [t.reshape(2, 4, 2, first_half, width) for t in third_terms]
    outer_terms = [outer_keep, swap(outer_send, DP, 1)]
    outer_terms = [t.reshape(2, 4, 2, first_half + shard, width) for t in outer_terms]
    third_send = [total_low(picks(third_terms, z ^ m, 1)) for m in (1, 2, 3)]
    third_z = [swap(third_send[m - 1], CTX, 2 * m) for m in (1, 2, 3)]
    inner_terms[1] = after(inner_terms[1], *third_send)
    inner_send = total_low(picks(inner_terms, 1 - bit_y, 0))
    inner_y = swap(inner_send, DP, 2)
    outer_terms[1] = after(outer_terms[1], inner_send)
    outer_send = total_low(picks(outer_terms, 1 - bit_x, 2))
    outer_x = swap(outer_send, CTX, 1)
    d_out = after(d_out, inner_send, outer_send, *third_send)
    d_blocks = d_out.reshape(2, groups, span + 8, stretch)

    d_x, w_grad, head_sums = attention_backward(
        core,
        d_blocks,
        x_seq,
        w_heads,
        vec,
        kext,
        trig,
        q_block,
        kb,
        v1,
        qp,
        save,
        scl,
        prob,
        devices,
        heads * shard + 8,
    )
    d_x, w_grad, head_sums, inner_y, outer_x, third_z = lax.optimization_barrier(
        (d_x, w_grad, head_sums, inner_y, outer_x, third_z)
    )
    d_x = exchange(d_x.reshape(groups, 2, stretch, width), False)
    w_both = small_rows(w_grad, jnp.stack([g, core]), head_sums, rest, wide, groups, shard)
    w_far = swap(w_both[1], DP, 1)
    outer_x, inner_y, third_z = after((outer_x, inner_y, third_z), w_both)
    outer_terms = picks(outer_terms, bit_x, 2) + [outer_x]
    outer_send = [total_low(picks(outer_terms, z ^ m, 1)) for m in (1, 2, 3)]
    outer_z = [swap(outer_send[m - 1], CTX, 2 * m) for m in (1, 2, 3)]
    inner_terms = picks(inner_terms, bit_y, 0) + [inner_y]
    inner_send = total_low(picks(inner_terms, 1 - bit_x, 2))
    inner_x = swap(inner_send, CTX, 1)
    w_far = after(w_far, inner_send, *outer_send)
    block_send = row_sum(1 - bit_y, w_both, w_far)
    block_y = swap(block_send, DP, 2)

    d_x_send = jnp.sum(pick(d_x, 1 - s, 1).astype(F32), axis=0).astype(BF)
    d_x_z = swap(d_x_send, CTX, 4)
    block = row_sum(bit_y, w_both, w_far, after(block_y, d_x_send))
    inner_sum = total_low(picks(inner_terms, bit_x, 2) + [after(inner_x, block)])
    third_terms = picks(third_terms, z, 1) + after(third_z, block)
    third_send = total_low(picks(third_terms, 1 - bit_y, 0))
    third_y = swap(third_send, DP, 2)
    block = lax.all_to_all(block, CTX, 0, 0, tiled=True)
    inner_send = [pick(inner_sum, z ^ m, 1) for m in (1, 2, 3)]
    inner_z = [swap(inner_send[m - 1], CTX, 2 * m) for m in (1, 2, 3)]
    outer_z = after(outer_z, *inner_send)
    outer_terms = picks(outer_terms, z, 1) + outer_z
    outer_y = swap(total_low(picks(outer_terms, 1 - bit_y, 0)), DP, 2)
    third_terms = picks(third_terms, bit_y, 0) + [after(third_y, *inner_send)]
    third_x = swap(total_low(picks(third_terms, 1 - bit_x, 0)), CTX, 1)
    third_own = sum(t.astype(F32) for t in picks(third_terms, bit_x, 0) + [third_x])
    outer_sum = sum(t.astype(F32) for t in picks(outer_terms, bit_y, 0) + [outer_y])
    outer_own = jnp.concatenate([third_own, outer_sum[:first_half]], axis=0)
    output_own = outer_sum[first_half:]
    finished = finish(block, heads, shard, width, inner_shard)
    query_own, key_own, value_own, position_own = finished[:4]
    v = finished[4:14]
    inner_z = after(inner_z, query_own)
    inner_own = sum(t.astype(F32) for t in [pick(inner_sum, z, 1)] + inner_z)
    inner_own = jnp.concatenate(list(inner_own), axis=1)
    d_x_own = jnp.sum(pick(d_x, s, 1).astype(F32), axis=0)
    input_terms = in_order(s, d_x_own, after(d_x_z, query_own).astype(F32), 0)
    input_grad = (first_grad + input_terms).astype(BF)
    sums_all = jnp.sum(d_out[:, span : span + 2].astype(F32), axis=(0, 1))
    sums_all = sums_all[: 3 * seqs].reshape(seqs, 3)
    mean_squares = sums_all / (lengths.astype(F32)[:, None] * width)
    return (
        result,
        input_grad,
        query_own,
        key_own,
        value_own,
        v[3],
        position_own,
        v[0],
        v[1],
        v[2],
        finished[14],
        output_own,
        v[4],
        v[5],
        v[6],
        inner_own,
        finished[15],
        outer_own,
        v[7],
        v[8],
        v[9],
        mean_squares,
    )


def solution(mesh):
    in_specs = (
        P(DP, CTX, None),
        P(DP, CTX, None),
        P(DP),
        P(DP, CTX),
        P(ALL, None),
        P(ALL, None),
        P(ALL, None),
        P(ALL),
        P(ALL, None),
        P(ALL),
        P(ALL),
        P(ALL),
        P(None, ALL),
        P(ALL, None),
        P(ALL),
        P(ALL),
        P(ALL),
        P(ALL, None),
        P(ALL),
        P(ALL, None),
        P(ALL),
        P(ALL),
        P(ALL),
    )
    out_specs = (
        P(DP, CTX, None),
        P(DP, CTX, None),
        P(ALL, None),
        P(ALL, None),
        P(ALL, None),
        P(ALL),
        P(ALL, None),
        P(ALL),
        P(ALL),
        P(ALL),
        P(None, ALL),
        P(ALL, None),
        P(ALL),
        P(ALL),
        P(ALL),
        P(ALL, None),
        P(ALL),
        P(ALL, None),
        P(ALL),
        P(ALL),
        P(ALL),
        P(DP, None),
    )
    body = head_layout if takes_head_layout(mesh) else per_device
    return jax.shard_map(
        body, mesh=mesh, in_specs=in_specs, out_specs=out_specs, check_vma=False
    )
```

```python
import functools

import jax
import jax.numpy as jnp
from jax import lax
from jax.experimental import pallas as pl
from jax.experimental.pallas import tpu as pltpu
from jax.sharding import PartitionSpec as P

DP = "dp"
CTX = "ctx"
ALL = (DP, CTX)
H = 12
DH = 64
KEY_BLOCK = 512
MICRO = 2
SEQ_MB = 1


epsilon = 1e-06
masked_score = -1e30
maximal_precision = lax.Precision.HIGHEST


def layer_norm(hidden, gain_values, shift_values):
    center = hidden - jnp.mean(hidden, axis=-1, keepdims=True)
    variance = jnp.mean(center * center, axis=-1, keepdims=True)
    return center * lax.rsqrt(variance + epsilon) * gain_values + shift_values


def gelu_tanh(inner):
    return jax.nn.gelu(inner, approximate=True)


def position_table(anchor, number, columns):
    offsets = (anchor + jnp.arange(number, dtype=jnp.int32)).astype(jnp.float32)
    exponent = 2.0 * jnp.arange(columns // 2, dtype=jnp.float32) / columns
    angles = offsets[:, None] * (10000.0 ** (-exponent))[None, :]
    return jnp.concatenate([jnp.sin(angles), jnp.cos(angles)], axis=1)


def skew_rows(unscaled_scores, keys_count):
    leading = unscaled_scores.shape[:-2]
    rows_count = unscaled_scores.shape[-2]
    span_cols = unscaled_scores.shape[-1]
    flattened = unscaled_scores.reshape(leading + (rows_count * span_cols,))
    flattened = jnp.pad(flattened, [(0, 0)] * len(leading) + [(0, rows_count)])
    return flattened.reshape(leading + (rows_count, span_cols + 1))[..., :keys_count][..., ::-1]


def unskew_rows(grads_block, span_cols):
    leading = grads_block.shape[:-2]
    rows_count = grads_block.shape[-2]
    keys_count = grads_block.shape[-1]
    padded = jnp.pad(
        grads_block[..., ::-1], [(0, 0)] * (len(leading) + 1) + [(0, span_cols + 1 - keys_count)]
    )
    flattened = padded.reshape(leading + (rows_count * (span_cols + 1),))
    return flattened[..., : rows_count * span_cols].reshape(leading + (rows_count, span_cols))


def block_scores(
    query_content,
    query_relative_term,
    type_terms,
    query_kinds,
    key_rows,
    key_kinds,
    key_valid,
    relative_rows,
):
    content = jnp.einsum(
        "bqhd,bkhd->bhqk", query_content, key_rows, preferred_element_type=jnp.float32
    )
    unscaled_scores = jnp.einsum(
        "uply,xly->ulpx", query_relative_term, relative_rows, preferred_element_type=jnp.float32
    )
    same_kind = query_kinds[:, :, None] == key_kinds[:, None, :]
    type_same = jnp.transpose(type_terms[..., 1], (0, 2, 1))[..., None]
    type_other = jnp.transpose(type_terms[..., 0], (0, 2, 1))[..., None]
    summed = (
        content
        + skew_rows(unscaled_scores, key_rows.shape[1])
        + jnp.where(same_kind[:, None], type_same, type_other)
    )
    return (jnp.where(key_valid[:, None, None, :], summed, masked_score), same_kind)


def block_grads(
    query_content,
    query_relative_term,
    type_terms,
    query_kinds,
    log_total,
    row_delta,
    grad_rows,
    key_rows,
    value_rows,
    key_kinds,
    key_valid,
    relative_rows,
):
    scores, same_kind = block_scores(
        query_content,
        query_relative_term,
        type_terms,
        query_kinds,
        key_rows,
        key_kinds,
        key_valid,
        relative_rows,
    )
    probability = jnp.exp(scores - log_total[..., None])
    value_grad = jnp.einsum(
        "bhqk,bqhd->bkhd",
        probability.astype(jnp.bfloat16),
        grad_rows,
        preferred_element_type=jnp.float32,
    )
    prob_grad = jnp.einsum(
        "bqhd,bkhd->bhqk", grad_rows, value_rows, preferred_element_type=jnp.float32
    )
    score_grad = (probability * (prob_grad - row_delta[..., None])).astype(jnp.bfloat16)
    content_grad = jnp.einsum(
        "bhqk,bkhd->bqhd", score_grad, key_rows, preferred_element_type=jnp.float32
    )
    key_grad = jnp.einsum(
        "bhqk,bqhd->bkhd", score_grad, query_content, preferred_element_type=jnp.float32
    )
    unscaled_gradient = unskew_rows(score_grad, relative_rows.shape[0])
    position_grad = jnp.einsum(
        "aioy,yin->aoin", unscaled_gradient, relative_rows, preferred_element_type=jnp.float32
    )
    rel_grad = jnp.einsum(
        "gcrj,grcl->jcl", unscaled_gradient, query_relative_term, preferred_element_type=jnp.float32
    )
    wide_grad = score_grad.astype(jnp.float32)
    same_sum = jnp.sum(jnp.where(same_kind[:, None], wide_grad, 0.0), axis=-1)
    other_sum = jnp.sum(jnp.where(same_kind[:, None], 0.0, wide_grad), axis=-1)
    type_grad = jnp.transpose(jnp.stack([other_sum, same_sum], axis=-1), (0, 2, 1, 3))
    return (content_grad, position_grad, type_grad, key_grad, value_grad, rel_grad)


def per_device(
    inputs,
    out_grad,
    lengths,
    token_types,
    query_weight,
    key_weight,
    value_weight,
    value_bias,
    position_weight,
    content_bias,
    position_bias,
    type_bias,
    type_embed,
    output_weight,
    output_bias,
    first_gain,
    first_shift,
    inner_weight,
    inner_bias,
    outer_weight,
    outer_bias,
    second_gain,
    second_shift,
):
    stretch = inputs.shape[1]
    width = inputs.shape[2]
    seq_len = stretch * lax.axis_size(CTX)
    stretch_start = lax.axis_index(CTX) * stretch
    window = seq_len + stretch - 1
    scale_query = DH ** (-0.5)
    own_positions = stretch_start + jnp.arange(stretch, dtype=jnp.int32)
    table_forward = position_table(stretch_start - seq_len + 1, window, width).astype(jnp.bfloat16)
    outputs_list = []
    input_grads = []
    stat_rows = []
    grads_total = None
    rel_total = jnp.zeros((window, width), jnp.float32)
    for micro_index in range(MICRO):
        first_seq = micro_index * SEQ_MB
        sequence_input = inputs[first_seq : first_seq + SEQ_MB]
        seq_grad = out_grad[first_seq : first_seq + SEQ_MB]
        seq_kinds = token_types[first_seq : first_seq + SEQ_MB].astype(jnp.bfloat16)
        length_col = lengths[first_seq : first_seq + SEQ_MB][:, None]
        seq_count = sequence_input.shape[0]
        heads_shape = (seq_count, stretch, H, DH)
        full_shape = (seq_count, seq_len, H, DH)
        row_valid = (own_positions[None, :] < length_col).astype(jnp.float32)[..., None]
        gathered = (
            lax.all_gather(query_weight, ALL, axis=0, tiled=True),
            lax.all_gather(key_weight, ALL, axis=0, tiled=True),
            lax.all_gather(value_weight, ALL, axis=0, tiled=True),
            lax.all_gather(value_bias, ALL, axis=0, tiled=True),
            lax.all_gather(position_weight, ALL, axis=0, tiled=True),
            lax.all_gather(content_bias, ALL, axis=0, tiled=True),
            lax.all_gather(position_bias, ALL, axis=0, tiled=True),
            lax.all_gather(type_bias, ALL, axis=0, tiled=True),
            lax.all_gather(type_embed, ALL, axis=1, tiled=True),
            lax.all_gather(output_weight, ALL, axis=0, tiled=True),
            lax.all_gather(output_bias, ALL, axis=0, tiled=True),
            lax.all_gather(first_gain, ALL, axis=0, tiled=True),
            lax.all_gather(first_shift, ALL, axis=0, tiled=True),
            lax.all_gather(inner_weight, ALL, axis=0, tiled=True),
            lax.all_gather(inner_bias, ALL, axis=0, tiled=True),
            lax.all_gather(outer_weight, ALL, axis=0, tiled=True),
            lax.all_gather(outer_bias, ALL, axis=0, tiled=True),
            lax.all_gather(second_gain, ALL, axis=0, tiled=True),
            lax.all_gather(second_shift, ALL, axis=0, tiled=True),
        )
        (
            query_matrix,
            key_matrix,
            value_matrix,
            value_add,
            position_mat,
            content_add,
            position_add,
            type_add,
            type_table,
            output_matrix,
            output_add,
            gain_one,
            shift_one,
            inner_matrix,
            inner_add,
            outer_matrix,
            outer_add,
            gain_two,
            shift_two,
        ) = gathered
        scaled = (
            jnp.dot(sequence_input, query_matrix, preferred_element_type=jnp.float32) * scale_query
        )
        query_content = (
            (scaled + content_add.astype(jnp.float32)).astype(jnp.bfloat16).reshape(heads_shape)
        )
        query_relative_term = (
            (scaled + position_add.astype(jnp.float32)).astype(jnp.bfloat16).reshape(heads_shape)
        )
        with_type = (scaled + type_add.astype(jnp.float32)).reshape(heads_shape)
        type_heads = type_table.astype(jnp.float32).reshape(2, H, DH)
        type_terms = jnp.einsum(
            "bqhd,shd->bqhs", with_type, type_heads, precision=maximal_precision
        )
        key_rows = jnp.dot(sequence_input, key_matrix, preferred_element_type=jnp.float32).astype(
            jnp.bfloat16
        )
        value_rows = (
            jnp.dot(sequence_input, value_matrix, preferred_element_type=jnp.float32)
            + value_add.astype(jnp.float32)
        ).astype(jnp.bfloat16)
        rel_forward = (
            jnp.dot(table_forward, position_mat, preferred_element_type=jnp.float32)
            .astype(jnp.bfloat16)
            .reshape(window, H, DH)
        )
        start_state = (
            jnp.full((seq_count, H, stretch), masked_score, jnp.float32),
            jnp.zeros((seq_count, H, stretch), jnp.float32),
            jnp.zeros(heads_shape, jnp.float32),
        )
        piece_keys = lax.all_gather(key_rows, CTX, axis=1, tiled=True)
        piece_values = lax.all_gather(value_rows, CTX, axis=1, tiled=True)
        piece_kinds = lax.all_gather(seq_kinds, CTX, axis=1, tiled=True)
        number = piece_keys.shape[1]
        block_rows = KEY_BLOCK

        def one_block(running, offset):
            run_max, run_total, run_acc = running
            part_keys = lax.dynamic_slice_in_dim(piece_keys, offset, block_rows, 1).reshape(
                seq_count, block_rows, H, DH
            )
            part_values = lax.dynamic_slice_in_dim(piece_values, offset, block_rows, 1).reshape(
                seq_count, block_rows, H, DH
            )
            part_kinds = lax.dynamic_slice_in_dim(piece_kinds, offset, block_rows, 1)
            relative_rows = lax.dynamic_slice_in_dim(
                rel_forward, seq_len - offset - block_rows, stretch + block_rows - 1, 0
            )
            key_valid = (offset + jnp.arange(block_rows, dtype=jnp.int32))[None, :] < length_col
            scores, same_kind = block_scores(
                query_content,
                query_relative_term,
                type_terms,
                seq_kinds,
                part_keys,
                part_kinds,
                key_valid,
                relative_rows,
            )
            new_max = jnp.maximum(run_max, jnp.max(scores, axis=-1))
            factor = jnp.exp(run_max - new_max)
            weights_block = jnp.exp(scores - new_max[..., None])
            run_total = run_total * factor + jnp.sum(weights_block, axis=-1)
            mixed_rows = jnp.einsum(
                "bhqk,bkhd->bqhd",
                weights_block.astype(jnp.bfloat16),
                part_values,
                preferred_element_type=jnp.float32,
            )
            run_acc = run_acc * jnp.transpose(factor, (0, 2, 1))[..., None] + mixed_rows
            return ((new_max, run_total, run_acc), None)

        offsets = jnp.arange(number // block_rows, dtype=jnp.int32) * block_rows
        result_state, unused = lax.scan(one_block, start_state, offsets)
        run_max, run_total, run_acc = result_state
        log_total = run_max + jnp.log(run_total)
        attended = run_acc / jnp.transpose(run_total, (0, 2, 1))[..., None]
        attended_reduced = attended.astype(jnp.bfloat16).reshape(seq_count, stretch, width)
        attn_out = jnp.dot(
            attended_reduced, output_matrix, preferred_element_type=jnp.float32
        ) + output_add.astype(jnp.float32)
        first_sum = sequence_input.astype(jnp.float32) + attn_out
        normed = layer_norm(first_sum, gain_one.astype(jnp.float32), shift_one.astype(jnp.float32))
        normed_reduced = normed.astype(jnp.bfloat16)
        inner = jnp.dot(
            normed_reduced, inner_matrix, preferred_element_type=jnp.float32
        ) + inner_add.astype(jnp.float32)
        activated_reduced = gelu_tanh(inner).astype(jnp.bfloat16)
        outer = jnp.dot(
            activated_reduced, outer_matrix, preferred_element_type=jnp.float32
        ) + outer_add.astype(jnp.float32)
        second_sum = normed + outer
        result = layer_norm(second_sum, gain_two.astype(jnp.float32), shift_two.astype(jnp.float32))
        outputs_list.append(result.astype(jnp.bfloat16))
        stat_rows.append(
            jnp.stack(
                [
                    jnp.sum(first_sum * first_sum * row_valid, axis=(1, 2)),
                    jnp.sum(attn_out * attn_out * row_valid, axis=(1, 2)),
                    jnp.sum(outer * outer * row_valid, axis=(1, 2)),
                ],
                axis=1,
            )
        )
        back_set = (
            lax.all_gather(query_weight, ALL, axis=0, tiled=True),
            lax.all_gather(key_weight, ALL, axis=0, tiled=True),
            lax.all_gather(value_weight, ALL, axis=0, tiled=True),
            lax.all_gather(value_bias, ALL, axis=0, tiled=True),
            lax.all_gather(position_weight, ALL, axis=0, tiled=True),
            lax.all_gather(content_bias, ALL, axis=0, tiled=True),
            lax.all_gather(position_bias, ALL, axis=0, tiled=True),
            lax.all_gather(type_bias, ALL, axis=0, tiled=True),
            lax.all_gather(type_embed, ALL, axis=1, tiled=True),
            lax.all_gather(output_weight, ALL, axis=0, tiled=True),
            lax.all_gather(output_bias, ALL, axis=0, tiled=True),
            lax.all_gather(first_gain, ALL, axis=0, tiled=True),
            lax.all_gather(first_shift, ALL, axis=0, tiled=True),
            lax.all_gather(inner_weight, ALL, axis=0, tiled=True),
            lax.all_gather(inner_bias, ALL, axis=0, tiled=True),
            lax.all_gather(outer_weight, ALL, axis=0, tiled=True),
            lax.all_gather(outer_bias, ALL, axis=0, tiled=True),
            lax.all_gather(second_gain, ALL, axis=0, tiled=True),
            lax.all_gather(second_shift, ALL, axis=0, tiled=True),
        )
        (
            query_matrix,
            key_matrix,
            value_matrix,
            value_add,
            position_mat,
            content_add,
            position_add,
            type_add,
            type_table,
            output_matrix,
            output_add,
            gain_one,
            shift_one,
            inner_matrix,
            inner_add,
            outer_matrix,
            outer_add,
            gain_two,
            shift_two,
        ) = back_set
        type_heads = type_table.astype(jnp.float32).reshape(2, H, DH)
        cotangent = seq_grad.astype(jnp.float32) * row_valid
        unused_two, second_back = jax.vjp(
            layer_norm, second_sum, gain_two.astype(jnp.float32), shift_two.astype(jnp.float32)
        )
        second_grad, gain_two_grad, shift_two_grad = second_back(cotangent)
        outer_reduced = second_grad.astype(jnp.bfloat16)
        outer_add_grad = jnp.sum(outer_reduced.astype(jnp.float32), axis=(0, 1))
        outer_mat_grad = jnp.einsum(
            "hpi,hpt->it", activated_reduced, outer_reduced, preferred_element_type=jnp.float32
        )
        activated_grad = jnp.einsum(
            "unk,rk->unr", outer_reduced, outer_matrix, preferred_element_type=jnp.float32
        )
        unused_three, gelu_back = jax.vjp(gelu_tanh, inner)
        inner_reduced = gelu_back(activated_grad)[0].astype(jnp.bfloat16)
        inner_add_grad = jnp.sum(inner_reduced.astype(jnp.float32), axis=(0, 1))
        inner_mat_grad = jnp.einsum(
            "psu,psy->uy", normed_reduced, inner_reduced, preferred_element_type=jnp.float32
        )
        normed_grad = second_grad + jnp.einsum(
            "tma,ra->tmr", inner_reduced, inner_matrix, preferred_element_type=jnp.float32
        )
        unused_four, first_back = jax.vjp(
            layer_norm, first_sum, gain_one.astype(jnp.float32), shift_one.astype(jnp.float32)
        )
        first_grad, gain_one_grad, shift_one_grad = first_back(normed_grad)
        attention_reduced = first_grad.astype(jnp.bfloat16)
        output_add_grad = jnp.sum(attention_reduced.astype(jnp.float32), axis=(0, 1))
        output_mat_grad = jnp.einsum(
            "yim,yig->mg", attended_reduced, attention_reduced, preferred_element_type=jnp.float32
        )
        grad_rows = (
            jnp.einsum(
                "jcy,py->jcp", attention_reduced, output_matrix, preferred_element_type=jnp.float32
            )
            .astype(jnp.bfloat16)
            .reshape(heads_shape)
        )
        row_delta = jnp.einsum(
            "bqhd,bqhd->bhq", grad_rows.astype(jnp.float32), attended, precision=maximal_precision
        )
        all_keys, all_values, all_kinds = (
            lax.all_gather(key_rows, CTX, axis=1, tiled=True),
            lax.all_gather(value_rows, CTX, axis=1, tiled=True),
            lax.all_gather(seq_kinds, CTX, axis=1, tiled=True),
        )

        def key_step(running, key_start):
            content_acc, position_acc, type_acc, key_acc, value_acc, rel_acc = running
            part_keys = lax.dynamic_slice_in_dim(all_keys, key_start, KEY_BLOCK, 1).reshape(
                seq_count, KEY_BLOCK, H, DH
            )
            part_values = lax.dynamic_slice_in_dim(all_values, key_start, KEY_BLOCK, 1).reshape(
                seq_count, KEY_BLOCK, H, DH
            )
            part_kinds = lax.dynamic_slice_in_dim(all_kinds, key_start, KEY_BLOCK, 1)
            rel_start = seq_len - key_start - KEY_BLOCK
            relative_rows = lax.dynamic_slice_in_dim(
                rel_forward, rel_start, stretch + KEY_BLOCK - 1, 0
            )
            key_valid = (key_start + jnp.arange(KEY_BLOCK, dtype=jnp.int32))[None, :] < length_col
            pieces = block_grads(
                query_content,
                query_relative_term,
                type_terms,
                seq_kinds,
                log_total,
                row_delta,
                grad_rows,
                part_keys,
                part_values,
                part_kinds,
                key_valid,
                relative_rows,
            )
            content_part, position_part, type_part, key_part, value_part, rel_part = pieces
            key_acc = lax.dynamic_update_slice_in_dim(key_acc, key_part, key_start, 1)
            value_acc = lax.dynamic_update_slice_in_dim(value_acc, value_part, key_start, 1)
            rel_old = lax.dynamic_slice_in_dim(rel_acc, rel_start, stretch + KEY_BLOCK - 1, 0)
            rel_acc = lax.dynamic_update_slice_in_dim(rel_acc, rel_old + rel_part, rel_start, 0)
            return (
                (
                    content_acc + content_part,
                    position_acc + position_part,
                    type_acc + type_part,
                    key_acc,
                    value_acc,
                    rel_acc,
                ),
                None,
            )

        start_grads = (
            jnp.zeros(heads_shape, jnp.float32),
            jnp.zeros(heads_shape, jnp.float32),
            jnp.zeros((seq_count, stretch, H, 2), jnp.float32),
            jnp.zeros(full_shape, jnp.float32),
            jnp.zeros(full_shape, jnp.float32),
            jnp.zeros((window, H, DH), jnp.float32),
        )
        final_grads, unused_five = lax.scan(
            key_step, start_grads, jnp.arange(seq_len // KEY_BLOCK, dtype=jnp.int32) * KEY_BLOCK
        )
        content_grad, position_grad, type_grad, key_all, value_all, rel_grad = final_grads
        key_grad, value_grad = (
            lax.psum_scatter(
                key_all.astype(jnp.bfloat16), CTX, scatter_dimension=1, tiled=True
            ).astype(jnp.float32),
            lax.psum_scatter(
                value_all.astype(jnp.bfloat16), CTX, scatter_dimension=1, tiled=True
            ).astype(jnp.float32),
        )
        type_part_grad = jnp.einsum(
            "bqhs,shd->bqhd", type_grad, type_heads, precision=maximal_precision
        )
        query_grad = content_grad + position_grad + type_part_grad
        content_add_grad = jnp.sum(content_grad, axis=(0, 1)).reshape(width)
        position_add_grad = jnp.sum(position_grad, axis=(0, 1)).reshape(width)
        type_add_grad = jnp.sum(type_part_grad, axis=(0, 1)).reshape(width)
        rel_total = rel_total + rel_grad.reshape(window, width)
        query_reduced = query_grad.astype(jnp.bfloat16).reshape(seq_count, stretch, width)
        key_reduced = key_grad.astype(jnp.bfloat16).reshape(seq_count, stretch, width)
        value_reduced = value_grad.astype(jnp.bfloat16).reshape(seq_count, stretch, width)
        type_table_grad = jnp.einsum(
            "bqhs,bqhd->shd", type_grad, with_type, precision=maximal_precision
        ).reshape(2, width)
        query_mat_grad = (
            jnp.einsum(
                "orh,org->hg", sequence_input, query_reduced, preferred_element_type=jnp.float32
            )
            * scale_query
        )
        key_mat_grad = jnp.einsum(
            "orh,org->hg", sequence_input, key_reduced, preferred_element_type=jnp.float32
        )
        value_mat_grad = jnp.einsum(
            "orh,org->hg", sequence_input, value_reduced, preferred_element_type=jnp.float32
        )
        value_add_grad = jnp.sum(value_reduced.astype(jnp.float32), axis=(0, 1))
        input_grad = (
            first_grad
            + jnp.einsum(
                "sux,fx->suf", query_reduced, query_matrix, preferred_element_type=jnp.float32
            )
            * scale_query
            + jnp.einsum("sux,fx->suf", key_reduced, key_matrix, preferred_element_type=jnp.float32)
            + jnp.einsum(
                "sux,fx->suf", value_reduced, value_matrix, preferred_element_type=jnp.float32
            )
        )
        input_grads.append(input_grad.astype(jnp.bfloat16))
        micro_grads = (
            query_mat_grad,
            key_mat_grad,
            value_mat_grad,
            value_add_grad,
            content_add_grad,
            position_add_grad,
            type_add_grad,
            type_table_grad,
            output_mat_grad,
            output_add_grad,
            gain_one_grad,
            shift_one_grad,
            inner_mat_grad,
            inner_add_grad,
            outer_mat_grad,
            outer_add_grad,
            gain_two_grad,
            shift_two_grad,
        )
        if grads_total is None:
            grads_total = micro_grads
        else:
            grads_total = jax.tree.map(jnp.add, grads_total, micro_grads)
    rel_high = rel_total.astype(jnp.bfloat16)
    rel_rest = (rel_total - rel_high.astype(jnp.float32)).astype(jnp.bfloat16)
    contract_rows = (((0,), (0,)), ((), ()))
    position_mat_grad = lax.dot_general(
        table_forward, rel_high, contract_rows, preferred_element_type=jnp.float32
    ) + lax.dot_general(table_forward, rel_rest, contract_rows, preferred_element_type=jnp.float32)
    (
        query_total,
        key_total,
        value_total,
        value_add_total,
        content_total,
        position_total,
        type_total,
        table_total,
        output_total,
        output_add_total,
        gain_one_total,
        shift_one_total,
        inner_total,
        inner_add_total,
        outer_total,
        outer_add_total,
        gain_two_total,
        shift_two_total,
    ) = grads_total
    reduced = (
        lax.psum_scatter(query_total, ALL, scatter_dimension=0, tiled=True),
        lax.psum_scatter(key_total, ALL, scatter_dimension=0, tiled=True),
        lax.psum_scatter(value_total, ALL, scatter_dimension=0, tiled=True),
        lax.psum_scatter(value_add_total, ALL, scatter_dimension=0, tiled=True),
        lax.psum_scatter(position_mat_grad, ALL, scatter_dimension=0, tiled=True),
        lax.psum_scatter(content_total, ALL, scatter_dimension=0, tiled=True),
        lax.psum_scatter(position_total, ALL, scatter_dimension=0, tiled=True),
        lax.psum_scatter(type_total, ALL, scatter_dimension=0, tiled=True),
        lax.psum_scatter(table_total, ALL, scatter_dimension=1, tiled=True),
        lax.psum_scatter(output_total, ALL, scatter_dimension=0, tiled=True),
        lax.psum_scatter(output_add_total, ALL, scatter_dimension=0, tiled=True),
        lax.psum_scatter(gain_one_total, ALL, scatter_dimension=0, tiled=True),
        lax.psum_scatter(shift_one_total, ALL, scatter_dimension=0, tiled=True),
        lax.psum_scatter(inner_total, ALL, scatter_dimension=0, tiled=True),
        lax.psum_scatter(inner_add_total, ALL, scatter_dimension=0, tiled=True),
        lax.psum_scatter(outer_total, ALL, scatter_dimension=0, tiled=True),
        lax.psum_scatter(outer_add_total, ALL, scatter_dimension=0, tiled=True),
        lax.psum_scatter(gain_two_total, ALL, scatter_dimension=0, tiled=True),
        lax.psum_scatter(shift_two_total, ALL, scatter_dimension=0, tiled=True),
    )
    sums_all = lax.psum(jnp.concatenate(stat_rows, axis=0), CTX)
    mean_squares = sums_all / (lengths.astype(jnp.float32)[:, None] * width)
    return (
        (jnp.concatenate(outputs_list, axis=0), jnp.concatenate(input_grads, axis=0))
        + tuple(reduced)
        + (mean_squares,)
    )


LANES = 128
BF = jnp.bfloat16
F32 = jnp.float32
ROWS_CC = (((1,), (1,)), ((), ()))
COLS_CC = (((0,), (0,)), ((), ()))
ROWCOL = (((1,), (0,)), ((), ()))


def mm(a, b, dims):
    return lax.dot_general(a, b, dims, preferred_element_type=F32)


def split3(v):
    hi = v.astype(BF).astype(F32)
    mid = (v - hi).astype(BF).astype(F32)
    lo = (v - hi - mid).astype(BF).astype(F32)
    return hi, mid, lo


def attention_forward_kernel(tile, x_ref, w_ref, vec_ref, kext_ref, trig_ref,
                             att_ref, qb_ref, kb_ref, v1_ref, qp_ref, save_ref, scl_ref, wh_ref, prob_ref,
                             kt_ref, qt_ref):
    step = pl.program_id(1)
    rows = x_ref.shape[0]
    width = x_ref.shape[1]
    half = width // 2
    lane = lax.broadcasted_iota(jnp.int32, (tile, LANES), 1)
    low = lane < DH

    @pl.when((pl.program_id(0) == 0) & (step == 0))
    def _():
        kt_ref[:, :width] = trig_ref[...]

    @pl.when(step == 0)
    def _():
        vec = vec_ref[0]
        w = w_ref[...].astype(F32).reshape(width, 2 * LANES).astype(BF)
        wh_ref[0] = w
        w_lane = lax.broadcasted_iota(jnp.int32, (width, LANES), 1)
        w_pos = jnp.where(w_lane < DH, pltpu.roll(w[:, LANES:].astype(F32), DH, 1), 0.0).astype(BF)

        def body(i, carry):
            at = slice(i * 256, (i + 1) * 256)
            lane = lax.broadcasted_iota(jnp.int32, (256, LANES), 1)
            low = lane < DH
            proj = mm(x_ref[at, :], w, ROWCOL)
            kext = kext_ref[at, :].astype(F32)
            kind = kext[:, DH + 3:DH + 4]
            scaled = jnp.where(low, proj[:, :LANES] * DH ** -0.5, 0.0)
            scl_ref[0, at, :] = scaled
            kb = jnp.where(low, pltpu.roll(proj[:, :LANES], DH, 1), kext).astype(BF)
            kb_ref[0, at, :] = kb
            kt_ref[at, width:] = kb
            one_v = (lane >= DH) & (lane < DH + 3)
            v1_ref[0, at, :] = jnp.where(low, proj[:, LANES:] + vec[3:4, :], jnp.where(one_v, 1.0, 0.0)).astype(BF)
            with_type = scaled + vec[2:3, :]
            term0 = jnp.sum(with_type * vec[4:5, :], axis=1, keepdims=True)
            term1 = jnp.sum(with_type * vec[5:6, :], axis=1, keepdims=True)
            base = jnp.where(kind > 0.5, term0, term1)
            slope = jnp.where(kind > 0.5, term1 - term0, term0 - term1)
            b_hi, b_mid, b_lo = split3(base)
            s_hi, s_mid, s_lo = split3(slope)
            ext = jnp.where(lane == DH, b_hi, 0.0)
            ext = jnp.where(lane == DH + 1, b_mid, ext)
            ext = jnp.where(lane == DH + 2, b_lo, ext)
            ext = jnp.where(lane == DH + 3, s_hi, ext)
            ext = jnp.where(lane == DH + 4, s_mid, ext)
            ext = jnp.where(lane == DH + 5, 1.0, ext)
            q_block = jnp.where(low, scaled + vec[0:1, :], ext).astype(BF)
            qb_ref[0, at, :] = q_block
            qt_ref[at, width:] = q_block
            qp = jnp.where(low, scaled + vec[1:2, :], 0.0).astype(BF)
            qp_ref[0, at, :] = qp
            grow = mm(qp, w_pos, ROWS_CC)
            q_sin = grow[:, :half]
            q_cos = grow[:, half:]
            c = trig_ref[at, :half].astype(F32)
            s = trig_ref[at, half:].astype(F32)
            qt_ref[at, :half] = (q_sin * s + q_cos * c).astype(BF)
            qt_ref[at, half:width] = (q_cos * s - q_sin * c).astype(BF)
            return carry

        for i in range(rows // 256):
            body(i, 0)

    att_parts = att_ref.shape[0]
    sub = 256
    count = tile // sub
    small_lane = lax.broadcasted_iota(jnp.int32, (sub, LANES), 1) < DH

    def scores_of(i):
        at = pl.ds(pl.multiple_of(step * tile + i * sub, sub), sub)
        return mm(qt_ref[at, :], kt_ref[...], ROWS_CC)

    later = scores_of(0)
    for i in range(count):
        scores = later
        if i + 1 < count:
            later = scores_of(i + 1)
        top = jnp.max(scores, axis=1, keepdims=True)
        prob = jnp.exp(scores - top).astype(BF)
        prob_ref[0, i * sub:(i + 1) * sub, :] = prob
        mixed = mm(prob, v1_ref[0], ROWCOL)
        total = mixed[:, DH:DH + 1]
        att = mixed / total
        save_ref[0, i * sub:(i + 1) * sub, :] = jnp.where(small_lane, att, 1.0 / total)
        att_t = jnp.transpose(att)[:DH, :].astype(BF)
        for n in range(sub // LANES):
            b = i * (sub // LANES) + n
            att_ref[b % att_parts, b // att_parts] = att_t[:, n * LANES:(n + 1) * LANES]


def attention_backward_kernel(tile, core_ref, do_ref, x_ref, w_ref, vec_ref, kext_ref, trig_ref,
                              qb_ref, kb_ref, v1_ref, qp_ref, save_ref, scl_ref, prob_ref,
                              dx_ref, dw_ref, small_ref,
                              kt_ref, dk_acc, dv_acc, d_ref, dwp_ref, dx_acc):
    step = pl.program_id(1)
    width = trig_ref.shape[1]
    half = width // 2
    lane = lax.broadcasted_iota(jnp.int32, (tile, LANES), 1)
    low = lane < DH

    @pl.when((pl.program_id(0) == 0) & (step == 0))
    def _():
        kt_ref[:, :width] = trig_ref[...]

    @pl.when(step == 0)
    def _():
        kt_ref[:, width:] = kb_ref[0]
        dk_acc[...] = jnp.zeros_like(dk_acc)
        dv_acc[...] = jnp.zeros_like(dv_acc)
        dwp_ref[...] = jnp.zeros_like(dwp_ref)
        small_ref[...] = jnp.zeros_like(small_ref)

    at = pl.ds(pl.multiple_of(step * tile, tile), tile)
    w = w_ref[0]
    w_lane = lax.broadcasted_iota(jnp.int32, (width, LANES), 1)
    w_pos = jnp.where(w_lane < DH, pltpu.roll(w[:, LANES:].astype(F32), DH, 1), 0.0).astype(BF)
    save = save_ref[0]
    inverse = save[:, DH:DH + 1]
    parts = do_ref.shape[0]
    do_t = jnp.concatenate([do_ref[i % parts, i // parts] for i in range(tile // LANES)], axis=1).astype(F32)
    d_out = jnp.transpose(jnp.concatenate([do_t, jnp.zeros_like(do_t)], axis=0))
    d_out = d_out * inverse
    delta = jnp.sum(d_out * save, axis=1, keepdims=True)
    d_hi, d_mid, d_lo = split3(-delta)
    q_block = qb_ref[0]
    ext = jnp.where(lane == DH, d_hi, d_out)
    ext = jnp.where(lane == DH + 1, d_mid, ext)
    ext = jnp.where(lane == DH + 2, d_lo, ext)
    d_ext = ext.astype(BF)
    prob = prob_ref[0]
    dv_acc[...] += mm(d_ext, prob, COLS_CC)
    d_score = (prob.astype(F32) * mm(d_ext, v1_ref[0], ROWS_CC)).astype(BF)
    dk_acc[...] += mm(q_block, d_score, COLS_CC)
    dq = mm(d_score, kt_ref[...], ROWCOL)
    c = trig_ref[at, :half].astype(F32)
    s = trig_ref[at, half:].astype(F32)
    du_c = dq[:, :half]
    du_s = dq[:, half:width]
    back = jnp.concatenate([s * du_c - c * du_s, c * du_c + s * du_s], axis=1).astype(BF)
    d_block = dq[:, width:]
    d_pos = mm(back, w_pos, ROWCOL)
    dwp_ref[...] += mm(qp_ref[0], back, COLS_CC)[:DH, :]
    vec = vec_ref[0]
    kind = kext_ref[...][:, DH + 3:DH + 4].astype(F32)
    every = d_block[:, DH:DH + 1]
    ones = d_block[:, DH + 3:DH + 4]
    g_same = jnp.where(kind > 0.5, ones, every - ones)
    g_other = jnp.where(kind > 0.5, every - ones, ones)
    type_part = g_other * vec[4:5, :] + g_same * vec[5:6, :]
    d_content = jnp.where(low, d_block, 0.0)
    with_type = jnp.where(low, scl_ref[0] + vec[2:3, :], 0.0)
    d_scaled = d_content + d_pos + type_part
    d_ref[:DH, at] = (jnp.transpose(d_scaled)[:DH, :] * DH ** -0.5).astype(BF)
    sums = [jnp.sum(v, axis=0, keepdims=True) for v in
            (d_content, d_pos, type_part, g_other * with_type, g_same * with_type)]
    small_ref[0] += jnp.concatenate(sums + [jnp.zeros((3, LANES), F32)], axis=0)

    @pl.when(step == pl.num_programs(1) - 1)
    def _():
        d_ref[DH:2 * DH] = dk_acc[:DH, :].astype(BF)
        dv_low = dv_acc[:DH, :].astype(BF)
        d_ref[2 * DH:] = dv_low
        dv_sum = jnp.sum(dv_low.astype(F32), axis=1, keepdims=True)
        dv_sum = jnp.transpose(jnp.broadcast_to(jnp.concatenate([dv_sum, dv_sum], axis=0), (LANES, LANES)))
        small_ref[0, 5:6, :] = dv_sum[:1, :]
        d_wt = mm(d_ref[...], x_ref[...], ROWCOL)
        d_w = jnp.transpose(jnp.concatenate([d_wt, dwp_ref[...]], axis=0))
        shard = dw_ref.shape[3]
        members = dw_ref.shape[2]
        for i in range(4 * members):
            dw_ref[(i // members % 2) ^ core_ref[0], i // (2 * members), i % members] = d_w[i * shard:(i + 1) * shard, :].astype(BF)
        d_x = lax.dot_general(d_ref[...], w_ref[0][:, :3 * DH], (((0,), (1,)), ((), ())), preferred_element_type=F32)

        @pl.when(pl.program_id(0) == 0)
        def _():
            dx_acc[...] = d_x

        @pl.when(pl.program_id(0) > 0)
        def _():
            dx_acc[...] += d_x

        @pl.when(pl.program_id(0) == pl.num_programs(0) - 1)
        def _():
            dx_ref[...] = dx_acc[...].astype(BF)


def attention_forward(x, w_block, first, count, heads, vec, kext, trig, previous=(), tile=1024):
    rows, width = x.shape
    owners = w_block.shape[0]
    shard = width // owners
    full = width + LANES
    per_head = lambda shape: pl.BlockSpec((1,) + shape, lambda h, t: (first + h, 0, 0))
    fixed = lambda shape: pl.BlockSpec(shape, lambda h, t: (0, 0))
    flops = count * rows * 2 * (width * 256 + rows * full + rows * LANES)
    S = jax.ShapeDtypeStruct
    kernel = functools.partial(attention_forward_kernel, tile)
    skip = len(previous)
    return pl.pallas_call(
        lambda *refs: kernel(*refs[:5], *refs[5 + skip:]),
        grid=(count, rows // tile),
        in_specs=[fixed((rows, width)), pl.BlockSpec((owners, shard, 2 * LANES), lambda h, t: (0, first + h, 0)),
                  per_head((8, LANES)), fixed((rows, LANES)), fixed((rows, width))]
        + [pl.BlockSpec(memory_space=pl.ANY)] * skip,
        out_specs=[pl.BlockSpec((2, tile // (2 * LANES), DH, LANES), lambda h, t: (0, t, first + h, 0)),
                   per_head((rows, LANES)), per_head((rows, LANES)), per_head((rows, LANES)),
                   per_head((rows, LANES)),
                   pl.BlockSpec((1, tile, LANES), lambda h, t: (first + h, t, 0)),
                   per_head((rows, LANES)), per_head((width, 2 * LANES)),
                   pl.BlockSpec((1, tile, rows), lambda h, t: (first + h, t, 0))],
        out_shape=[S((2, rows // (2 * LANES), heads * DH, LANES), BF), S((heads, rows, LANES), BF),
                   S((heads, rows, LANES), BF), S((heads, rows, LANES), BF), S((heads, rows, LANES), BF),
                   S((heads, rows, LANES), F32), S((heads, rows, LANES), F32), S((heads, width, 2 * LANES), BF),
                   S((heads, rows, rows), BF)],
        input_output_aliases={5 + i: i for i in range(skip)},
        scratch_shapes=[pltpu.VMEM((rows, full), BF), pltpu.VMEM((rows, full), BF)],
        compiler_params=pltpu.CompilerParams(dimension_semantics=("arbitrary", "arbitrary"),
                                             vmem_limit_bytes=63 * 2 ** 20),
        cost_estimate=pl.CostEstimate(flops=flops, bytes_accessed=rows * width * 16, transcendentals=count * rows * rows),
        name="attention_forward",
    )(x, w_block, vec, kext, trig, *previous)


def attention_backward(core, d_out, x, w, vec, kext, trig, qb, kb, v1, qp, save, scl, prob, owners, block_rows, tile=1024):
    heads, rows, _ = qb.shape
    width = x.shape[1]
    full = width + LANES
    shard = width // owners
    per_head = lambda shape: pl.BlockSpec((1,) + shape, lambda h, t: (h, 0, 0))
    per_tile = lambda cols: pl.BlockSpec((1, tile, cols), lambda h, t: (h, t, 0))
    fixed = lambda shape: pl.BlockSpec(shape, lambda h, t: (0, 0))
    flops = heads * rows * 2 * (2 * rows * full + 3 * rows * LANES)
    return pl.pallas_call(
        functools.partial(attention_backward_kernel, tile),
        grid=(heads, rows // tile),
        in_specs=[pl.BlockSpec(memory_space=pltpu.SMEM), pl.BlockSpec((2, tile // (2 * LANES), DH, LANES), lambda h, t: (0, t, h, 0)), fixed((rows, width)),
                  per_head((width, 256)), per_head((8, LANES)),
                  pl.BlockSpec((tile, LANES), lambda h, t: (t, 0)), fixed((rows, width)),
                  per_tile(LANES), per_head((rows, LANES)), per_head((rows, LANES)), per_tile(LANES),
                  per_tile(LANES), per_tile(LANES), per_tile(rows)],
        out_specs=[fixed((rows, width)), pl.BlockSpec((2, 2, owners // 4, shard, 2 * LANES), lambda h, t: (0, 0, 0, h, 0)),
                   per_head((8, LANES))],
        out_shape=[jax.ShapeDtypeStruct((rows, width), BF),
                   jax.ShapeDtypeStruct((2, 2, owners // 4, block_rows, 2 * LANES), BF),
                   jax.ShapeDtypeStruct((heads, 8, LANES), F32)],
        scratch_shapes=[pltpu.VMEM((rows, full), BF),
                        pltpu.VMEM((LANES, rows), F32), pltpu.VMEM((LANES, rows), F32),
                        pltpu.VMEM((3 * DH, rows), BF), pltpu.VMEM((DH, width), F32),
                        pltpu.VMEM((rows, width), F32)],
        compiler_params=pltpu.CompilerParams(dimension_semantics=("arbitrary", "arbitrary"),
                                             vmem_limit_bytes=63 * 2 ** 20),
        cost_estimate=pl.CostEstimate(flops=flops, bytes_accessed=rows * width * 20, transcendentals=heads * rows * rows),
        name="attention_backward",
    )(core.reshape(1), d_out, x, w, vec, kext, trig, qb, kb, v1, qp, save, scl, prob)


def key_extension(kinds, valid):
    rows = kinds.shape[0]
    lane = jnp.arange(LANES)[None, :]
    k = kinds[:, None]
    out = jnp.where((lane >= DH) & (lane < DH + 3) | (lane >= DH + 6) & (lane < DH + 9), 1.0, 0.0)
    out = jnp.where((lane == DH + 3) | (lane == DH + 4), k, out)
    out = jnp.where(lane == DH + 5, jnp.where(valid[:, None] > 0, 0.0, -1e30), out)
    return jnp.broadcast_to(out, (rows, LANES)).astype(BF)


def pack_kernel(heads, groups, *refs):
    mats, smalls, (wide_ref, kinds_ref, inner_ref, outer_ref, output_ref, out_ref, packed_ref, third_ref) = refs[:4], refs[4:16], refs[16:]
    rows, width = mats[0].shape
    for g in range(groups):
        for h in range(heads):
            at = pl.ds((g * heads + h) * DH, DH)
            value = jnp.concatenate([m[:, at] for m in mats], axis=1)
            for c in range(g, out_ref.shape[0], groups):
                out_ref[c, h * rows:(h + 1) * rows, :] = value
    pad = jnp.zeros((1, LANES - rows), F32)
    lines = [jnp.concatenate([v[...].astype(F32), pad], axis=1) for v in smalls]
    none = jnp.zeros((1, LANES), F32)
    inner = jnp.concatenate([wide_ref[...].astype(F32), jnp.zeros((1, LANES - wide_ref.shape[1]), F32)], axis=1)
    left = jnp.concatenate(lines[:8], axis=0)
    kinds = kinds_ref[...].astype(F32)
    right = jnp.concatenate(lines[8:] + [inner, kinds, none], axis=0)
    both = jnp.concatenate([left, right], axis=1).astype(BF)
    for c in range(out_ref.shape[0]):
        out_ref[c, heads * rows:, :] = both
    count = inner_ref.shape[1] // width
    for i in range(count):
        packed_ref[i * rows:(i + 1) * rows, :] = inner_ref[:, i * width:(i + 1) * width]
    packed_ref[count * rows:, :] = outer_ref[...]
    third_ref[...] = output_ref[...]


def pack(mats, smalls, wide, kinds, inner, outer, output, heads, groups, members):
    rows, width = mats[0].shape
    third = output.shape[0]
    total = inner.shape[1] // width * rows + outer.shape[0]
    return pl.pallas_call(
        functools.partial(pack_kernel, heads, groups),
        out_shape=[jax.ShapeDtypeStruct((members, heads * rows + 8, 2 * LANES), BF),
                   jax.ShapeDtypeStruct((total, width), BF), jax.ShapeDtypeStruct((third, width), BF)],
        name="pack_columns",
    )(*mats, *smalls, wide, kinds, inner, outer, output)


def unpack_kernel(heads, groups, shard, g_ref, block_ref, vecs_ref, wide_ref, vec_ref):
    owners = block_ref.shape[0]
    wide = wide_ref.shape[1] // owners
    for o in range(owners):
        t = block_ref[o].astype(F32)
        vecs_ref[:8, o * shard:(o + 1) * shard] = t[:, :shard]
        vecs_ref[8:, o * shard:(o + 1) * shard] = t[:, LANES:LANES + shard]
        wide_ref[:, o * wide:(o + 1) * wide] = t[4:5, LANES:LANES + wide]
    zeros = jnp.zeros((8, LANES - DH), F32)
    for g in range(groups):
        @pl.when(g_ref[0] == g)
        def _():
            for h in range(heads):
                part = vecs_ref[:8, (g * heads + h) * DH:(g * heads + h + 1) * DH]
                vec_ref[h] = jnp.concatenate([part, zeros], axis=1)


def unpack(block, g, heads, groups, shard, wide):
    owners, rows, _ = block.shape
    return pl.pallas_call(
        functools.partial(unpack_kernel, heads, groups, shard),
        grid=(1,),
        in_specs=[pl.BlockSpec(memory_space=pltpu.SMEM),
                  pl.BlockSpec((owners, 8, 2 * LANES), lambda i: (0, rows // 8 - 1, 0))],
        out_specs=[pl.BlockSpec((16, owners * shard), lambda i: (0, 0)), pl.BlockSpec((1, owners * wide), lambda i: (0, 0)),
                   pl.BlockSpec((heads, 8, LANES), lambda i: (0, 0, 0))],
        out_shape=[jax.ShapeDtypeStruct((16, owners * shard), F32), jax.ShapeDtypeStruct((1, owners * wide), F32),
                   jax.ShapeDtypeStruct((heads, 8, LANES), F32)],
        name="unpack_small",
    )(g.reshape(1), block)


def small_kernel(heads, groups, shard, g_ref, heads_ref, rest_ref, wide_ref, unused_ref, out_ref, table_ref):
    members = out_ref.shape[2]
    owners = 4 * members
    wide = wide_ref.shape[1] // owners
    table_ref[:6] = jnp.zeros((6, table_ref.shape[1]), F32)
    for g in range(groups):
        @pl.when(g_ref[0] == g)
        def _():
            for h in range(heads):
                table_ref[:6, (g * heads + h) * DH:(g * heads + h + 1) * DH] = heads_ref[h, :6, :DH]
    table_ref[6:12] = rest_ref[...]
    pad = jnp.zeros((8, LANES - shard), F32)
    for o in range(owners):
        left = table_ref[:8, o * shard:(o + 1) * shard]
        right = jnp.concatenate([table_ref[8:12, o * shard:(o + 1) * shard], jnp.zeros((4, LANES - shard), F32)], axis=1)
        inner = jnp.concatenate([wide_ref[:, o * wide:(o + 1) * wide], jnp.zeros((1, LANES - wide), F32)], axis=1)
        right = jnp.concatenate([right, inner, jnp.zeros((3, LANES), F32)], axis=0)
        out_ref[(o // members % 2) ^ g_ref[1], o // (2 * members), o % members] = jnp.concatenate([left, pad, right], axis=1).astype(BF)


def small_rows(block, g, head_sums, rest, wide_sums, groups, shard):
    members, rows = block.shape[2:4]
    owners = 4 * members
    heads = head_sums.shape[0]
    whole = lambda a: pl.BlockSpec(a.shape, lambda i: (0,) * a.ndim)
    return pl.pallas_call(
        functools.partial(small_kernel, heads, groups, shard),
        grid=(1,),
        in_specs=[pl.BlockSpec(memory_space=pltpu.SMEM), whole(head_sums), whole(rest), whole(wide_sums),
                  pl.BlockSpec(memory_space=pl.ANY)],
        out_specs=pl.BlockSpec((2, 2, members, 8, 2 * LANES), lambda i: (0, 0, 0, rows // 8 - 1, 0)),
        out_shape=jax.ShapeDtypeStruct(block.shape, BF),
        input_output_aliases={4: 0},
        scratch_shapes=[pltpu.VMEM((16, owners * shard), F32)],
        cost_estimate=pl.CostEstimate(flops=2 * 10 ** 10, bytes_accessed=2 ** 20, transcendentals=0),
        name="small_gradients",
    )(g, head_sums, rest, wide_sums, block)


def finish_kernel(heads, block_ref, *refs):
    outs, vectors, pair_ref, wide_ref = refs[:4], refs[4:14], refs[14], refs[15]
    groups = block_ref.shape[0] // 2
    shard = outs[0].shape[0]
    total = sum(block_ref[g, heads * shard:, :].astype(F32) for g in range(2 * groups))
    for n, i in enumerate((0, 1, 2, 5, 6, 7)):
        vectors[n][...] = total[i, :shard]
    for i in range(4):
        vectors[6 + i][...] = total[i, LANES:LANES + shard]
    pair_ref[...] = total[3:5, :shard]
    wide_ref[...] = total[4, LANES:LANES + wide_ref.shape[0]]
    for g in range(groups):
        for h in range(heads):
            part = block_ref[g, h * shard:(h + 1) * shard, :].astype(F32)
            part = part + block_ref[groups + g, h * shard:(h + 1) * shard, :].astype(F32)
            at = (g * heads + h) * DH
            for m in range(4):
                outs[m][:, at:at + DH] = part[:, m * DH:(m + 1) * DH]


def finish(block, heads, shard, width, wide):
    S = jax.ShapeDtypeStruct
    return pl.pallas_call(
        functools.partial(finish_kernel, heads),
        out_shape=[S((shard, width), F32)] * 4 + [S((shard,), F32)] * 10 + [S((2, shard), F32), S((wide,), F32)],
        name="finish_columns",
    )(block)


def row_sum_kernel(bit_ref, keep_ref, first_ref, *refs):
    bit = bit_ref[0]
    total = keep_ref[0, bit].astype(F32) + first_ref[bit].astype(F32)
    for ref in refs[:-1]:
        total = total + ref[...].astype(F32)
    refs[-1][...] = total.astype(BF)


def row_sum(bit, keep, first, *more):
    vmem = pl.BlockSpec(memory_space=pltpu.VMEM)
    return pl.pallas_call(
        row_sum_kernel,
        in_specs=[pl.BlockSpec(memory_space=pltpu.SMEM)] + [vmem] * (2 + len(more)),
        out_specs=vmem,
        out_shape=jax.ShapeDtypeStruct(first.shape[1:], BF),
        cost_estimate=pl.CostEstimate(flops=2 * 10 ** 10, bytes_accessed=2 ** 20, transcendentals=0),
        name="row_sum",
    )(bit.reshape(1), keep, first, *more)


def token_kernel(core_ref, valid_ref, mixed_ref, x_ref, og_ref, vec_ref, wide_ref,
                 inner_one, inner_two, inner_three, inner_four, outer_one, outer_two, outer_three, outer_four, third_one, third_two,
                 result_ref, first_ref, grad_ref, gi_keep, gi_send, go_keep, go_send, gt_keep, gt_send, rest_ref, gw_ref,
                 packed, wi, act, slope, normed_t, acc, gi_ref, go_ref, sems, back_sems):
    core, bit_y, bit_x = core_ref[0], core_ref[1], core_ref[2]
    seqs, width, stretch = mixed_ref.shape
    tokens = seqs * stretch
    count = wi.shape[1] // width
    members = 2 * packed.shape[1]
    block = width // count
    shard = block // members
    wide = packed.shape[3] - (count + 1) * shard
    base = count * shard
    copies = []
    for i, (src, k) in enumerate(((third_one, core), (third_two, 1 - core))):
        for y in range(2):
            copies.append(pltpu.make_async_copy(src.at[:, y], packed.at[2 * y + k, :, :, base + wide:, :], sems.at[26 + 2 * i + y]))
    sources = ((outer_one, core, bit_x), (outer_two, 1 - core, bit_x), (outer_three, core, 1 - bit_x), (outer_four, 1 - core, 1 - bit_x))
    for i, (src, k, x) in enumerate(sources):
        for y in range(2):
            copies.append(pltpu.make_async_copy(src.at[y], packed.at[2 * y + k, :, x, base:base + wide, :], sems.at[4 + 2 * i + y]))
    sources = ((inner_one, core, bit_y), (inner_two, 1 - core, bit_y), (inner_three, core, 1 - bit_y), (inner_four, 1 - core, 1 - bit_y))
    for i, (src, k, y) in enumerate(sources):
        for x in range(2):
            copies.append(pltpu.make_async_copy(src.at[x], packed.at[2 * y + k, :, x, :base, :], sems.at[12 + 2 * i + x]))
    for copy in copies:
        copy.start()
    for copy in copies[:4]:
        copy.wait()
    w_out = packed[:, :, :, base + wide:, :].astype(F32).reshape(width, width).astype(BF)
    def w_outer(j):
        return packed[j, :, :, base:base + wide, :].reshape(width, width)

    vec = vec_ref[...]
    line = lambda i: vec[i:i + 1, :]
    mean = lambda v: jnp.mean(v, axis=1, keepdims=True)
    attn = jnp.concatenate([mm(mixed_ref[b], w_out, COLS_CC) for b in range(seqs)], axis=0) + line(6)
    first = x_ref[...].astype(F32) + attn
    center = first - mean(first)
    r_one = lax.rsqrt(mean(center * center) + epsilon)
    hat_one = center * r_one
    normed = hat_one * line(7) + line(8)
    low = normed.astype(BF)
    normed_t[...] = jnp.transpose(normed).astype(BF)
    acc[...] = jnp.zeros_like(acc)

    for copy in copies[4:]:
        copy.wait()
    for i in range(count):
        wi[:, i * width:(i + 1) * width] = packed[:, :, :, i * shard:(i + 1) * shard, :].astype(F32).reshape(width, width).astype(BF)

    def forward(j, carry):
        at = pl.ds(pl.multiple_of(j * width, width), width)
        u = mm(low, wi[:, at], ROWCOL) + wide_ref[:, at]
        c = 0.7978845608028654
        sq = u * u
        t = jnp.tanh(c * u * (1.0 + 0.044715 * sq))
        half = 0.5 * (1.0 + t)
        a = (u * half).astype(BF)
        act[:, at] = a
        slope[:, at] = half + 0.5 * u * (1.0 - t * t) * (c * (1.0 + 3 * 0.044715 * sq))
        acc[...] += mm(a, w_outer(j), ROWCOL)
        return carry

    lax.fori_loop(0, count, forward, 0)
    outer = acc[...] + line(9)
    second = normed + outer
    center = second - mean(second)
    r_two = lax.rsqrt(mean(center * center) + epsilon)
    hat_two = center * r_two
    result_ref[...] = (hat_two * line(10) + line(11)).astype(BF)
    valid = valid_ref[...]
    cot = og_ref[...].astype(F32) * valid
    d_hat = cot * line(10)
    d_second = r_two * (d_hat - mean(d_hat) - hat_two * mean(d_hat * hat_two))
    d_low = d_second.astype(BF)
    total = lambda v: jnp.sum(v, axis=0, keepdims=True)
    outer_sum = total(d_low.astype(F32))
    two = [total(cot * hat_two), total(cot)]
    acc[...] = d_second

    part = wide // 2

    def inner_back(j):
        return [
            pltpu.make_async_copy(gi_ref.at[which, y, j], (gi_keep, gi_send)[which].at[y, j], back_sems.at[j, 2 * which + y])
            for which in range(2) for y in range(2)]

    def upper(which, y, j):
        low_part = pltpu.make_async_copy(go_ref.at[which, y, :, :part, :], (gt_keep, gt_send)[which].at[y], sems.at[20 + j])
        high_part = pltpu.make_async_copy(
            go_ref.at[which, y, :, part:wide, :], (go_keep, go_send)[which].at[y, :, :part, :], sems.at[30 + j])
        return low_part, high_part

    def lower(which, y):
        target = (go_keep, go_send)[which]
        return pltpu.make_async_copy(go_ref.at[which, y, :, wide:, :], target.at[y, :, part:, :], sems.at[2 * which + y])

    def backward(j, carry):
        at = pl.ds(pl.multiple_of(j * width, width), width)
        d_act = mm(d_low, w_outer(j), ROWS_CC)
        d_in = d_act * slope[:, at]
        d_in_low = d_in.astype(BF)
        gw_ref[:, at] = total(d_in_low.astype(F32))
        acc[...] += mm(d_in_low, wi[:, at], ROWS_CC)
        go = mm(act[:, at], d_low, COLS_CC)
        which = (j % 2) ^ core
        go_ref[which, j // 2, :, :wide, :] = go.astype(BF).reshape(members, wide, width)

        @pl.when(which == 0)
        def _():
            for copy in upper(0, j // 2, j):
                copy.start()

        @pl.when(which == 1)
        def _():
            for copy in upper(1, j // 2, j):
                copy.start()

        for b in range(count):
            gi = mm(normed_t[b * block:(b + 1) * block, :], d_in_low, ROWCOL)
            gi_ref[(b % 2) ^ core, b // 2, j] = gi.reshape(members, shard, width).astype(BF)
        for copy in inner_back(j):
            copy.start()
        return carry

    lax.fori_loop(0, count, backward, 0)
    d_normed = acc[...]
    one = [total(d_normed * hat_one), total(d_normed)]
    d_hat = d_normed * line(7)
    d_first = r_one * (d_hat - mean(d_hat) - hat_one * mean(d_hat * hat_one))
    first_ref[...] = d_first
    a_low = d_first.astype(BF)
    rest_ref[...] = jnp.concatenate([total(a_low.astype(F32))] + one + [outer_sum] + two, axis=0)
    grad = mm(w_out, a_low, ROWS_CC).astype(BF)
    span = grad_ref.shape[1] - 8
    groups = width // span
    lane = lax.broadcasted_iota(jnp.int32, (1, stretch), 1)
    sums = jnp.zeros((1, stretch), F32)
    everything = lambda v: jnp.sum(jnp.sum(v, axis=0, keepdims=True), axis=1, keepdims=True)
    for b in range(seqs):
        at = slice(b * stretch, (b + 1) * stretch)
        for i, v in enumerate((first, attn, outer)):
            sums = jnp.where(lane == 3 * b + i, everything(v[at] * v[at] * valid[at]), sums)
    high = sums.astype(BF).astype(F32)
    riders = jnp.concatenate([high, sums - high, jnp.zeros((6, stretch), F32)], axis=0).astype(BF)
    for b in range(seqs):
        for g in range(groups):
            grad_ref[b * groups + g, :span, :] = grad[g * span:(g + 1) * span, b * stretch:(b + 1) * stretch]
            grad_ref[b * groups + g, span:, :] = riders
    out = mm(mixed_ref[0], a_low[:stretch], ROWCOL)
    for b in range(1, seqs):
        out += mm(mixed_ref[b], a_low[b * stretch:(b + 1) * stretch], ROWCOL)
    for b in range(count):
        for i in range(members):
            at = b * block + i * shard
            go_ref[(b % 2) ^ core, b // 2, i, wide:, :] = out[at:at + shard, :].astype(BF)
    lowers = [lower(which, y) for which in range(2) for y in range(2)]
    for back in lowers:
        back.start()
    for j in range(count):
        for copy in upper(0, 0, j):
            copy.wait()
    for j in range(count):
        for copy in inner_back(j):
            copy.wait()
    for back in lowers:
        back.wait()


def token_block(core, valid, mixed, x, out_grad, vectors, inner_add, inner_parts, outer_parts, third_parts, span):
    seqs, width, stretch = mixed.shape
    tokens = seqs * stretch
    ff = inner_add.shape[1]
    count = ff // width
    members = inner_parts[0].shape[0] * inner_parts[0].shape[1]
    owners = members * count
    rows = ff // owners + width // owners
    half_rows = ff // owners // 2
    base = ff // width * (width // owners)
    groups = width // span
    vmem = pl.BlockSpec(memory_space=pltpu.VMEM)
    hbm = pl.BlockSpec(memory_space=pl.ANY)
    S = jax.ShapeDtypeStruct
    return pl.pallas_call(
        token_kernel,
        in_specs=[pl.BlockSpec(memory_space=pltpu.SMEM)] + [vmem] * 6 + [hbm] * 10,
        out_specs=[vmem] * 3 + [hbm] * 6 + [vmem] * 2,
        out_shape=[S((tokens, width), BF), S((tokens, width), F32), S((seqs * groups, span + 8, stretch), BF),
                   S((2, count, members, width // owners, width), BF), S((2, count, members, width // owners, width), BF),
                   S((2, members, rows - half_rows, width), BF), S((2, members, rows - half_rows, width), BF),
                   S((2, members, half_rows, width), BF), S((2, members, half_rows, width), BF),
                   S((6, width), F32), S((1, ff), F32)],
        scratch_shapes=[pltpu.VMEM((count, members // 2, 2, (count + 1) * (width // owners) + ff // owners, width), BF), pltpu.VMEM((width, ff), BF),
                        pltpu.VMEM((tokens, ff), BF), pltpu.VMEM((tokens, ff), F32),
                        pltpu.VMEM((width, tokens), BF), pltpu.VMEM((tokens, width), F32),
                        pltpu.VMEM((2, 2, count, members, width // owners, width), BF), pltpu.VMEM((2, 2, members, rows, width), BF),
                        pltpu.SemaphoreType.DMA((34,)), pltpu.SemaphoreType.DMA((count, 4))],
        compiler_params=pltpu.CompilerParams(vmem_limit_bytes=63 * 2 ** 20),
        cost_estimate=pl.CostEstimate(flops=tokens * 2 * width * (6 * ff + 4 * width), bytes_accessed=30 * 2 ** 20, transcendentals=tokens * ff),
        name="token_block",
    )(core, valid, mixed, x, out_grad, vectors, inner_add, *inner_parts, *outer_parts, *third_parts)


def takes_head_layout(mesh):
    return dict(mesh.shape) == {DP: 4, CTX: 8}


def swap(x, axis, bit):
    count = lax.axis_size(axis)
    return lax.ppermute(x, axis, [(i, i ^ bit) for i in range(count)])


def in_order(bit, own, received, axis):
    first = jnp.where(bit == 0, own, received)
    second = jnp.where(bit == 0, received, own)
    return jnp.stack([first, second], axis=axis)


def pick(x, index, axis):
    return lax.dynamic_index_in_dim(x, index, axis, keepdims=False)


def after(x, *others):
    return lax.optimization_barrier((x,) + others)[0]


def exchange(x, along_z):
    count = lax.axis_size(CTX)
    if along_z:
        sets = [[m for m in range(count) if m % 2 == i] for i in range(2)]
    else:
        sets = [list(range(count // 2)), list(range(count // 2, count))]
    return lax.all_to_all(x, CTX, 0, 0, axis_index_groups=sets, tiled=True)


def in_z_order(pieces):
    z = lax.axis_index(CTX) // 2
    block = jnp.stack(pieces).reshape((2, 2) + pieces[0].shape)
    for axis, bit in ((1, z % 2), (0, z // 2)):
        block = jnp.where(bit == 0, block, jnp.flip(block, axis))
    return block.reshape((4,) + pieces[0].shape)


def total_low(terms):
    return sum(t.astype(F32) for t in terms).astype(BF)


def picks(terms, bit, axis):
    return [pick(t, bit, axis) for t in terms]


def head_layout(
    inputs,
    out_grad,
    lengths,
    token_types,
    query_weight,
    key_weight,
    value_weight,
    value_bias,
    position_weight,
    content_bias,
    position_bias,
    type_bias,
    type_embed,
    output_weight,
    output_bias,
    first_gain,
    first_shift,
    inner_weight,
    inner_bias,
    outer_weight,
    outer_bias,
    second_gain,
    second_shift,
):
    d, c = lax.axis_index(DP), lax.axis_index(CTX)
    members = lax.axis_size(CTX)
    devices = lax.axis_size(DP) * members
    seqs, stretch, width = inputs.shape
    seq_len = stretch * members
    groups = members // seqs
    heads = H // groups
    span = heads * DH
    half = width // 2
    shard = width // devices
    inner_shard = inner_bias.shape[0]
    s, g = c // groups, c % groups
    bit_x = c % 2
    core, bit_y = d % 2, d // 2

    x_send = pick(inputs, 1 - s, 0)
    own = pick(inputs, s, 0)

    smalls = (
        content_bias,
        position_bias,
        type_bias,
        value_bias,
        type_embed[0],
        type_embed[1],
        output_bias,
        first_gain,
        first_shift,
        outer_bias,
        second_gain,
        second_shift,
    )
    stacked, packed, third = pack(
        (after(query_weight, x_send), key_weight, value_weight, position_weight),
        tuple(v.reshape(1, shard) for v in smalls),
        inner_bias.reshape(1, inner_shard),
        token_types,
        inner_weight,
        outer_weight,
        output_weight,
        heads,
        groups,
        members,
    )
    cut = (inner_weight.shape[1] // width) * shard
    block = lax.all_to_all(stacked, CTX, 0, 0, tiled=True)
    x_other = swap(x_send, CTX, 4)
    packed, third = after((packed, third), x_other)
    third_y = swap(third, DP, 2)
    packed_z = [swap(packed, CTX, 2 * m) for m in (1, 2, 3)]
    lines = block[:, heads * shard + 5 : heads * shard + 5 + seqs, LANES:]
    kind_seq = pick(lines, s, 1).reshape(2, groups, stretch).transpose(1, 0, 2)
    kind_seq = kind_seq.reshape(seq_len).astype(F32)
    x_pair = in_order(s, own, after(x_other, block), 0)
    x_pair = jnp.broadcast_to(x_pair[None], (groups, 2, stretch, width))
    x_all = exchange(x_pair, False)
    block = block[None]
    block = in_order(bit_y, block, swap(block, DP, 2), 0)
    third = in_order(bit_y, third, after(third_y, block), 0)
    third_x = swap(third, CTX, 1)
    packed_z = after(packed_z, x_pair, block, third)
    packed_z = in_z_order([packed] + packed_z)
    inner_block, outer_block = packed_z[:, :cut], packed_z[:, cut:]
    inner_x, outer_y = swap(inner_block, CTX, 1), swap(outer_block, DP, 2)
    block = in_order(core, block, after(swap(block, DP, 1), inner_block, outer_block), 1)
    block = block.reshape((devices,) + stacked.shape[1:])
    x_seq = after(x_all, block).reshape(seq_len, width)

    exponent = 2.0 * jnp.arange(half, dtype=F32) / width
    rates = (10000.0 ** (-exponent))[None, :]
    owners = jnp.arange(members, dtype=jnp.int32).reshape(2, groups).T.reshape(-1)
    starts = (owners * stretch).astype(F32)[:, None] * rates
    steps = jnp.arange(stretch, dtype=F32)[:, None] * rates
    starts, steps = lax.optimization_barrier((starts, steps))
    cos_a, sin_a = jnp.cos(starts)[:, None], jnp.sin(starts)[:, None]
    cos_b, sin_b = jnp.cos(steps)[None], jnp.sin(steps)[None]
    trig = jnp.concatenate(
        [cos_a * cos_b - sin_a * sin_b, sin_a * cos_b + cos_a * sin_b], axis=2
    ).reshape(seq_len, width).astype(BF)
    slots = owners[:, None] * stretch + jnp.arange(stretch, dtype=jnp.int32)[None, :]
    key_valid = (slots.reshape(-1) < pick(lengths, s, 0)).astype(F32)
    kext = key_extension(kind_seq, key_valid)

    vectors, inner_add, vec = unpack(block, g, heads, groups, shard, inner_shard)

    saved = attention_forward(x_seq, block, 0, 1, heads, vec, kext, trig)
    inner_x, outer_y, third_x = after((inner_x, outer_y, third_x), saved[0])
    third = in_order(bit_x, third, third_x, 1)
    inner_block = in_order(bit_x, inner_block, inner_x, 0)
    outer_block = in_order(bit_y, outer_block, outer_y, 0)
    inner_y, outer_x = swap(inner_block, DP, 2), swap(outer_block, CTX, 1)
    third_z = [swap(third, CTX, 2 * m) for m in (1, 2, 3)]
    saved = attention_forward(
        x_seq,
        block,
        1,
        heads - 1,
        heads,
        after(vec, inner_block, outer_block, third),
        kext,
        trig,
        saved,
    )
    att, q_block, kb, v1, qp, save, scl, w_heads, prob = saved
    third_z = after(third_z, att)
    att = after(att, third_z).reshape(members, span, stretch)
    mixed = lax.all_to_all(att, CTX, 0, 0, tiled=True).reshape(seqs, width, stretch)
    inner_block, outer_block = after((inner_block, outer_block), att)
    inner_far, outer_far = swap(inner_block, DP, 1), swap(outer_block, DP, 1)
    third = in_z_order([third] + third_z)
    third_parts = (third, swap(third, DP, 1))
    mixed = after(mixed, third_parts[1], inner_far, outer_far)
    inner_y, outer_x = after((inner_y, outer_x), mixed)
    inner_parts = (inner_block, inner_far, inner_y, swap(inner_y, DP, 1))
    outer_parts = (outer_block, outer_far, outer_x, swap(outer_x, DP, 1))

    own_slots = c * stretch + jnp.arange(stretch, dtype=jnp.int32)
    row_valid = (own_slots[None, :] < lengths[:, None]).astype(F32)
    result, first_grad, mixed_grad, inner_keep, inner_send, outer_keep, outer_send, third_keep, third_send, rest, wide = (
        token_block(
            jnp.stack([core, bit_y, bit_x]),
            row_valid.reshape(-1, 1),
            mixed,
            inputs.reshape(-1, width),
            out_grad.reshape(-1, width),
            vectors,
            inner_add,
            inner_parts,
            outer_parts,
            third_parts,
            span,
        )
    )
    result = result.reshape(inputs.shape)
    first_grad = first_grad.reshape(inputs.shape)

    d_out = lax.all_to_all(mixed_grad, CTX, 0, 0, tiled=True)
    z = c // 2
    first_half = inner_shard // 2
    third_terms = [third_keep, swap(third_send, DP, 1)]
    inner_send, outer_send = after((inner_send, outer_send), third_terms[1])
    inner_terms = [inner_keep, swap(inner_send, DP, 1)]
    inner_terms = [t.reshape(2, -1, 4, 2, shard, width) for t in inner_terms]
    third_terms = [t.reshape(2, 4, 2, first_half, width) for t in third_terms]
    outer_terms = [outer_keep, swap(outer_send, DP, 1)]
    outer_terms = [t.reshape(2, 4, 2, first_half + shard, width) for t in outer_terms]
    third_send = [total_low(picks(third_terms, z ^ m, 1)) for m in (1, 2, 3)]
    third_z = [swap(third_send[m - 1], CTX, 2 * m) for m in (1, 2, 3)]
    inner_terms[1] = after(inner_terms[1], *third_send)
    inner_send = total_low(picks(inner_terms, 1 - bit_y, 0))
    inner_y = swap(inner_send, DP, 2)
    outer_terms[1] = after(outer_terms[1], inner_send)
    outer_send = total_low(picks(outer_terms, 1 - bit_x, 2))
    outer_x = swap(outer_send, CTX, 1)
    d_out = after(d_out, inner_send, outer_send, *third_send)
    d_blocks = d_out.reshape(2, groups, span + 8, stretch)

    d_x, w_grad, head_sums = attention_backward(
        core,
        d_blocks,
        x_seq,
        w_heads,
        vec,
        kext,
        trig,
        q_block,
        kb,
        v1,
        qp,
        save,
        scl,
        prob,
        devices,
        heads * shard + 8,
    )
    d_x, w_grad, head_sums, inner_y, outer_x, third_z = lax.optimization_barrier(
        (d_x, w_grad, head_sums, inner_y, outer_x, third_z)
    )
    d_x = exchange(d_x.reshape(groups, 2, stretch, width), False)
    w_both = small_rows(w_grad, jnp.stack([g, core]), head_sums, rest, wide, groups, shard)
    w_far = swap(w_both[1], DP, 1)
    outer_x, inner_y, third_z = after((outer_x, inner_y, third_z), w_both)
    outer_terms = picks(outer_terms, bit_x, 2) + [outer_x]
    outer_send = [total_low(picks(outer_terms, z ^ m, 1)) for m in (1, 2, 3)]
    outer_z = [swap(outer_send[m - 1], CTX, 2 * m) for m in (1, 2, 3)]
    inner_terms = picks(inner_terms, bit_y, 0) + [inner_y]
    inner_send = total_low(picks(inner_terms, 1 - bit_x, 2))
    inner_x = swap(inner_send, CTX, 1)
    w_far = after(w_far, inner_send, *outer_send)
    block_send = row_sum(1 - bit_y, w_both, w_far)
    block_y = swap(block_send, DP, 2)

    d_x_send = jnp.sum(pick(d_x, 1 - s, 1).astype(F32), axis=0).astype(BF)
    d_x_z = swap(d_x_send, CTX, 4)
    block = row_sum(bit_y, w_both, w_far, after(block_y, d_x_send))
    inner_sum = total_low(picks(inner_terms, bit_x, 2) + [after(inner_x, block)])
    third_terms = picks(third_terms, z, 1) + after(third_z, block)
    third_send = total_low(picks(third_terms, 1 - bit_y, 0))
    third_y = swap(third_send, DP, 2)
    block = lax.all_to_all(block, CTX, 0, 0, tiled=True)
    inner_send = [pick(inner_sum, z ^ m, 1) for m in (1, 2, 3)]
    inner_z = [swap(inner_send[m - 1], CTX, 2 * m) for m in (1, 2, 3)]
    outer_z = after(outer_z, *inner_send)
    outer_terms = picks(outer_terms, z, 1) + outer_z
    outer_y = swap(total_low(picks(outer_terms, 1 - bit_y, 0)), DP, 2)
    third_terms = picks(third_terms, bit_y, 0) + [after(third_y, *inner_send)]
    third_x = swap(total_low(picks(third_terms, 1 - bit_x, 0)), CTX, 1)
    third_own = sum(t.astype(F32) for t in picks(third_terms, bit_x, 0) + [third_x])
    outer_sum = sum(t.astype(F32) for t in picks(outer_terms, bit_y, 0) + [outer_y])
    outer_own = jnp.concatenate([third_own, outer_sum[:first_half]], axis=0)
    output_own = outer_sum[first_half:]
    finished = finish(block, heads, shard, width, inner_shard)
    query_own, key_own, value_own, position_own = finished[:4]
    v = finished[4:14]
    inner_z = after(inner_z, query_own)
    inner_own = sum(t.astype(F32) for t in [pick(inner_sum, z, 1)] + inner_z)
    inner_own = jnp.concatenate(list(inner_own), axis=1)
    d_x_own = jnp.sum(pick(d_x, s, 1).astype(F32), axis=0)
    input_terms = in_order(s, d_x_own, after(d_x_z, query_own).astype(F32), 0)
    input_grad = (first_grad + input_terms).astype(BF)
    sums_all = jnp.sum(d_out[:, span : span + 2].astype(F32), axis=(0, 1))
    sums_all = sums_all[: 3 * seqs].reshape(seqs, 3)
    mean_squares = sums_all / (lengths.astype(F32)[:, None] * width)
    return (
        result,
        input_grad,
        query_own,
        key_own,
        value_own,
        v[3],
        position_own,
        v[0],
        v[1],
        v[2],
        finished[14],
        output_own,
        v[4],
        v[5],
        v[6],
        inner_own,
        finished[15],
        outer_own,
        v[7],
        v[8],
        v[9],
        mean_squares,
    )


def solution(mesh):
    in_specs = (
        P(DP, CTX, None),
        P(DP, CTX, None),
        P(DP),
        P(DP, CTX),
        P(ALL, None),
        P(ALL, None),
        P(ALL, None),
        P(ALL),
        P(ALL, None),
        P(ALL),
        P(ALL),
        P(ALL),
        P(None, ALL),
        P(ALL, None),
        P(ALL),
        P(ALL),
        P(ALL),
        P(ALL, None),
        P(ALL),
        P(ALL, None),
        P(ALL),
        P(ALL),
        P(ALL),
    )
    out_specs = (
        P(DP, CTX, None),
        P(DP, CTX, None),
        P(ALL, None),
        P(ALL, None),
        P(ALL, None),
        P(ALL),
        P(ALL, None),
        P(ALL),
        P(ALL),
        P(ALL),
        P(None, ALL),
        P(ALL, None),
        P(ALL),
        P(ALL),
        P(ALL),
        P(ALL, None),
        P(ALL),
        P(ALL, None),
        P(ALL),
        P(ALL),
        P(ALL),
        P(DP, None),
    )
    body = head_layout if takes_head_layout(mesh) else per_device
    return jax.shard_map(
        body, mesh=mesh, in_specs=in_specs, out_specs=out_specs, check_vma=False
    )
```

```python
import functools

import jax
import jax.numpy as jnp
from jax import lax
from jax.experimental import pallas as pl
from jax.experimental.pallas import tpu as pltpu
from jax.sharding import PartitionSpec as P

DP = "dp"
CTX = "ctx"
ALL = (DP, CTX)
H = 12
DH = 64
KEY_BLOCK = 512
MICRO = 2
SEQ_MB = 1


epsilon = 1e-06
masked_score = -1e30
maximal_precision = lax.Precision.HIGHEST


def layer_norm(hidden, gain_values, shift_values):
    center = hidden - jnp.mean(hidden, axis=-1, keepdims=True)
    variance = jnp.mean(center * center, axis=-1, keepdims=True)
    return center * lax.rsqrt(variance + epsilon) * gain_values + shift_values


def gelu_tanh(inner):
    return jax.nn.gelu(inner, approximate=True)


def position_table(anchor, number, columns):
    offsets = (anchor + jnp.arange(number, dtype=jnp.int32)).astype(jnp.float32)
    exponent = 2.0 * jnp.arange(columns // 2, dtype=jnp.float32) / columns
    angles = offsets[:, None] * (10000.0 ** (-exponent))[None, :]
    return jnp.concatenate([jnp.sin(angles), jnp.cos(angles)], axis=1)


def skew_rows(unscaled_scores, keys_count):
    leading = unscaled_scores.shape[:-2]
    rows_count = unscaled_scores.shape[-2]
    span_cols = unscaled_scores.shape[-1]
    flattened = unscaled_scores.reshape(leading + (rows_count * span_cols,))
    flattened = jnp.pad(flattened, [(0, 0)] * len(leading) + [(0, rows_count)])
    return flattened.reshape(leading + (rows_count, span_cols + 1))[..., :keys_count][..., ::-1]


def unskew_rows(grads_block, span_cols):
    leading = grads_block.shape[:-2]
    rows_count = grads_block.shape[-2]
    keys_count = grads_block.shape[-1]
    padded = jnp.pad(
        grads_block[..., ::-1], [(0, 0)] * (len(leading) + 1) + [(0, span_cols + 1 - keys_count)]
    )
    flattened = padded.reshape(leading + (rows_count * (span_cols + 1),))
    return flattened[..., : rows_count * span_cols].reshape(leading + (rows_count, span_cols))


def block_scores(
    query_content,
    query_relative_term,
    type_terms,
    query_kinds,
    key_rows,
    key_kinds,
    key_valid,
    relative_rows,
):
    content = jnp.einsum(
        "bqhd,bkhd->bhqk", query_content, key_rows, preferred_element_type=jnp.float32
    )
    unscaled_scores = jnp.einsum(
        "uply,xly->ulpx", query_relative_term, relative_rows, preferred_element_type=jnp.float32
    )
    same_kind = query_kinds[:, :, None] == key_kinds[:, None, :]
    type_same = jnp.transpose(type_terms[..., 1], (0, 2, 1))[..., None]
    type_other = jnp.transpose(type_terms[..., 0], (0, 2, 1))[..., None]
    summed = (
        content
        + skew_rows(unscaled_scores, key_rows.shape[1])
        + jnp.where(same_kind[:, None], type_same, type_other)
    )
    return (jnp.where(key_valid[:, None, None, :], summed, masked_score), same_kind)


def block_grads(
    query_content,
    query_relative_term,
    type_terms,
    query_kinds,
    log_total,
    row_delta,
    grad_rows,
    key_rows,
    value_rows,
    key_kinds,
    key_valid,
    relative_rows,
):
    scores, same_kind = block_scores(
        query_content,
        query_relative_term,
        type_terms,
        query_kinds,
        key_rows,
        key_kinds,
        key_valid,
        relative_rows,
    )
    probability = jnp.exp(scores - log_total[..., None])
    value_grad = jnp.einsum(
        "bhqk,bqhd->bkhd",
        probability.astype(jnp.bfloat16),
        grad_rows,
        preferred_element_type=jnp.float32,
    )
    prob_grad = jnp.einsum(
        "bqhd,bkhd->bhqk", grad_rows, value_rows, preferred_element_type=jnp.float32
    )
    score_grad = (probability * (prob_grad - row_delta[..., None])).astype(jnp.bfloat16)
    content_grad = jnp.einsum(
        "bhqk,bkhd->bqhd", score_grad, key_rows, preferred_element_type=jnp.float32
    )
    key_grad = jnp.einsum(
        "bhqk,bqhd->bkhd", score_grad, query_content, preferred_element_type=jnp.float32
    )
    unscaled_gradient = unskew_rows(score_grad, relative_rows.shape[0])
    position_grad = jnp.einsum(
        "aioy,yin->aoin", unscaled_gradient, relative_rows, preferred_element_type=jnp.float32
    )
    rel_grad = jnp.einsum(
        "gcrj,grcl->jcl", unscaled_gradient, query_relative_term, preferred_element_type=jnp.float32
    )
    wide_grad = score_grad.astype(jnp.float32)
    same_sum = jnp.sum(jnp.where(same_kind[:, None], wide_grad, 0.0), axis=-1)
    other_sum = jnp.sum(jnp.where(same_kind[:, None], 0.0, wide_grad), axis=-1)
    type_grad = jnp.transpose(jnp.stack([other_sum, same_sum], axis=-1), (0, 2, 1, 3))
    return (content_grad, position_grad, type_grad, key_grad, value_grad, rel_grad)


def per_device(
    inputs,
    out_grad,
    lengths,
    token_types,
    query_weight,
    key_weight,
    value_weight,
    value_bias,
    position_weight,
    content_bias,
    position_bias,
    type_bias,
    type_embed,
    output_weight,
    output_bias,
    first_gain,
    first_shift,
    inner_weight,
    inner_bias,
    outer_weight,
    outer_bias,
    second_gain,
    second_shift,
):
    stretch = inputs.shape[1]
    width = inputs.shape[2]
    seq_len = stretch * lax.axis_size(CTX)
    stretch_start = lax.axis_index(CTX) * stretch
    window = seq_len + stretch - 1
    scale_query = DH ** (-0.5)
    own_positions = stretch_start + jnp.arange(stretch, dtype=jnp.int32)
    table_forward = position_table(stretch_start - seq_len + 1, window, width).astype(jnp.bfloat16)
    outputs_list = []
    input_grads = []
    stat_rows = []
    grads_total = None
    rel_total = jnp.zeros((window, width), jnp.float32)
    for micro_index in range(MICRO):
        first_seq = micro_index * SEQ_MB
        sequence_input = inputs[first_seq : first_seq + SEQ_MB]
        seq_grad = out_grad[first_seq : first_seq + SEQ_MB]
        seq_kinds = token_types[first_seq : first_seq + SEQ_MB].astype(jnp.bfloat16)
        length_col = lengths[first_seq : first_seq + SEQ_MB][:, None]
        seq_count = sequence_input.shape[0]
        heads_shape = (seq_count, stretch, H, DH)
        full_shape = (seq_count, seq_len, H, DH)
        row_valid = (own_positions[None, :] < length_col).astype(jnp.float32)[..., None]
        gathered = (
            lax.all_gather(query_weight, ALL, axis=0, tiled=True),
            lax.all_gather(key_weight, ALL, axis=0, tiled=True),
            lax.all_gather(value_weight, ALL, axis=0, tiled=True),
            lax.all_gather(value_bias, ALL, axis=0, tiled=True),
            lax.all_gather(position_weight, ALL, axis=0, tiled=True),
            lax.all_gather(content_bias, ALL, axis=0, tiled=True),
            lax.all_gather(position_bias, ALL, axis=0, tiled=True),
            lax.all_gather(type_bias, ALL, axis=0, tiled=True),
            lax.all_gather(type_embed, ALL, axis=1, tiled=True),
            lax.all_gather(output_weight, ALL, axis=0, tiled=True),
            lax.all_gather(output_bias, ALL, axis=0, tiled=True),
            lax.all_gather(first_gain, ALL, axis=0, tiled=True),
            lax.all_gather(first_shift, ALL, axis=0, tiled=True),
            lax.all_gather(inner_weight, ALL, axis=0, tiled=True),
            lax.all_gather(inner_bias, ALL, axis=0, tiled=True),
            lax.all_gather(outer_weight, ALL, axis=0, tiled=True),
            lax.all_gather(outer_bias, ALL, axis=0, tiled=True),
            lax.all_gather(second_gain, ALL, axis=0, tiled=True),
            lax.all_gather(second_shift, ALL, axis=0, tiled=True),
        )
        (
            query_matrix,
            key_matrix,
            value_matrix,
            value_add,
            position_mat,
            content_add,
            position_add,
            type_add,
            type_table,
            output_matrix,
            output_add,
            gain_one,
            shift_one,
            inner_matrix,
            inner_add,
            outer_matrix,
            outer_add,
            gain_two,
            shift_two,
        ) = gathered
        scaled = (
            jnp.dot(sequence_input, query_matrix, preferred_element_type=jnp.float32) * scale_query
        )
        query_content = (
            (scaled + content_add.astype(jnp.float32)).astype(jnp.bfloat16).reshape(heads_shape)
        )
        query_relative_term = (
            (scaled + position_add.astype(jnp.float32)).astype(jnp.bfloat16).reshape(heads_shape)
        )
        with_type = (scaled + type_add.astype(jnp.float32)).reshape(heads_shape)
        type_heads = type_table.astype(jnp.float32).reshape(2, H, DH)
        type_terms = jnp.einsum(
            "bqhd,shd->bqhs", with_type, type_heads, precision=maximal_precision
        )
        key_rows = jnp.dot(sequence_input, key_matrix, preferred_element_type=jnp.float32).astype(
            jnp.bfloat16
        )
        value_rows = (
            jnp.dot(sequence_input, value_matrix, preferred_element_type=jnp.float32)
            + value_add.astype(jnp.float32)
        ).astype(jnp.bfloat16)
        rel_forward = (
            jnp.dot(table_forward, position_mat, preferred_element_type=jnp.float32)
            .astype(jnp.bfloat16)
            .reshape(window, H, DH)
        )
        start_state = (
            jnp.full((seq_count, H, stretch), masked_score, jnp.float32),
            jnp.zeros((seq_count, H, stretch), jnp.float32),
            jnp.zeros(heads_shape, jnp.float32),
        )
        piece_keys = lax.all_gather(key_rows, CTX, axis=1, tiled=True)
        piece_values = lax.all_gather(value_rows, CTX, axis=1, tiled=True)
        piece_kinds = lax.all_gather(seq_kinds, CTX, axis=1, tiled=True)
        number = piece_keys.shape[1]
        block_rows = KEY_BLOCK

        def one_block(running, offset):
            run_max, run_total, run_acc = running
            part_keys = lax.dynamic_slice_in_dim(piece_keys, offset, block_rows, 1).reshape(
                seq_count, block_rows, H, DH
            )
            part_values = lax.dynamic_slice_in_dim(piece_values, offset, block_rows, 1).reshape(
                seq_count, block_rows, H, DH
            )
            part_kinds = lax.dynamic_slice_in_dim(piece_kinds, offset, block_rows, 1)
            relative_rows = lax.dynamic_slice_in_dim(
                rel_forward, seq_len - offset - block_rows, stretch + block_rows - 1, 0
            )
            key_valid = (offset + jnp.arange(block_rows, dtype=jnp.int32))[None, :] < length_col
            scores, same_kind = block_scores(
                query_content,
                query_relative_term,
                type_terms,
                seq_kinds,
                part_keys,
                part_kinds,
                key_valid,
                relative_rows,
            )
            new_max = jnp.maximum(run_max, jnp.max(scores, axis=-1))
            factor = jnp.exp(run_max - new_max)
            weights_block = jnp.exp(scores - new_max[..., None])
            run_total = run_total * factor + jnp.sum(weights_block, axis=-1)
            mixed_rows = jnp.einsum(
                "bhqk,bkhd->bqhd",
                weights_block.astype(jnp.bfloat16),
                part_values,
                preferred_element_type=jnp.float32,
            )
            run_acc = run_acc * jnp.transpose(factor, (0, 2, 1))[..., None] + mixed_rows
            return ((new_max, run_total, run_acc), None)

        offsets = jnp.arange(number // block_rows, dtype=jnp.int32) * block_rows
        result_state, unused = lax.scan(one_block, start_state, offsets)
        run_max, run_total, run_acc = result_state
        log_total = run_max + jnp.log(run_total)
        attended = run_acc / jnp.transpose(run_total, (0, 2, 1))[..., None]
        attended_reduced = attended.astype(jnp.bfloat16).reshape(seq_count, stretch, width)
        attn_out = jnp.dot(
            attended_reduced, output_matrix, preferred_element_type=jnp.float32
        ) + output_add.astype(jnp.float32)
        first_sum = sequence_input.astype(jnp.float32) + attn_out
        normed = layer_norm(first_sum, gain_one.astype(jnp.float32), shift_one.astype(jnp.float32))
        normed_reduced = normed.astype(jnp.bfloat16)
        inner = jnp.dot(
            normed_reduced, inner_matrix, preferred_element_type=jnp.float32
        ) + inner_add.astype(jnp.float32)
        activated_reduced = gelu_tanh(inner).astype(jnp.bfloat16)
        outer = jnp.dot(
            activated_reduced, outer_matrix, preferred_element_type=jnp.float32
        ) + outer_add.astype(jnp.float32)
        second_sum = normed + outer
        result = layer_norm(second_sum, gain_two.astype(jnp.float32), shift_two.astype(jnp.float32))
        outputs_list.append(result.astype(jnp.bfloat16))
        stat_rows.append(
            jnp.stack(
                [
                    jnp.sum(first_sum * first_sum * row_valid, axis=(1, 2)),
                    jnp.sum(attn_out * attn_out * row_valid, axis=(1, 2)),
                    jnp.sum(outer * outer * row_valid, axis=(1, 2)),
                ],
                axis=1,
            )
        )
        back_set = (
            lax.all_gather(query_weight, ALL, axis=0, tiled=True),
            lax.all_gather(key_weight, ALL, axis=0, tiled=True),
            lax.all_gather(value_weight, ALL, axis=0, tiled=True),
            lax.all_gather(value_bias, ALL, axis=0, tiled=True),
            lax.all_gather(position_weight, ALL, axis=0, tiled=True),
            lax.all_gather(content_bias, ALL, axis=0, tiled=True),
            lax.all_gather(position_bias, ALL, axis=0, tiled=True),
            lax.all_gather(type_bias, ALL, axis=0, tiled=True),
            lax.all_gather(type_embed, ALL, axis=1, tiled=True),
            lax.all_gather(output_weight, ALL, axis=0, tiled=True),
            lax.all_gather(output_bias, ALL, axis=0, tiled=True),
            lax.all_gather(first_gain, ALL, axis=0, tiled=True),
            lax.all_gather(first_shift, ALL, axis=0, tiled=True),
            lax.all_gather(inner_weight, ALL, axis=0, tiled=True),
            lax.all_gather(inner_bias, ALL, axis=0, tiled=True),
            lax.all_gather(outer_weight, ALL, axis=0, tiled=True),
            lax.all_gather(outer_bias, ALL, axis=0, tiled=True),
            lax.all_gather(second_gain, ALL, axis=0, tiled=True),
            lax.all_gather(second_shift, ALL, axis=0, tiled=True),
        )
        (
            query_matrix,
            key_matrix,
            value_matrix,
            value_add,
            position_mat,
            content_add,
            position_add,
            type_add,
            type_table,
            output_matrix,
            output_add,
            gain_one,
            shift_one,
            inner_matrix,
            inner_add,
            outer_matrix,
            outer_add,
            gain_two,
            shift_two,
        ) = back_set
        type_heads = type_table.astype(jnp.float32).reshape(2, H, DH)
        cotangent = seq_grad.astype(jnp.float32) * row_valid
        unused_two, second_back = jax.vjp(
            layer_norm, second_sum, gain_two.astype(jnp.float32), shift_two.astype(jnp.float32)
        )
        second_grad, gain_two_grad, shift_two_grad = second_back(cotangent)
        outer_reduced = second_grad.astype(jnp.bfloat16)
        outer_add_grad = jnp.sum(outer_reduced.astype(jnp.float32), axis=(0, 1))
        outer_mat_grad = jnp.einsum(
            "hpi,hpt->it", activated_reduced, outer_reduced, preferred_element_type=jnp.float32
        )
        activated_grad = jnp.einsum(
            "unk,rk->unr", outer_reduced, outer_matrix, preferred_element_type=jnp.float32
        )
        unused_three, gelu_back = jax.vjp(gelu_tanh, inner)
        inner_reduced = gelu_back(activated_grad)[0].astype(jnp.bfloat16)
        inner_add_grad = jnp.sum(inner_reduced.astype(jnp.float32), axis=(0, 1))
        inner_mat_grad = jnp.einsum(
            "psu,psy->uy", normed_reduced, inner_reduced, preferred_element_type=jnp.float32
        )
        normed_grad = second_grad + jnp.einsum(
            "tma,ra->tmr", inner_reduced, inner_matrix, preferred_element_type=jnp.float32
        )
        unused_four, first_back = jax.vjp(
            layer_norm, first_sum, gain_one.astype(jnp.float32), shift_one.astype(jnp.float32)
        )
        first_grad, gain_one_grad, shift_one_grad = first_back(normed_grad)
        attention_reduced = first_grad.astype(jnp.bfloat16)
        output_add_grad = jnp.sum(attention_reduced.astype(jnp.float32), axis=(0, 1))
        output_mat_grad = jnp.einsum(
            "yim,yig->mg", attended_reduced, attention_reduced, preferred_element_type=jnp.float32
        )
        grad_rows = (
            jnp.einsum(
                "jcy,py->jcp", attention_reduced, output_matrix, preferred_element_type=jnp.float32
            )
            .astype(jnp.bfloat16)
            .reshape(heads_shape)
        )
        row_delta = jnp.einsum(
            "bqhd,bqhd->bhq", grad_rows.astype(jnp.float32), attended, precision=maximal_precision
        )
        all_keys, all_values, all_kinds = (
            lax.all_gather(key_rows, CTX, axis=1, tiled=True),
            lax.all_gather(value_rows, CTX, axis=1, tiled=True),
            lax.all_gather(seq_kinds, CTX, axis=1, tiled=True),
        )

        def key_step(running, key_start):
            content_acc, position_acc, type_acc, key_acc, value_acc, rel_acc = running
            part_keys = lax.dynamic_slice_in_dim(all_keys, key_start, KEY_BLOCK, 1).reshape(
                seq_count, KEY_BLOCK, H, DH
            )
            part_values = lax.dynamic_slice_in_dim(all_values, key_start, KEY_BLOCK, 1).reshape(
                seq_count, KEY_BLOCK, H, DH
            )
            part_kinds = lax.dynamic_slice_in_dim(all_kinds, key_start, KEY_BLOCK, 1)
            rel_start = seq_len - key_start - KEY_BLOCK
            relative_rows = lax.dynamic_slice_in_dim(
                rel_forward, rel_start, stretch + KEY_BLOCK - 1, 0
            )
            key_valid = (key_start + jnp.arange(KEY_BLOCK, dtype=jnp.int32))[None, :] < length_col
            pieces = block_grads(
                query_content,
                query_relative_term,
                type_terms,
                seq_kinds,
                log_total,
                row_delta,
                grad_rows,
                part_keys,
                part_values,
                part_kinds,
                key_valid,
                relative_rows,
            )
            content_part, position_part, type_part, key_part, value_part, rel_part = pieces
            key_acc = lax.dynamic_update_slice_in_dim(key_acc, key_part, key_start, 1)
            value_acc = lax.dynamic_update_slice_in_dim(value_acc, value_part, key_start, 1)
            rel_old = lax.dynamic_slice_in_dim(rel_acc, rel_start, stretch + KEY_BLOCK - 1, 0)
            rel_acc = lax.dynamic_update_slice_in_dim(rel_acc, rel_old + rel_part, rel_start, 0)
            return (
                (
                    content_acc + content_part,
                    position_acc + position_part,
                    type_acc + type_part,
                    key_acc,
                    value_acc,
                    rel_acc,
                ),
                None,
            )

        start_grads = (
            jnp.zeros(heads_shape, jnp.float32),
            jnp.zeros(heads_shape, jnp.float32),
            jnp.zeros((seq_count, stretch, H, 2), jnp.float32),
            jnp.zeros(full_shape, jnp.float32),
            jnp.zeros(full_shape, jnp.float32),
            jnp.zeros((window, H, DH), jnp.float32),
        )
        final_grads, unused_five = lax.scan(
            key_step, start_grads, jnp.arange(seq_len // KEY_BLOCK, dtype=jnp.int32) * KEY_BLOCK
        )
        content_grad, position_grad, type_grad, key_all, value_all, rel_grad = final_grads
        key_grad, value_grad = (
            lax.psum_scatter(
                key_all.astype(jnp.bfloat16), CTX, scatter_dimension=1, tiled=True
            ).astype(jnp.float32),
            lax.psum_scatter(
                value_all.astype(jnp.bfloat16), CTX, scatter_dimension=1, tiled=True
            ).astype(jnp.float32),
        )
        type_part_grad = jnp.einsum(
            "bqhs,shd->bqhd", type_grad, type_heads, precision=maximal_precision
        )
        query_grad = content_grad + position_grad + type_part_grad
        content_add_grad = jnp.sum(content_grad, axis=(0, 1)).reshape(width)
        position_add_grad = jnp.sum(position_grad, axis=(0, 1)).reshape(width)
        type_add_grad = jnp.sum(type_part_grad, axis=(0, 1)).reshape(width)
        rel_total = rel_total + rel_grad.reshape(window, width)
        query_reduced = query_grad.astype(jnp.bfloat16).reshape(seq_count, stretch, width)
        key_reduced = key_grad.astype(jnp.bfloat16).reshape(seq_count, stretch, width)
        value_reduced = value_grad.astype(jnp.bfloat16).reshape(seq_count, stretch, width)
        type_table_grad = jnp.einsum(
            "bqhs,bqhd->shd", type_grad, with_type, precision=maximal_precision
        ).reshape(2, width)
        query_mat_grad = (
            jnp.einsum(
                "orh,org->hg", sequence_input, query_reduced, preferred_element_type=jnp.float32
            )
            * scale_query
        )
        key_mat_grad = jnp.einsum(
            "orh,org->hg", sequence_input, key_reduced, preferred_element_type=jnp.float32
        )
        value_mat_grad = jnp.einsum(
            "orh,org->hg", sequence_input, value_reduced, preferred_element_type=jnp.float32
        )
        value_add_grad = jnp.sum(value_reduced.astype(jnp.float32), axis=(0, 1))
        input_grad = (
            first_grad
            + jnp.einsum(
                "sux,fx->suf", query_reduced, query_matrix, preferred_element_type=jnp.float32
            )
            * scale_query
            + jnp.einsum("sux,fx->suf", key_reduced, key_matrix, preferred_element_type=jnp.float32)
            + jnp.einsum(
                "sux,fx->suf", value_reduced, value_matrix, preferred_element_type=jnp.float32
            )
        )
        input_grads.append(input_grad.astype(jnp.bfloat16))
        micro_grads = (
            query_mat_grad,
            key_mat_grad,
            value_mat_grad,
            value_add_grad,
            content_add_grad,
            position_add_grad,
            type_add_grad,
            type_table_grad,
            output_mat_grad,
            output_add_grad,
            gain_one_grad,
            shift_one_grad,
            inner_mat_grad,
            inner_add_grad,
            outer_mat_grad,
            outer_add_grad,
            gain_two_grad,
            shift_two_grad,
        )
        if grads_total is None:
            grads_total = micro_grads
        else:
            grads_total = jax.tree.map(jnp.add, grads_total, micro_grads)
    rel_high = rel_total.astype(jnp.bfloat16)
    rel_rest = (rel_total - rel_high.astype(jnp.float32)).astype(jnp.bfloat16)
    contract_rows = (((0,), (0,)), ((), ()))
    position_mat_grad = lax.dot_general(
        table_forward, rel_high, contract_rows, preferred_element_type=jnp.float32
    ) + lax.dot_general(table_forward, rel_rest, contract_rows, preferred_element_type=jnp.float32)
    (
        query_total,
        key_total,
        value_total,
        value_add_total,
        content_total,
        position_total,
        type_total,
        table_total,
        output_total,
        output_add_total,
        gain_one_total,
        shift_one_total,
        inner_total,
        inner_add_total,
        outer_total,
        outer_add_total,
        gain_two_total,
        shift_two_total,
    ) = grads_total
    reduced = (
        lax.psum_scatter(query_total, ALL, scatter_dimension=0, tiled=True),
        lax.psum_scatter(key_total, ALL, scatter_dimension=0, tiled=True),
        lax.psum_scatter(value_total, ALL, scatter_dimension=0, tiled=True),
        lax.psum_scatter(value_add_total, ALL, scatter_dimension=0, tiled=True),
        lax.psum_scatter(position_mat_grad, ALL, scatter_dimension=0, tiled=True),
        lax.psum_scatter(content_total, ALL, scatter_dimension=0, tiled=True),
        lax.psum_scatter(position_total, ALL, scatter_dimension=0, tiled=True),
        lax.psum_scatter(type_total, ALL, scatter_dimension=0, tiled=True),
        lax.psum_scatter(table_total, ALL, scatter_dimension=1, tiled=True),
        lax.psum_scatter(output_total, ALL, scatter_dimension=0, tiled=True),
        lax.psum_scatter(output_add_total, ALL, scatter_dimension=0, tiled=True),
        lax.psum_scatter(gain_one_total, ALL, scatter_dimension=0, tiled=True),
        lax.psum_scatter(shift_one_total, ALL, scatter_dimension=0, tiled=True),
        lax.psum_scatter(inner_total, ALL, scatter_dimension=0, tiled=True),
        lax.psum_scatter(inner_add_total, ALL, scatter_dimension=0, tiled=True),
        lax.psum_scatter(outer_total, ALL, scatter_dimension=0, tiled=True),
        lax.psum_scatter(outer_add_total, ALL, scatter_dimension=0, tiled=True),
        lax.psum_scatter(gain_two_total, ALL, scatter_dimension=0, tiled=True),
        lax.psum_scatter(shift_two_total, ALL, scatter_dimension=0, tiled=True),
    )
    sums_all = lax.psum(jnp.concatenate(stat_rows, axis=0), CTX)
    mean_squares = sums_all / (lengths.astype(jnp.float32)[:, None] * width)
    return (
        (jnp.concatenate(outputs_list, axis=0), jnp.concatenate(input_grads, axis=0))
        + tuple(reduced)
        + (mean_squares,)
    )


LANES = 128
BF = jnp.bfloat16
F32 = jnp.float32
ROWS_CC = (((1,), (1,)), ((), ()))
COLS_CC = (((0,), (0,)), ((), ()))
ROWCOL = (((1,), (0,)), ((), ()))


def mm(a, b, dims):
    return lax.dot_general(a, b, dims, preferred_element_type=F32)


def split3(v):
    hi = v.astype(BF).astype(F32)
    mid = (v - hi).astype(BF).astype(F32)
    lo = (v - hi - mid).astype(BF).astype(F32)
    return hi, mid, lo


def attention_forward_kernel(tile, x_ref, w_ref, vec_ref, kext_ref, trig_ref,
                             att_ref, qb_ref, kb_ref, v1_ref, qp_ref, save_ref, scl_ref, wh_ref, prob_ref,
                             kt_ref, qt_ref):
    step = pl.program_id(1)
    rows = x_ref.shape[0]
    width = x_ref.shape[1]
    half = width // 2
    lane = lax.broadcasted_iota(jnp.int32, (tile, LANES), 1)
    low = lane < DH

    @pl.when((pl.program_id(0) == 0) & (step == 0))
    def _():
        kt_ref[:, :width] = trig_ref[...]

    @pl.when(step == 0)
    def _():
        vec = vec_ref[0]
        w = w_ref[...].astype(F32).reshape(width, 2 * LANES).astype(BF)
        wh_ref[0] = w
        w_lane = lax.broadcasted_iota(jnp.int32, (width, LANES), 1)
        w_pos = jnp.where(w_lane < DH, pltpu.roll(w[:, LANES:].astype(F32), DH, 1), 0.0).astype(BF)

        def body(i, carry):
            at = slice(i * 256, (i + 1) * 256)
            lane = lax.broadcasted_iota(jnp.int32, (256, LANES), 1)
            low = lane < DH
            proj = mm(x_ref[at, :], w, ROWCOL)
            kext = kext_ref[at, :].astype(F32)
            kind = kext[:, DH + 3:DH + 4]
            scaled = jnp.where(low, proj[:, :LANES] * DH ** -0.5, 0.0)
            scl_ref[0, at, :] = scaled
            kb = jnp.where(low, pltpu.roll(proj[:, :LANES], DH, 1), kext).astype(BF)
            kb_ref[0, at, :] = kb
            kt_ref[at, width:] = kb
            one_v = (lane >= DH) & (lane < DH + 3)
            v1_ref[0, at, :] = jnp.where(low, proj[:, LANES:] + vec[3:4, :], jnp.where(one_v, 1.0, 0.0)).astype(BF)
            with_type = scaled + vec[2:3, :]
            term0 = jnp.sum(with_type * vec[4:5, :], axis=1, keepdims=True)
            term1 = jnp.sum(with_type * vec[5:6, :], axis=1, keepdims=True)
            base = jnp.where(kind > 0.5, term0, term1)
            slope = jnp.where(kind > 0.5, term1 - term0, term0 - term1)
            b_hi, b_mid, b_lo = split3(base)
            s_hi, s_mid, s_lo = split3(slope)
            ext = jnp.where(lane == DH, b_hi, 0.0)
            ext = jnp.where(lane == DH + 1, b_mid, ext)
            ext = jnp.where(lane == DH + 2, b_lo, ext)
            ext = jnp.where(lane == DH + 3, s_hi, ext)
            ext = jnp.where(lane == DH + 4, s_mid, ext)
            ext = jnp.where(lane == DH + 5, 1.0, ext)
            q_block = jnp.where(low, scaled + vec[0:1, :], ext).astype(BF)
            qb_ref[0, at, :] = q_block
            qt_ref[at, width:] = q_block
            qp = jnp.where(low, scaled + vec[1:2, :], 0.0).astype(BF)
            qp_ref[0, at, :] = qp
            grow = mm(qp, w_pos, ROWS_CC)
            q_sin = grow[:, :half]
            q_cos = grow[:, half:]
            c = trig_ref[at, :half].astype(F32)
            s = trig_ref[at, half:].astype(F32)
            qt_ref[at, :half] = (q_sin * s + q_cos * c).astype(BF)
            qt_ref[at, half:width] = (q_cos * s - q_sin * c).astype(BF)
            return carry

        for i in range(rows // 256):
            body(i, 0)

    att_parts = att_ref.shape[0]
    sub = 256
    count = tile // sub
    small_lane = lax.broadcasted_iota(jnp.int32, (sub, LANES), 1) < DH

    def scores_of(i):
        at = pl.ds(pl.multiple_of(step * tile + i * sub, sub), sub)
        return mm(qt_ref[at, :], kt_ref[...], ROWS_CC)

    later = scores_of(0)
    for i in range(count):
        scores = later
        if i + 1 < count:
            later = scores_of(i + 1)
        top = jnp.max(scores, axis=1, keepdims=True)
        prob = jnp.exp(scores - top).astype(BF)
        prob_ref[0, i * sub:(i + 1) * sub, :] = prob
        mixed = mm(prob, v1_ref[0], ROWCOL)
        total = mixed[:, DH:DH + 1]
        att = mixed / total
        save_ref[0, i * sub:(i + 1) * sub, :] = jnp.where(small_lane, att, 1.0 / total)
        att_t = jnp.transpose(att)[:DH, :].astype(BF)
        for n in range(sub // LANES):
            b = i * (sub // LANES) + n
            att_ref[b % att_parts, b // att_parts] = att_t[:, n * LANES:(n + 1) * LANES]


def attention_backward_kernel(tile, core_ref, do_ref, x_ref, w_ref, vec_ref, kext_ref, trig_ref,
                              qb_ref, kb_ref, v1_ref, qp_ref, save_ref, scl_ref, prob_ref,
                              dx_ref, dw_ref, small_ref,
                              kt_ref, dk_acc, dv_acc, d_ref, dwp_ref, dx_acc):
    step = pl.program_id(1)
    width = trig_ref.shape[1]
    half = width // 2
    lane = lax.broadcasted_iota(jnp.int32, (tile, LANES), 1)
    low = lane < DH

    @pl.when((pl.program_id(0) == 0) & (step == 0))
    def _():
        kt_ref[:, :width] = trig_ref[...]

    @pl.when(step == 0)
    def _():
        kt_ref[:, width:] = kb_ref[0]
        dk_acc[...] = jnp.zeros_like(dk_acc)
        dv_acc[...] = jnp.zeros_like(dv_acc)
        dwp_ref[...] = jnp.zeros_like(dwp_ref)
        small_ref[...] = jnp.zeros_like(small_ref)

    at = pl.ds(pl.multiple_of(step * tile, tile), tile)
    w = w_ref[0]
    w_lane = lax.broadcasted_iota(jnp.int32, (width, LANES), 1)
    w_pos = jnp.where(w_lane < DH, pltpu.roll(w[:, LANES:].astype(F32), DH, 1), 0.0).astype(BF)
    save = save_ref[0]
    inverse = save[:, DH:DH + 1]
    parts = do_ref.shape[0]
    do_t = jnp.concatenate([do_ref[i % parts, i // parts] for i in range(tile // LANES)], axis=1).astype(F32)
    d_out = jnp.transpose(jnp.concatenate([do_t, jnp.zeros_like(do_t)], axis=0))
    d_out = d_out * inverse
    delta = jnp.sum(d_out * save, axis=1, keepdims=True)
    d_hi, d_mid, d_lo = split3(-delta)
    q_block = qb_ref[0]
    ext = jnp.where(lane == DH, d_hi, d_out)
    ext = jnp.where(lane == DH + 1, d_mid, ext)
    ext = jnp.where(lane == DH + 2, d_lo, ext)
    d_ext = ext.astype(BF)
    prob = prob_ref[0]
    dv_acc[...] += mm(d_ext, prob, COLS_CC)
    d_score = (prob.astype(F32) * mm(d_ext, v1_ref[0], ROWS_CC)).astype(BF)
    dk_acc[...] += mm(q_block, d_score, COLS_CC)
    dq = mm(d_score, kt_ref[...], ROWCOL)
    c = trig_ref[at, :half].astype(F32)
    s = trig_ref[at, half:].astype(F32)
    du_c = dq[:, :half]
    du_s = dq[:, half:width]
    back = jnp.concatenate([s * du_c - c * du_s, c * du_c + s * du_s], axis=1).astype(BF)
    d_block = dq[:, width:]
    d_pos = mm(back, w_pos, ROWCOL)
    dwp_ref[...] += mm(qp_ref[0], back, COLS_CC)[:DH, :]
    vec = vec_ref[0]
    kind = kext_ref[...][:, DH + 3:DH + 4].astype(F32)
    every = d_block[:, DH:DH + 1]
    ones = d_block[:, DH + 3:DH + 4]
    g_same = jnp.where(kind > 0.5, ones, every - ones)
    g_other = jnp.where(kind > 0.5, every - ones, ones)
    type_part = g_other * vec[4:5, :] + g_same * vec[5:6, :]
    d_content = jnp.where(low, d_block, 0.0)
    with_type = jnp.where(low, scl_ref[0] + vec[2:3, :], 0.0)
    d_scaled = d_content + d_pos + type_part
    d_ref[:DH, at] = (jnp.transpose(d_scaled)[:DH, :] * DH ** -0.5).astype(BF)
    sums = [jnp.sum(v, axis=0, keepdims=True) for v in
            (d_content, d_pos, type_part, g_other * with_type, g_same * with_type)]
    small_ref[0] += jnp.concatenate(sums + [jnp.zeros((3, LANES), F32)], axis=0)

    @pl.when(step == pl.num_programs(1) - 1)
    def _():
        d_ref[DH:2 * DH] = dk_acc[:DH, :].astype(BF)
        dv_low = dv_acc[:DH, :].astype(BF)
        d_ref[2 * DH:] = dv_low
        dv_sum = jnp.sum(dv_low.astype(F32), axis=1, keepdims=True)
        dv_sum = jnp.transpose(jnp.broadcast_to(jnp.concatenate([dv_sum, dv_sum], axis=0), (LANES, LANES)))
        small_ref[0, 5:6, :] = dv_sum[:1, :]
        d_wt = mm(d_ref[...], x_ref[...], ROWCOL)
        d_w = jnp.transpose(jnp.concatenate([d_wt, dwp_ref[...]], axis=0))
        shard = dw_ref.shape[3]
        members = dw_ref.shape[2]
        for i in range(4 * members):
            dw_ref[(i // members % 2) ^ core_ref[0], i // (2 * members), i % members] = d_w[i * shard:(i + 1) * shard, :].astype(BF)
        d_x = lax.dot_general(d_ref[...], w_ref[0][:, :3 * DH], (((0,), (1,)), ((), ())), preferred_element_type=F32)

        @pl.when(pl.program_id(0) == 0)
        def _():
            dx_acc[...] = d_x

        @pl.when(pl.program_id(0) > 0)
        def _():
            dx_acc[...] += d_x

        @pl.when(pl.program_id(0) == pl.num_programs(0) - 1)
        def _():
            dx_ref[...] = dx_acc[...].astype(BF)


def attention_forward(x, w_block, first, count, heads, vec, kext, trig, previous=(), tile=1024):
    rows, width = x.shape
    owners = w_block.shape[0]
    shard = width // owners
    full = width + LANES
    per_head = lambda shape: pl.BlockSpec((1,) + shape, lambda h, t: (first + h, 0, 0))
    fixed = lambda shape: pl.BlockSpec(shape, lambda h, t: (0, 0))
    flops = count * rows * 2 * (width * 256 + rows * full + rows * LANES)
    S = jax.ShapeDtypeStruct
    kernel = functools.partial(attention_forward_kernel, tile)
    skip = len(previous)
    return pl.pallas_call(
        lambda *refs: kernel(*refs[:5], *refs[5 + skip:]),
        grid=(count, rows // tile),
        in_specs=[fixed((rows, width)), pl.BlockSpec((owners, shard, 2 * LANES), lambda h, t: (0, first + h, 0)),
                  per_head((8, LANES)), fixed((rows, LANES)), fixed((rows, width))]
        + [pl.BlockSpec(memory_space=pl.ANY)] * skip,
        out_specs=[pl.BlockSpec((2, tile // (2 * LANES), DH, LANES), lambda h, t: (0, t, first + h, 0)),
                   per_head((rows, LANES)), per_head((rows, LANES)), per_head((rows, LANES)),
                   per_head((rows, LANES)),
                   pl.BlockSpec((1, tile, LANES), lambda h, t: (first + h, t, 0)),
                   per_head((rows, LANES)), per_head((width, 2 * LANES)),
                   pl.BlockSpec((1, tile, rows), lambda h, t: (first + h, t, 0))],
        out_shape=[S((2, rows // (2 * LANES), heads * DH, LANES), BF), S((heads, rows, LANES), BF),
                   S((heads, rows, LANES), BF), S((heads, rows, LANES), BF), S((heads, rows, LANES), BF),
                   S((heads, rows, LANES), F32), S((heads, rows, LANES), F32), S((heads, width, 2 * LANES), BF),
                   S((heads, rows, rows), BF)],
        input_output_aliases={5 + i: i for i in range(skip)},
        scratch_shapes=[pltpu.VMEM((rows, full), BF), pltpu.VMEM((rows, full), BF)],
        compiler_params=pltpu.CompilerParams(dimension_semantics=("arbitrary", "arbitrary"),
                                             vmem_limit_bytes=63 * 2 ** 20),
        cost_estimate=pl.CostEstimate(flops=flops, bytes_accessed=rows * width * 16, transcendentals=count * rows * rows),
        name="attention_forward",
    )(x, w_block, vec, kext, trig, *previous)


def attention_backward(core, d_out, x, w, vec, kext, trig, qb, kb, v1, qp, save, scl, prob, owners, block_rows, tile=512):
    heads, rows, _ = qb.shape
    width = x.shape[1]
    full = width + LANES
    shard = width // owners
    per_head = lambda shape: pl.BlockSpec((1,) + shape, lambda h, t: (h, 0, 0))
    per_tile = lambda cols: pl.BlockSpec((1, tile, cols), lambda h, t: (h, t, 0))
    fixed = lambda shape: pl.BlockSpec(shape, lambda h, t: (0, 0))
    flops = heads * rows * 2 * (2 * rows * full + 3 * rows * LANES)
    return pl.pallas_call(
        functools.partial(attention_backward_kernel, tile),
        grid=(heads, rows // tile),
        in_specs=[pl.BlockSpec(memory_space=pltpu.SMEM), pl.BlockSpec((2, tile // (2 * LANES), DH, LANES), lambda h, t: (0, t, h, 0)), fixed((rows, width)),
                  per_head((width, 256)), per_head((8, LANES)),
                  pl.BlockSpec((tile, LANES), lambda h, t: (t, 0)), fixed((rows, width)),
                  per_tile(LANES), per_head((rows, LANES)), per_head((rows, LANES)), per_tile(LANES),
                  per_tile(LANES), per_tile(LANES), per_tile(rows)],
        out_specs=[fixed((rows, width)), pl.BlockSpec((2, 2, owners // 4, shard, 2 * LANES), lambda h, t: (0, 0, 0, h, 0)),
                   per_head((8, LANES))],
        out_shape=[jax.ShapeDtypeStruct((rows, width), BF),
                   jax.ShapeDtypeStruct((2, 2, owners // 4, block_rows, 2 * LANES), BF),
                   jax.ShapeDtypeStruct((heads, 8, LANES), F32)],
        scratch_shapes=[pltpu.VMEM((rows, full), BF),
                        pltpu.VMEM((LANES, rows), F32), pltpu.VMEM((LANES, rows), F32),
                        pltpu.VMEM((3 * DH, rows), BF), pltpu.VMEM((DH, width), F32),
                        pltpu.VMEM((rows, width), F32)],
        compiler_params=pltpu.CompilerParams(dimension_semantics=("arbitrary", "arbitrary"),
                                             vmem_limit_bytes=63 * 2 ** 20),
        cost_estimate=pl.CostEstimate(flops=flops, bytes_accessed=rows * width * 20, transcendentals=heads * rows * rows),
        name="attention_backward",
    )(core.reshape(1), d_out, x, w, vec, kext, trig, qb, kb, v1, qp, save, scl, prob)


def key_extension(kinds, valid):
    rows = kinds.shape[0]
    lane = jnp.arange(LANES)[None, :]
    k = kinds[:, None]
    out = jnp.where((lane >= DH) & (lane < DH + 3) | (lane >= DH + 6) & (lane < DH + 9), 1.0, 0.0)
    out = jnp.where((lane == DH + 3) | (lane == DH + 4), k, out)
    out = jnp.where(lane == DH + 5, jnp.where(valid[:, None] > 0, 0.0, -1e30), out)
    return jnp.broadcast_to(out, (rows, LANES)).astype(BF)


def pack_kernel(heads, groups, *refs):
    mats, smalls, (wide_ref, kinds_ref, inner_ref, outer_ref, output_ref, out_ref, packed_ref, third_ref) = refs[:4], refs[4:16], refs[16:]
    rows, width = mats[0].shape
    for g in range(groups):
        for h in range(heads):
            at = pl.ds((g * heads + h) * DH, DH)
            value = jnp.concatenate([m[:, at] for m in mats], axis=1)
            for c in range(g, out_ref.shape[0], groups):
                out_ref[c, h * rows:(h + 1) * rows, :] = value
    pad = jnp.zeros((1, LANES - rows), F32)
    lines = [jnp.concatenate([v[...].astype(F32), pad], axis=1) for v in smalls]
    none = jnp.zeros((1, LANES), F32)
    inner = jnp.concatenate([wide_ref[...].astype(F32), jnp.zeros((1, LANES - wide_ref.shape[1]), F32)], axis=1)
    left = jnp.concatenate(lines[:8], axis=0)
    kinds = kinds_ref[...].astype(F32)
    right = jnp.concatenate(lines[8:] + [inner, kinds, none], axis=0)
    both = jnp.concatenate([left, right], axis=1).astype(BF)
    for c in range(out_ref.shape[0]):
        out_ref[c, heads * rows:, :] = both
    count = inner_ref.shape[1] // width
    for i in range(count):
        packed_ref[i * rows:(i + 1) * rows, :] = inner_ref[:, i * width:(i + 1) * width]
    packed_ref[count * rows:, :] = outer_ref[...]
    third_ref[...] = output_ref[...]


def pack(mats, smalls, wide, kinds, inner, outer, output, heads, groups, members):
    rows, width = mats[0].shape
    third = output.shape[0]
    total = inner.shape[1] // width * rows + outer.shape[0]
    return pl.pallas_call(
        functools.partial(pack_kernel, heads, groups),
        out_shape=[jax.ShapeDtypeStruct((members, heads * rows + 8, 2 * LANES), BF),
                   jax.ShapeDtypeStruct((total, width), BF), jax.ShapeDtypeStruct((third, width), BF)],
        name="pack_columns",
    )(*mats, *smalls, wide, kinds, inner, outer, output)


def unpack_kernel(heads, groups, shard, g_ref, block_ref, vecs_ref, wide_ref, vec_ref):
    owners = block_ref.shape[0]
    wide = wide_ref.shape[1] // owners
    for o in range(owners):
        t = block_ref[o].astype(F32)
        vecs_ref[:8, o * shard:(o + 1) * shard] = t[:, :shard]
        vecs_ref[8:, o * shard:(o + 1) * shard] = t[:, LANES:LANES + shard]
        wide_ref[:, o * wide:(o + 1) * wide] = t[4:5, LANES:LANES + wide]
    zeros = jnp.zeros((8, LANES - DH), F32)
    for g in range(groups):
        @pl.when(g_ref[0] == g)
        def _():
            for h in range(heads):
                part = vecs_ref[:8, (g * heads + h) * DH:(g * heads + h + 1) * DH]
                vec_ref[h] = jnp.concatenate([part, zeros], axis=1)


def unpack(block, g, heads, groups, shard, wide):
    owners, rows, _ = block.shape
    return pl.pallas_call(
        functools.partial(unpack_kernel, heads, groups, shard),
        grid=(1,),
        in_specs=[pl.BlockSpec(memory_space=pltpu.SMEM),
                  pl.BlockSpec((owners, 8, 2 * LANES), lambda i: (0, rows // 8 - 1, 0))],
        out_specs=[pl.BlockSpec((16, owners * shard), lambda i: (0, 0)), pl.BlockSpec((1, owners * wide), lambda i: (0, 0)),
                   pl.BlockSpec((heads, 8, LANES), lambda i: (0, 0, 0))],
        out_shape=[jax.ShapeDtypeStruct((16, owners * shard), F32), jax.ShapeDtypeStruct((1, owners * wide), F32),
                   jax.ShapeDtypeStruct((heads, 8, LANES), F32)],
        name="unpack_small",
    )(g.reshape(1), block)


def small_kernel(heads, groups, shard, g_ref, heads_ref, rest_ref, wide_ref, unused_ref, out_ref, table_ref):
    members = out_ref.shape[2]
    owners = 4 * members
    wide = wide_ref.shape[1] // owners
    table_ref[:6] = jnp.zeros((6, table_ref.shape[1]), F32)
    for g in range(groups):
        @pl.when(g_ref[0] == g)
        def _():
            for h in range(heads):
                table_ref[:6, (g * heads + h) * DH:(g * heads + h + 1) * DH] = heads_ref[h, :6, :DH]
    table_ref[6:12] = rest_ref[...]
    pad = jnp.zeros((8, LANES - shard), F32)
    for o in range(owners):
        left = table_ref[:8, o * shard:(o + 1) * shard]
        right = jnp.concatenate([table_ref[8:12, o * shard:(o + 1) * shard], jnp.zeros((4, LANES - shard), F32)], axis=1)
        inner = jnp.concatenate([wide_ref[:, o * wide:(o + 1) * wide], jnp.zeros((1, LANES - wide), F32)], axis=1)
        right = jnp.concatenate([right, inner, jnp.zeros((3, LANES), F32)], axis=0)
        out_ref[(o // members % 2) ^ g_ref[1], o // (2 * members), o % members] = jnp.concatenate([left, pad, right], axis=1).astype(BF)


def small_rows(block, g, head_sums, rest, wide_sums, groups, shard):
    members, rows = block.shape[2:4]
    owners = 4 * members
    heads = head_sums.shape[0]
    whole = lambda a: pl.BlockSpec(a.shape, lambda i: (0,) * a.ndim)
    return pl.pallas_call(
        functools.partial(small_kernel, heads, groups, shard),
        grid=(1,),
        in_specs=[pl.BlockSpec(memory_space=pltpu.SMEM), whole(head_sums), whole(rest), whole(wide_sums),
                  pl.BlockSpec(memory_space=pl.ANY)],
        out_specs=pl.BlockSpec((2, 2, members, 8, 2 * LANES), lambda i: (0, 0, 0, rows // 8 - 1, 0)),
        out_shape=jax.ShapeDtypeStruct(block.shape, BF),
        input_output_aliases={4: 0},
        scratch_shapes=[pltpu.VMEM((16, owners * shard), F32)],
        cost_estimate=pl.CostEstimate(flops=2 * 10 ** 10, bytes_accessed=2 ** 20, transcendentals=0),
        name="small_gradients",
    )(g, head_sums, rest, wide_sums, block)


def finish_kernel(heads, block_ref, *refs):
    outs, vectors, pair_ref, wide_ref = refs[:4], refs[4:14], refs[14], refs[15]
    groups = block_ref.shape[0] // 2
    shard = outs[0].shape[0]
    total = sum(block_ref[g, heads * shard:, :].astype(F32) for g in range(2 * groups))
    for n, i in enumerate((0, 1, 2, 5, 6, 7)):
        vectors[n][...] = total[i, :shard]
    for i in range(4):
        vectors[6 + i][...] = total[i, LANES:LANES + shard]
    pair_ref[...] = total[3:5, :shard]
    wide_ref[...] = total[4, LANES:LANES + wide_ref.shape[0]]
    for g in range(groups):
        for h in range(heads):
            part = block_ref[g, h * shard:(h + 1) * shard, :].astype(F32)
            part = part + block_ref[groups + g, h * shard:(h + 1) * shard, :].astype(F32)
            at = (g * heads + h) * DH
            for m in range(4):
                outs[m][:, at:at + DH] = part[:, m * DH:(m + 1) * DH]


def finish(block, heads, shard, width, wide):
    S = jax.ShapeDtypeStruct
    return pl.pallas_call(
        functools.partial(finish_kernel, heads),
        out_shape=[S((shard, width), F32)] * 4 + [S((shard,), F32)] * 10 + [S((2, shard), F32), S((wide,), F32)],
        name="finish_columns",
    )(block)


def row_sum_kernel(bit_ref, keep_ref, first_ref, *refs):
    bit = bit_ref[0]
    total = keep_ref[0, bit].astype(F32) + first_ref[bit].astype(F32)
    for ref in refs[:-1]:
        total = total + ref[...].astype(F32)
    refs[-1][...] = total.astype(BF)


def row_sum(bit, keep, first, *more):
    vmem = pl.BlockSpec(memory_space=pltpu.VMEM)
    return pl.pallas_call(
        row_sum_kernel,
        in_specs=[pl.BlockSpec(memory_space=pltpu.SMEM)] + [vmem] * (2 + len(more)),
        out_specs=vmem,
        out_shape=jax.ShapeDtypeStruct(first.shape[1:], BF),
        cost_estimate=pl.CostEstimate(flops=2 * 10 ** 10, bytes_accessed=2 ** 20, transcendentals=0),
        name="row_sum",
    )(bit.reshape(1), keep, first, *more)


def token_kernel(core_ref, valid_ref, mixed_ref, x_ref, og_ref, vec_ref, wide_ref,
                 inner_one, inner_two, inner_three, inner_four, outer_one, outer_two, outer_three, outer_four, third_one, third_two,
                 result_ref, first_ref, grad_ref, gi_keep, gi_send, go_keep, go_send, gt_keep, gt_send, rest_ref, gw_ref,
                 packed, wi, act, slope, normed_t, acc, gi_ref, go_ref, sems, back_sems):
    core, bit_y, bit_x = core_ref[0], core_ref[1], core_ref[2]
    seqs, width, stretch = mixed_ref.shape
    tokens = seqs * stretch
    count = wi.shape[1] // width
    members = 2 * packed.shape[1]
    block = width // count
    shard = block // members
    wide = packed.shape[3] - (count + 1) * shard
    base = count * shard
    copies = []
    for i, (src, k) in enumerate(((third_one, core), (third_two, 1 - core))):
        for y in range(2):
            copies.append(pltpu.make_async_copy(src.at[:, y], packed.at[2 * y + k, :, :, base + wide:, :], sems.at[26 + 2 * i + y]))
    sources = ((outer_one, core, bit_x), (outer_two, 1 - core, bit_x), (outer_three, core, 1 - bit_x), (outer_four, 1 - core, 1 - bit_x))
    for i, (src, k, x) in enumerate(sources):
        for y in range(2):
            copies.append(pltpu.make_async_copy(src.at[y], packed.at[2 * y + k, :, x, base:base + wide, :], sems.at[4 + 2 * i + y]))
    sources = ((inner_one, core, bit_y), (inner_two, 1 - core, bit_y), (inner_three, core, 1 - bit_y), (inner_four, 1 - core, 1 - bit_y))
    for i, (src, k, y) in enumerate(sources):
        for x in range(2):
            copies.append(pltpu.make_async_copy(src.at[x], packed.at[2 * y + k, :, x, :base, :], sems.at[12 + 2 * i + x]))
    for copy in copies:
        copy.start()
    for copy in copies[:4]:
        copy.wait()
    w_out = packed[:, :, :, base + wide:, :].astype(F32).reshape(width, width).astype(BF)
    def w_outer(j):
        return packed[j, :, :, base:base + wide, :].reshape(width, width)

    vec = vec_ref[...]
    line = lambda i: vec[i:i + 1, :]
    mean = lambda v: jnp.mean(v, axis=1, keepdims=True)
    attn = jnp.concatenate([mm(mixed_ref[b], w_out, COLS_CC) for b in range(seqs)], axis=0) + line(6)
    first = x_ref[...].astype(F32) + attn
    center = first - mean(first)
    r_one = lax.rsqrt(mean(center * center) + epsilon)
    hat_one = center * r_one
    normed = hat_one * line(7) + line(8)
    low = normed.astype(BF)
    normed_t[...] = jnp.transpose(normed).astype(BF)
    acc[...] = jnp.zeros_like(acc)

    for copy in copies[4:]:
        copy.wait()
    for i in range(count):
        wi[:, i * width:(i + 1) * width] = packed[:, :, :, i * shard:(i + 1) * shard, :].astype(F32).reshape(width, width).astype(BF)

    def forward(j, carry):
        at = pl.ds(pl.multiple_of(j * width, width), width)
        u = mm(low, wi[:, at], ROWCOL) + wide_ref[:, at]
        c = 0.7978845608028654
        sq = u * u
        t = jnp.tanh(c * u * (1.0 + 0.044715 * sq))
        half = 0.5 * (1.0 + t)
        a = (u * half).astype(BF)
        act[:, at] = a
        slope[:, at] = half + 0.5 * u * (1.0 - t * t) * (c * (1.0 + 3 * 0.044715 * sq))
        acc[...] += mm(a, w_outer(j), ROWCOL)
        return carry

    lax.fori_loop(0, count, forward, 0)
    outer = acc[...] + line(9)
    second = normed + outer
    center = second - mean(second)
    r_two = lax.rsqrt(mean(center * center) + epsilon)
    hat_two = center * r_two
    result_ref[...] = (hat_two * line(10) + line(11)).astype(BF)
    valid = valid_ref[...]
    cot = og_ref[...].astype(F32) * valid
    d_hat = cot * line(10)
    d_second = r_two * (d_hat - mean(d_hat) - hat_two * mean(d_hat * hat_two))
    d_low = d_second.astype(BF)
    total = lambda v: jnp.sum(v, axis=0, keepdims=True)
    outer_sum = total(d_low.astype(F32))
    two = [total(cot * hat_two), total(cot)]
    acc[...] = d_second

    part = wide // 2

    def inner_back(j):
        return [
            pltpu.make_async_copy(gi_ref.at[which, y, j], (gi_keep, gi_send)[which].at[y, j], back_sems.at[j, 2 * which + y])
            for which in range(2) for y in range(2)]

    def upper(which, y, j):
        low_part = pltpu.make_async_copy(go_ref.at[which, y, :, :part, :], (gt_keep, gt_send)[which].at[y], sems.at[20 + j])
        high_part = pltpu.make_async_copy(
            go_ref.at[which, y, :, part:wide, :], (go_keep, go_send)[which].at[y, :, :part, :], sems.at[30 + j])
        return low_part, high_part

    def lower(which, y):
        target = (go_keep, go_send)[which]
        return pltpu.make_async_copy(go_ref.at[which, y, :, wide:, :], target.at[y, :, part:, :], sems.at[2 * which + y])

    def backward(j, carry):
        at = pl.ds(pl.multiple_of(j * width, width), width)
        d_act = mm(d_low, w_outer(j), ROWS_CC)
        d_in = d_act * slope[:, at]
        d_in_low = d_in.astype(BF)
        gw_ref[:, at] = total(d_in_low.astype(F32))
        acc[...] += mm(d_in_low, wi[:, at], ROWS_CC)
        go = mm(act[:, at], d_low, COLS_CC)
        which = (j % 2) ^ core
        go_ref[which, j // 2, :, :wide, :] = go.astype(BF).reshape(members, wide, width)

        @pl.when(which == 0)
        def _():
            for copy in upper(0, j // 2, j):
                copy.start()

        @pl.when(which == 1)
        def _():
            for copy in upper(1, j // 2, j):
                copy.start()

        for b in range(count):
            gi = mm(normed_t[b * block:(b + 1) * block, :], d_in_low, ROWCOL)
            gi_ref[(b % 2) ^ core, b // 2, j] = gi.reshape(members, shard, width).astype(BF)
        for copy in inner_back(j):
            copy.start()
        return carry

    lax.fori_loop(0, count, backward, 0)
    d_normed = acc[...]
    one = [total(d_normed * hat_one), total(d_normed)]
    d_hat = d_normed * line(7)
    d_first = r_one * (d_hat - mean(d_hat) - hat_one * mean(d_hat * hat_one))
    first_ref[...] = d_first
    a_low = d_first.astype(BF)
    rest_ref[...] = jnp.concatenate([total(a_low.astype(F32))] + one + [outer_sum] + two, axis=0)
    grad = mm(w_out, a_low, ROWS_CC).astype(BF)
    span = grad_ref.shape[1] - 8
    groups = width // span
    lane = lax.broadcasted_iota(jnp.int32, (1, stretch), 1)
    sums = jnp.zeros((1, stretch), F32)
    everything = lambda v: jnp.sum(jnp.sum(v, axis=0, keepdims=True), axis=1, keepdims=True)
    for b in range(seqs):
        at = slice(b * stretch, (b + 1) * stretch)
        for i, v in enumerate((first, attn, outer)):
            sums = jnp.where(lane == 3 * b + i, everything(v[at] * v[at] * valid[at]), sums)
    high = sums.astype(BF).astype(F32)
    riders = jnp.concatenate([high, sums - high, jnp.zeros((6, stretch), F32)], axis=0).astype(BF)
    for b in range(seqs):
        for g in range(groups):
            grad_ref[b * groups + g, :span, :] = grad[g * span:(g + 1) * span, b * stretch:(b + 1) * stretch]
            grad_ref[b * groups + g, span:, :] = riders
    out = mm(mixed_ref[0], a_low[:stretch], ROWCOL)
    for b in range(1, seqs):
        out += mm(mixed_ref[b], a_low[b * stretch:(b + 1) * stretch], ROWCOL)
    for b in range(count):
        for i in range(members):
            at = b * block + i * shard
            go_ref[(b % 2) ^ core, b // 2, i, wide:, :] = out[at:at + shard, :].astype(BF)
    lowers = [lower(which, y) for which in range(2) for y in range(2)]
    for back in lowers:
        back.start()
    for j in range(count):
        for copy in upper(0, 0, j):
            copy.wait()
    for j in range(count):
        for copy in inner_back(j):
            copy.wait()
    for back in lowers:
        back.wait()


def token_block(core, valid, mixed, x, out_grad, vectors, inner_add, inner_parts, outer_parts, third_parts, span):
    seqs, width, stretch = mixed.shape
    tokens = seqs * stretch
    ff = inner_add.shape[1]
    count = ff // width
    members = inner_parts[0].shape[0] * inner_parts[0].shape[1]
    owners = members * count
    rows = ff // owners + width // owners
    half_rows = ff // owners // 2
    base = ff // width * (width // owners)
    groups = width // span
    vmem = pl.BlockSpec(memory_space=pltpu.VMEM)
    hbm = pl.BlockSpec(memory_space=pl.ANY)
    S = jax.ShapeDtypeStruct
    return pl.pallas_call(
        token_kernel,
        in_specs=[pl.BlockSpec(memory_space=pltpu.SMEM)] + [vmem] * 6 + [hbm] * 10,
        out_specs=[vmem] * 3 + [hbm] * 6 + [vmem] * 2,
        out_shape=[S((tokens, width), BF), S((tokens, width), F32), S((seqs * groups, span + 8, stretch), BF),
                   S((2, count, members, width // owners, width), BF), S((2, count, members, width // owners, width), BF),
                   S((2, members, rows - half_rows, width), BF), S((2, members, rows - half_rows, width), BF),
                   S((2, members, half_rows, width), BF), S((2, members, half_rows, width), BF),
                   S((6, width), F32), S((1, ff), F32)],
        scratch_shapes=[pltpu.VMEM((count, members // 2, 2, (count + 1) * (width // owners) + ff // owners, width), BF), pltpu.VMEM((width, ff), BF),
                        pltpu.VMEM((tokens, ff), BF), pltpu.VMEM((tokens, ff), F32),
                        pltpu.VMEM((width, tokens), BF), pltpu.VMEM((tokens, width), F32),
                        pltpu.VMEM((2, 2, count, members, width // owners, width), BF), pltpu.VMEM((2, 2, members, rows, width), BF),
                        pltpu.SemaphoreType.DMA((34,)), pltpu.SemaphoreType.DMA((count, 4))],
        compiler_params=pltpu.CompilerParams(vmem_limit_bytes=63 * 2 ** 20),
        cost_estimate=pl.CostEstimate(flops=tokens * 2 * width * (6 * ff + 4 * width), bytes_accessed=30 * 2 ** 20, transcendentals=tokens * ff),
        name="token_block",
    )(core, valid, mixed, x, out_grad, vectors, inner_add, *inner_parts, *outer_parts, *third_parts)


def takes_head_layout(mesh):
    return dict(mesh.shape) == {DP: 4, CTX: 8}


def swap(x, axis, bit):
    count = lax.axis_size(axis)
    return lax.ppermute(x, axis, [(i, i ^ bit) for i in range(count)])


def in_order(bit, own, received, axis):
    first = jnp.where(bit == 0, own, received)
    second = jnp.where(bit == 0, received, own)
    return jnp.stack([first, second], axis=axis)


def pick(x, index, axis):
    return lax.dynamic_index_in_dim(x, index, axis, keepdims=False)


def after(x, *others):
    return lax.optimization_barrier((x,) + others)[0]


def exchange(x, along_z):
    count = lax.axis_size(CTX)
    if along_z:
        sets = [[m for m in range(count) if m % 2 == i] for i in range(2)]
    else:
        sets = [list(range(count // 2)), list(range(count // 2, count))]
    return lax.all_to_all(x, CTX, 0, 0, axis_index_groups=sets, tiled=True)


def in_z_order(pieces):
    z = lax.axis_index(CTX) // 2
    block = jnp.stack(pieces).reshape((2, 2) + pieces[0].shape)
    for axis, bit in ((1, z % 2), (0, z // 2)):
        block = jnp.where(bit == 0, block, jnp.flip(block, axis))
    return block.reshape((4,) + pieces[0].shape)


def total_low(terms):
    return sum(t.astype(F32) for t in terms).astype(BF)


def picks(terms, bit, axis):
    return [pick(t, bit, axis) for t in terms]


def head_layout(
    inputs,
    out_grad,
    lengths,
    token_types,
    query_weight,
    key_weight,
    value_weight,
    value_bias,
    position_weight,
    content_bias,
    position_bias,
    type_bias,
    type_embed,
    output_weight,
    output_bias,
    first_gain,
    first_shift,
    inner_weight,
    inner_bias,
    outer_weight,
    outer_bias,
    second_gain,
    second_shift,
):
    d, c = lax.axis_index(DP), lax.axis_index(CTX)
    members = lax.axis_size(CTX)
    devices = lax.axis_size(DP) * members
    seqs, stretch, width = inputs.shape
    seq_len = stretch * members
    groups = members // seqs
    heads = H // groups
    span = heads * DH
    half = width // 2
    shard = width // devices
    inner_shard = inner_bias.shape[0]
    s, g = c // groups, c % groups
    bit_x = c % 2
    core, bit_y = d % 2, d // 2

    x_send = pick(inputs, 1 - s, 0)
    own = pick(inputs, s, 0)

    smalls = (
        content_bias,
        position_bias,
        type_bias,
        value_bias,
        type_embed[0],
        type_embed[1],
        output_bias,
        first_gain,
        first_shift,
        outer_bias,
        second_gain,
        second_shift,
    )
    stacked, packed, third = pack(
        (after(query_weight, x_send), key_weight, value_weight, position_weight),
        tuple(v.reshape(1, shard) for v in smalls),
        inner_bias.reshape(1, inner_shard),
        token_types,
        inner_weight,
        outer_weight,
        output_weight,
        heads,
        groups,
        members,
    )
    cut = (inner_weight.shape[1] // width) * shard
    block = lax.all_to_all(stacked, CTX, 0, 0, tiled=True)
    x_other = swap(x_send, CTX, 4)
    packed, third = after((packed, third), x_other)
    third_y = swap(third, DP, 2)
    packed_z = [swap(packed, CTX, 2 * m) for m in (1, 2, 3)]
    lines = block[:, heads * shard + 5 : heads * shard + 5 + seqs, LANES:]
    kind_seq = pick(lines, s, 1).reshape(2, groups, stretch).transpose(1, 0, 2)
    kind_seq = kind_seq.reshape(seq_len).astype(F32)
    x_pair = in_order(s, own, after(x_other, block), 0)
    x_pair = jnp.broadcast_to(x_pair[None], (groups, 2, stretch, width))
    x_all = exchange(x_pair, False)
    block = block[None]
    block = in_order(bit_y, block, swap(block, DP, 2), 0)
    third = in_order(bit_y, third, after(third_y, block), 0)
    third_x = swap(third, CTX, 1)
    packed_z = after(packed_z, x_pair, block, third)
    packed_z = in_z_order([packed] + packed_z)
    inner_block, outer_block = packed_z[:, :cut], packed_z[:, cut:]
    inner_x, outer_y = swap(inner_block, CTX, 1), swap(outer_block, DP, 2)
    block = in_order(core, block, after(swap(block, DP, 1), inner_block, outer_block), 1)
    block = block.reshape((devices,) + stacked.shape[1:])
    x_seq = after(x_all, block).reshape(seq_len, width)

    exponent = 2.0 * jnp.arange(half, dtype=F32) / width
    rates = (10000.0 ** (-exponent))[None, :]
    owners = jnp.arange(members, dtype=jnp.int32).reshape(2, groups).T.reshape(-1)
    starts = (owners * stretch).astype(F32)[:, None] * rates
    steps = jnp.arange(stretch, dtype=F32)[:, None] * rates
    starts, steps = lax.optimization_barrier((starts, steps))
    cos_a, sin_a = jnp.cos(starts)[:, None], jnp.sin(starts)[:, None]
    cos_b, sin_b = jnp.cos(steps)[None], jnp.sin(steps)[None]
    trig = jnp.concatenate(
        [cos_a * cos_b - sin_a * sin_b, sin_a * cos_b + cos_a * sin_b], axis=2
    ).reshape(seq_len, width).astype(BF)
    slots = owners[:, None] * stretch + jnp.arange(stretch, dtype=jnp.int32)[None, :]
    key_valid = (slots.reshape(-1) < pick(lengths, s, 0)).astype(F32)
    kext = key_extension(kind_seq, key_valid)

    vectors, inner_add, vec = unpack(block, g, heads, groups, shard, inner_shard)

    saved = attention_forward(x_seq, block, 0, 1, heads, vec, kext, trig)
    inner_x, outer_y, third_x = after((inner_x, outer_y, third_x), saved[0])
    third = in_order(bit_x, third, third_x, 1)
    inner_block = in_order(bit_x, inner_block, inner_x, 0)
    outer_block = in_order(bit_y, outer_block, outer_y, 0)
    inner_y, outer_x = swap(inner_block, DP, 2), swap(outer_block, CTX, 1)
    third_z = [swap(third, CTX, 2 * m) for m in (1, 2, 3)]
    saved = attention_forward(
        x_seq,
        block,
        1,
        heads - 1,
        heads,
        after(vec, inner_block, outer_block, third),
        kext,
        trig,
        saved,
    )
    att, q_block, kb, v1, qp, save, scl, w_heads, prob = saved
    third_z = after(third_z, att)
    att = after(att, third_z).reshape(members, span, stretch)
    mixed = lax.all_to_all(att, CTX, 0, 0, tiled=True).reshape(seqs, width, stretch)
    inner_block, outer_block = after((inner_block, outer_block), att)
    inner_far, outer_far = swap(inner_block, DP, 1), swap(outer_block, DP, 1)
    third = in_z_order([third] + third_z)
    third_parts = (third, swap(third, DP, 1))
    mixed = after(mixed, third_parts[1], inner_far, outer_far)
    inner_y, outer_x = after((inner_y, outer_x), mixed)
    inner_parts = (inner_block, inner_far, inner_y, swap(inner_y, DP, 1))
    outer_parts = (outer_block, outer_far, outer_x, swap(outer_x, DP, 1))

    own_slots = c * stretch + jnp.arange(stretch, dtype=jnp.int32)
    row_valid = (own_slots[None, :] < lengths[:, None]).astype(F32)
    result, first_grad, mixed_grad, inner_keep, inner_send, outer_keep, outer_send, third_keep, third_send, rest, wide = (
        token_block(
            jnp.stack([core, bit_y, bit_x]),
            row_valid.reshape(-1, 1),
            mixed,
            inputs.reshape(-1, width),
            out_grad.reshape(-1, width),
            vectors,
            inner_add,
            inner_parts,
            outer_parts,
            third_parts,
            span,
        )
    )
    result = result.reshape(inputs.shape)
    first_grad = first_grad.reshape(inputs.shape)

    d_out = lax.all_to_all(mixed_grad, CTX, 0, 0, tiled=True)
    z = c // 2
    first_half = inner_shard // 2
    third_terms = [third_keep, swap(third_send, DP, 1)]
    inner_send, outer_send = after((inner_send, outer_send), third_terms[1])
    inner_terms = [inner_keep, swap(inner_send, DP, 1)]
    inner_terms = [t.reshape(2, -1, 4, 2, shard, width) for t in inner_terms]
    third_terms = [t.reshape(2, 4, 2, first_half, width) for t in third_terms]
    outer_terms = [outer_keep, swap(outer_send, DP, 1)]
    outer_terms = [t.reshape(2, 4, 2, first_half + shard, width) for t in outer_terms]
    third_send = [total_low(picks(third_terms, z ^ m, 1)) for m in (1, 2, 3)]
    third_z = [swap(third_send[m - 1], CTX, 2 * m) for m in (1, 2, 3)]
    inner_terms[1] = after(inner_terms[1], *third_send)
    inner_send = total_low(picks(inner_terms, 1 - bit_y, 0))
    inner_y = swap(inner_send, DP, 2)
    outer_terms[1] = after(outer_terms[1], inner_send)
    outer_send = total_low(picks(outer_terms, 1 - bit_x, 2))
    outer_x = swap(outer_send, CTX, 1)
    d_out = after(d_out, inner_send, outer_send, *third_send)
    d_blocks = d_out.reshape(2, groups, span + 8, stretch)

    d_x, w_grad, head_sums = attention_backward(
        core,
        d_blocks,
        x_seq,
        w_heads,
        vec,
        kext,
        trig,
        q_block,
        kb,
        v1,
        qp,
        save,
        scl,
        prob,
        devices,
        heads * shard + 8,
    )
    d_x, w_grad, head_sums, inner_y, outer_x, third_z = lax.optimization_barrier(
        (d_x, w_grad, head_sums, inner_y, outer_x, third_z)
    )
    d_x = exchange(d_x.reshape(groups, 2, stretch, width), False)
    w_both = small_rows(w_grad, jnp.stack([g, core]), head_sums, rest, wide, groups, shard)
    w_far = swap(w_both[1], DP, 1)
    outer_x, inner_y, third_z = after((outer_x, inner_y, third_z), w_both)
    outer_terms = picks(outer_terms, bit_x, 2) + [outer_x]
    outer_send = [total_low(picks(outer_terms, z ^ m, 1)) for m in (1, 2, 3)]
    outer_z = [swap(outer_send[m - 1], CTX, 2 * m) for m in (1, 2, 3)]
    inner_terms = picks(inner_terms, bit_y, 0) + [inner_y]
    inner_send = total_low(picks(inner_terms, 1 - bit_x, 2))
    inner_x = swap(inner_send, CTX, 1)
    w_far = after(w_far, inner_send, *outer_send)
    block_send = row_sum(1 - bit_y, w_both, w_far)
    block_y = swap(block_send, DP, 2)

    d_x_send = jnp.sum(pick(d_x, 1 - s, 1).astype(F32), axis=0).astype(BF)
    d_x_z = swap(d_x_send, CTX, 4)
    block = row_sum(bit_y, w_both, w_far, after(block_y, d_x_send))
    inner_sum = total_low(picks(inner_terms, bit_x, 2) + [after(inner_x, block)])
    third_terms = picks(third_terms, z, 1) + after(third_z, block)
    third_send = total_low(picks(third_terms, 1 - bit_y, 0))
    third_y = swap(third_send, DP, 2)
    block = lax.all_to_all(block, CTX, 0, 0, tiled=True)
    inner_send = [pick(inner_sum, z ^ m, 1) for m in (1, 2, 3)]
    inner_z = [swap(inner_send[m - 1], CTX, 2 * m) for m in (1, 2, 3)]
    outer_z = after(outer_z, *inner_send)
    outer_terms = picks(outer_terms, z, 1) + outer_z
    outer_y = swap(total_low(picks(outer_terms, 1 - bit_y, 0)), DP, 2)
    third_terms = picks(third_terms, bit_y, 0) + [after(third_y, *inner_send)]
    third_x = swap(total_low(picks(third_terms, 1 - bit_x, 0)), CTX, 1)
    third_own = sum(t.astype(F32) for t in picks(third_terms, bit_x, 0) + [third_x])
    outer_sum = sum(t.astype(F32) for t in picks(outer_terms, bit_y, 0) + [outer_y])
    outer_own = jnp.concatenate([third_own, outer_sum[:first_half]], axis=0)
    output_own = outer_sum[first_half:]
    finished = finish(block, heads, shard, width, inner_shard)
    query_own, key_own, value_own, position_own = finished[:4]
    v = finished[4:14]
    inner_z = after(inner_z, query_own)
    inner_own = sum(t.astype(F32) for t in [pick(inner_sum, z, 1)] + inner_z)
    inner_own = jnp.concatenate(list(inner_own), axis=1)
    d_x_own = jnp.sum(pick(d_x, s, 1).astype(F32), axis=0)
    input_terms = in_order(s, d_x_own, after(d_x_z, query_own).astype(F32), 0)
    input_grad = (first_grad + input_terms).astype(BF)
    sums_all = jnp.sum(d_out[:, span : span + 2].astype(F32), axis=(0, 1))
    sums_all = sums_all[: 3 * seqs].reshape(seqs, 3)
    mean_squares = sums_all / (lengths.astype(F32)[:, None] * width)
    return (
        result,
        input_grad,
        query_own,
        key_own,
        value_own,
        v[3],
        position_own,
        v[0],
        v[1],
        v[2],
        finished[14],
        output_own,
        v[4],
        v[5],
        v[6],
        inner_own,
        finished[15],
        outer_own,
        v[7],
        v[8],
        v[9],
        mean_squares,
    )


def solution(mesh):
    in_specs = (
        P(DP, CTX, None),
        P(DP, CTX, None),
        P(DP),
        P(DP, CTX),
        P(ALL, None),
        P(ALL, None),
        P(ALL, None),
        P(ALL),
        P(ALL, None),
        P(ALL),
        P(ALL),
        P(ALL),
        P(None, ALL),
        P(ALL, None),
        P(ALL),
        P(ALL),
        P(ALL),
        P(ALL, None),
        P(ALL),
        P(ALL, None),
        P(ALL),
        P(ALL),
        P(ALL),
    )
    out_specs = (
        P(DP, CTX, None),
        P(DP, CTX, None),
        P(ALL, None),
        P(ALL, None),
        P(ALL, None),
        P(ALL),
        P(ALL, None),
        P(ALL),
        P(ALL),
        P(ALL),
        P(None, ALL),
        P(ALL, None),
        P(ALL),
        P(ALL),
        P(ALL),
        P(ALL, None),
        P(ALL),
        P(ALL, None),
        P(ALL),
        P(ALL),
        P(ALL),
        P(DP, None),
    )
    body = head_layout if takes_head_layout(mesh) else per_device
    return jax.shard_map(
        body, mesh=mesh, in_specs=in_specs, out_specs=out_specs, check_vma=False
    )
```
